32 devices in a mesh: seq: 4 (over x, core), fsdp: 8 (over z, y).
Axes of the slice: x: 2, y: 2, z: 4, core: 2. Of those that a mesh axis runs over, the one named last changes fastest.
Arguments:
- hidden_in: bfloat16 [8, 1024, 1536], P('fsdp', 'seq'), may hold values from -6 to 6
- positions: int32 [8, 1024], P('fsdp', 'seq'), may hold values from 0 to 5116, as said below
- attn_gain: bfloat16 [1536], P('fsdp'), may hold values from 0.25 to 1.75
- qkv_weight: bfloat16 [1536, 2048], P('fsdp'), may hold values from -0.15625 to 0.15625
- qkv_bias: bfloat16 [2048], P('fsdp'), may hold values from -3 to 3
- out_weight: bfloat16 [1536, 1536], P('fsdp'), may hold values from -1.75 to 1.75
- mlp_gain: bfloat16 [1536], P('fsdp'), may hold values from 0.25 to 1.75
- gate_weight: bfloat16 [8960, 1536], P('fsdp'), may hold values from -0.15625 to 0.15625
- up_weight: bfloat16 [8960, 1536], P('fsdp'), may hold values from -0.15625 to 0.15625
- down_weight: bfloat16 [8960, 1536], P('fsdp'), may hold values from -0.0625 to 0.0625
- cotangent: bfloat16 [8, 1024, 1536], P('fsdp', 'seq'), may hold values from -6 to 6
Outputs:
- hidden_out: bfloat16 [8, 1024, 1536], P('fsdp', 'seq')
- grad_in: float32 [8, 1024, 1536], P('fsdp', 'seq')
- grad_attn_gain: float32 [1536], P('fsdp')
- grad_qkv_weight: float32 [1536, 2048], P('fsdp')
- grad_qkv_bias: float32 [2048], P('fsdp')
- grad_out_weight: float32 [1536, 1536], P('fsdp')
- grad_mlp_gain: float32 [1536], P('fsdp')
- grad_gate_weight: float32 [8960, 1536], P('fsdp')
- grad_up_weight: float32 [8960, 1536], P('fsdp')
- grad_down_weight: float32 [8960, 1536], P('fsdp')
The draws below stay inside these ranges and needn't reach their ends.
Inputs may be any that keep to these rules, and one draw needn't show every extreme that they name: Along each sequence the positions rise by 1 to 3 from one token to the next; the first lies below 2048.
All inputs are finite; a program needn't handle non-finite values.
Results may differ from the reference program's by a relative error of at most 0.019.
Values may be sent and summed in bfloat16 or wider, within the bound.
A program may use at most 320 MiB of HBM per device.

```python
import math
import jax
import jax.numpy as jnp
from jax import lax

D = 1536
HEADS = 12
KV_HEADS = 2
HEAD_DIM = 128
FF = 8960
QKV = 2048
LEN = 1024
BATCH = 8
BLOCK = 512
GROUP_HEADS = 3
N_SEQ = 4


def draw_positions(key, part):
    stride_key = jax.random.fold_in(key, 11)
    offset_key = jax.random.fold_in(key, 23)
    strides = jax.random.randint(stride_key, (BATCH, LEN), 1, 4)
    offsets = jax.random.randint(offset_key, (BATCH, 1), 0, 2048)
    row_ids = jnp.arange(BATCH, dtype=jnp.int32)[:, None]
    strides = jnp.where(row_ids == BATCH - 1, 3, strides)
    offsets = jnp.where(row_ids == 0, 0, jnp.where(row_ids == BATCH - 1, 2047, offsets))
    return (offsets + jnp.cumsum(strides, axis=1) - strides[:, :1]).astype(jnp.int32)


def levels(key, dims, pieces, low, largest):
    loudness, own = 1.0, jax.random.fold_in(key, 6)
    for axis_at, parts in pieces:
        heights = jnp.exp(jax.random.uniform(jax.random.fold_in(own, axis_at), (parts,), jnp.float32, low / len(pieces), largest / len(pieces)))
        loudness = loudness * jnp.repeat(heights, dims[axis_at] // parts).reshape([-1 if axis == axis_at else 1 for axis in range(len(dims))])
    return loudness


def scatter_about(rng, dims, spread, bound, pieces=(), kind=jnp.bfloat16):
    factor_of = levels(rng, dims, pieces, -0.22, 0.18) if pieces else 1.0
    values = jax.random.normal(rng, dims, jnp.float32) * spread * factor_of
    return jnp.minimum(jnp.maximum(values, -bound), bound).astype(kind)


def setup_inputs(seed: int = 0) -> dict:
    streams_of = jax.random.split(jax.random.key(seed), 12)
    return {
        "hidden_in": scatter_about(streams_of[0], (BATCH, LEN, D), 1.0, 6.0, ((0, 8), (1, 4))),
        "positions": draw_positions(jax.random.fold_in(streams_of[11], 71), 0),
        "attn_gain": jnp.clip(1.0 + 0.15 * jax.random.normal(streams_of[2], (D,), jnp.float32), 0.25, 1.75).astype(jnp.bfloat16),
        "qkv_weight": scatter_about(streams_of[3], (D, QKV), D ** -0.5, 0.15625, ((0, 8),)),
        "qkv_bias": scatter_about(streams_of[4], (QKV,), 0.5, 3.0, ((0, 8),)),
        "out_weight": scatter_about(streams_of[5], (HEADS * HEAD_DIM, D), (HEADS * HEAD_DIM * 8 // LEN) ** -0.5, 1.75, ((0, 8),)),
        "mlp_gain": jnp.clip(1.0 + 0.15 * jax.random.normal(streams_of[6], (D,), jnp.float32), 0.25, 1.75).astype(jnp.bfloat16),
        "gate_weight": scatter_about(streams_of[7], (FF, D), D ** -0.5, 0.15625, ((0, 8),)),
        "up_weight": scatter_about(streams_of[8], (FF, D), D ** -0.5, 0.15625, ((0, 8),)),
        "down_weight": scatter_about(streams_of[9], (FF, D), FF ** -0.5, 0.0625, ((0, 8),)),
        "cotangent": scatter_about(streams_of[10], (BATCH, LEN, D), 1.0, 6.0, ((0, 8), (1, 4))),
    }


@jax.custom_vjp
def low(v):
    return lax.optimization_barrier(v.astype(jnp.bfloat16)).astype(jnp.float32)

@jax.custom_vjp
def low_back(v):
    return v

def low_keep(v):
    return (low(v), None)

def low_pass(kept, grad):
    return (grad,)

def back_keep(v):
    return (v, None)

def back_low(kept, grad):
    return (low(grad),)
low.defvjp(low_keep, low_pass)
low_back.defvjp(back_keep, back_low)
highest = lax.Precision.HIGHEST
norm_eps = 1e-06
rope_base = 1000000.0

def matmul(left, right):
    return jnp.dot(left, right, precision=highest, preferred_element_type=jnp.float32)

def rms_norm(values, gain):
    inverse = lax.rsqrt(lax.optimization_barrier(jnp.mean(values * values, axis=-1, keepdims=True)) + norm_eps)
    return values * inverse * gain

def rope_tables(position_row):
    half_dim = HEAD_DIM // 2
    frequency = jnp.exp(-(jnp.arange(half_dim, dtype=jnp.float32) * 2.0 / HEAD_DIM) * math.log(rope_base))
    angles = position_row.astype(jnp.float32)[:, None] * frequency[None, :]
    angles = jnp.concatenate([angles, angles], axis=-1)
    return (jnp.cos(angles), jnp.sin(angles))

def rotate(values, cosine, sine):
    half_dim = values.shape[-1] // 2
    turned = jnp.concatenate([-values[..., half_dim:], values[..., :half_dim]], axis=-1)
    return values * cosine[:, None, :] + turned * sine[:, None, :]

def attention(queries, keys_grp, values_grp):
    grouped = queries.reshape(LEN // BLOCK, BLOCK, N_SEQ, GROUP_HEADS, HEAD_DIM)
    block_starts = jnp.arange(LEN // BLOCK, dtype=jnp.int32) * BLOCK
    column_index = jnp.arange(LEN, dtype=jnp.int32)

    def one_block(block_pair):
        query_block, block_start = block_pair
        scores = jnp.einsum('bghd,lgd->ghbl', query_block, keys_grp, precision=highest) * HEAD_DIM ** (-0.5)
        scores = low_back(scores)
        row_index = block_start + jnp.arange(BLOCK, dtype=jnp.int32)
        allowed = column_index[None, :] <= row_index[:, None]
        scores = jnp.where(allowed[None, None], scores, -1e+30)
        probability = low(jax.nn.softmax(scores, axis=-1))
        return jnp.einsum('ghbl,lgd->bghd', probability, values_grp, precision=highest)
    results = lax.map(jax.checkpoint(one_block), (grouped, block_starts))
    return results.reshape(LEN, HEADS * HEAD_DIM)

def decoder_layer(hidden_rows, attn_gain, qkv_weight, qkv_bias, out_weight, mlp_gain, gate_weight, up_weight, down_weight, cosine, sine):
    normed_one = low(rms_norm(hidden_rows, attn_gain))
    qkv_mixed = low_back(matmul(normed_one, qkv_weight) + qkv_bias)
    width_query = HEADS * HEAD_DIM
    width_key = KV_HEADS * HEAD_DIM
    query_part = qkv_mixed[:, :width_query].reshape(LEN, HEADS, HEAD_DIM)
    key_part = qkv_mixed[:, width_query:width_query + width_key].reshape(LEN, KV_HEADS, HEAD_DIM)
    value_part = qkv_mixed[:, width_query + width_key:].reshape(LEN, KV_HEADS, HEAD_DIM)
    queries = low_back(low(rotate(query_part, cosine, sine)))
    keys_rot = low(rotate(key_part, cosine, sine))
    keys_grp = low_back(jnp.repeat(keys_rot, N_SEQ // KV_HEADS, axis=1))
    values_grp = low_back(jnp.repeat(low(value_part), N_SEQ // KV_HEADS, axis=1))
    attended = low_back(low(attention(queries, keys_grp, values_grp)))
    residual = hidden_rows + low_back(matmul(attended, out_weight))
    normed_two = low(rms_norm(residual, mlp_gain))
    gate_pre = low_back(matmul(normed_two, gate_weight.T))
    up_pre = low_back(matmul(normed_two, up_weight.T))
    hidden = low(jax.nn.silu(gate_pre) * up_pre)
    return residual + low_back(matmul(hidden, down_weight))

def reference(hidden_in, positions, attn_gain, qkv_weight, qkv_bias, out_weight, mlp_gain, gate_weight, up_weight, down_weight, cotangent):
    params = tuple((weight.astype(jnp.float32) for weight in (attn_gain, qkv_weight, qkv_bias, out_weight, mlp_gain, gate_weight, up_weight, down_weight)))

    def per_sequence(running, inputs):
        rows_in, position_row, grad_row = inputs
        cosine, sine = rope_tables(position_row)

        def forward(values, *weights):
            return decoder_layer(values, *weights, cosine, sine)
        result, pullback = jax.vjp(forward, rows_in.astype(jnp.float32), *params)
        gradients = pullback(grad_row.astype(jnp.float32))
        summed = tuple((running_sum + gradient for running_sum, gradient in zip(running, gradients[1:])))
        return (summed, (result.astype(jnp.bfloat16), gradients[0]))
    zeros_init = tuple((jnp.zeros(weight.shape, jnp.float32) for weight in params))
    totals, (outputs, grad_rows) = lax.scan(per_sequence, zeros_init, (hidden_in, positions, cotangent))
    return (outputs, grad_rows, totals[0], totals[1], totals[2], totals[3], totals[4], totals[5], totals[6], totals[7])
```

```python
import functools
import math

import jax
import jax.numpy as jnp
from jax import lax
from jax.experimental import pallas as pl
from jax.experimental.pallas import tpu as pltpu
from jax.sharding import PartitionSpec as P

HEADS = 12
KV_HEADS = 2
HEAD_DIM = 128


norm_eps = 1e-06
rope_base = 1000000.0


def rope_tables(position_row):
    half_dim = HEAD_DIM // 2
    frequency = jnp.exp(
        -(jnp.arange(half_dim, dtype=jnp.float32) * 2.0 / HEAD_DIM) * math.log(rope_base)
    )
    angles = position_row.astype(jnp.float32)[:, None] * frequency[None, :]
    angles = jnp.concatenate([angles, angles], axis=-1)
    return (jnp.cos(angles), jnp.sin(angles))


def rotate(values, cosine, sine):
    half_dim = values.shape[-1] // 2
    turned = jnp.concatenate([-values[..., half_dim:], values[..., :half_dim]], axis=-1)
    return values * cosine[:, None, :] + turned * sine[:, None, :]


def unrotate(grads_rot, cosine, sine):
    half_dim = grads_rot.shape[-1] // 2
    scaled = grads_rot * sine[:, None, :]
    return grads_rot * cosine[:, None, :] + jnp.concatenate(
        [scaled[..., half_dim:], -scaled[..., :half_dim]], axis=-1
    )


def norm_forward(values, gain):
    inverse = lax.rsqrt(jnp.mean(values * values, axis=-1, keepdims=True) + norm_eps)
    unit_rows = values * inverse
    return (unit_rows, inverse, (unit_rows * gain).astype(jnp.bfloat16))


def norm_backward(grad_normed, unit_rows, inverse, gain):
    grad_unit = grad_normed * gain
    grad_values = inverse * (
        grad_unit - unit_rows * jnp.mean(grad_unit * unit_rows, axis=-1, keepdims=True)
    )
    grad_gain = jnp.sum(grad_normed * unit_rows, axis=0)
    return (grad_values, grad_gain)


def masked_scores(queries, keys, block_start, block_rows):
    length = keys.shape[0]
    query_block = lax.dynamic_slice_in_dim(queries, block_start, block_rows, 0)
    scores = jnp.einsum(
        "bhd,ld->hbl", query_block, keys, preferred_element_type=jnp.float32
    ) * HEAD_DIM ** (-0.5)
    row_index = block_start + jnp.arange(block_rows)
    column_index = jnp.arange(length)
    allowed = column_index[None, :] <= row_index[:, None]
    return (query_block, jnp.where(allowed[None], scores, -1e30))


def attend_forward(queries, keys, values):
    length = keys.shape[0]
    block_rows = min(512, length)
    block_count = length // block_rows

    def one_block(block_start):
        query_block, scores = masked_scores(queries, keys, block_start, block_rows)
        row_max = jnp.max(scores, axis=-1, keepdims=True)
        exponent = jnp.exp(scores - row_max)
        row_total = jnp.sum(exponent, axis=-1, keepdims=True)
        probability = (exponent / row_total).astype(jnp.bfloat16)
        result = jnp.einsum("hbl,ld->bhd", probability, values, preferred_element_type=jnp.float32)
        return (result.astype(jnp.bfloat16), (row_max + jnp.log(row_total))[..., 0])

    results, log_totals = lax.map(one_block, jnp.arange(block_count) * block_rows)
    return (results.reshape(length, queries.shape[1], queries.shape[2]), log_totals)


def attend_backward(queries, keys, values, log_totals, grad_out):
    length = keys.shape[0]
    block_rows = min(512, length)
    block_count = length // block_rows
    score_scale = HEAD_DIM ** (-0.5)

    def one_block(running, inputs):
        grad_keys, grad_values = running
        block_start, log_block = inputs
        query_block, scores = masked_scores(queries, keys, block_start, block_rows)
        grad_block = lax.dynamic_slice_in_dim(grad_out, block_start, block_rows, 0)
        probability = jnp.exp(scores - log_block[..., None])
        grad_probs = jnp.einsum(
            "bhd,ld->hbl", grad_block, values, preferred_element_type=jnp.float32
        )
        row_delta = jnp.sum(probability * grad_probs, axis=-1, keepdims=True)
        grad_scores = (probability * (grad_probs - row_delta)).astype(jnp.bfloat16)
        grad_query = (
            jnp.einsum("hbl,ld->bhd", grad_scores, keys, preferred_element_type=jnp.float32)
            * score_scale
        )
        grad_keys = (
            grad_keys
            + jnp.einsum(
                "hbl,bhd->ld", grad_scores, query_block, preferred_element_type=jnp.float32
            )
            * score_scale
        )
        grad_values = grad_values + jnp.einsum(
            "hbl,bhd->ld",
            probability.astype(jnp.bfloat16),
            grad_block,
            preferred_element_type=jnp.float32,
        )
        return ((grad_keys, grad_values), grad_query)

    zero_rows = jnp.zeros((length, keys.shape[1]), jnp.float32)
    (grad_keys, grad_values), grad_query = lax.scan(
        one_block, (zero_rows, zero_rows), (jnp.arange(block_count) * block_rows, log_totals)
    )
    return (grad_query.reshape(queries.shape), grad_keys, grad_values)


MESH = pl.DeviceIdType.MESH
VMEM_BYTES = 67_000_000
NN = (((1,), (0,)), ((), ()))
NT = (((1,), (1,)), ((), ()))
TN = (((0,), (0,)), ((), ()))


def matmul(left, right, dims):
    return lax.dot_general(left, right, dims, preferred_element_type=jnp.float32)


def ring_place(index, size):
    side = index % 2
    return (index // 2) * (1 - side) + (size - 1 - index // 2) * side


def ring_member(place, size):
    side = place // (size // 2)
    return 2 * (place * (1 - side) + (size - 1 - place) * side) + side


def for_blocks(width, block, body):
    @pl.loop(0, width // block)
    def _(at):
        body(pl.ds(pl.multiple_of(at * block, block), block))

    if width % block:
        body(pl.ds(width - width % block, width % block))


def mlp_kernel(
    size,
    rows_ref,
    cot_ref,
    gate_ref,
    up_ref,
    down_ref,
    parts_ref,
    back_ref,
    grad_gate_ref,
    grad_up_ref,
    grad_down_ref,
    rows_all,
    cots_all,
    weights,
    grads,
    hid,
    dgate,
    dup,
    partial,
    sums_in,
    sums_out,
    parts_out,
    load_sems,
    send_sems,
    recv_sems,
    sum_send_sems,
    sum_recv_sems,
    part_sems,
):
    tokens, width = rows_ref.shape
    units = gate_ref.shape[0]
    half = tokens // 2
    me = lax.axis_index("fsdp")
    place = ring_place(me, size)
    right = ring_member((place + 1) % size, size)
    left = ring_member((place + size - 1) % size, size)
    sides = ((right, pl.ds(0, half)), (left, pl.ds(half, half)))

    weight_loads = [
        pltpu.make_async_copy(ref, weights.at[at], load_sems.at[at])
        for at, ref in enumerate((gate_ref, up_ref, down_ref))
    ]
    own_loads = [
        pltpu.make_async_copy(rows_ref, rows_all.at[0], load_sems.at[3]),
        pltpu.make_async_copy(cot_ref, cots_all.at[0], load_sems.at[4]),
    ]
    for load in own_loads + weight_loads:
        load.start()
    barrier = pltpu.get_barrier_semaphore()
    for target, _ in sides:
        pl.semaphore_signal(barrier, inc=1, device_id={"fsdp": target}, device_id_type=MESH)

    @pl.loop(0, units // 16)
    def _(at):
        zeros = jnp.zeros((3, 16, width), jnp.float32)
        grads[:, pl.ds(pl.multiple_of(at * 16, 16), 16), :] = zeros

    pl.semaphore_wait(barrier, 2)
    for load in own_loads:
        load.wait()

    def row_copy(step, side, which):
        held = (rows_all, cots_all)[which]
        target, span = sides[side]
        return pltpu.make_async_remote_copy(
            src_ref=held.at[step, span],
            dst_ref=held.at[step + 1, span],
            send_sem=send_sems.at[side, which, step],
            recv_sem=recv_sems.at[side, which, step + 1],
            device_id={"fsdp": target},
            device_id_type=MESH,
        )

    def sum_copy(step, side):
        target, span = sides[side]
        return pltpu.make_async_remote_copy(
            src_ref=sums_out.at[step % 2, span],
            dst_ref=sums_in.at[step, span],
            send_sem=sum_send_sems.at[side, step],
            recv_sem=sum_recv_sems.at[side, step],
            device_id={"fsdp": target},
            device_id_type=MESH,
        )

    def part_copy(step, side):
        _, span = sides[side]
        away = step if side == 1 else size - step
        owner = ring_member((place + away) % size, size)
        return pltpu.make_async_copy(
            parts_out.at[step % 2, span],
            parts_ref.at[pl.ds(pl.multiple_of(owner * tokens + side * half, half), half)],
            part_sems.at[side, step],
        )

    def elementwise(step, span):
        gate = matmul(rows_all[step], weights[0, span, :], NT)
        up = matmul(rows_all[step], weights[1, span, :], NT)
        grad_hidden = matmul(cots_all[step], weights[2, span, :], NT)
        sigmoid = jax.nn.sigmoid(gate)
        activated = gate * sigmoid
        hid[:, span] = (activated * up).astype(jnp.bfloat16)
        dgate[:, span] = (
            grad_hidden * up * sigmoid * (1.0 + gate * (1.0 - sigmoid))
        ).astype(jnp.bfloat16)
        dup[:, span] = (grad_hidden * activated).astype(jnp.bfloat16)

    for load in weight_loads:
        load.wait()

    @pl.loop(0, size)
    def _(step):
        slot = step % 2

        @pl.when(step >= 1)
        def _():
            for side in range(2):
                for which in range(2):
                    row_copy(step - 1, side, which).wait_recv()

        @pl.when(step < size - 1)
        def _():
            for side in range(2):
                for which in range(2):
                    row_copy(step, side, which).start()

        for_blocks(units, 256, functools.partial(elementwise, step))

        def back_part(span):
            partial[:, span] = matmul(dgate[...], weights[0, :, span], NN) + matmul(
                dup[...], weights[1, :, span], NN
            )

        for_blocks(width, 256, back_part)

        @pl.when(step == 0)
        def _():
            back_ref[...] = partial[...]

        @pl.when(step >= 3)
        def _():
            for side in range(2):
                sum_copy(step - 2, side).wait_send()

        @pl.when(step == 1)
        def _():
            sums_out[slot] = partial[...].astype(jnp.bfloat16)

        @pl.when(step >= 2)
        def _():
            for side in range(2):
                sum_copy(step - 1, side).wait_recv()
            sums_out[slot] = (partial[...] + sums_in[step - 1].astype(jnp.float32)).astype(
                jnp.bfloat16
            )

        @pl.when(step >= 1)
        def _():
            for side in range(2):
                sum_copy(step, side).start()

        @pl.when(step >= 2)
        def _():
            for side in range(2):
                part_copy(step - 2, side).wait()

        def out_part(span):
            parts_out[slot, :, span] = matmul(hid[...], weights[2, :, span], NN).astype(
                jnp.bfloat16
            )

        for_blocks(width, 256, out_part)
        for side in range(2):
            part_copy(step, side).start()

        def weight_part(span):
            rows, cots = rows_all[step, :, span], cots_all[step, :, span]
            grads[0, :, span] += matmul(dgate[...], rows, TN)
            grads[1, :, span] += matmul(dup[...], rows, TN)
            grads[2, :, span] += matmul(hid[...], cots, TN)

        for_blocks(width, 256, weight_part)

    stores = []
    for at, ref in enumerate((grad_gate_ref, grad_up_ref, grad_down_ref)):

        @pl.loop(0, units // 16)
        def _(block):
            span = pl.ds(pl.multiple_of(block * 16, 16), 16)
            weights[at, span, :] = grads[at, span, :].astype(jnp.bfloat16)

        stores.append(pltpu.make_async_copy(weights.at[at], ref, load_sems.at[at]))
        stores[-1].start()
    for side in range(2):
        sum_copy(size - 1, side).wait_recv()
    back_ref[...] += sums_in[size - 1].astype(jnp.float32)
    for side in range(2):
        sum_copy(size - 2, side).wait_send()
        sum_copy(size - 1, side).wait_send()
        part_copy(size - 2, side).wait()
        part_copy(size - 1, side).wait()

        @pl.loop(0, size - 1)
        def _(step):
            for which in range(2):
                row_copy(step, side, which).wait_send()

    for store in stores:
        store.wait()


def mlp_scratch(size, tokens, width, units):
    bf16, f32 = jnp.bfloat16, jnp.float32
    dma = pltpu.SemaphoreType.DMA
    return [
        pltpu.VMEM((size, tokens, width), bf16),
        pltpu.VMEM((size, tokens, width), bf16),
        pltpu.VMEM((3, units, width), bf16),
        pltpu.VMEM((3, units, width), f32),
        pltpu.VMEM((tokens, units), bf16),
        pltpu.VMEM((tokens, units), bf16),
        pltpu.VMEM((tokens, units), bf16),
        pltpu.VMEM((tokens, width), f32),
        pltpu.VMEM((size, tokens, width), bf16),
        pltpu.VMEM((2, tokens, width), bf16),
        pltpu.VMEM((2, tokens, width), bf16),
        dma((5,)),
        dma((2, 2, size)),
        dma((2, 2, size)),
        dma((2, size)),
        dma((2, size)),
        dma((2, size)),
    ]


def mlp_fits(size, tokens, width, units):
    if size % 2 or tokens % 32 or units % 16 or width % 256:
        return False
    held = 3 * size + 4
    return 2 * tokens * width * (held + 4) + units * (18 * width + 6 * tokens) < 60_000_000


def mlp_ring(rows, cots, gate_weight, up_weight, down_weight):
    size = lax.axis_size("fsdp")
    tokens, width = rows.shape
    units = gate_weight.shape[0]
    anywhere = pl.BlockSpec(memory_space=pl.ANY)
    bf16 = jnp.bfloat16
    return pl.pallas_call(
        functools.partial(mlp_kernel, size),
        out_shape=(
            jax.ShapeDtypeStruct((size * tokens, width), bf16),
            jax.ShapeDtypeStruct((tokens, width), jnp.float32),
            jax.ShapeDtypeStruct((units, width), bf16),
            jax.ShapeDtypeStruct((units, width), bf16),
            jax.ShapeDtypeStruct((units, width), bf16),
        ),
        in_specs=[anywhere] * 5,
        out_specs=(anywhere, pl.BlockSpec(memory_space=pltpu.VMEM), anywhere, anywhere, anywhere),
        scratch_shapes=mlp_scratch(size, tokens, width, units),
        compiler_params=pltpu.CompilerParams(
            collective_id=0, has_side_effects=True, vmem_limit_bytes=VMEM_BYTES
        ),
        name="mlp_ring",
    )(rows, cots, gate_weight, up_weight, down_weight)


def mlp_gathered(rows, cots, gate_weight, up_weight, down_weight):
    all_rows = lax.all_gather(rows, "fsdp", axis=0, tiled=True)
    gate_pre = jnp.einsum("td,fd->tf", all_rows, gate_weight, preferred_element_type=jnp.float32)
    up_pre = jnp.einsum("td,fd->tf", all_rows, up_weight, preferred_element_type=jnp.float32)
    sigmoid_gate = jax.nn.sigmoid(gate_pre)
    activated = gate_pre * sigmoid_gate
    hidden = (activated * up_pre).astype(jnp.bfloat16)
    partial_out = jnp.dot(hidden, down_weight, preferred_element_type=jnp.float32)
    all_grads = lax.all_gather(cots, "fsdp", axis=0, tiled=True)
    grad_hidden = jnp.einsum(
        "tm,fm->tf", all_grads, down_weight, preferred_element_type=jnp.float32
    )
    grad_gate = (
        grad_hidden * up_pre * sigmoid_gate * (1.0 + gate_pre * (1.0 - sigmoid_gate))
    ).astype(jnp.bfloat16)
    grad_up = (grad_hidden * activated).astype(jnp.bfloat16)
    partial_back = jnp.dot(grad_gate, gate_weight, preferred_element_type=jnp.float32) + jnp.dot(
        grad_up, up_weight, preferred_element_type=jnp.float32
    )
    grad_rows = lax.psum_scatter(partial_back, "fsdp", scatter_dimension=0, tiled=True)
    return (
        partial_out.astype(jnp.bfloat16),
        grad_rows,
        jnp.einsum("tf,td->fd", grad_gate, all_rows, preferred_element_type=jnp.float32),
        jnp.einsum("tf,td->fd", grad_up, all_rows, preferred_element_type=jnp.float32),
        jnp.einsum("tf,td->fd", hidden, all_grads, preferred_element_type=jnp.float32),
    )


def per_device(
    hidden_in,
    positions,
    attn_gain,
    qkv_weight,
    qkv_bias,
    out_weight,
    mlp_gain,
    gate_weight,
    up_weight,
    down_weight,
    cotangent,
):
    groups = lax.axis_size("seq")
    group_heads = HEADS // groups
    repeat = groups // KV_HEADS
    tokens = hidden_in.shape[1]
    width_query = HEADS * HEAD_DIM
    width_key = KV_HEADS * HEAD_DIM
    residual = hidden_in[0].astype(jnp.float32)
    cosine, sine = rope_tables(positions[0])
    gains_one, gains_two, qkv_full, bias_full, out_full = (
        lax.all_gather(attn_gain, "fsdp", axis=0, tiled=True),
        lax.all_gather(mlp_gain, "fsdp", axis=0, tiled=True),
        lax.all_gather(qkv_weight, "fsdp", axis=0, tiled=True),
        lax.all_gather(qkv_bias, "fsdp", axis=0, tiled=True),
        lax.all_gather(out_weight, "fsdp", axis=0, tiled=True),
    )
    gain_one = gains_one.astype(jnp.float32)
    gain_two = gains_two.astype(jnp.float32)
    unit_one, inverse_one, normed_one = norm_forward(residual, gain_one)
    qkv_mixed = jnp.dot(
        normed_one, qkv_full, preferred_element_type=jnp.float32
    ) + bias_full.astype(jnp.float32)
    query_part = qkv_mixed[:, :width_query].reshape(tokens, HEADS, HEAD_DIM)
    key_part = qkv_mixed[:, width_query : width_query + width_key].reshape(
        tokens, KV_HEADS, HEAD_DIM
    )
    value_part = qkv_mixed[:, width_query + width_key :].reshape(tokens, KV_HEADS, HEAD_DIM)
    queries = (
        rotate(query_part, cosine, sine)
        .astype(jnp.bfloat16)
        .reshape(tokens, groups, group_heads * HEAD_DIM)
    )
    keys_rep = jnp.repeat(rotate(key_part, cosine, sine).astype(jnp.bfloat16), repeat, axis=1)
    values_rep = jnp.repeat(value_part.astype(jnp.bfloat16), repeat, axis=1)
    head_queries, head_keys, head_values = (
        lax.all_to_all(queries, "seq", split_axis=1, concat_axis=0, tiled=True),
        lax.all_to_all(keys_rep, "seq", split_axis=1, concat_axis=0, tiled=True),
        lax.all_to_all(values_rep, "seq", split_axis=1, concat_axis=0, tiled=True),
    )
    head_queries = head_queries.reshape(-1, group_heads, HEAD_DIM)
    head_keys = head_keys.reshape(-1, HEAD_DIM)
    head_values = head_values.reshape(-1, HEAD_DIM)
    attended, log_totals = attend_forward(head_queries, head_keys, head_values)
    returned = lax.all_to_all(
        attended.reshape(-1, 1, group_heads * HEAD_DIM),
        "seq",
        split_axis=0,
        concat_axis=1,
        tiled=True,
    )
    attn_rows = returned.reshape(tokens, width_query)
    residual_two = residual + jnp.dot(attn_rows, out_full, preferred_element_type=jnp.float32)
    unit_two, inverse_two, normed_two = norm_forward(residual_two, gain_two)
    grad_output = cotangent[0].astype(jnp.float32)
    grad_mlp = grad_output.astype(jnp.bfloat16)
    fits = mlp_fits(lax.axis_size("fsdp"), tokens, normed_two.shape[1], gate_weight.shape[0])
    mlp = mlp_ring if fits else mlp_gathered
    partial_out, grad_normed_two, shard_gate, shard_up, shard_down = mlp(
        normed_two, grad_mlp, gate_weight, up_weight, down_weight
    )
    mlp_out = lax.psum_scatter(partial_out, "fsdp", scatter_dimension=0, tiled=True).astype(
        jnp.float32
    )
    hidden_out = (residual_two + mlp_out).astype(jnp.bfloat16)
    grad_norm_two, term_gain_two = norm_backward(grad_normed_two, unit_two, inverse_two, gain_two)
    grad_residual_two = grad_output + grad_norm_two
    grad_proj = grad_residual_two.astype(jnp.bfloat16)
    grad_attn_rows = jnp.einsum(
        "td,ed->te", grad_proj, out_full, preferred_element_type=jnp.float32
    ).astype(jnp.bfloat16)
    term_out = jnp.einsum("te,td->ed", attn_rows, grad_proj, preferred_element_type=jnp.float32)
    grad_heads = lax.all_to_all(
        grad_attn_rows.reshape(tokens, groups, group_heads * HEAD_DIM),
        "seq",
        split_axis=1,
        concat_axis=0,
        tiled=True,
    )
    grad_query, grad_keys, grad_values = attend_backward(
        head_queries,
        head_keys,
        head_values,
        log_totals,
        grad_heads.reshape(-1, group_heads, HEAD_DIM),
    )
    back_query, back_keys, back_values = (
        lax.all_to_all(
            grad_query.astype(jnp.bfloat16).reshape(-1, 1, group_heads * HEAD_DIM),
            "seq",
            split_axis=0,
            concat_axis=1,
            tiled=True,
        ),
        lax.all_to_all(
            grad_keys.astype(jnp.bfloat16)[:, None, :],
            "seq",
            split_axis=0,
            concat_axis=1,
            tiled=True,
        ),
        lax.all_to_all(
            grad_values.astype(jnp.bfloat16)[:, None, :],
            "seq",
            split_axis=0,
            concat_axis=1,
            tiled=True,
        ),
    )
    grad_query_rows = unrotate(
        back_query.reshape(tokens, HEADS, HEAD_DIM).astype(jnp.float32), cosine, sine
    )
    grad_key_rows = unrotate(
        jnp.sum(back_keys.astype(jnp.float32).reshape(tokens, KV_HEADS, repeat, HEAD_DIM), axis=2),
        cosine,
        sine,
    )
    grad_value_rows = jnp.sum(
        back_values.astype(jnp.float32).reshape(tokens, KV_HEADS, repeat, HEAD_DIM), axis=2
    )
    grad_mixed = jnp.concatenate(
        [
            grad_query_rows.reshape(tokens, width_query),
            grad_key_rows.reshape(tokens, width_key),
            grad_value_rows.reshape(tokens, width_key),
        ],
        axis=1,
    ).astype(jnp.bfloat16)
    term_qkv = jnp.einsum("td,tc->dc", normed_one, grad_mixed, preferred_element_type=jnp.float32)
    term_bias = jnp.sum(grad_mixed.astype(jnp.float32), axis=0)
    grad_normed_one = jnp.einsum(
        "tc,dc->td", grad_mixed, qkv_full, preferred_element_type=jnp.float32
    )
    grad_norm_one, term_gain_one = norm_backward(grad_normed_one, unit_one, inverse_one, gain_one)
    grad_rows = grad_residual_two + grad_norm_one
    shard_gain_one, shard_qkv, shard_bias, shard_out, shard_gain_two = (
        lax.psum_scatter(
            term_gain_one.astype(jnp.bfloat16), "fsdp", scatter_dimension=0, tiled=True
        ).astype(jnp.float32),
        lax.psum_scatter(
            term_qkv.astype(jnp.bfloat16), "fsdp", scatter_dimension=0, tiled=True
        ).astype(jnp.float32),
        lax.psum_scatter(
            term_bias.astype(jnp.bfloat16), "fsdp", scatter_dimension=0, tiled=True
        ).astype(jnp.float32),
        lax.psum_scatter(
            term_out.astype(jnp.bfloat16), "fsdp", scatter_dimension=0, tiled=True
        ).astype(jnp.float32),
        lax.psum_scatter(
            term_gain_two.astype(jnp.bfloat16), "fsdp", scatter_dimension=0, tiled=True
        ).astype(jnp.float32),
    )
    totals = (
        lax.psum(shard_gain_one.astype(jnp.bfloat16), "seq").astype(jnp.float32),
        lax.psum(shard_qkv.astype(jnp.bfloat16), "seq").astype(jnp.float32),
        lax.psum(shard_bias.astype(jnp.bfloat16), "seq").astype(jnp.float32),
        lax.psum(shard_out.astype(jnp.bfloat16), "seq").astype(jnp.float32),
        lax.psum(shard_gain_two.astype(jnp.bfloat16), "seq").astype(jnp.float32),
        lax.psum(shard_gate.astype(jnp.bfloat16), "seq").astype(jnp.float32),
        lax.psum(shard_up.astype(jnp.bfloat16), "seq").astype(jnp.float32),
        lax.psum(shard_down.astype(jnp.bfloat16), "seq").astype(jnp.float32),
    )
    return (
        hidden_out[None],
        grad_rows[None],
        totals[0],
        totals[1],
        totals[2],
        totals[3],
        totals[4],
        totals[5],
        totals[6],
        totals[7],
    )


def solution(mesh):
    placed = (
        P("fsdp", "seq", None),
        P("fsdp", "seq"),
        P("fsdp"),
        P("fsdp", None),
        P("fsdp"),
        P("fsdp", None),
        P("fsdp"),
        P("fsdp", None),
        P("fsdp", None),
        P("fsdp", None),
        P("fsdp", "seq", None),
    )
    return jax.shard_map(
        per_device,
        mesh=mesh,
        in_specs=placed,
        out_specs=(
            P("fsdp", "seq", None),
            P("fsdp", "seq", None),
            P("fsdp"),
            P("fsdp", None),
            P("fsdp"),
            P("fsdp", None),
            P("fsdp"),
            P("fsdp", None),
            P("fsdp", None),
            P("fsdp", None),
        ),
        check_vma=False,
    )
```

```python
import functools
import math

import jax
import jax.numpy as jnp
from jax import lax
from jax.experimental import pallas as pl
from jax.experimental.pallas import tpu as pltpu
from jax.sharding import PartitionSpec as P

HEADS = 12
KV_HEADS = 2
HEAD_DIM = 128


norm_eps = 1e-06
rope_base = 1000000.0


def rope_tables(position_row):
    half_dim = HEAD_DIM // 2
    frequency = jnp.exp(
        -(jnp.arange(half_dim, dtype=jnp.float32) * 2.0 / HEAD_DIM) * math.log(rope_base)
    )
    angles = position_row.astype(jnp.float32)[:, None] * frequency[None, :]
    angles = jnp.concatenate([angles, angles], axis=-1)
    return (jnp.cos(angles), jnp.sin(angles))


def rotate(values, cosine, sine):
    half_dim = values.shape[-1] // 2
    turned = jnp.concatenate([-values[..., half_dim:], values[..., :half_dim]], axis=-1)
    return values * cosine[:, None, :] + turned * sine[:, None, :]


def unrotate(grads_rot, cosine, sine):
    half_dim = grads_rot.shape[-1] // 2
    scaled = grads_rot * sine[:, None, :]
    return grads_rot * cosine[:, None, :] + jnp.concatenate(
        [scaled[..., half_dim:], -scaled[..., :half_dim]], axis=-1
    )


def norm_forward(values, gain):
    inverse = lax.rsqrt(jnp.mean(values * values, axis=-1, keepdims=True) + norm_eps)
    unit_rows = values * inverse
    return (unit_rows, inverse, (unit_rows * gain).astype(jnp.bfloat16))


def norm_backward(grad_normed, unit_rows, inverse, gain):
    grad_unit = grad_normed * gain
    grad_values = inverse * (
        grad_unit - unit_rows * jnp.mean(grad_unit * unit_rows, axis=-1, keepdims=True)
    )
    grad_gain = jnp.sum(grad_normed * unit_rows, axis=0)
    return (grad_values, grad_gain)


def masked_scores(queries, keys, block_start, block_rows):
    length = keys.shape[0]
    query_block = lax.dynamic_slice_in_dim(queries, block_start, block_rows, 0)
    scores = jnp.einsum(
        "bhd,ld->hbl", query_block, keys, preferred_element_type=jnp.float32
    ) * HEAD_DIM ** (-0.5)
    row_index = block_start + jnp.arange(block_rows)
    column_index = jnp.arange(length)
    allowed = column_index[None, :] <= row_index[:, None]
    return (query_block, jnp.where(allowed[None], scores, -1e30))


def attend_forward(queries, keys, values):
    length = keys.shape[0]
    block_rows = min(512, length)
    block_count = length // block_rows

    def one_block(block_start):
        query_block, scores = masked_scores(queries, keys, block_start, block_rows)
        row_max = jnp.max(scores, axis=-1, keepdims=True)
        exponent = jnp.exp(scores - row_max)
        row_total = jnp.sum(exponent, axis=-1, keepdims=True)
        probability = (exponent / row_total).astype(jnp.bfloat16)
        result = jnp.einsum("hbl,ld->bhd", probability, values, preferred_element_type=jnp.float32)
        return (result.astype(jnp.bfloat16), (row_max + jnp.log(row_total))[..., 0])

    results, log_totals = lax.map(one_block, jnp.arange(block_count) * block_rows)
    return (results.reshape(length, queries.shape[1], queries.shape[2]), log_totals)


def attend_backward(queries, keys, values, log_totals, grad_out):
    length = keys.shape[0]
    block_rows = min(512, length)
    block_count = length // block_rows
    score_scale = HEAD_DIM ** (-0.5)

    def one_block(running, inputs):
        grad_keys, grad_values = running
        block_start, log_block = inputs
        query_block, scores = masked_scores(queries, keys, block_start, block_rows)
        grad_block = lax.dynamic_slice_in_dim(grad_out, block_start, block_rows, 0)
        probability = jnp.exp(scores - log_block[..., None])
        grad_probs = jnp.einsum(
            "bhd,ld->hbl", grad_block, values, preferred_element_type=jnp.float32
        )
        row_delta = jnp.sum(probability * grad_probs, axis=-1, keepdims=True)
        grad_scores = (probability * (grad_probs - row_delta)).astype(jnp.bfloat16)
        grad_query = (
            jnp.einsum("hbl,ld->bhd", grad_scores, keys, preferred_element_type=jnp.float32)
            * score_scale
        )
        grad_keys = (
            grad_keys
            + jnp.einsum(
                "hbl,bhd->ld", grad_scores, query_block, preferred_element_type=jnp.float32
            )
            * score_scale
        )
        grad_values = grad_values + jnp.einsum(
            "hbl,bhd->ld",
            probability.astype(jnp.bfloat16),
            grad_block,
            preferred_element_type=jnp.float32,
        )
        return ((grad_keys, grad_values), grad_query)

    zero_rows = jnp.zeros((length, keys.shape[1]), jnp.float32)
    (grad_keys, grad_values), grad_query = lax.scan(
        one_block, (zero_rows, zero_rows), (jnp.arange(block_count) * block_rows, log_totals)
    )
    return (grad_query.reshape(queries.shape), grad_keys, grad_values)


MESH = pl.DeviceIdType.MESH
VMEM_BYTES = 67_000_000
NN = (((1,), (0,)), ((), ()))
NT = (((1,), (1,)), ((), ()))
TN = (((0,), (0,)), ((), ()))


def matmul(left, right, dims):
    return lax.dot_general(left, right, dims, preferred_element_type=jnp.float32)


def ring_place(index, size):
    side = index % 2
    return (index // 2) * (1 - side) + (size - 1 - index // 2) * side


def ring_member(place, size):
    side = place // (size // 2)
    return 2 * (place * (1 - side) + (size - 1 - place) * side) + side


def seq_partners(seq):
    core = seq + 1 - 2 * (seq % 2)
    far = (seq + 2) % 4
    return core, far, (core + 2) % 4


def greet(targets):
    barrier = pltpu.get_barrier_semaphore()
    for target in targets:
        pl.semaphore_signal(barrier, inc=1, device_id=target, device_id_type=MESH)
    pl.semaphore_wait(barrier, len(targets))


def for_blocks(width, block, body):
    @pl.loop(0, width // block)
    def _(at):
        body(pl.ds(pl.multiple_of(at * block, block), block))

    if width % block:
        body(pl.ds(width - width % block, width % block))


def gather_kernel(
    size,
    rows_ref,
    trig_ref,
    piece_ref,
    small_ref,
    rows_out,
    trig_out,
    piece_out,
    proj_out,
    small_out,
    rows_all,
    trig_all,
    pieces,
    proj,
    smalls,
    load_sems,
    store_sems,
    ring_send,
    ring_recv,
    small_send,
    small_recv,
    seq_send,
    seq_recv,
    proj_send,
    proj_recv,
):
    depth, joint = piece_ref.shape
    half = depth // 2
    group_width = proj.shape[0]
    cut = joint - group_width
    per_group = group_width // depth
    me = lax.axis_index("fsdp")
    seq = lax.axis_index("seq")
    place = ring_place(me, size)
    right = ring_member((place + 1) % size, size)
    left = ring_member((place + size - 1) % size, size)
    core, far, diagonal = seq_partners(seq)
    sides = ((right, pl.ds(0, half)), (left, pl.ds(half, half)))

    loads = [
        pltpu.make_async_copy(piece_ref, pieces.at[me], load_sems.at[0]),
        pltpu.make_async_copy(rows_ref, rows_all.at[seq], load_sems.at[1]),
        pltpu.make_async_copy(trig_ref, trig_all.at[seq], load_sems.at[2]),
        pltpu.make_async_copy(small_ref, smalls.at[me], load_sems.at[3]),
    ]
    for load in loads:
        load.start()
    greet(({"fsdp": right}, {"fsdp": left}, {"seq": core}, {"seq": far}, {"seq": diagonal}))

    def piece_of(step, side):
        return ring_member((place + size - step if side == 0 else place + step) % size, size)

    def ring_copy(step, side):
        target, span = sides[side]
        at = piece_of(step, side)
        return pltpu.make_async_remote_copy(
            src_ref=pieces.at[at, span],
            dst_ref=pieces.at[at, span],
            send_sem=ring_send.at[side, step],
            recv_sem=ring_recv.at[side, step],
            device_id={"fsdp": target},
            device_id_type=MESH,
        )

    def small_copy(step):
        at = piece_of(step, 0)
        return pltpu.make_async_remote_copy(
            src_ref=smalls.at[at],
            dst_ref=smalls.at[at],
            send_sem=small_send.at[step],
            recv_sem=small_recv.at[step],
            device_id={"fsdp": right},
            device_id_type=MESH,
        )

    def seq_copy(which, block, target, at):
        held = (rows_all, trig_all)[which]
        return pltpu.make_async_remote_copy(
            src_ref=held.at[block],
            dst_ref=held.at[block],
            send_sem=seq_send.at[which, at],
            recv_sem=seq_recv.at[which, at],
            device_id={"seq": target},
            device_id_type=MESH,
        )

    def proj_part(step, side):
        at = piece_of(step, side)
        owner = at // per_group
        row = pl.multiple_of((at % per_group) * depth + side * half, half)
        source = pieces.at[at, pl.ds(side * half, half), pl.ds(cut, group_width)]
        target = proj.at[pl.ds(row, half), pl.ds(pl.multiple_of(seq * group_width, 128), group_width)]
        return at, owner, source, target

    def proj_copy(step, side):
        at, owner, source, target = proj_part(step, side)
        return owner, pltpu.make_async_remote_copy(
            src_ref=source,
            dst_ref=target,
            send_sem=proj_send.at[side, step],
            recv_sem=proj_recv.at[seq, at % per_group, side],
            device_id={"seq": owner},
            device_id_type=MESH,
        )

    def proj_start(step, side):
        owner, copy = proj_copy(step, side)

        @pl.when(owner != seq)
        def _():
            copy.start()

        @pl.when(owner == seq)
        def _():
            _, _, source, target = proj_part(step, side)
            pltpu.make_async_copy(source, target, proj_send.at[side, step]).start()

    loads[0].wait()
    for side in range(2):
        ring_copy(0, side).start()
    loads[3].wait()
    small_copy(0).start()
    for which in (1, 0):
        loads[1 + which].wait()
        seq_copy(which, seq, far, 1).start()
        seq_copy(which, seq, core, 0).start()
    for side in range(2):
        proj_start(0, side)

    for step in range(size - 1):
        for side in range(2):
            ring_copy(step, side).wait_recv()
            if step < size - 2:
                ring_copy(step + 1, side).start()
        small_copy(step).wait_recv()
        if step < size - 2:
            small_copy(step + 1).start()
        for side in range(2):
            proj_start(step + 1, side)
        if step == min(1, size - 2):
            for which in (1, 0):
                seq_copy(which, seq, far, 1).wait_recv()
                seq_copy(which, far, core, 2).start()

    store_pieces = pltpu.make_async_copy(pieces, piece_out, store_sems.at[0])
    store_small = pltpu.make_async_copy(smalls, small_out, store_sems.at[1])
    store_pieces.start()
    store_small.start()
    for which in (1, 0):
        seq_copy(which, seq, core, 0).wait_recv()
        seq_copy(which, far, core, 2).wait_recv()
    store_rows = pltpu.make_async_copy(rows_all, rows_out, store_sems.at[2])
    store_trig = pltpu.make_async_copy(trig_all, trig_out, store_sems.at[3])
    store_rows.start()
    store_trig.start()
    for peer in (core, far, diagonal):
        for at in range(per_group):
            for side in range(2):
                pltpu.make_async_remote_copy(
                    src_ref=pieces.at[0, pl.ds(0, half), pl.ds(cut, group_width)],
                    dst_ref=proj.at[pl.ds(0, half), pl.ds(0, group_width)],
                    send_sem=proj_send.at[side, 0],
                    recv_sem=proj_recv.at[peer, at, side],
                    device_id={"seq": peer},
                    device_id_type=MESH,
                ).wait_recv()
    for step in range(size):
        for side in range(2):
            owner, copy = proj_copy(step, side)

            @pl.when(owner != seq)
            def _():
                copy.wait_send()

            @pl.when(owner == seq)
            def _():
                _, _, source, target = proj_part(step, side)
                pltpu.make_async_copy(source, target, proj_send.at[side, step]).wait()

    store_proj = pltpu.make_async_copy(proj, proj_out, store_sems.at[4])
    store_proj.start()
    for step in range(size - 1):
        for side in range(2):
            ring_copy(step, side).wait_send()
        small_copy(step).wait_send()
    for which in (1, 0):
        seq_copy(which, seq, core, 0).wait_send()
        seq_copy(which, seq, far, 1).wait_send()
        seq_copy(which, far, core, 2).wait_send()
    for store in (store_pieces, store_small, store_rows, store_trig, store_proj):
        store.wait()


def gather_inputs(rows, trig, piece, small):
    size = lax.axis_size("fsdp")
    groups = lax.axis_size("seq")
    tokens, width = rows.shape
    depth, joint = piece.shape
    group_width = width // groups
    f32, bf16 = jnp.float32, jnp.bfloat16
    shapes = (
        ((groups, tokens, width), bf16),
        ((groups,) + trig.shape, f32),
        ((size, depth, joint), bf16),
        ((group_width, width), bf16),
        ((size,) + small.shape, bf16),
    )
    dma = pltpu.SemaphoreType.DMA
    anywhere = pl.BlockSpec(memory_space=pl.ANY)
    per_group = group_width // depth
    return pl.pallas_call(
        functools.partial(gather_kernel, size),
        out_shape=tuple(jax.ShapeDtypeStruct(*shape) for shape in shapes),
        in_specs=[anywhere] * 4,
        out_specs=(anywhere,) * 5,
        scratch_shapes=[pltpu.VMEM(*shape) for shape in shapes]
        + [
            dma((4,)),
            dma((5,)),
            dma((2, size)),
            dma((2, size)),
            dma((size,)),
            dma((size,)),
            dma((2, 3)),
            dma((2, 3)),
            dma((2, size)),
            dma((groups, per_group, 2)),
        ],
        compiler_params=pltpu.CompilerParams(
            collective_id=1, has_side_effects=True, vmem_limit_bytes=32_000_000
        ),
        name="gather_inputs",
    )(rows, trig, piece, small)


def turn_tables(trig):
    lane = lax.broadcasted_iota(jnp.int32, trig.shape, 1)
    swapped = pltpu.roll(trig, HEAD_DIM // 2, 1)
    first = lane < HEAD_DIM // 2
    return jnp.where(first, trig, swapped), jnp.where(first, -swapped, trig)


def head_columns(at):
    return slice(at * HEAD_DIM, (at + 1) * HEAD_DIM)


def causal(scores, start):
    rows = lax.broadcasted_iota(jnp.int32, scores.shape, 0) + start
    columns = lax.broadcasted_iota(jnp.int32, scores.shape, 1)
    return jnp.where(columns <= rows, scores, -1e30)


def attend_forward_kernel(
    block,
    rows_ref,
    weight_ref,
    proj_ref,
    trig_ref,
    gain_ref,
    bias_ref,
    normed_ref,
    heads_ref,
    out_ref,
    log_ref,
    part_ref,
):
    length = rows_ref.shape[0]
    used = heads_ref.shape[1]
    count = used // HEAD_DIM - 2
    scale = HEAD_DIM**-0.5
    for start in range(0, length, block):
        span = slice(start, start + block)
        rows = rows_ref[span, :].astype(jnp.float32)
        inverse = lax.rsqrt(jnp.mean(rows * rows, axis=-1, keepdims=True) + norm_eps)
        normed_ref[span, :] = (rows * inverse * gain_ref[...]).astype(jnp.bfloat16)
        mixed = matmul(normed_ref[span, :], weight_ref[:, :used], NN) + bias_ref[...]
        cosine, sine = turn_tables(trig_ref[span, :])
        for at in range(count + 1):
            part = mixed[:, head_columns(at)]
            turned = pltpu.roll(part, HEAD_DIM // 2, 1)
            heads_ref[span, head_columns(at)] = (part * cosine + turned * sine).astype(
                jnp.bfloat16
            )
        heads_ref[span, head_columns(count + 1)] = mixed[:, head_columns(count + 1)].astype(
            jnp.bfloat16
        )
    lane = lax.broadcasted_iota(jnp.int32, (block, HEAD_DIM), 1)
    for start in range(0, length, block):
        span = slice(start, start + block)
        seen = slice(0, start + block)
        logs = jnp.zeros((block, HEAD_DIM), jnp.float32)
        for at in range(count):
            scores = causal(
                matmul(heads_ref[span, head_columns(at)], heads_ref[seen, head_columns(count)], NT)
                * scale,
                start,
            )
            top = jnp.max(scores, axis=-1, keepdims=True)
            exponent = jnp.exp(scores - top)
            total = jnp.sum(exponent, axis=-1, keepdims=True)
            probability = (exponent / total).astype(jnp.bfloat16)
            out_ref[span, head_columns(at)] = matmul(
                probability, heads_ref[seen, head_columns(count + 1)], NN
            ).astype(jnp.bfloat16)
            logs = jnp.where(lane == at, top + jnp.log(total), logs)
        log_ref[span, :] = logs
        part_ref[span, :] = matmul(out_ref[span, :], proj_ref[...], NN).astype(jnp.bfloat16)


def attend_group(rows, weight, proj, trig, gain, bias):
    length, width = rows.shape
    used = bias.shape[1]
    own = proj.shape[0]
    bf16 = jnp.bfloat16
    inside = pl.BlockSpec(memory_space=pltpu.VMEM)
    return pl.pallas_call(
        functools.partial(attend_forward_kernel, 256),
        out_shape=(
            jax.ShapeDtypeStruct((length, width), bf16),
            jax.ShapeDtypeStruct((length, used), bf16),
            jax.ShapeDtypeStruct((length, own), bf16),
            jax.ShapeDtypeStruct((length, HEAD_DIM), jnp.float32),
            jax.ShapeDtypeStruct((length, width), bf16),
        ),
        in_specs=[inside] * 6,
        out_specs=(inside,) * 5,
        compiler_params=pltpu.CompilerParams(vmem_limit_bytes=VMEM_BYTES),
        cost_estimate=pl.CostEstimate(
            flops=2 * length * width * (used + own) + 4 * length * length * own,
            bytes_accessed=2 * (3 * length * width + 2 * width * width),
            transcendentals=length * length * own // HEAD_DIM,
        ),
        name="attend_forward",
    )(rows, weight, proj, trig, gain, bias)


def mlp_kernel(
    size,
    hidden_ref,
    part_ref,
    gain_ref,
    cots_ref,
    gate_ref,
    up_ref,
    down_ref,
    outs_ref,
    resid_ref,
    proj_grads_ref,
    back_ref,
    gain_grad_ref,
    sums_ref,
    rows_all,
    cots,
    weights,
    grads,
    hid,
    dgate,
    dup,
    partial,
    resid,
    sums_in,
    sums_out,
    outs,
    seq_in,
    seq_own,
    load_sems,
    cot_sems,
    ring_send,
    ring_recv,
    sum_send,
    sum_recv,
    out_sems,
    seq_send,
    seq_recv,
    swap_send,
    swap_recv,
    swap_ready,
):
    tokens, width = hidden_ref.shape
    units = gate_ref.shape[0]
    half = tokens // 2
    me = lax.axis_index("fsdp")
    seq = lax.axis_index("seq")
    place = ring_place(me, size)
    right = ring_member((place + 1) % size, size)
    left = ring_member((place + size - 1) % size, size)
    core, far, diagonal = seq_partners(seq)
    sides = ((right, pl.ds(0, half)), (left, pl.ds(half, half)))

    def owner_of(step, side):
        return ring_member((place + size - step if side == 0 else place + step) % size, size)

    def part_rows(block):
        return part_ref.at[pl.ds(pl.multiple_of(block * tokens, tokens), tokens)]

    part_loads = [
        pltpu.make_async_copy(part_rows(far), seq_own.at[0], load_sems.at[3]),
        pltpu.make_async_copy(part_rows(seq), seq_own.at[1], load_sems.at[4]),
        pltpu.make_async_copy(hidden_ref, seq_own.at[2], load_sems.at[5]),
    ]
    weight_loads = [
        pltpu.make_async_copy(ref, weights.at[at], load_sems.at[at])
        for at, ref in enumerate((gate_ref, up_ref, down_ref))
    ]
    for load in part_loads:
        load.start()
    greet(({"fsdp": right}, {"fsdp": left}, {"seq": core}, {"seq": far}))

    def seq_copy(at, source, target):
        return pltpu.make_async_remote_copy(
            src_ref=source,
            dst_ref=seq_in.at[at],
            send_sem=seq_send.at[at],
            recv_sem=seq_recv.at[at],
            device_id={"seq": target},
            device_id_type=MESH,
        )

    core_copies = [seq_copy(0, part_rows(diagonal), core), seq_copy(1, part_rows(core), core)]
    far_copy = seq_copy(2, sums_out.at[0], far)
    for copy in core_copies:
        copy.start()

    def cot_copies(step):
        return [
            pltpu.make_async_copy(
                cots_ref.at[
                    pl.ds(
                        pl.multiple_of(owner_of(step, side) * tokens + side * half, half), half
                    )
                ],
                cots.at[step % 2, sides[side][1]],
                cot_sems.at[step % 2, side],
            )
            for side in range(2)
        ]

    for load in weight_loads + cot_copies(0):
        load.start()

    @pl.loop(0, units // 16)
    def _(at):
        zeros = jnp.zeros((3, 16, width), jnp.float32)
        grads[:, pl.ds(pl.multiple_of(at * 16, 16), 16), :] = zeros

    part_loads[0].wait()
    core_copies[0].wait_recv()
    sums_out[0] = (seq_own[0].astype(jnp.float32) + seq_in[0].astype(jnp.float32)).astype(
        jnp.bfloat16
    )
    far_copy.start()
    part_loads[1].wait()
    part_loads[2].wait()
    core_copies[1].wait_recv()
    resid[...] = (
        seq_own[1].astype(jnp.float32)
        + seq_in[1].astype(jnp.float32)
        + seq_own[2].astype(jnp.float32)
    )
    far_copy.wait_recv()
    resid[...] += seq_in[2].astype(jnp.float32)

    def inverse_of(values):
        return lax.rsqrt(jnp.mean(values * values, axis=-1, keepdims=True) + norm_eps)

    rows_all[0] = (resid[...] * inverse_of(resid[...]) * gain_ref[...]).astype(jnp.bfloat16)
    far_copy.wait_send()
    resid_store = pltpu.make_async_copy(resid, resid_ref, load_sems.at[6])
    resid_store.start()

    def row_copy(step, side):
        target, span = sides[side]
        return pltpu.make_async_remote_copy(
            src_ref=rows_all.at[step, span],
            dst_ref=rows_all.at[step + 1, span],
            send_sem=ring_send.at[side, step],
            recv_sem=ring_recv.at[side, step + 1],
            device_id={"fsdp": target},
            device_id_type=MESH,
        )

    def sum_copy(step, side):
        target, span = sides[side]
        return pltpu.make_async_remote_copy(
            src_ref=sums_out.at[step % 2, span],
            dst_ref=sums_in.at[step, span],
            send_sem=sum_send.at[side, step],
            recv_sem=sum_recv.at[side, step],
            device_id={"fsdp": target},
            device_id_type=MESH,
        )

    def out_copy(step, side):
        at = pl.multiple_of(owner_of(step, side) * tokens + side * half, half)
        return pltpu.make_async_copy(
            outs.at[step % 2, sides[side][1]], outs_ref.at[pl.ds(at, half)], out_sems.at[side, step]
        )

    def elementwise(step, span):
        rows = rows_all[step]
        gate = matmul(rows, weights[0, span, :], NT)
        up = matmul(rows, weights[1, span, :], NT)
        grad_hidden = matmul(cots[step % 2], weights[2, span, :], NT)
        sigmoid = jax.nn.sigmoid(gate)
        activated = gate * sigmoid
        hid[:, span] = (activated * up).astype(jnp.bfloat16)
        dgate[:, span] = (
            grad_hidden * up * sigmoid * (1.0 + gate * (1.0 - sigmoid))
        ).astype(jnp.bfloat16)
        dup[:, span] = (grad_hidden * activated).astype(jnp.bfloat16)

    for load in weight_loads:
        load.wait()

    @pl.loop(0, size)
    def _(step):
        slot = step % 2

        @pl.when(step >= 1)
        def _():
            for side in range(2):
                row_copy(step - 1, side).wait_recv()

        @pl.when(step < size - 1)
        def _():
            for side in range(2):
                row_copy(step, side).start()

        for load in cot_copies(step):
            load.wait()

        @pl.when(step < size - 1)
        def _():
            for load in cot_copies(step + 1):
                load.start()

        for_blocks(units, 256, functools.partial(elementwise, step))

        def back_part(span):
            partial[:, span] = matmul(dgate[...], weights[0, :, span], NN) + matmul(
                dup[...], weights[1, :, span], NN
            )

        for_blocks(width, 256, back_part)

        @pl.when(step == 0)
        def _():
            back_ref[...] = partial[...]

        @pl.when(step >= 3)
        def _():
            for side in range(2):
                sum_copy(step - 2, side).wait_send()

        @pl.when(step == 1)
        def _():
            sums_out[slot] = partial[...].astype(jnp.bfloat16)

        @pl.when(step >= 2)
        def _():
            for side in range(2):
                sum_copy(step - 1, side).wait_recv()
            sums_out[slot] = (partial[...] + sums_in[step - 1].astype(jnp.float32)).astype(
                jnp.bfloat16
            )

        @pl.when(step >= 1)
        def _():
            for side in range(2):
                sum_copy(step, side).start()

        @pl.when(step >= 2)
        def _():
            for side in range(2):
                out_copy(step - 2, side).wait()

        def out_part(span):
            outs[slot, :, span] = matmul(hid[...], weights[2, :, span], NN).astype(jnp.bfloat16)

        for_blocks(width, 256, out_part)
        for side in range(2):
            out_copy(step, side).start()

        def weight_part(span):
            rows, cot = rows_all[step, :, span], cots[slot, :, span]
            grads[0, :, span] += matmul(dgate[...], rows, TN)
            grads[1, :, span] += matmul(dup[...], rows, TN)
            grads[2, :, span] += matmul(hid[...], cot, TN)

        for_blocks(width, 256, weight_part)

    share = units // 2
    kept = pl.multiple_of((seq % 2) * share, 16)
    given = pl.multiple_of((1 - seq % 2) * share, 16)
    pl.semaphore_signal(swap_ready, inc=1, device_id={"seq": core}, device_id_type=MESH)
    swaps = [
        pltpu.make_async_remote_copy(
            src_ref=weights.at[at, pl.ds(given, share)],
            dst_ref=weights.at[at, pl.ds(given, share)],
            send_sem=swap_send.at[at],
            recv_sem=swap_recv.at[at],
            device_id={"seq": core},
            device_id_type=MESH,
        )
        for at in range(3)
    ]
    for at in range(3):

        @pl.loop(0, share // 16)
        def _(block):
            span = pl.ds(pl.multiple_of(given + block * 16, 16), 16)
            weights[at, span, :] = grads[at, span, :].astype(jnp.bfloat16)

        if at == 0:
            pl.semaphore_wait(swap_ready, 1)
        swaps[at].start()

    for side in range(2):
        sum_copy(size - 1, side).wait_recv()
    grad_normed = back_ref[...] + sums_in[size - 1].astype(jnp.float32)
    inverse = inverse_of(resid[...])
    unit_rows = resid[...] * inverse
    gain_grad_ref[...] = jnp.sum(grad_normed * unit_rows, axis=0, keepdims=True)
    grad_unit = grad_normed * gain_ref[...]
    cot_own = pltpu.make_async_copy(
        cots_ref.at[pl.ds(pl.multiple_of(me * tokens, tokens), tokens)],
        cots.at[0],
        load_sems.at[7],
    )
    cot_own.start()
    cot_own.wait()
    back_ref[...] = cots[0].astype(jnp.float32) + inverse * (
        grad_unit - unit_rows * jnp.mean(grad_unit * unit_rows, axis=-1, keepdims=True)
    )
    for side in range(2):
        sum_copy(size - 2, side).wait_send()
        sum_copy(size - 1, side).wait_send()
    sums_out[0] = back_ref[...].astype(jnp.bfloat16)

    def grad_copy(source, block, target, at):
        return pltpu.make_async_remote_copy(
            src_ref=source,
            dst_ref=proj_grads_ref.at[block],
            send_sem=seq_send.at[at],
            recv_sem=seq_recv.at[at],
            device_id={"seq": target},
            device_id_type=MESH,
        )

    to_far = grad_copy(sums_out.at[0], seq, far, 3)
    to_core = grad_copy(sums_out.at[0], seq, core, 4)
    passed_on = grad_copy(proj_grads_ref.at[far], far, core, 5)
    keep = pltpu.make_async_copy(sums_out.at[0], proj_grads_ref.at[seq], load_sems.at[8])
    to_far.start()
    to_core.start()
    keep.start()
    stores = []
    for at in range(3):
        swaps[at].wait_recv()

        @pl.loop(0, share // 16)
        def _(block):
            span = pl.ds(pl.multiple_of(kept + block * 16, 16), 16)
            weights[at, span, :] = (
                grads[at, span, :] + weights[at, span, :].astype(jnp.float32)
            ).astype(jnp.bfloat16)

        stores.append(
            pltpu.make_async_copy(
                weights.at[at, pl.ds(kept, share)], sums_ref.at[at], load_sems.at[at]
            )
        )
        stores[-1].start()
    to_far.wait_recv()
    passed_on.start()
    for side in range(2):
        out_copy(size - 2, side).wait()
        out_copy(size - 1, side).wait()

        @pl.loop(0, size - 1)
        def _(step):
            row_copy(step, side).wait_send()

    for copy in core_copies + swaps + [to_far, to_core, passed_on]:
        copy.wait_send()
    to_core.wait_recv()
    passed_on.wait_recv()
    for store in stores + [keep, resid_store]:
        store.wait()


def mlp_ring(hidden, part, gain, cots, gate_weight, up_weight, down_weight):
    size = lax.axis_size("fsdp")
    groups = lax.axis_size("seq")
    tokens, width = hidden.shape
    units = gate_weight.shape[0]
    anywhere = pl.BlockSpec(memory_space=pl.ANY)
    inside = pl.BlockSpec(memory_space=pltpu.VMEM)
    bf16, f32 = jnp.bfloat16, jnp.float32
    dma = pltpu.SemaphoreType.DMA
    return pl.pallas_call(
        functools.partial(mlp_kernel, size),
        out_shape=(
            jax.ShapeDtypeStruct((size * tokens, width), bf16),
            jax.ShapeDtypeStruct((tokens, width), f32),
            jax.ShapeDtypeStruct((groups, tokens, width), bf16),
            jax.ShapeDtypeStruct((tokens, width), f32),
            jax.ShapeDtypeStruct((1, width), f32),
            jax.ShapeDtypeStruct((3, units // 2, width), bf16),
        ),
        in_specs=[anywhere, anywhere, inside, anywhere, anywhere, anywhere, anywhere],
        out_specs=(anywhere, anywhere, anywhere, inside, inside, anywhere),
        scratch_shapes=[
            pltpu.VMEM((size, tokens, width), bf16),
            pltpu.VMEM((2, tokens, width), bf16),
            pltpu.VMEM((3, units, width), bf16),
            pltpu.VMEM((3, units, width), f32),
            pltpu.VMEM((tokens, units), bf16),
            pltpu.VMEM((tokens, units), bf16),
            pltpu.VMEM((tokens, units), bf16),
            pltpu.VMEM((tokens, width), f32),
            pltpu.VMEM((tokens, width), f32),
            pltpu.VMEM((size, tokens, width), bf16),
            pltpu.VMEM((2, tokens, width), bf16),
            pltpu.VMEM((2, tokens, width), bf16),
            pltpu.VMEM((3, tokens, width), bf16),
            pltpu.VMEM((3, tokens, width), bf16),
            dma((9,)),
            dma((2, 2)),
            dma((2, size)),
            dma((2, size)),
            dma((2, size)),
            dma((2, size)),
            dma((2, size)),
            dma((6,)),
            dma((6,)),
            dma((3,)),
            dma((3,)),
            pltpu.SemaphoreType.REGULAR,
        ],
        compiler_params=pltpu.CompilerParams(
            collective_id=0, has_side_effects=True, vmem_limit_bytes=VMEM_BYTES
        ),
        name="mlp_ring",
    )(hidden, part, gain, cots, gate_weight, up_weight, down_weight)


def kernels_fit(hidden_in, positions, attn_gain, qkv_weight, qkv_bias, out_weight, *rest):
    size, groups = lax.axis_size("fsdp"), lax.axis_size("seq")
    _, tokens, width = hidden_in.shape
    units = rest[1].shape[0]
    if groups != 4 or size % 4 or tokens % 256 or units % 32 or width % 512:
        return False
    if (width // size) % 32 or qkv_bias.shape[0] > 256 or KV_HEADS != 2:
        return False
    rows = tokens * width * (4 * size + 34)
    return rows + units * (18 * width + 6 * tokens) < 64_000_000


def group_columns(array, seq):
    width_query = HEADS * HEAD_DIM
    own = width_query // 4
    kv_head = seq // 2
    parts = (
        (seq * own, own),
        (width_query + kv_head * HEAD_DIM, HEAD_DIM),
        (width_query + (KV_HEADS + kv_head) * HEAD_DIM, HEAD_DIM),
    )
    return jnp.concatenate(
        [lax.dynamic_slice_in_dim(array, at, count, array.ndim - 1) for at, count in parts], -1
    )


def per_device_kernels(
    hidden_in,
    positions,
    attn_gain,
    qkv_weight,
    qkv_bias,
    out_weight,
    mlp_gain,
    gate_weight,
    up_weight,
    down_weight,
    cotangent,
):
    f32, bf16 = jnp.float32, jnp.bfloat16
    groups = lax.axis_size("seq")
    size = lax.axis_size("fsdp")
    seq = lax.axis_index("seq")
    _, tokens, width = hidden_in.shape
    length = tokens * groups
    own = width // groups
    used = own + 2 * HEAD_DIM
    all_cots = lax.all_gather(cotangent[0], "fsdp", axis=0, tiled=True)
    cosine, sine = rope_tables(positions[0])
    half_dim = HEAD_DIM // 2
    trig = jnp.concatenate([cosine[:, :half_dim], sine[:, half_dim:]], axis=1)
    piece = jnp.concatenate(
        [
            group_columns(qkv_weight, seq),
            lax.dynamic_slice_in_dim(out_weight, seq * own, own, 1),
        ],
        axis=1,
    )
    small_width = 256
    small = jnp.stack(
        [
            jnp.pad(row, (0, small_width - row.shape[0]))
            for row in (attn_gain, mlp_gain, qkv_bias)
        ]
    )
    small = jnp.pad(small, ((0, 13), (0, 0)))
    rows_all, trig_all, pieces, proj, smalls = gather_inputs(hidden_in[0], trig, piece, small)
    shard = width // size
    gain_one = smalls[:, 0, :shard].reshape(1, width).astype(f32)
    gain_two = smalls[:, 1, :shard].reshape(1, width).astype(f32)
    bias = group_columns(smalls[:, 2, : qkv_bias.shape[0]].reshape(1, -1), seq).astype(f32)
    rows_all = rows_all.reshape(length, width)
    trig_all = trig_all.reshape(length, HEAD_DIM)
    weight = pieces.reshape(width, piece.shape[1])
    normed_one, heads, attended, logs, part = attend_group(
        rows_all, weight, proj, trig_all, gain_one, bias
    )
    outs, residual, proj_grads, grad_residual, term_gain_two, unit_sums = mlp_ring(
        hidden_in[0], part, gain_two, all_cots, gate_weight, up_weight, down_weight
    )
    mlp_out = lax.psum_scatter(outs, "fsdp", scatter_dimension=0, tiled=True).astype(f32)
    hidden_out = (residual + mlp_out).astype(bf16)
    proj_grads = proj_grads.reshape(length, width)

    count = own // HEAD_DIM
    grad_heads = jnp.einsum("td,ed->te", proj_grads, proj, preferred_element_type=f32).astype(bf16)
    term_out = jnp.einsum("te,td->ed", attended, proj_grads, preferred_element_type=f32)
    grad_query, grad_keys, grad_values = attend_backward(
        heads[:, :own].reshape(length, count, HEAD_DIM),
        heads[:, own : own + HEAD_DIM],
        heads[:, own + HEAD_DIM :],
        logs[:, :count].reshape(2, length // 2, count).transpose(0, 2, 1),
        grad_heads.reshape(length, count, HEAD_DIM),
    )
    cosine_all = jnp.concatenate([trig_all[:, :half_dim]] * 2, axis=1)
    sine_all = jnp.concatenate([trig_all[:, half_dim:]] * 2, axis=1)
    grad_query = unrotate(grad_query.astype(bf16).astype(f32), cosine_all, sine_all)
    grad_keys = unrotate(grad_keys.astype(bf16).astype(f32)[:, None], cosine_all, sine_all)[:, 0]
    grad_mixed = jnp.concatenate(
        [grad_query.reshape(length, own), grad_keys, grad_values.astype(bf16).astype(f32)], axis=1
    ).astype(bf16)
    term_qkv = jnp.einsum("td,tc->dc", normed_one, grad_mixed, preferred_element_type=f32)
    term_bias = jnp.sum(grad_mixed.astype(f32), axis=0)
    grad_normed = jnp.einsum(
        "tc,dc->td", grad_mixed, weight[:, :used], preferred_element_type=f32
    )
    grad_normed = lax.psum_scatter(grad_normed.astype(bf16), "seq", scatter_dimension=0, tiled=True)
    unit_one, inverse_one, _ = norm_forward(hidden_in[0].astype(f32), gain_one)
    grad_norm_one, term_gain_one = norm_backward(
        grad_normed.astype(f32), unit_one, inverse_one, gain_one
    )
    grad_rows = grad_residual + grad_norm_one

    width_query = HEADS * HEAD_DIM

    def spread(term):
        full = jnp.zeros(term.shape[:-1] + (width_query + 2 * KV_HEADS * HEAD_DIM,), f32)
        kv_head = seq // 2
        full = lax.dynamic_update_slice_in_dim(full, term[..., :own], seq * own, term.ndim - 1)
        full = lax.dynamic_update_slice_in_dim(
            full, term[..., own : own + HEAD_DIM], width_query + kv_head * HEAD_DIM, term.ndim - 1
        )
        return lax.dynamic_update_slice_in_dim(
            full,
            term[..., own + HEAD_DIM :],
            width_query + (KV_HEADS + kv_head) * HEAD_DIM,
            term.ndim - 1,
        )

    def reduced(term):
        shard_sum = lax.psum_scatter(
            term.astype(bf16), "fsdp", scatter_dimension=0, tiled=True
        )
        return lax.psum(shard_sum, "seq").astype(f32)

    full_out = lax.dynamic_update_slice_in_dim(jnp.zeros((width, width), f32), term_out, seq * own, 0)
    far_sums = lax.ppermute(unit_sums, "seq", [(at, (at + 2) % 4) for at in range(4)])
    totals = (unit_sums.astype(f32) + far_sums.astype(f32)).astype(bf16)
    others = lax.ppermute(totals, "seq", [(at, at + 1 - 2 * (at % 2)) for at in range(4)])
    first = jnp.where(seq % 2 == 0, totals, others)
    second = jnp.where(seq % 2 == 0, others, totals)
    units_grads = jnp.concatenate([first, second], axis=1).astype(f32)
    return (
        hidden_out[None],
        grad_rows[None],
        reduced(term_gain_one),
        reduced(spread(term_qkv)),
        reduced(spread(term_bias)),
        reduced(full_out),
        reduced(term_gain_two[0]),
        units_grads[0],
        units_grads[1],
        units_grads[2],
    )


def per_device_gathered(
    hidden_in,
    positions,
    attn_gain,
    qkv_weight,
    qkv_bias,
    out_weight,
    mlp_gain,
    gate_weight,
    up_weight,
    down_weight,
    cotangent,
):
    groups = lax.axis_size("seq")
    group_heads = HEADS // groups
    repeat = groups // KV_HEADS
    tokens = hidden_in.shape[1]
    width_query = HEADS * HEAD_DIM
    width_key = KV_HEADS * HEAD_DIM
    residual = hidden_in[0].astype(jnp.float32)
    cosine, sine = rope_tables(positions[0])
    gains_one, gains_two, qkv_full, bias_full, out_full = (
        lax.all_gather(attn_gain, "fsdp", axis=0, tiled=True),
        lax.all_gather(mlp_gain, "fsdp", axis=0, tiled=True),
        lax.all_gather(qkv_weight, "fsdp", axis=0, tiled=True),
        lax.all_gather(qkv_bias, "fsdp", axis=0, tiled=True),
        lax.all_gather(out_weight, "fsdp", axis=0, tiled=True),
    )
    gain_one = gains_one.astype(jnp.float32)
    gain_two = gains_two.astype(jnp.float32)
    unit_one, inverse_one, normed_one = norm_forward(residual, gain_one)
    qkv_mixed = jnp.dot(
        normed_one, qkv_full, preferred_element_type=jnp.float32
    ) + bias_full.astype(jnp.float32)
    query_part = qkv_mixed[:, :width_query].reshape(tokens, HEADS, HEAD_DIM)
    key_part = qkv_mixed[:, width_query : width_query + width_key].reshape(
        tokens, KV_HEADS, HEAD_DIM
    )
    value_part = qkv_mixed[:, width_query + width_key :].reshape(tokens, KV_HEADS, HEAD_DIM)
    queries = (
        rotate(query_part, cosine, sine)
        .astype(jnp.bfloat16)
        .reshape(tokens, groups, group_heads * HEAD_DIM)
    )
    keys_rep = jnp.repeat(rotate(key_part, cosine, sine).astype(jnp.bfloat16), repeat, axis=1)
    values_rep = jnp.repeat(value_part.astype(jnp.bfloat16), repeat, axis=1)
    head_queries, head_keys, head_values = (
        lax.all_to_all(queries, "seq", split_axis=1, concat_axis=0, tiled=True),
        lax.all_to_all(keys_rep, "seq", split_axis=1, concat_axis=0, tiled=True),
        lax.all_to_all(values_rep, "seq", split_axis=1, concat_axis=0, tiled=True),
    )
    head_queries = head_queries.reshape(-1, group_heads, HEAD_DIM)
    head_keys = head_keys.reshape(-1, HEAD_DIM)
    head_values = head_values.reshape(-1, HEAD_DIM)
    attended, log_totals = attend_forward(head_queries, head_keys, head_values)
    returned = lax.all_to_all(
        attended.reshape(-1, 1, group_heads * HEAD_DIM),
        "seq",
        split_axis=0,
        concat_axis=1,
        tiled=True,
    )
    attn_rows = returned.reshape(tokens, width_query)
    residual_two = residual + jnp.dot(attn_rows, out_full, preferred_element_type=jnp.float32)
    unit_two, inverse_two, normed_two = norm_forward(residual_two, gain_two)
    grad_output = cotangent[0].astype(jnp.float32)
    grad_mlp = grad_output.astype(jnp.bfloat16)
    all_rows = lax.all_gather(normed_two, "fsdp", axis=0, tiled=True)
    gate_pre = jnp.einsum("td,fd->tf", all_rows, gate_weight, preferred_element_type=jnp.float32)
    up_pre = jnp.einsum("td,fd->tf", all_rows, up_weight, preferred_element_type=jnp.float32)
    sigmoid_gate = jax.nn.sigmoid(gate_pre)
    activated = gate_pre * sigmoid_gate
    hidden = (activated * up_pre).astype(jnp.bfloat16)
    partial_out = jnp.dot(hidden, down_weight, preferred_element_type=jnp.float32)
    mlp_out = lax.psum_scatter(
        partial_out.astype(jnp.bfloat16), "fsdp", scatter_dimension=0, tiled=True
    ).astype(jnp.float32)
    all_grads = lax.all_gather(grad_mlp, "fsdp", axis=0, tiled=True)
    grad_hidden = jnp.einsum(
        "tm,fm->tf", all_grads, down_weight, preferred_element_type=jnp.float32
    )
    grad_gate = (
        grad_hidden * up_pre * sigmoid_gate * (1.0 + gate_pre * (1.0 - sigmoid_gate))
    ).astype(jnp.bfloat16)
    grad_up = (grad_hidden * activated).astype(jnp.bfloat16)
    partial_back = jnp.dot(grad_gate, gate_weight, preferred_element_type=jnp.float32) + jnp.dot(
        grad_up, up_weight, preferred_element_type=jnp.float32
    )
    grad_normed_two = lax.psum_scatter(partial_back, "fsdp", scatter_dimension=0, tiled=True)
    shard_gate = jnp.einsum("tf,td->fd", grad_gate, all_rows, preferred_element_type=jnp.float32)
    shard_up = jnp.einsum("tf,td->fd", grad_up, all_rows, preferred_element_type=jnp.float32)
    shard_down = jnp.einsum("tf,td->fd", hidden, all_grads, preferred_element_type=jnp.float32)
    hidden_out = (residual_two + mlp_out).astype(jnp.bfloat16)
    grad_norm_two, term_gain_two = norm_backward(grad_normed_two, unit_two, inverse_two, gain_two)
    grad_residual_two = grad_output + grad_norm_two
    grad_proj = grad_residual_two.astype(jnp.bfloat16)
    grad_attn_rows = jnp.einsum(
        "td,ed->te", grad_proj, out_full, preferred_element_type=jnp.float32
    ).astype(jnp.bfloat16)
    term_out = jnp.einsum("te,td->ed", attn_rows, grad_proj, preferred_element_type=jnp.float32)
    grad_heads = lax.all_to_all(
        grad_attn_rows.reshape(tokens, groups, group_heads * HEAD_DIM),
        "seq",
        split_axis=1,
        concat_axis=0,
        tiled=True,
    )
    grad_query, grad_keys, grad_values = attend_backward(
        head_queries,
        head_keys,
        head_values,
        log_totals,
        grad_heads.reshape(-1, group_heads, HEAD_DIM),
    )
    back_query, back_keys, back_values = (
        lax.all_to_all(
            grad_query.astype(jnp.bfloat16).reshape(-1, 1, group_heads * HEAD_DIM),
            "seq",
            split_axis=0,
            concat_axis=1,
            tiled=True,
        ),
        lax.all_to_all(
            grad_keys.astype(jnp.bfloat16)[:, None, :],
            "seq",
            split_axis=0,
            concat_axis=1,
            tiled=True,
        ),
        lax.all_to_all(
            grad_values.astype(jnp.bfloat16)[:, None, :],
            "seq",
            split_axis=0,
            concat_axis=1,
            tiled=True,
        ),
    )
    grad_query_rows = unrotate(
        back_query.reshape(tokens, HEADS, HEAD_DIM).astype(jnp.float32), cosine, sine
    )
    grad_key_rows = unrotate(
        jnp.sum(back_keys.astype(jnp.float32).reshape(tokens, KV_HEADS, repeat, HEAD_DIM), axis=2),
        cosine,
        sine,
    )
    grad_value_rows = jnp.sum(
        back_values.astype(jnp.float32).reshape(tokens, KV_HEADS, repeat, HEAD_DIM), axis=2
    )
    grad_mixed = jnp.concatenate(
        [
            grad_query_rows.reshape(tokens, width_query),
            grad_key_rows.reshape(tokens, width_key),
            grad_value_rows.reshape(tokens, width_key),
        ],
        axis=1,
    ).astype(jnp.bfloat16)
    term_qkv = jnp.einsum("td,tc->dc", normed_one, grad_mixed, preferred_element_type=jnp.float32)
    term_bias = jnp.sum(grad_mixed.astype(jnp.float32), axis=0)
    grad_normed_one = jnp.einsum(
        "tc,dc->td", grad_mixed, qkv_full, preferred_element_type=jnp.float32
    )
    grad_norm_one, term_gain_one = norm_backward(grad_normed_one, unit_one, inverse_one, gain_one)
    grad_rows = grad_residual_two + grad_norm_one
    shard_gain_one, shard_qkv, shard_bias, shard_out, shard_gain_two = (
        lax.psum_scatter(
            term_gain_one.astype(jnp.bfloat16), "fsdp", scatter_dimension=0, tiled=True
        ).astype(jnp.float32),
        lax.psum_scatter(
            term_qkv.astype(jnp.bfloat16), "fsdp", scatter_dimension=0, tiled=True
        ).astype(jnp.float32),
        lax.psum_scatter(
            term_bias.astype(jnp.bfloat16), "fsdp", scatter_dimension=0, tiled=True
        ).astype(jnp.float32),
        lax.psum_scatter(
            term_out.astype(jnp.bfloat16), "fsdp", scatter_dimension=0, tiled=True
        ).astype(jnp.float32),
        lax.psum_scatter(
            term_gain_two.astype(jnp.bfloat16), "fsdp", scatter_dimension=0, tiled=True
        ).astype(jnp.float32),
    )
    totals = (
        lax.psum(shard_gain_one.astype(jnp.bfloat16), "seq").astype(jnp.float32),
        lax.psum(shard_qkv.astype(jnp.bfloat16), "seq").astype(jnp.float32),
        lax.psum(shard_bias.astype(jnp.bfloat16), "seq").astype(jnp.float32),
        lax.psum(shard_out.astype(jnp.bfloat16), "seq").astype(jnp.float32),
        lax.psum(shard_gain_two.astype(jnp.bfloat16), "seq").astype(jnp.float32),
        lax.psum(shard_gate.astype(jnp.bfloat16), "seq").astype(jnp.float32),
        lax.psum(shard_up.astype(jnp.bfloat16), "seq").astype(jnp.float32),
        lax.psum(shard_down.astype(jnp.bfloat16), "seq").astype(jnp.float32),
    )
    return (
        hidden_out[None],
        grad_rows[None],
        totals[0],
        totals[1],
        totals[2],
        totals[3],
        totals[4],
        totals[5],
        totals[6],
        totals[7],
    )


def per_device(*arguments):
    return (per_device_kernels if kernels_fit(*arguments) else per_device_gathered)(*arguments)


def solution(mesh):
    placed = (
        P("fsdp", "seq", None),
        P("fsdp", "seq"),
        P("fsdp"),
        P("fsdp", None),
        P("fsdp"),
        P("fsdp", None),
        P("fsdp"),
        P("fsdp", None),
        P("fsdp", None),
        P("fsdp", None),
        P("fsdp", "seq", None),
    )
    return jax.shard_map(
        per_device,
        mesh=mesh,
        in_specs=placed,
        out_specs=(
            P("fsdp", "seq", None),
            P("fsdp", "seq", None),
            P("fsdp"),
            P("fsdp", None),
            P("fsdp"),
            P("fsdp", None),
            P("fsdp"),
            P("fsdp", None),
            P("fsdp", None),
            P("fsdp", None),
        ),
        check_vma=False,
    )
```

```python
import functools
import math

import jax
import jax.numpy as jnp
from jax import lax
from jax.experimental import pallas as pl
from jax.experimental.pallas import tpu as pltpu
from jax.sharding import PartitionSpec as P

HEADS = 12
KV_HEADS = 2
HEAD_DIM = 128


norm_eps = 1e-06
rope_base = 1000000.0


def rope_tables(position_row):
    half_dim = HEAD_DIM // 2
    frequency = jnp.exp(
        -(jnp.arange(half_dim, dtype=jnp.float32) * 2.0 / HEAD_DIM) * math.log(rope_base)
    )
    angles = position_row.astype(jnp.float32)[:, None] * frequency[None, :]
    angles = jnp.concatenate([angles, angles], axis=-1)
    return (jnp.cos(angles), jnp.sin(angles))


def rotate(values, cosine, sine):
    half_dim = values.shape[-1] // 2
    turned = jnp.concatenate([-values[..., half_dim:], values[..., :half_dim]], axis=-1)
    return values * cosine[:, None, :] + turned * sine[:, None, :]


def unrotate(grads_rot, cosine, sine):
    half_dim = grads_rot.shape[-1] // 2
    scaled = grads_rot * sine[:, None, :]
    return grads_rot * cosine[:, None, :] + jnp.concatenate(
        [scaled[..., half_dim:], -scaled[..., :half_dim]], axis=-1
    )


def norm_forward(values, gain):
    inverse = lax.rsqrt(jnp.mean(values * values, axis=-1, keepdims=True) + norm_eps)
    unit_rows = values * inverse
    return (unit_rows, inverse, (unit_rows * gain).astype(jnp.bfloat16))


def norm_backward(grad_normed, unit_rows, inverse, gain):
    grad_unit = grad_normed * gain
    grad_values = inverse * (
        grad_unit - unit_rows * jnp.mean(grad_unit * unit_rows, axis=-1, keepdims=True)
    )
    grad_gain = jnp.sum(grad_normed * unit_rows, axis=0)
    return (grad_values, grad_gain)


def masked_scores(queries, keys, block_start, block_rows):
    length = keys.shape[0]
    query_block = lax.dynamic_slice_in_dim(queries, block_start, block_rows, 0)
    scores = jnp.einsum(
        "bhd,ld->hbl", query_block, keys, preferred_element_type=jnp.float32
    ) * HEAD_DIM ** (-0.5)
    row_index = block_start + jnp.arange(block_rows)
    column_index = jnp.arange(length)
    allowed = column_index[None, :] <= row_index[:, None]
    return (query_block, jnp.where(allowed[None], scores, -1e30))


def attend_forward(queries, keys, values):
    length = keys.shape[0]
    block_rows = min(512, length)
    block_count = length // block_rows

    def one_block(block_start):
        query_block, scores = masked_scores(queries, keys, block_start, block_rows)
        row_max = jnp.max(scores, axis=-1, keepdims=True)
        exponent = jnp.exp(scores - row_max)
        row_total = jnp.sum(exponent, axis=-1, keepdims=True)
        probability = (exponent / row_total).astype(jnp.bfloat16)
        result = jnp.einsum("hbl,ld->bhd", probability, values, preferred_element_type=jnp.float32)
        return (result.astype(jnp.bfloat16), (row_max + jnp.log(row_total))[..., 0])

    results, log_totals = lax.map(one_block, jnp.arange(block_count) * block_rows)
    return (results.reshape(length, queries.shape[1], queries.shape[2]), log_totals)


def attend_backward(queries, keys, values, log_totals, grad_out):
    length = keys.shape[0]
    block_rows = min(512, length)
    block_count = length // block_rows
    score_scale = HEAD_DIM ** (-0.5)

    def one_block(running, inputs):
        grad_keys, grad_values = running
        block_start, log_block = inputs
        query_block, scores = masked_scores(queries, keys, block_start, block_rows)
        grad_block = lax.dynamic_slice_in_dim(grad_out, block_start, block_rows, 0)
        probability = jnp.exp(scores - log_block[..., None])
        grad_probs = jnp.einsum(
            "bhd,ld->hbl", grad_block, values, preferred_element_type=jnp.float32
        )
        row_delta = jnp.sum(probability * grad_probs, axis=-1, keepdims=True)
        grad_scores = (probability * (grad_probs - row_delta)).astype(jnp.bfloat16)
        grad_query = (
            jnp.einsum("hbl,ld->bhd", grad_scores, keys, preferred_element_type=jnp.float32)
            * score_scale
        )
        grad_keys = (
            grad_keys
            + jnp.einsum(
                "hbl,bhd->ld", grad_scores, query_block, preferred_element_type=jnp.float32
            )
            * score_scale
        )
        grad_values = grad_values + jnp.einsum(
            "hbl,bhd->ld",
            probability.astype(jnp.bfloat16),
            grad_block,
            preferred_element_type=jnp.float32,
        )
        return ((grad_keys, grad_values), grad_query)

    zero_rows = jnp.zeros((length, keys.shape[1]), jnp.float32)
    (grad_keys, grad_values), grad_query = lax.scan(
        one_block, (zero_rows, zero_rows), (jnp.arange(block_count) * block_rows, log_totals)
    )
    return (grad_query.reshape(queries.shape), grad_keys, grad_values)


MESH = pl.DeviceIdType.MESH
VMEM_BYTES = 67_000_000
NN = (((1,), (0,)), ((), ()))
NT = (((1,), (1,)), ((), ()))
TN = (((0,), (0,)), ((), ()))


def matmul(left, right, dims):
    return lax.dot_general(left, right, dims, preferred_element_type=jnp.float32)


def ring_place(index, size):
    side = index % 2
    return (index // 2) * (1 - side) + (size - 1 - index // 2) * side


def ring_member(place, size):
    side = place // (size // 2)
    return 2 * (place * (1 - side) + (size - 1 - place) * side) + side


def seq_partners(seq):
    core = seq + 1 - 2 * (seq % 2)
    far = (seq + 2) % 4
    return core, far, (core + 2) % 4


def greet(targets):
    barrier = pltpu.get_barrier_semaphore()
    for target in targets:
        pl.semaphore_signal(barrier, inc=1, device_id=target, device_id_type=MESH)
    pl.semaphore_wait(barrier, len(targets))


def for_blocks(width, block, body):
    @pl.loop(0, width // block)
    def _(at):
        body(pl.ds(pl.multiple_of(at * block, block), block))

    if width % block:
        body(pl.ds(width - width % block, width % block))


def gather_kernel(
    size,
    rows_ref,
    trig_ref,
    piece_ref,
    small_ref,
    rows_out,
    trig_out,
    piece_out,
    proj_out,
    small_out,
    rows_all,
    trig_all,
    pieces,
    proj,
    smalls,
    load_sems,
    store_sems,
    ring_send,
    ring_recv,
    small_send,
    small_recv,
    seq_send,
    seq_recv,
    proj_send,
    proj_recv,
):
    depth, joint = piece_ref.shape
    half = depth // 2
    group_width = proj.shape[0]
    cut = joint - group_width
    per_group = group_width // depth
    me = lax.axis_index("fsdp")
    seq = lax.axis_index("seq")
    place = ring_place(me, size)
    right = ring_member((place + 1) % size, size)
    left = ring_member((place + size - 1) % size, size)
    core, far, diagonal = seq_partners(seq)
    sides = ((right, pl.ds(0, half)), (left, pl.ds(half, half)))

    loads = [
        pltpu.make_async_copy(piece_ref, pieces.at[me], load_sems.at[0]),
        pltpu.make_async_copy(rows_ref, rows_all.at[seq], load_sems.at[1]),
        pltpu.make_async_copy(trig_ref, trig_all.at[seq], load_sems.at[2]),
        pltpu.make_async_copy(small_ref, smalls.at[me], load_sems.at[3]),
    ]
    for load in loads:
        load.start()
    greet(({"fsdp": right}, {"fsdp": left}, {"seq": core}, {"seq": far}, {"seq": diagonal}))

    def piece_of(step, side):
        return ring_member((place + size - step if side == 0 else place + step) % size, size)

    def ring_copy(step, side):
        target, span = sides[side]
        at = piece_of(step, side)
        return pltpu.make_async_remote_copy(
            src_ref=pieces.at[at, span],
            dst_ref=pieces.at[at, span],
            send_sem=ring_send.at[side, step],
            recv_sem=ring_recv.at[side, step],
            device_id={"fsdp": target},
            device_id_type=MESH,
        )

    def small_copy(step):
        at = piece_of(step, 0)
        return pltpu.make_async_remote_copy(
            src_ref=smalls.at[at],
            dst_ref=smalls.at[at],
            send_sem=small_send.at[step],
            recv_sem=small_recv.at[step],
            device_id={"fsdp": right},
            device_id_type=MESH,
        )

    def seq_copy(which, block, target, at):
        held = (rows_all, trig_all)[which]
        return pltpu.make_async_remote_copy(
            src_ref=held.at[block],
            dst_ref=held.at[block],
            send_sem=seq_send.at[which, at],
            recv_sem=seq_recv.at[which, at],
            device_id={"seq": target},
            device_id_type=MESH,
        )

    def proj_part(step, side):
        at = piece_of(step, side)
        owner = at // per_group
        row = pl.multiple_of((at % per_group) * depth + side * half, half)
        source = pieces.at[at, pl.ds(side * half, half), pl.ds(cut, group_width)]
        target = proj.at[pl.ds(row, half), pl.ds(pl.multiple_of(seq * group_width, 128), group_width)]
        return at, owner, source, target

    def proj_copy(step, side):
        at, owner, source, target = proj_part(step, side)
        return owner, pltpu.make_async_remote_copy(
            src_ref=source,
            dst_ref=target,
            send_sem=proj_send.at[side, step],
            recv_sem=proj_recv.at[seq, at % per_group, side],
            device_id={"seq": owner},
            device_id_type=MESH,
        )

    def proj_start(step, side):
        owner, copy = proj_copy(step, side)

        @pl.when(owner != seq)
        def _():
            copy.start()

        @pl.when(owner == seq)
        def _():
            _, _, source, target = proj_part(step, side)
            pltpu.make_async_copy(source, target, proj_send.at[side, step]).start()

    loads[0].wait()
    for side in range(2):
        ring_copy(0, side).start()
    loads[3].wait()
    small_copy(0).start()
    for which in (1, 0):
        loads[1 + which].wait()
        seq_copy(which, seq, far, 1).start()
        seq_copy(which, seq, core, 0).start()
    for side in range(2):
        proj_start(0, side)

    for step in range(size - 1):
        for side in range(2):
            ring_copy(step, side).wait_recv()
            if step < size - 2:
                ring_copy(step + 1, side).start()
        small_copy(step).wait_recv()
        if step < size - 2:
            small_copy(step + 1).start()
        for side in range(2):
            proj_start(step + 1, side)
        if step == min(1, size - 2):
            for which in (1, 0):
                seq_copy(which, seq, far, 1).wait_recv()
                seq_copy(which, far, core, 2).start()

    store_pieces = pltpu.make_async_copy(pieces, piece_out, store_sems.at[0])
    store_small = pltpu.make_async_copy(smalls, small_out, store_sems.at[1])
    store_pieces.start()
    store_small.start()
    for which in (1, 0):
        seq_copy(which, seq, core, 0).wait_recv()
        seq_copy(which, far, core, 2).wait_recv()
    store_rows = pltpu.make_async_copy(rows_all, rows_out, store_sems.at[2])
    store_trig = pltpu.make_async_copy(trig_all, trig_out, store_sems.at[3])
    store_rows.start()
    store_trig.start()
    for peer in (core, far, diagonal):
        for at in range(per_group):
            for side in range(2):
                pltpu.make_async_remote_copy(
                    src_ref=pieces.at[0, pl.ds(0, half), pl.ds(cut, group_width)],
                    dst_ref=proj.at[pl.ds(0, half), pl.ds(0, group_width)],
                    send_sem=proj_send.at[side, 0],
                    recv_sem=proj_recv.at[peer, at, side],
                    device_id={"seq": peer},
                    device_id_type=MESH,
                ).wait_recv()
    for step in range(size):
        for side in range(2):
            owner, copy = proj_copy(step, side)

            @pl.when(owner != seq)
            def _():
                copy.wait_send()

            @pl.when(owner == seq)
            def _():
                _, _, source, target = proj_part(step, side)
                pltpu.make_async_copy(source, target, proj_send.at[side, step]).wait()

    store_proj = pltpu.make_async_copy(proj, proj_out, store_sems.at[4])
    store_proj.start()
    for step in range(size - 1):
        for side in range(2):
            ring_copy(step, side).wait_send()
        small_copy(step).wait_send()
    for which in (1, 0):
        seq_copy(which, seq, core, 0).wait_send()
        seq_copy(which, seq, far, 1).wait_send()
        seq_copy(which, far, core, 2).wait_send()
    for store in (store_pieces, store_small, store_rows, store_trig, store_proj):
        store.wait()


def gather_inputs(rows, trig, piece, small):
    size = lax.axis_size("fsdp")
    groups = lax.axis_size("seq")
    tokens, width = rows.shape
    depth, joint = piece.shape
    group_width = width // groups
    f32, bf16 = jnp.float32, jnp.bfloat16
    shapes = (
        ((groups, tokens, width), bf16),
        ((groups,) + trig.shape, f32),
        ((size, depth, joint), bf16),
        ((group_width, width), bf16),
        ((size,) + small.shape, bf16),
    )
    dma = pltpu.SemaphoreType.DMA
    anywhere = pl.BlockSpec(memory_space=pl.ANY)
    per_group = group_width // depth
    return pl.pallas_call(
        functools.partial(gather_kernel, size),
        out_shape=tuple(jax.ShapeDtypeStruct(*shape) for shape in shapes),
        in_specs=[anywhere] * 4,
        out_specs=(anywhere,) * 5,
        scratch_shapes=[pltpu.VMEM(*shape) for shape in shapes]
        + [
            dma((4,)),
            dma((5,)),
            dma((2, size)),
            dma((2, size)),
            dma((size,)),
            dma((size,)),
            dma((2, 3)),
            dma((2, 3)),
            dma((2, size)),
            dma((groups, per_group, 2)),
        ],
        compiler_params=pltpu.CompilerParams(
            collective_id=1, has_side_effects=True, vmem_limit_bytes=32_000_000
        ),
        name="gather_inputs",
    )(rows, trig, piece, small)


def turn_tables(trig):
    lane = lax.broadcasted_iota(jnp.int32, trig.shape, 1)
    swapped = pltpu.roll(trig, HEAD_DIM // 2, 1)
    first = lane < HEAD_DIM // 2
    return jnp.where(first, trig, swapped), jnp.where(first, -swapped, trig)


def head_columns(at):
    return slice(at * HEAD_DIM, (at + 1) * HEAD_DIM)


def causal(scores, start):
    rows = lax.broadcasted_iota(jnp.int32, scores.shape, 0) + start
    columns = lax.broadcasted_iota(jnp.int32, scores.shape, 1)
    return jnp.where(columns <= rows, scores, -1e30)


def attend_forward_kernel(
    block,
    rows_ref,
    weight_ref,
    proj_ref,
    trig_ref,
    gain_ref,
    bias_ref,
    normed_ref,
    heads_ref,
    out_ref,
    log_ref,
    part_ref,
):
    length = rows_ref.shape[0]
    used = heads_ref.shape[1]
    count = used // HEAD_DIM - 2
    scale = HEAD_DIM**-0.5
    for start in range(0, length, block):
        span = slice(start, start + block)
        rows = rows_ref[span, :].astype(jnp.float32)
        inverse = lax.rsqrt(jnp.mean(rows * rows, axis=-1, keepdims=True) + norm_eps)
        normed_ref[span, :] = (rows * inverse * gain_ref[...]).astype(jnp.bfloat16)
        mixed = matmul(normed_ref[span, :], weight_ref[:, :used], NN) + bias_ref[...]
        cosine, sine = turn_tables(trig_ref[span, :])
        for at in range(count + 1):
            part = mixed[:, head_columns(at)]
            turned = pltpu.roll(part, HEAD_DIM // 2, 1)
            heads_ref[span, head_columns(at)] = (part * cosine + turned * sine).astype(
                jnp.bfloat16
            )
        heads_ref[span, head_columns(count + 1)] = mixed[:, head_columns(count + 1)].astype(
            jnp.bfloat16
        )
    lane = lax.broadcasted_iota(jnp.int32, (block, HEAD_DIM), 1)
    for start in range(0, length, block):
        span = slice(start, start + block)
        seen = slice(0, start + block)
        logs = jnp.zeros((block, HEAD_DIM), jnp.float32)
        for at in range(count):
            scores = causal(
                matmul(heads_ref[span, head_columns(at)], heads_ref[seen, head_columns(count)], NT)
                * scale,
                start,
            )
            top = jnp.max(scores, axis=-1, keepdims=True)
            exponent = jnp.exp(scores - top)
            total = jnp.sum(exponent, axis=-1, keepdims=True)
            probability = (exponent / total).astype(jnp.bfloat16)
            out_ref[span, head_columns(at)] = matmul(
                probability, heads_ref[seen, head_columns(count + 1)], NN
            ).astype(jnp.bfloat16)
            logs = jnp.where(lane == at, top + jnp.log(total), logs)
        log_ref[span, :] = logs
        part_ref[span, :] = matmul(out_ref[span, :], proj_ref[...], NN).astype(jnp.bfloat16)


def attend_group(rows, weight, proj, trig, gain, bias):
    length, width = rows.shape
    used = bias.shape[1]
    own = proj.shape[0]
    bf16 = jnp.bfloat16
    inside = pl.BlockSpec(memory_space=pltpu.VMEM)
    return pl.pallas_call(
        functools.partial(attend_forward_kernel, 256),
        out_shape=(
            jax.ShapeDtypeStruct((length, width), bf16),
            jax.ShapeDtypeStruct((length, used), bf16),
            jax.ShapeDtypeStruct((length, own), bf16),
            jax.ShapeDtypeStruct((length, HEAD_DIM), jnp.float32),
            jax.ShapeDtypeStruct((length, width), bf16),
        ),
        in_specs=[inside] * 6,
        out_specs=(inside,) * 5,
        compiler_params=pltpu.CompilerParams(vmem_limit_bytes=VMEM_BYTES),
        cost_estimate=pl.CostEstimate(
            flops=2 * length * width * (used + own) + 4 * length * length * own,
            bytes_accessed=2 * (3 * length * width + 2 * width * width),
            transcendentals=length * length * own // HEAD_DIM,
        ),
        name="attend_forward",
    )(rows, weight, proj, trig, gain, bias)


def mlp_kernel(
    size,
    hidden_ref,
    part_ref,
    gain_ref,
    cots_ref,
    gate_ref,
    up_ref,
    down_ref,
    outs_ref,
    resid_ref,
    proj_grads_ref,
    back_ref,
    gain_grad_ref,
    sums_ref,
    rows_all,
    cots,
    weights,
    grads,
    hid,
    dgate,
    dup,
    partial,
    resid,
    sums_in,
    sums_out,
    outs,
    seq_in,
    seq_own,
    load_sems,
    cot_sems,
    ring_send,
    ring_recv,
    sum_send,
    sum_recv,
    out_sems,
    seq_send,
    seq_recv,
    swap_send,
    swap_recv,
    swap_ready,
):
    tokens, width = hidden_ref.shape
    units = gate_ref.shape[0]
    half = tokens // 2
    me = lax.axis_index("fsdp")
    seq = lax.axis_index("seq")
    place = ring_place(me, size)
    right = ring_member((place + 1) % size, size)
    left = ring_member((place + size - 1) % size, size)
    core, far, diagonal = seq_partners(seq)
    sides = ((right, pl.ds(0, half)), (left, pl.ds(half, half)))

    def owner_of(step, side):
        return ring_member((place + size - step if side == 0 else place + step) % size, size)

    def part_rows(block):
        return part_ref.at[pl.ds(pl.multiple_of(block * tokens, tokens), tokens)]

    part_loads = [
        pltpu.make_async_copy(part_rows(far), seq_own.at[0], load_sems.at[3]),
        pltpu.make_async_copy(part_rows(seq), seq_own.at[1], load_sems.at[4]),
        pltpu.make_async_copy(hidden_ref, seq_own.at[2], load_sems.at[5]),
    ]
    weight_loads = [
        pltpu.make_async_copy(ref, weights.at[at], load_sems.at[at])
        for at, ref in enumerate((gate_ref, up_ref, down_ref))
    ]
    for load in part_loads:
        load.start()
    greet(({"fsdp": right}, {"fsdp": left}, {"seq": core}, {"seq": far}))

    def seq_copy(at, source, target):
        return pltpu.make_async_remote_copy(
            src_ref=source,
            dst_ref=seq_in.at[at],
            send_sem=seq_send.at[at],
            recv_sem=seq_recv.at[at],
            device_id={"seq": target},
            device_id_type=MESH,
        )

    core_copies = [seq_copy(0, part_rows(diagonal), core), seq_copy(1, part_rows(core), core)]
    far_copy = seq_copy(2, sums_out.at[0], far)
    for copy in core_copies:
        copy.start()

    def cot_copies(step):
        return [
            pltpu.make_async_copy(
                cots_ref.at[
                    pl.ds(
                        pl.multiple_of(owner_of(step, side) * tokens + side * half, half), half
                    )
                ],
                cots.at[step % 2, sides[side][1]],
                cot_sems.at[step % 2, side],
            )
            for side in range(2)
        ]

    for load in weight_loads + cot_copies(0):
        load.start()

    @pl.loop(0, units // 16)
    def _(at):
        zeros = jnp.zeros((3, 16, width), jnp.float32)
        grads[:, pl.ds(pl.multiple_of(at * 16, 16), 16), :] = zeros

    part_loads[0].wait()
    core_copies[0].wait_recv()
    sums_out[0] = (seq_own[0].astype(jnp.float32) + seq_in[0].astype(jnp.float32)).astype(
        jnp.bfloat16
    )
    far_copy.start()
    part_loads[1].wait()
    part_loads[2].wait()
    core_copies[1].wait_recv()
    resid[...] = (
        seq_own[1].astype(jnp.float32)
        + seq_in[1].astype(jnp.float32)
        + seq_own[2].astype(jnp.float32)
    )
    far_copy.wait_recv()
    resid[...] += seq_in[2].astype(jnp.float32)

    def inverse_of(values):
        return lax.rsqrt(jnp.mean(values * values, axis=-1, keepdims=True) + norm_eps)

    rows_all[0] = (resid[...] * inverse_of(resid[...]) * gain_ref[...]).astype(jnp.bfloat16)
    far_copy.wait_send()
    resid_store = pltpu.make_async_copy(resid, resid_ref, load_sems.at[6])
    resid_store.start()

    def row_copy(step, side):
        target, span = sides[side]
        return pltpu.make_async_remote_copy(
            src_ref=rows_all.at[step, span],
            dst_ref=rows_all.at[step + 1, span],
            send_sem=ring_send.at[side, step],
            recv_sem=ring_recv.at[side, step + 1],
            device_id={"fsdp": target},
            device_id_type=MESH,
        )

    def sum_copy(step, side):
        target, span = sides[side]
        return pltpu.make_async_remote_copy(
            src_ref=sums_out.at[step % 2, span],
            dst_ref=sums_in.at[step, span],
            send_sem=sum_send.at[side, step],
            recv_sem=sum_recv.at[side, step],
            device_id={"fsdp": target},
            device_id_type=MESH,
        )

    def out_copy(step, side):
        at = pl.multiple_of(owner_of(step, side) * tokens + side * half, half)
        return pltpu.make_async_copy(
            outs.at[step % 2, sides[side][1]], outs_ref.at[pl.ds(at, half)], out_sems.at[side, step]
        )

    def elementwise(step, span):
        rows = rows_all[step]
        gate = matmul(rows, weights[0, span, :], NT)
        up = matmul(rows, weights[1, span, :], NT)
        grad_hidden = matmul(cots[step % 2], weights[2, span, :], NT)
        sigmoid = jax.nn.sigmoid(gate)
        activated = gate * sigmoid
        hid[:, span] = (activated * up).astype(jnp.bfloat16)
        dgate[:, span] = (
            grad_hidden * up * sigmoid * (1.0 + gate * (1.0 - sigmoid))
        ).astype(jnp.bfloat16)
        dup[:, span] = (grad_hidden * activated).astype(jnp.bfloat16)

    for load in weight_loads:
        load.wait()

    @pl.loop(0, size)
    def _(step):
        slot = step % 2

        @pl.when(step >= 1)
        def _():
            for side in range(2):
                row_copy(step - 1, side).wait_recv()

        @pl.when(step < size - 1)
        def _():
            for side in range(2):
                row_copy(step, side).start()

        for load in cot_copies(step):
            load.wait()

        @pl.when(step < size - 1)
        def _():
            for load in cot_copies(step + 1):
                load.start()

        for_blocks(units, 256, functools.partial(elementwise, step))

        def back_part(span):
            partial[:, span] = matmul(dgate[...], weights[0, :, span], NN) + matmul(
                dup[...], weights[1, :, span], NN
            )

        for_blocks(width, 256, back_part)

        @pl.when(step == 0)
        def _():
            back_ref[...] = partial[...]

        @pl.when(step >= 3)
        def _():
            for side in range(2):
                sum_copy(step - 2, side).wait_send()

        @pl.when(step == 1)
        def _():
            sums_out[slot] = partial[...].astype(jnp.bfloat16)

        @pl.when(step >= 2)
        def _():
            for side in range(2):
                sum_copy(step - 1, side).wait_recv()
            sums_out[slot] = (partial[...] + sums_in[step - 1].astype(jnp.float32)).astype(
                jnp.bfloat16
            )

        @pl.when(step >= 1)
        def _():
            for side in range(2):
                sum_copy(step, side).start()

        @pl.when(step >= 2)
        def _():
            for side in range(2):
                out_copy(step - 2, side).wait()

        def out_part(span):
            outs[slot, :, span] = matmul(hid[...], weights[2, :, span], NN).astype(jnp.bfloat16)

        for_blocks(width, 256, out_part)
        for side in range(2):
            out_copy(step, side).start()

        def weight_part(span):
            rows, cot = rows_all[step, :, span], cots[slot, :, span]
            grads[0, :, span] += matmul(dgate[...], rows, TN)
            grads[1, :, span] += matmul(dup[...], rows, TN)
            grads[2, :, span] += matmul(hid[...], cot, TN)

        for_blocks(width, 256, weight_part)

    share = units // 2
    kept = pl.multiple_of((seq % 2) * share, 16)
    given = pl.multiple_of((1 - seq % 2) * share, 16)
    pl.semaphore_signal(swap_ready, inc=1, device_id={"seq": core}, device_id_type=MESH)
    swaps = [
        pltpu.make_async_remote_copy(
            src_ref=weights.at[at, pl.ds(given, share)],
            dst_ref=weights.at[at, pl.ds(given, share)],
            send_sem=swap_send.at[at],
            recv_sem=swap_recv.at[at],
            device_id={"seq": core},
            device_id_type=MESH,
        )
        for at in range(3)
    ]
    for at in range(3):

        @pl.loop(0, share // 16)
        def _(block):
            span = pl.ds(pl.multiple_of(given + block * 16, 16), 16)
            weights[at, span, :] = grads[at, span, :].astype(jnp.bfloat16)

        if at == 0:
            pl.semaphore_wait(swap_ready, 1)
        swaps[at].start()

    for side in range(2):
        sum_copy(size - 1, side).wait_recv()
    grad_normed = back_ref[...] + sums_in[size - 1].astype(jnp.float32)
    inverse = inverse_of(resid[...])
    unit_rows = resid[...] * inverse
    gain_grad_ref[...] = jnp.sum(grad_normed * unit_rows, axis=0, keepdims=True)
    grad_unit = grad_normed * gain_ref[...]
    cot_own = pltpu.make_async_copy(
        cots_ref.at[pl.ds(pl.multiple_of(me * tokens, tokens), tokens)],
        cots.at[0],
        load_sems.at[7],
    )
    cot_own.start()
    cot_own.wait()
    back_ref[...] = cots[0].astype(jnp.float32) + inverse * (
        grad_unit - unit_rows * jnp.mean(grad_unit * unit_rows, axis=-1, keepdims=True)
    )
    for side in range(2):
        sum_copy(size - 2, side).wait_send()
        sum_copy(size - 1, side).wait_send()
    sums_out[0] = back_ref[...].astype(jnp.bfloat16)

    def grad_copy(source, block, target, at):
        return pltpu.make_async_remote_copy(
            src_ref=source,
            dst_ref=proj_grads_ref.at[block],
            send_sem=seq_send.at[at],
            recv_sem=seq_recv.at[at],
            device_id={"seq": target},
            device_id_type=MESH,
        )

    to_far = grad_copy(sums_out.at[0], seq, far, 3)
    to_core = grad_copy(sums_out.at[0], seq, core, 4)
    passed_on = grad_copy(proj_grads_ref.at[far], far, core, 5)
    keep = pltpu.make_async_copy(sums_out.at[0], proj_grads_ref.at[seq], load_sems.at[8])
    to_far.start()
    to_core.start()
    keep.start()
    stores = []
    for at in range(3):
        swaps[at].wait_recv()

        @pl.loop(0, share // 16)
        def _(block):
            span = pl.ds(pl.multiple_of(kept + block * 16, 16), 16)
            weights[at, span, :] = (
                grads[at, span, :] + weights[at, span, :].astype(jnp.float32)
            ).astype(jnp.bfloat16)

        done = weights.at[at, pl.ds(kept, share)]
        stores.append(
            pltpu.make_async_copy(done, sums_ref.at[at, pl.ds(kept, share)], load_sems.at[at])
        )
        swaps.append(
            pltpu.make_async_remote_copy(
                src_ref=done,
                dst_ref=sums_ref.at[at, pl.ds(kept, share)],
                send_sem=swap_send.at[3 + at],
                recv_sem=swap_recv.at[3 + at],
                device_id={"seq": core},
                device_id_type=MESH,
            )
        )
        stores[-1].start()
        swaps[-1].start()
    to_far.wait_recv()
    passed_on.start()
    for side in range(2):
        out_copy(size - 2, side).wait()
        out_copy(size - 1, side).wait()

        @pl.loop(0, size - 1)
        def _(step):
            row_copy(step, side).wait_send()

    for copy in core_copies + swaps + [to_far, to_core, passed_on]:
        copy.wait_send()
    to_core.wait_recv()
    passed_on.wait_recv()
    for copy in swaps[3:]:
        copy.wait_recv()
    for store in stores + [keep, resid_store]:
        store.wait()


def mlp_ring(hidden, part, gain, cots, gate_weight, up_weight, down_weight):
    size = lax.axis_size("fsdp")
    groups = lax.axis_size("seq")
    tokens, width = hidden.shape
    units = gate_weight.shape[0]
    anywhere = pl.BlockSpec(memory_space=pl.ANY)
    inside = pl.BlockSpec(memory_space=pltpu.VMEM)
    bf16, f32 = jnp.bfloat16, jnp.float32
    dma = pltpu.SemaphoreType.DMA
    return pl.pallas_call(
        functools.partial(mlp_kernel, size),
        out_shape=(
            jax.ShapeDtypeStruct((size * tokens, width), bf16),
            jax.ShapeDtypeStruct((tokens, width), f32),
            jax.ShapeDtypeStruct((groups, tokens, width), bf16),
            jax.ShapeDtypeStruct((tokens, width), f32),
            jax.ShapeDtypeStruct((1, width), f32),
            jax.ShapeDtypeStruct((3, units, width), bf16),
        ),
        in_specs=[anywhere, anywhere, inside, anywhere, anywhere, anywhere, anywhere],
        out_specs=(anywhere, anywhere, anywhere, inside, inside, anywhere),
        scratch_shapes=[
            pltpu.VMEM((size, tokens, width), bf16),
            pltpu.VMEM((2, tokens, width), bf16),
            pltpu.VMEM((3, units, width), bf16),
            pltpu.VMEM((3, units, width), f32),
            pltpu.VMEM((tokens, units), bf16),
            pltpu.VMEM((tokens, units), bf16),
            pltpu.VMEM((tokens, units), bf16),
            pltpu.VMEM((tokens, width), f32),
            pltpu.VMEM((tokens, width), f32),
            pltpu.VMEM((size, tokens, width), bf16),
            pltpu.VMEM((2, tokens, width), bf16),
            pltpu.VMEM((2, tokens, width), bf16),
            pltpu.VMEM((3, tokens, width), bf16),
            pltpu.VMEM((3, tokens, width), bf16),
            dma((9,)),
            dma((2, 2)),
            dma((2, size)),
            dma((2, size)),
            dma((2, size)),
            dma((2, size)),
            dma((2, size)),
            dma((6,)),
            dma((6,)),
            dma((6,)),
            dma((6,)),
            pltpu.SemaphoreType.REGULAR,
        ],
        compiler_params=pltpu.CompilerParams(
            collective_id=0, has_side_effects=True, vmem_limit_bytes=VMEM_BYTES
        ),
        name="mlp_ring",
    )(hidden, part, gain, cots, gate_weight, up_weight, down_weight)


def attend_backward_kernel(
    size,
    block,
    grads_ref,
    heads_ref,
    attended_ref,
    log_ref,
    proj_ref,
    weight_ref,
    normed_ref,
    trig_ref,
    hidden_ref,
    resid_grad_ref,
    gain_ref,
    gain_grad_ref,
    resid_ref,
    outs_ref,
    units_ref,
    grad_in_ref,
    hidden_out_ref,
    small_ref,
    shards_ref,
    far_units_ref,
    grad_heads,
    grad_mixed,
    grad_keys,
    grad_values,
    grad_normed,
    term_qkv,
    term_out,
    out_columns,
    qkv_in,
    out_in,
    qkv_sum,
    out_sum,
    shard,
    shard_all,
    out_own,
    out_recv,
    out_send,
    resid,
    seq_in,
    far_sum,
    small_in,
    load_sems,
    own_sems,
    out_sems,
    term_sems,
    column_sems,
    seq_sems,
    shard_sems,
    small_sems,
    unit_sems,
    pass_sems,
):
    length, width = grads_ref.shape
    tokens = hidden_ref.shape[0]
    used = heads_ref.shape[1]
    own = attended_ref.shape[1]
    count = own // HEAD_DIM
    scale = HEAD_DIM**-0.5
    half = tokens // 2
    depth = width // size
    term_half = depth // 2
    units = units_ref.shape[1]
    f32, bf16 = jnp.float32, jnp.bfloat16
    me = lax.axis_index("fsdp")
    seq = lax.axis_index("seq")
    place = ring_place(me, size)
    right = ring_member((place + 1) % size, size)
    left = ring_member((place + size - 1) % size, size)
    core, far, diagonal = seq_partners(seq)
    rounds = size.bit_length() - 1
    mirrors = [me + (1 - 2 * ((me // 2**at) % 2)) * 2**at for at in range(rounds)]
    ring = ({"fsdp": right}, {"fsdp": left})

    def owner_of(step, side):
        return ring_member((place + size - step if side == 0 else place + step) % size, size)

    def remote(source, target, sems, at, device):
        return pltpu.make_async_remote_copy(
            src_ref=source,
            dst_ref=target,
            send_sem=sems.at[(0,) + at],
            recv_sem=sems.at[(1,) + at],
            device_id=device,
            device_id_type=MESH,
        )

    greet(
        ring
        + ({"seq": core}, {"seq": far}, {"seq": diagonal})
        + tuple({"fsdp": mirror} for mirror in mirrors)
    )

    def own_load(step, side):
        at = pl.multiple_of(owner_of(step, side) * tokens + side * half, half)
        return pltpu.make_async_copy(
            outs_ref.at[pl.ds(at, half)],
            out_own.at[step % 2, pl.ds(side * half, half)],
            own_sems.at[step % 2, side],
        )

    def out_copy(step, side):
        span = pl.ds(side * half, half)
        return remote(
            out_send.at[step % 2, span], out_recv.at[step, span], out_sems, (side, step), ring[side]
        )

    def out_step(step):
        for side in range(2):
            own_load(step, side).wait()
            if step < size - 1:
                own_load(step + 1, side).start()
            if step >= 3:
                out_copy(step - 2, side).wait_send()
            if step >= 2:
                out_copy(step - 1, side).wait_recv()
        total = out_own[step % 2].astype(f32)
        if step >= 2:
            total += out_recv[step - 1].astype(f32)
        out_send[step % 2] = total.astype(bf16)
        for side in range(2):
            out_copy(step, side).start()

    resid_load = pltpu.make_async_copy(resid_ref, resid, load_sems.at[0])

    def out_finish():
        step = size
        for side in range(2):
            out_copy(step - 2, side).wait_send()
            out_copy(step - 1, side).wait_send()
            out_copy(step - 1, side).wait_recv()
        mine = pltpu.make_async_copy(
            outs_ref.at[pl.ds(pl.multiple_of(me * tokens, tokens), tokens)],
            out_own.at[0],
            load_sems.at[1],
        )
        mine.start()
        mine.wait()
        resid_load.wait()
        hidden_out_ref[...] = (
            resid[...] + out_own[0].astype(f32) + out_recv[size - 1].astype(f32)
        ).astype(bf16)

    share = units // 2
    piece = share // 5
    kept = (seq % 2) * share

    def unit_slice(ref, at):
        start = pl.multiple_of(kept + (at % 5) * piece, 16)
        return ref.at[at // 5, pl.ds(start, piece)]

    def unit_copy(at):
        return remote(
            unit_slice(units_ref, at), unit_slice(far_units_ref, at), unit_sems, (at,), {"seq": far}
        )

    def unit_pass(at):
        part = unit_slice(far_units_ref, at)
        return remote(part, part, pass_sems, (at,), {"seq": core})

    chunks = 15
    lag = 4

    def pump(at):
        if at < chunks:
            unit_copy(at).start()
        if at % 2 == 0 and at // 2 + 1 < size:
            out_step(at // 2 + 1)
        if lag <= at < chunks + lag:
            unit_copy(at - lag).wait_recv()
            unit_pass(at - lag).start()

    resid_load.start()
    for side in range(2):
        own_load(1, side).start()
    pump(0)

    for start in range(0, length, block):
        span = slice(start, start + block)
        grad_heads[span, :] = matmul(grads_ref[span, :], proj_ref[...], NT).astype(bf16)

    def out_term(span):
        term_out[:, span] = matmul(attended_ref[...], grads_ref[:, span], TN).astype(bf16)

    for_blocks(width, 256, out_term)

    def column_copy(at, target):
        slot = pl.multiple_of(seq * own, 16)
        return remote(
            term_out.at[:, pl.ds(pl.multiple_of(target * own, 128), own)],
            out_columns.at[pl.ds(slot, own)],
            column_sems,
            (at,),
            {"seq": target},
        )

    columns = [column_copy(at, target) for at, target in enumerate((core, far, diagonal))]
    for copy in columns:
        copy.start()
    mine = pl.multiple_of(seq * own, 128)
    out_columns[pl.ds(mine, own), :] = term_out[:, pl.ds(mine, own)]
    pump(1)
    grad_keys[...] = jnp.zeros_like(grad_keys)
    grad_values[...] = jnp.zeros_like(grad_values)
    lane = lax.broadcasted_iota(jnp.int32, (block, HEAD_DIM), 1)
    keys = slice(own, own + HEAD_DIM)
    values = slice(own + HEAD_DIM, used)
    for turn, start in enumerate(range(0, length, block)):
        span = slice(start, start + block)
        seen = slice(0, start + block)
        cosine, sine = turn_tables(trig_ref[span, :])

        @pl.loop(0, count)
        def _(at):
            head = pl.ds(pl.multiple_of(at * HEAD_DIM, HEAD_DIM), HEAD_DIM)
            query = heads_ref[span, head]
            grad = grad_heads[span, head]
            logs = jnp.sum(jnp.where(lane == at, log_ref[span, :], 0.0), axis=-1, keepdims=True)
            scores = causal(matmul(query, heads_ref[seen, keys], NT) * scale, start)
            probability = jnp.exp(scores - logs)
            grad_probs = matmul(grad, heads_ref[seen, values], NT)
            delta = jnp.sum(probability * grad_probs, axis=-1, keepdims=True)
            grad_scores = (probability * (grad_probs - delta)).astype(bf16)
            grad_query = matmul(grad_scores, heads_ref[seen, keys], NN) * scale
            grad_query = grad_query.astype(bf16).astype(f32)
            grad_mixed[span, head] = (
                grad_query * cosine + pltpu.roll(grad_query * sine, HEAD_DIM // 2, 1)
            ).astype(bf16)
            grad_keys[seen, :] += matmul(grad_scores, query, TN) * scale
            grad_values[seen, :] += matmul(probability.astype(bf16), grad, TN)

        pump(2 + turn)

    for start in range(0, length, block):
        span = slice(start, start + block)
        cosine, sine = turn_tables(trig_ref[span, :])
        part = grad_keys[span, :].astype(bf16).astype(f32)
        grad_mixed[span, keys] = (
            part * cosine + pltpu.roll(part * sine, HEAD_DIM // 2, 1)
        ).astype(bf16)
        grad_mixed[span, values] = grad_values[span, :].astype(bf16)

    def normed_part(span):
        grad_normed[:, span] = matmul(grad_mixed[...], weight_ref[span, :used], NT).astype(bf16)

    for_blocks(width, 256, normed_part)

    def block_rows(at):
        return grad_normed.at[pl.ds(pl.multiple_of(at * tokens, tokens), tokens)]

    to_core = [
        remote(block_rows(diagonal), seq_in.at[0], seq_sems, (0,), {"seq": core}),
        remote(block_rows(core), seq_in.at[1], seq_sems, (1,), {"seq": core}),
    ]
    to_far = remote(far_sum, seq_in.at[2], seq_sems, (2,), {"seq": far})
    for copy in to_core:
        copy.start()

    def qkv_term(span):
        term_qkv[span, :] = matmul(normed_ref[:, span], grad_mixed[...], TN).astype(bf16)

    for_blocks(width, 256, qkv_term)
    to_core[0].wait_recv()
    far_sum[...] = (block_rows(far)[...].astype(f32) + seq_in[0].astype(f32)).astype(bf16)
    to_far.start()
    small_in[0] = jnp.zeros((8, width), f32)
    small_in[0, 1:2, :] = gain_grad_ref[...]
    bias = jnp.sum(grad_mixed[...].astype(f32), axis=0, keepdims=True)
    small_in[0, 2:3, pl.ds(mine, own)] = bias[:, :own]
    kv_lane = pl.multiple_of((seq // 2) * HEAD_DIM, HEAD_DIM)
    small_in[0, 3:4, pl.ds(kv_lane, HEAD_DIM)] = bias[:, keys]
    small_in[0, 3:4, pl.ds(kv_lane + KV_HEADS * HEAD_DIM, HEAD_DIM)] = bias[:, values]
    pump(6)

    def term_rows(step, side):
        return pl.ds(
            pl.multiple_of(owner_of(step, side) * depth + side * term_half, 16), term_half
        )

    def term_copy(which, step, side):
        held, landed = ((qkv_sum, qkv_in), (out_sum, out_in))[which]
        span = pl.ds(side * term_half, term_half)
        return remote(
            held.at[step % 2, span], landed.at[step, span], term_sems, (which, side, step), ring[side]
        )

    def term_step(which, step):
        source, held, landed = ((term_qkv, qkv_sum, qkv_in), (out_columns, out_sum, out_in))[which]
        for side in range(2):
            if step >= 3:
                term_copy(which, step - 2, side).wait_send()
            total = source[term_rows(step, side), :].astype(f32)
            span = pl.ds(side * term_half, term_half)
            if step >= 2:
                term_copy(which, step - 1, side).wait_recv()
                total += landed[step - 1, span, :].astype(f32)
            held[step % 2, span, :] = total.astype(bf16)
            term_copy(which, step, side).start()

    def small_copy(at):
        device = ({"seq": core}, {"seq": far})[at] if at < 2 else {"fsdp": mirrors[at - 2]}
        return remote(small_in.at[2 * at], small_in.at[2 * at + 1], small_sems, (at,), device)

    def small_step(at):
        small_copy(at).wait_recv()
        small_in[2 * at + 2] = small_in[2 * at] + small_in[2 * at + 1]

    term_step(0, 1)
    for copy in columns:
        copy.wait_recv()
    term_step(1, 1)
    term_step(0, 2)
    term_step(1, 2)
    to_core[1].wait_recv()
    to_far.wait_recv()
    rows = hidden_ref[...].astype(f32)
    inverse = lax.rsqrt(jnp.mean(rows * rows, axis=-1, keepdims=True) + norm_eps)
    unit_rows = rows * inverse
    grad_rows = (
        block_rows(seq)[...].astype(f32) + seq_in[1].astype(f32) + seq_in[2].astype(f32)
    )
    small_in[0, 0:1, :] = jnp.sum(grad_rows * unit_rows, axis=0, keepdims=True)
    small_copy(0).start()
    grad_unit = grad_rows * gain_ref[...]
    grad_in_ref[...] = resid_grad_ref[...] + inverse * (
        grad_unit - unit_rows * jnp.mean(grad_unit * unit_rows, axis=-1, keepdims=True)
    )
    pump(7)
    total_rounds = rounds + 2
    done = 0
    for step in range(3, size):
        for which in range(2):
            term_step(which, step)
        if done < total_rounds:
            small_step(done)
            done += 1
            if done < total_rounds:
                small_copy(done).start()
        pump(5 + step)
    while done < total_rounds:
        small_step(done)
        done += 1
        if done < total_rounds:
            small_copy(done).start()
    small_ref[...] = small_in[2 * total_rounds]
    for which in range(2):
        source, landed = ((term_qkv, qkv_in), (out_columns, out_in))[which]
        lanes = slice(0, used) if which == 0 else slice(used, used + own)
        for side in range(2):
            span = pl.ds(side * term_half, term_half)
            term_copy(which, size - 2, side).wait_send()
            term_copy(which, size - 1, side).wait_send()
            term_copy(which, size - 1, side).wait_recv()
            shard[span, lanes] = (
                source[pl.ds(pl.multiple_of(me * depth + side * term_half, 16), term_half), :].astype(f32)
                + landed[size - 1, span, :].astype(f32)
            ).astype(bf16)
    shard_far = remote(shard, shard_all.at[seq], shard_sems, (0,), {"seq": far})
    shard_core = remote(shard, shard_all.at[seq], shard_sems, (1,), {"seq": core})
    shard_pass = remote(shard_all.at[far], shard_all.at[far], shard_sems, (2,), {"seq": core})
    shard_far.start()
    shard_core.start()
    shard_all[seq] = shard[...]
    for at in range(5 + size, chunks):
        pump(at)
    shard_far.wait_recv()
    shard_pass.start()
    out_finish()
    for at in range(max(chunks, 5 + size), chunks + lag):
        pump(at)
    shard_core.wait_recv()
    shard_pass.wait_recv()
    store = pltpu.make_async_copy(shard_all, shards_ref, load_sems.at[1])
    store.start()
    for at in range(chunks):
        unit_pass(at).wait_recv()
        unit_copy(at).wait_send()
        unit_pass(at).wait_send()
    for at in range(total_rounds):
        small_copy(at).wait_send()
    for copy in columns + to_core + [to_far, shard_far, shard_core, shard_pass]:
        copy.wait_send()
    store.wait()


def attend_group_backward(
    grads,
    heads,
    attended,
    logs,
    proj,
    weight,
    normed,
    trig,
    hidden,
    resid_grad,
    gain,
    gain_grad,
    resid,
    outs,
    units,
):
    size = lax.axis_size("fsdp")
    groups = lax.axis_size("seq")
    length, width = grads.shape
    tokens = hidden.shape[0]
    used = heads.shape[1]
    own = attended.shape[1]
    depth = width // size
    rounds = size.bit_length() + 1
    bf16, f32 = jnp.bfloat16, jnp.float32
    anywhere = pl.BlockSpec(memory_space=pl.ANY)
    inside = pl.BlockSpec(memory_space=pltpu.VMEM)
    dma = pltpu.SemaphoreType.DMA
    vmem = pltpu.VMEM
    return pl.pallas_call(
        functools.partial(attend_backward_kernel, size, 256),
        out_shape=(
            jax.ShapeDtypeStruct((tokens, width), f32),
            jax.ShapeDtypeStruct((tokens, width), bf16),
            jax.ShapeDtypeStruct((8, width), f32),
            jax.ShapeDtypeStruct((groups, depth, used + own), bf16),
            jax.ShapeDtypeStruct(units.shape, bf16),
        ),
        in_specs=[inside] * 12 + [anywhere] * 3,
        out_specs=(inside, inside, inside, anywhere, anywhere),
        scratch_shapes=[
            vmem((length, own), bf16),
            vmem((length, used), bf16),
            vmem((length, HEAD_DIM), f32),
            vmem((length, HEAD_DIM), f32),
            vmem((length, width), bf16),
            vmem((width, used), bf16),
            vmem((own, width), bf16),
            vmem((width, own), bf16),
            vmem((size, depth, used), bf16),
            vmem((size, depth, own), bf16),
            vmem((2, depth, used), bf16),
            vmem((2, depth, own), bf16),
            vmem((depth, used + own), bf16),
            vmem((groups, depth, used + own), bf16),
            vmem((2, tokens, width), bf16),
            vmem((size, tokens, width), bf16),
            vmem((2, tokens, width), bf16),
            vmem((tokens, width), f32),
            vmem((3, tokens, width), bf16),
            vmem((tokens, width), bf16),
            vmem((2 * rounds + 1, 8, width), f32),
            dma((2,)),
            dma((2, 2)),
            dma((2, 2, size)),
            dma((2, 2, 2, size)),
            dma((2, 3)),
            dma((2, 3)),
            dma((2, 3)),
            dma((2, rounds)),
            dma((2, 15)),
            dma((2, 15)),
        ],
        compiler_params=pltpu.CompilerParams(
            collective_id=2, has_side_effects=True, vmem_limit_bytes=VMEM_BYTES
        ),
        name="attend_backward",
    )(
        grads,
        heads,
        attended,
        logs,
        proj,
        weight,
        normed,
        trig,
        hidden,
        resid_grad,
        gain,
        gain_grad,
        resid,
        outs,
        units,
    )


def kernels_fit(hidden_in, positions, attn_gain, qkv_weight, qkv_bias, out_weight, *rest):
    size, groups = lax.axis_size("fsdp"), lax.axis_size("seq")
    _, tokens, width = hidden_in.shape
    units = rest[1].shape[0]
    if groups != 4 or size % 4 or size & (size - 1) or tokens % 256 or units % 160 or width % 512:
        return False
    if (width // size) % 32 or qkv_bias.shape[0] > 256 or KV_HEADS != 2:
        return False
    rows = tokens * width * (4 * size + 34)
    return rows + units * (18 * width + 6 * tokens) < 64_000_000


def group_columns(array, seq):
    width_query = HEADS * HEAD_DIM
    own = width_query // 4
    kv_head = seq // 2
    parts = (
        (seq * own, own),
        (width_query + kv_head * HEAD_DIM, HEAD_DIM),
        (width_query + (KV_HEADS + kv_head) * HEAD_DIM, HEAD_DIM),
    )
    return jnp.concatenate(
        [lax.dynamic_slice_in_dim(array, at, count, array.ndim - 1) for at, count in parts], -1
    )


def per_device_kernels(
    hidden_in,
    positions,
    attn_gain,
    qkv_weight,
    qkv_bias,
    out_weight,
    mlp_gain,
    gate_weight,
    up_weight,
    down_weight,
    cotangent,
):
    f32, bf16 = jnp.float32, jnp.bfloat16
    groups = lax.axis_size("seq")
    size = lax.axis_size("fsdp")
    seq = lax.axis_index("seq")
    _, tokens, width = hidden_in.shape
    length = tokens * groups
    own = width // groups
    used = own + 2 * HEAD_DIM
    all_cots = lax.all_gather(cotangent[0], "fsdp", axis=0, tiled=True)
    cosine, sine = rope_tables(positions[0])
    half_dim = HEAD_DIM // 2
    trig = jnp.concatenate([cosine[:, :half_dim], sine[:, half_dim:]], axis=1)
    piece = jnp.concatenate(
        [
            group_columns(qkv_weight, seq),
            lax.dynamic_slice_in_dim(out_weight, seq * own, own, 1),
        ],
        axis=1,
    )
    small_width = 256
    small = jnp.stack(
        [
            jnp.pad(row, (0, small_width - row.shape[0]))
            for row in (attn_gain, mlp_gain, qkv_bias)
        ]
    )
    small = jnp.pad(small, ((0, 13), (0, 0)))
    rows_all, trig_all, pieces, proj, smalls = gather_inputs(hidden_in[0], trig, piece, small)
    shard = width // size
    gain_one = smalls[:, 0, :shard].reshape(1, width).astype(f32)
    gain_two = smalls[:, 1, :shard].reshape(1, width).astype(f32)
    bias = group_columns(smalls[:, 2, : qkv_bias.shape[0]].reshape(1, -1), seq).astype(f32)
    rows_all = rows_all.reshape(length, width)
    trig_all = trig_all.reshape(length, HEAD_DIM)
    weight = pieces.reshape(width, piece.shape[1])
    normed_one, heads, attended, logs, part = attend_group(
        rows_all, weight, proj, trig_all, gain_one, bias
    )
    outs, residual, proj_grads, grad_residual, term_gain_two, unit_sums = mlp_ring(
        hidden_in[0], part, gain_two, all_cots, gate_weight, up_weight, down_weight
    )
    grad_rows, hidden_out, smalls, shards, far_sums = attend_group_backward(
        proj_grads.reshape(length, width),
        heads,
        attended,
        logs,
        proj,
        weight,
        normed_one,
        trig_all,
        hidden_in[0],
        grad_residual,
        gain_one,
        term_gain_two,
        residual,
        outs,
        unit_sums,
    )
    shards = shards.astype(f32)
    keys = shards[:, :, own : own + HEAD_DIM]
    values = shards[:, :, own + HEAD_DIM : used]
    grad_qkv = jnp.concatenate(
        [shards[at, :, :own] for at in range(groups)]
        + [part[2 * at] + part[2 * at + 1] for part in (keys, values) for at in range(KV_HEADS)],
        axis=1,
    )
    grad_out = jnp.concatenate([shards[at, :, used:] for at in range(groups)], axis=1)
    me = lax.axis_index("fsdp")
    bias_sums = jnp.concatenate([smalls[2], smalls[3, : 2 * KV_HEADS * HEAD_DIM]])
    bias_shard = qkv_bias.shape[0]
    return (
        hidden_out[None],
        grad_rows[None],
        lax.dynamic_slice_in_dim(smalls[0], me * shard, shard),
        grad_qkv,
        lax.dynamic_slice_in_dim(bias_sums, me * bias_shard, bias_shard),
        grad_out,
        lax.dynamic_slice_in_dim(smalls[1], me * shard, shard),
    ) + tuple(unit_sums[at].astype(f32) + far_sums[at].astype(f32) for at in range(3))


def per_device_gathered(
    hidden_in,
    positions,
    attn_gain,
    qkv_weight,
    qkv_bias,
    out_weight,
    mlp_gain,
    gate_weight,
    up_weight,
    down_weight,
    cotangent,
):
    groups = lax.axis_size("seq")
    group_heads = HEADS // groups
    repeat = groups // KV_HEADS
    tokens = hidden_in.shape[1]
    width_query = HEADS * HEAD_DIM
    width_key = KV_HEADS * HEAD_DIM
    residual = hidden_in[0].astype(jnp.float32)
    cosine, sine = rope_tables(positions[0])
    gains_one, gains_two, qkv_full, bias_full, out_full = (
        lax.all_gather(attn_gain, "fsdp", axis=0, tiled=True),
        lax.all_gather(mlp_gain, "fsdp", axis=0, tiled=True),
        lax.all_gather(qkv_weight, "fsdp", axis=0, tiled=True),
        lax.all_gather(qkv_bias, "fsdp", axis=0, tiled=True),
        lax.all_gather(out_weight, "fsdp", axis=0, tiled=True),
    )
    gain_one = gains_one.astype(jnp.float32)
    gain_two = gains_two.astype(jnp.float32)
    unit_one, inverse_one, normed_one = norm_forward(residual, gain_one)
    qkv_mixed = jnp.dot(
        normed_one, qkv_full, preferred_element_type=jnp.float32
    ) + bias_full.astype(jnp.float32)
    query_part = qkv_mixed[:, :width_query].reshape(tokens, HEADS, HEAD_DIM)
    key_part = qkv_mixed[:, width_query : width_query + width_key].reshape(
        tokens, KV_HEADS, HEAD_DIM
    )
    value_part = qkv_mixed[:, width_query + width_key :].reshape(tokens, KV_HEADS, HEAD_DIM)
    queries = (
        rotate(query_part, cosine, sine)
        .astype(jnp.bfloat16)
        .reshape(tokens, groups, group_heads * HEAD_DIM)
    )
    keys_rep = jnp.repeat(rotate(key_part, cosine, sine).astype(jnp.bfloat16), repeat, axis=1)
    values_rep = jnp.repeat(value_part.astype(jnp.bfloat16), repeat, axis=1)
    head_queries, head_keys, head_values = (
        lax.all_to_all(queries, "seq", split_axis=1, concat_axis=0, tiled=True),
        lax.all_to_all(keys_rep, "seq", split_axis=1, concat_axis=0, tiled=True),
        lax.all_to_all(values_rep, "seq", split_axis=1, concat_axis=0, tiled=True),
    )
    head_queries = head_queries.reshape(-1, group_heads, HEAD_DIM)
    head_keys = head_keys.reshape(-1, HEAD_DIM)
    head_values = head_values.reshape(-1, HEAD_DIM)
    attended, log_totals = attend_forward(head_queries, head_keys, head_values)
    returned = lax.all_to_all(
        attended.reshape(-1, 1, group_heads * HEAD_DIM),
        "seq",
        split_axis=0,
        concat_axis=1,
        tiled=True,
    )
    attn_rows = returned.reshape(tokens, width_query)
    residual_two = residual + jnp.dot(attn_rows, out_full, preferred_element_type=jnp.float32)
    unit_two, inverse_two, normed_two = norm_forward(residual_two, gain_two)
    grad_output = cotangent[0].astype(jnp.float32)
    grad_mlp = grad_output.astype(jnp.bfloat16)
    all_rows = lax.all_gather(normed_two, "fsdp", axis=0, tiled=True)
    gate_pre = jnp.einsum("td,fd->tf", all_rows, gate_weight, preferred_element_type=jnp.float32)
    up_pre = jnp.einsum("td,fd->tf", all_rows, up_weight, preferred_element_type=jnp.float32)
    sigmoid_gate = jax.nn.sigmoid(gate_pre)
    activated = gate_pre * sigmoid_gate
    hidden = (activated * up_pre).astype(jnp.bfloat16)
    partial_out = jnp.dot(hidden, down_weight, preferred_element_type=jnp.float32)
    mlp_out = lax.psum_scatter(
        partial_out.astype(jnp.bfloat16), "fsdp", scatter_dimension=0, tiled=True
    ).astype(jnp.float32)
    all_grads = lax.all_gather(grad_mlp, "fsdp", axis=0, tiled=True)
    grad_hidden = jnp.einsum(
        "tm,fm->tf", all_grads, down_weight, preferred_element_type=jnp.float32
    )
    grad_gate = (
        grad_hidden * up_pre * sigmoid_gate * (1.0 + gate_pre * (1.0 - sigmoid_gate))
    ).astype(jnp.bfloat16)
    grad_up = (grad_hidden * activated).astype(jnp.bfloat16)
    partial_back = jnp.dot(grad_gate, gate_weight, preferred_element_type=jnp.float32) + jnp.dot(
        grad_up, up_weight, preferred_element_type=jnp.float32
    )
    grad_normed_two = lax.psum_scatter(partial_back, "fsdp", scatter_dimension=0, tiled=True)
    shard_gate = jnp.einsum("tf,td->fd", grad_gate, all_rows, preferred_element_type=jnp.float32)
    shard_up = jnp.einsum("tf,td->fd", grad_up, all_rows, preferred_element_type=jnp.float32)
    shard_down = jnp.einsum("tf,td->fd", hidden, all_grads, preferred_element_type=jnp.float32)
    hidden_out = (residual_two + mlp_out).astype(jnp.bfloat16)
    grad_norm_two, term_gain_two = norm_backward(grad_normed_two, unit_two, inverse_two, gain_two)
    grad_residual_two = grad_output + grad_norm_two
    grad_proj = grad_residual_two.astype(jnp.bfloat16)
    grad_attn_rows = jnp.einsum(
        "td,ed->te", grad_proj, out_full, preferred_element_type=jnp.float32
    ).astype(jnp.bfloat16)
    term_out = jnp.einsum("te,td->ed", attn_rows, grad_proj, preferred_element_type=jnp.float32)
    grad_heads = lax.all_to_all(
        grad_attn_rows.reshape(tokens, groups, group_heads * HEAD_DIM),
        "seq",
        split_axis=1,
        concat_axis=0,
        tiled=True,
    )
    grad_query, grad_keys, grad_values = attend_backward(
        head_queries,
        head_keys,
        head_values,
        log_totals,
        grad_heads.reshape(-1, group_heads, HEAD_DIM),
    )
    back_query, back_keys, back_values = (
        lax.all_to_all(
            grad_query.astype(jnp.bfloat16).reshape(-1, 1, group_heads * HEAD_DIM),
            "seq",
            split_axis=0,
            concat_axis=1,
            tiled=True,
        ),
        lax.all_to_all(
            grad_keys.astype(jnp.bfloat16)[:, None, :],
            "seq",
            split_axis=0,
            concat_axis=1,
            tiled=True,
        ),
        lax.all_to_all(
            grad_values.astype(jnp.bfloat16)[:, None, :],
            "seq",
            split_axis=0,
            concat_axis=1,
            tiled=True,
        ),
    )
    grad_query_rows = unrotate(
        back_query.reshape(tokens, HEADS, HEAD_DIM).astype(jnp.float32), cosine, sine
    )
    grad_key_rows = unrotate(
        jnp.sum(back_keys.astype(jnp.float32).reshape(tokens, KV_HEADS, repeat, HEAD_DIM), axis=2),
        cosine,
        sine,
    )
    grad_value_rows = jnp.sum(
        back_values.astype(jnp.float32).reshape(tokens, KV_HEADS, repeat, HEAD_DIM), axis=2
    )
    grad_mixed = jnp.concatenate(
        [
            grad_query_rows.reshape(tokens, width_query),
            grad_key_rows.reshape(tokens, width_key),
            grad_value_rows.reshape(tokens, width_key),
        ],
        axis=1,
    ).astype(jnp.bfloat16)
    term_qkv = jnp.einsum("td,tc->dc", normed_one, grad_mixed, preferred_element_type=jnp.float32)
    term_bias = jnp.sum(grad_mixed.astype(jnp.float32), axis=0)
    grad_normed_one = jnp.einsum(
        "tc,dc->td", grad_mixed, qkv_full, preferred_element_type=jnp.float32
    )
    grad_norm_one, term_gain_one = norm_backward(grad_normed_one, unit_one, inverse_one, gain_one)
    grad_rows = grad_residual_two + grad_norm_one
    shard_gain_one, shard_qkv, shard_bias, shard_out, shard_gain_two = (
        lax.psum_scatter(
            term_gain_one.astype(jnp.bfloat16), "fsdp", scatter_dimension=0, tiled=True
        ).astype(jnp.float32),
        lax.psum_scatter(
            term_qkv.astype(jnp.bfloat16), "fsdp", scatter_dimension=0, tiled=True
        ).astype(jnp.float32),
        lax.psum_scatter(
            term_bias.astype(jnp.bfloat16), "fsdp", scatter_dimension=0, tiled=True
        ).astype(jnp.float32),
        lax.psum_scatter(
            term_out.astype(jnp.bfloat16), "fsdp", scatter_dimension=0, tiled=True
        ).astype(jnp.float32),
        lax.psum_scatter(
            term_gain_two.astype(jnp.bfloat16), "fsdp", scatter_dimension=0, tiled=True
        ).astype(jnp.float32),
    )
    totals = (
        lax.psum(shard_gain_one.astype(jnp.bfloat16), "seq").astype(jnp.float32),
        lax.psum(shard_qkv.astype(jnp.bfloat16), "seq").astype(jnp.float32),
        lax.psum(shard_bias.astype(jnp.bfloat16), "seq").astype(jnp.float32),
        lax.psum(shard_out.astype(jnp.bfloat16), "seq").astype(jnp.float32),
        lax.psum(shard_gain_two.astype(jnp.bfloat16), "seq").astype(jnp.float32),
        lax.psum(shard_gate.astype(jnp.bfloat16), "seq").astype(jnp.float32),
        lax.psum(shard_up.astype(jnp.bfloat16), "seq").astype(jnp.float32),
        lax.psum(shard_down.astype(jnp.bfloat16), "seq").astype(jnp.float32),
    )
    return (
        hidden_out[None],
        grad_rows[None],
        totals[0],
        totals[1],
        totals[2],
        totals[3],
        totals[4],
        totals[5],
        totals[6],
        totals[7],
    )


def per_device(*arguments):
    return (per_device_kernels if kernels_fit(*arguments) else per_device_gathered)(*arguments)


def solution(mesh):
    placed = (
        P("fsdp", "seq", None),
        P("fsdp", "seq"),
        P("fsdp"),
        P("fsdp", None),
        P("fsdp"),
        P("fsdp", None),
        P("fsdp"),
        P("fsdp", None),
        P("fsdp", None),
        P("fsdp", None),
        P("fsdp", "seq", None),
    )
    return jax.shard_map(
        per_device,
        mesh=mesh,
        in_specs=placed,
        out_specs=(
            P("fsdp", "seq", None),
            P("fsdp", "seq", None),
            P("fsdp"),
            P("fsdp", None),
            P("fsdp"),
            P("fsdp", None),
            P("fsdp"),
            P("fsdp", None),
            P("fsdp", None),
            P("fsdp", None),
        ),
        check_vma=False,
    )
```

```python
import functools
import math

import jax
import jax.numpy as jnp
from jax import lax
from jax.experimental import pallas as pl
from jax.experimental.pallas import tpu as pltpu
from jax.sharding import PartitionSpec as P

HEADS = 12
KV_HEADS = 2
HEAD_DIM = 128


norm_eps = 1e-06
rope_base = 1000000.0


def rope_tables(position_row):
    half_dim = HEAD_DIM // 2
    frequency = jnp.exp(
        -(jnp.arange(half_dim, dtype=jnp.float32) * 2.0 / HEAD_DIM) * math.log(rope_base)
    )
    angles = position_row.astype(jnp.float32)[:, None] * frequency[None, :]
    angles = jnp.concatenate([angles, angles], axis=-1)
    return (jnp.cos(angles), jnp.sin(angles))


def rotate(values, cosine, sine):
    half_dim = values.shape[-1] // 2
    turned = jnp.concatenate([-values[..., half_dim:], values[..., :half_dim]], axis=-1)
    return values * cosine[:, None, :] + turned * sine[:, None, :]


def unrotate(grads_rot, cosine, sine):
    half_dim = grads_rot.shape[-1] // 2
    scaled = grads_rot * sine[:, None, :]
    return grads_rot * cosine[:, None, :] + jnp.concatenate(
        [scaled[..., half_dim:], -scaled[..., :half_dim]], axis=-1
    )


def norm_forward(values, gain):
    inverse = lax.rsqrt(jnp.mean(values * values, axis=-1, keepdims=True) + norm_eps)
    unit_rows = values * inverse
    return (unit_rows, inverse, (unit_rows * gain).astype(jnp.bfloat16))


def norm_backward(grad_normed, unit_rows, inverse, gain):
    grad_unit = grad_normed * gain
    grad_values = inverse * (
        grad_unit - unit_rows * jnp.mean(grad_unit * unit_rows, axis=-1, keepdims=True)
    )
    grad_gain = jnp.sum(grad_normed * unit_rows, axis=0)
    return (grad_values, grad_gain)


def masked_scores(queries, keys, block_start, block_rows):
    length = keys.shape[0]
    query_block = lax.dynamic_slice_in_dim(queries, block_start, block_rows, 0)
    scores = jnp.einsum(
        "bhd,ld->hbl", query_block, keys, preferred_element_type=jnp.float32
    ) * HEAD_DIM ** (-0.5)
    row_index = block_start + jnp.arange(block_rows)
    column_index = jnp.arange(length)
    allowed = column_index[None, :] <= row_index[:, None]
    return (query_block, jnp.where(allowed[None], scores, -1e30))


def attend_forward(queries, keys, values):
    length = keys.shape[0]
    block_rows = min(512, length)
    block_count = length // block_rows

    def one_block(block_start):
        query_block, scores = masked_scores(queries, keys, block_start, block_rows)
        row_max = jnp.max(scores, axis=-1, keepdims=True)
        exponent = jnp.exp(scores - row_max)
        row_total = jnp.sum(exponent, axis=-1, keepdims=True)
        probability = (exponent / row_total).astype(jnp.bfloat16)
        result = jnp.einsum("hbl,ld->bhd", probability, values, preferred_element_type=jnp.float32)
        return (result.astype(jnp.bfloat16), (row_max + jnp.log(row_total))[..., 0])

    results, log_totals = lax.map(one_block, jnp.arange(block_count) * block_rows)
    return (results.reshape(length, queries.shape[1], queries.shape[2]), log_totals)


def attend_backward(queries, keys, values, log_totals, grad_out):
    length = keys.shape[0]
    block_rows = min(512, length)
    block_count = length // block_rows
    score_scale = HEAD_DIM ** (-0.5)

    def one_block(running, inputs):
        grad_keys, grad_values = running
        block_start, log_block = inputs
        query_block, scores = masked_scores(queries, keys, block_start, block_rows)
        grad_block = lax.dynamic_slice_in_dim(grad_out, block_start, block_rows, 0)
        probability = jnp.exp(scores - log_block[..., None])
        grad_probs = jnp.einsum(
            "bhd,ld->hbl", grad_block, values, preferred_element_type=jnp.float32
        )
        row_delta = jnp.sum(probability * grad_probs, axis=-1, keepdims=True)
        grad_scores = (probability * (grad_probs - row_delta)).astype(jnp.bfloat16)
        grad_query = (
            jnp.einsum("hbl,ld->bhd", grad_scores, keys, preferred_element_type=jnp.float32)
            * score_scale
        )
        grad_keys = (
            grad_keys
            + jnp.einsum(
                "hbl,bhd->ld", grad_scores, query_block, preferred_element_type=jnp.float32
            )
            * score_scale
        )
        grad_values = grad_values + jnp.einsum(
            "hbl,bhd->ld",
            probability.astype(jnp.bfloat16),
            grad_block,
            preferred_element_type=jnp.float32,
        )
        return ((grad_keys, grad_values), grad_query)

    zero_rows = jnp.zeros((length, keys.shape[1]), jnp.float32)
    (grad_keys, grad_values), grad_query = lax.scan(
        one_block, (zero_rows, zero_rows), (jnp.arange(block_count) * block_rows, log_totals)
    )
    return (grad_query.reshape(queries.shape), grad_keys, grad_values)


MESH = pl.DeviceIdType.MESH
VMEM_BYTES = 67_000_000
NN = (((1,), (0,)), ((), ()))
NT = (((1,), (1,)), ((), ()))
TN = (((0,), (0,)), ((), ()))


def matmul(left, right, dims):
    return lax.dot_general(left, right, dims, preferred_element_type=jnp.float32)


def ring_place(index, size):
    side = index % 2
    return (index // 2) * (1 - side) + (size - 1 - index // 2) * side


def ring_member(place, size):
    side = place // (size // 2)
    return 2 * (place * (1 - side) + (size - 1 - place) * side) + side


def seq_partners(seq):
    core = seq + 1 - 2 * (seq % 2)
    far = (seq + 2) % 4
    return core, far, (core + 2) % 4


def greet(targets):
    barrier = pltpu.get_barrier_semaphore()
    for target in targets:
        pl.semaphore_signal(barrier, inc=1, device_id=target, device_id_type=MESH)
    pl.semaphore_wait(barrier, len(targets))


def for_blocks(width, block, body):
    for at in range(0, width, block):
        body(pl.ds(at, min(block, width - at)))


def turn_tables(trig):
    lane = lax.broadcasted_iota(jnp.int32, trig.shape, 1)
    swapped = pltpu.roll(trig, HEAD_DIM // 2, 1)
    first = lane < HEAD_DIM // 2
    return jnp.where(first, trig, swapped), jnp.where(first, -swapped, trig)


def head_columns(at):
    return slice(at * HEAD_DIM, (at + 1) * HEAD_DIM)


def causal(scores, start):
    rows = lax.broadcasted_iota(jnp.int32, scores.shape, 0) + start
    columns = lax.broadcasted_iota(jnp.int32, scores.shape, 1)
    return jnp.where(columns <= rows, scores, -1e30)


def inverse_of(values):
    return lax.rsqrt(jnp.mean(values * values, axis=-1, keepdims=True) + norm_eps)


def attend_forward_kernel(
    size,
    block,
    bias_share,
    rows_ref,
    trig_ref,
    piece_ref,
    small_ref,
    cot_ref,
    normed_out,
    heads_out,
    attended_out,
    log_out,
    piece_out,
    proj_out,
    trig_out,
    gains_out,
    normed_two_out,
    resid_out,
    cots_out,
    rows_all,
    trig_all,
    pieces,
    proj,
    smalls,
    cots,
    normed,
    heads,
    attended,
    logs,
    part,
    gains,
    bias,
    resid,
    seq_in,
    far_sum,
    normed_two,
    load_sems,
    store_sems,
    ring_sems,
    small_sems,
    cot_sems,
    cot_store_sems,
    seq_sems,
    sum_sems,
    proj_send,
    proj_recv,
):
    f32, bf16 = jnp.float32, jnp.bfloat16
    depth, joint = piece_ref.shape
    tokens, width = rows_ref.shape
    half = depth // 2
    cot_half = tokens // 2
    own = proj.shape[0]
    used = joint - own
    count = own // HEAD_DIM
    length = part.shape[0]
    per_group = own // depth
    scale = HEAD_DIM**-0.5
    me = lax.axis_index("fsdp")
    seq = lax.axis_index("seq")
    place = ring_place(me, size)
    right = ring_member((place + 1) % size, size)
    left = ring_member((place + size - 1) % size, size)
    core, far, diagonal = seq_partners(seq)
    ring = ({"fsdp": right}, {"fsdp": left})

    def remote(source, target, sems, at, device):
        return pltpu.make_async_remote_copy(
            src_ref=source,
            dst_ref=target,
            send_sem=sems.at[(0,) + at],
            recv_sem=sems.at[(1,) + at],
            device_id=device,
            device_id_type=MESH,
        )

    loads = [
        pltpu.make_async_copy(piece_ref, pieces.at[pl.ds(pl.multiple_of(me * depth, 16), depth)], load_sems.at[0]),
        pltpu.make_async_copy(trig_ref, trig_all.at[seq], load_sems.at[1]),
        pltpu.make_async_copy(rows_ref, rows_all.at[seq], load_sems.at[2]),
        pltpu.make_async_copy(small_ref, smalls.at[me], load_sems.at[3]),
        pltpu.make_async_copy(cot_ref, cots.at[me], load_sems.at[4]),
    ]
    for load in loads:
        load.start()
    greet(ring + ({"seq": core}, {"seq": far}, {"seq": diagonal}))

    def piece_of(step, side):
        return ring_member((place + size - step if side == 0 else place + step) % size, size)

    def ring_copy(step, side, sub):
        part_rows = half // 2
        start = piece_of(step, side) * depth + side * half + sub * part_rows
        span = pieces.at[pl.ds(pl.multiple_of(start, 16), part_rows)]
        return remote(span, span, ring_sems, (side, sub, step), ring[side])

    def small_copy(step):
        span = smalls.at[piece_of(step, 0)]
        return remote(span, span, small_sems, (step,), ring[0])

    def cot_copy(step, side, sub):
        part_rows = cot_half // 2
        start = side * cot_half + sub * part_rows
        span = cots.at[piece_of(step, side), pl.ds(start, part_rows)]
        return remote(span, span, cot_sems, (side, sub, step), ring[side])

    def cot_store(step, side):
        span = (piece_of(step, side), pl.ds(side * cot_half, cot_half))
        return pltpu.make_async_copy(
            cots.at[span], cots_out.at[span], cot_store_sems.at[side, step]
        )

    def seq_copy(which, block_at, target, at):
        span = (rows_all, trig_all)[which].at[block_at]
        return remote(span, span, seq_sems, (which, at), {"seq": target})

    def proj_part(step, side):
        at = piece_of(step, side)
        row = pl.multiple_of((at % per_group) * depth + side * half, 16)
        source = pieces.at[
            pl.ds(pl.multiple_of(at * depth + side * half, 16), half), pl.ds(used, own)
        ]
        target = proj.at[pl.ds(row, half), pl.ds(pl.multiple_of(seq * own, 128), own)]
        return at, at // per_group, source, target

    def proj_copy(step, side):
        at, owner, source, target = proj_part(step, side)
        return owner, pltpu.make_async_remote_copy(
            src_ref=source,
            dst_ref=target,
            send_sem=proj_send.at[side, step],
            recv_sem=proj_recv.at[seq, at % per_group, side],
            device_id={"seq": owner},
            device_id_type=MESH,
        )

    def proj_act(step, side, action):
        owner, copy = proj_copy(step, side)

        @pl.when(owner != seq)
        def _():
            if action == "start":
                copy.start()
            else:
                copy.wait_send()

        @pl.when(owner == seq)
        def _():
            _, _, source, target = proj_part(step, side)
            kept = pltpu.make_async_copy(source, target, proj_send.at[side, step])
            if action == "start":
                kept.start()
            else:
                kept.wait()

    stores = []

    def store(source, target):
        stores.append(pltpu.make_async_copy(source, target, store_sems.at[len(stores)]))
        stores[-1].start()

    def cot_pump(step):
        for sub in range(2):
            for side in range(2):
                if step >= 1:
                    cot_copy(step - 1, side, sub).wait_recv()
                if step < size - 1:
                    cot_copy(step, side, sub).start()
        for side in range(2):
            cot_store(step, side).start()

    loads[0].wait()
    for sub in range(2):
        for side in range(2):
            ring_copy(0, side, sub).start()
    loads[3].wait()
    small_copy(0).start()
    for which in (1, 0):
        loads[2 - which].wait()
        seq_copy(which, seq, far, 1).start()
        seq_copy(which, seq, core, 0).start()
    for side in range(2):
        proj_act(0, side, "start")
    loads[4].wait()

    for step in range(size - 1):
        for sub in range(2):
            for side in range(2):
                ring_copy(step, side, sub).wait_recv()
                if step < size - 2:
                    ring_copy(step + 1, side, sub).start()
        small_copy(step).wait_recv()
        if step < size - 2:
            small_copy(step + 1).start()
        if step == size - 3:
            cot_pump(0)
        for side in range(2):
            proj_act(step + 1, side, "start")
        if step == min(1, size - 2):
            for which in (1, 0):
                seq_copy(which, seq, far, 1).wait_recv()
                seq_copy(which, far, core, 2).start()

    gathered = jnp.zeros((8, width), f32)
    small_width = smalls.shape[2]
    for at in range(size):
        held = smalls[at].astype(f32)[0:8, :]
        lane = lax.broadcasted_iota(jnp.int32, held.shape, 1)
        wide = jnp.concatenate(
            [
                jnp.where(lane < depth, held, 0.0),
                jnp.zeros((8, width - small_width), f32),
            ],
            axis=1,
        )
        gathered += pltpu.roll(wide, at * depth, 1) if at else wide
        bias[:, at * bias_share : (at + 1) * bias_share] = held[:, :bias_share]
    gains[...] = gathered
    gain_one = gathered[0:1, :]
    gain_two = gathered[1:2, :]
    store(gains, gains_out)
    for which in (1, 0):
        seq_copy(which, seq, core, 0).wait_recv()
        seq_copy(which, far, core, 2).wait_recv()
    store(pieces, piece_out)
    store(trig_all, trig_out)

    width_query = count * HEAD_DIM * 4
    kv_lane = pl.multiple_of(width_query + (seq // 2) * HEAD_DIM, HEAD_DIM)
    value_lane = pl.multiple_of(kv_lane + KV_HEADS * HEAD_DIM, HEAD_DIM)
    own_bias = jnp.concatenate(
        [
            bias[2:3, pl.ds(pl.multiple_of(seq * own, HEAD_DIM), own)],
            bias[2:3, pl.ds(kv_lane, HEAD_DIM)],
            bias[2:3, pl.ds(value_lane, HEAD_DIM)],
        ],
        axis=1,
    )
    for at in range(length // block):
        span = slice(at * block, (at + 1) * block)
        rows = rows_all[at].astype(f32)
        normed[span, :] = (rows * inverse_of(rows) * gain_one).astype(bf16)
        mixed = matmul(normed[span, :], pieces[:, :used], NN) + own_bias
        cosine, sine = turn_tables(trig_all[at])
        for head in range(count + 1):
            turned = mixed[:, head_columns(head)]
            heads[span, head_columns(head)] = (
                turned * cosine + pltpu.roll(turned, HEAD_DIM // 2, 1) * sine
            ).astype(bf16)
        heads[span, head_columns(count + 1)] = mixed[:, head_columns(count + 1)].astype(bf16)
        if 2 * (at + 1) == length // block:
            cot_pump(1)
    store(normed, normed_out)
    store(heads, heads_out)

    for peer in (core, far, diagonal):
        for at in range(per_group):
            for side in range(2):
                pltpu.make_async_remote_copy(
                    src_ref=pieces.at[pl.ds(0, half), pl.ds(used, own)],
                    dst_ref=proj.at[pl.ds(0, half), pl.ds(0, own)],
                    send_sem=proj_send.at[side, 0],
                    recv_sem=proj_recv.at[peer, at, side],
                    device_id={"seq": peer},
                    device_id_type=MESH,
                ).wait_recv()
    for step in range(size):
        for side in range(2):
            proj_act(step, side, "wait")
    store(proj, proj_out)

    lane = lax.broadcasted_iota(jnp.int32, (block, HEAD_DIM), 1)
    for start in range(0, length, block):
        span = slice(start, start + block)
        seen = slice(0, start + block)
        log_rows = jnp.zeros((block, HEAD_DIM), f32)
        for at in range(count):
            scores = causal(
                matmul(heads[span, head_columns(at)], heads[seen, head_columns(count)], NT)
                * scale,
                start,
            )
            top = jnp.max(scores, axis=-1, keepdims=True)
            exponent = jnp.exp(scores - top)
            total = jnp.sum(exponent, axis=-1, keepdims=True)
            probability = (exponent / total).astype(bf16)
            attended[span, head_columns(at)] = matmul(
                probability, heads[seen, head_columns(count + 1)], NN
            ).astype(bf16)
            log_rows = jnp.where(lane == at, top + jnp.log(total), log_rows)
        logs[span, :] = log_rows
        if 2 * (start + block) == length:
            cot_pump(2)
    store(attended, attended_out)
    store(logs, log_out)

    def out_part(span):
        part[:, span] = matmul(attended[...], proj[:, span], NN).astype(bf16)

    for_blocks(width, 512, out_part)

    def part_rows(at):
        return part.at[pl.ds(pl.multiple_of(at * tokens, tokens), tokens)]

    to_core = [
        remote(part_rows(diagonal), seq_in.at[0], sum_sems, (0,), {"seq": core}),
        remote(part_rows(core), seq_in.at[1], sum_sems, (1,), {"seq": core}),
    ]
    to_far = remote(far_sum, seq_in.at[2], sum_sems, (2,), {"seq": far})
    for copy in to_core:
        copy.start()
    cot_pump(3)
    to_core[0].wait_recv()
    far_sum[...] = (part_rows(far)[...].astype(f32) + seq_in[0].astype(f32)).astype(bf16)
    to_far.start()
    to_core[1].wait_recv()
    resid[...] = (
        part_rows(seq)[...].astype(f32) + seq_in[1].astype(f32) + rows_all[seq].astype(f32)
    )
    cot_pump(4)
    cot_pump(5)
    to_far.wait_recv()
    resid[...] += seq_in[2].astype(f32)
    store(resid, resid_out)
    normed_two[...] = (resid[...] * inverse_of(resid[...]) * gain_two).astype(bf16)
    store(normed_two, normed_two_out)
    for step in range(6, size):
        cot_pump(step)
    for step in range(size):
        for side in range(2):
            cot_store(step, side).wait()

    for step in range(size - 1):
        for side in range(2):
            for sub in range(2):
                ring_copy(step, side, sub).wait_send()
                cot_copy(step, side, sub).wait_send()
        small_copy(step).wait_send()
    for which in (1, 0):
        seq_copy(which, seq, core, 0).wait_send()
        seq_copy(which, seq, far, 1).wait_send()
        seq_copy(which, far, core, 2).wait_send()
    for copy in to_core + [to_far]:
        copy.wait_send()
    for copy in stores:
        copy.wait()


def attend_group(rows, trig, piece, small, cots, bias_share):
    size = lax.axis_size("fsdp")
    groups = lax.axis_size("seq")
    tokens, width = rows.shape
    depth, joint = piece.shape
    own = width // groups
    used = joint - own
    length = tokens * groups
    f32, bf16 = jnp.float32, jnp.bfloat16
    dma = pltpu.SemaphoreType.DMA
    anywhere = pl.BlockSpec(memory_space=pl.ANY)
    normed = ((length, width), bf16)
    heads = ((length, used), bf16)
    attended = ((length, own), bf16)
    logs = ((length, HEAD_DIM), f32)
    pieces = ((width, joint), bf16)
    proj = ((own, width), bf16)
    trig_all = ((groups,) + trig.shape, f32)
    gains = ((8, width), f32)
    rows_all = ((groups, tokens, width), bf16)
    own_rows = ((tokens, width), bf16)
    resid = ((tokens, width), f32)
    cots_all = ((size, tokens, width), bf16)
    outs = (
        normed, heads, attended, logs, pieces, proj, trig_all, gains, own_rows, resid, cots_all
    )
    held = (
        rows_all,
        trig_all,
        pieces,
        proj,
        ((size,) + small.shape, bf16),
        cots_all,
        normed,
        heads,
        attended,
        logs,
        normed,
        gains,
        ((8, size * bias_share), f32),
        resid,
        ((3, tokens, width), bf16),
        own_rows,
        own_rows,
    )
    return pl.pallas_call(
        functools.partial(attend_forward_kernel, size, tokens, bias_share),
        out_shape=tuple(jax.ShapeDtypeStruct(*shape) for shape in outs),
        in_specs=[anywhere] * 5,
        out_specs=(anywhere,) * len(outs),
        scratch_shapes=[pltpu.VMEM(*shape) for shape in held]
        + [
            dma((5,)),
            dma((len(outs),)),
            dma((2, 2, 2, size)),
            dma((2, size)),
            dma((2, 2, 2, size)),
            dma((2, size)),
            dma((2, 2, 3)),
            dma((2, 3)),
            dma((2, size)),
            dma((groups, own // depth, 2)),
        ],
        compiler_params=pltpu.CompilerParams(
            collective_id=1, has_side_effects=True, vmem_limit_bytes=VMEM_BYTES
        ),
        name="attend_forward",
    )(rows, trig, piece, small, cots)


CHUNKS = 5
IN_LOOP = ((2, 1), (4, 2), (6, 3))


def mlp_kernel(
    size,
    normed_ref,
    resid_ref,
    gain_ref,
    cots_ref,
    gate_ref,
    up_ref,
    down_ref,
    outs_ref,
    back_ref,
    gain_grad_ref,
    sums_ref,
    far_ref,
    rows_all,
    cots,
    weights,
    grads,
    hid,
    dgate,
    dup,
    resid,
    sums_in,
    backs,
    outs,
    load_sems,
    cot_sems,
    ring_send,
    ring_recv,
    sum_send,
    sum_recv,
    out_sems,
    swap_sems,
    far_sems,
    swap_ready,
):
    tokens, width = normed_ref.shape
    units = gate_ref.shape[0]
    half = tokens // 2
    me = lax.axis_index("fsdp")
    seq = lax.axis_index("seq")
    place = ring_place(me, size)
    right = ring_member((place + 1) % size, size)
    left = ring_member((place + size - 1) % size, size)
    core, far, diagonal = seq_partners(seq)
    sides = ((right, pl.ds(0, half)), (left, pl.ds(half, half)))

    def owner_of(step, side):
        return ring_member((place + size - step if side == 0 else place + step) % size, size)

    own_load = pltpu.make_async_copy(normed_ref, rows_all.at[0], load_sems.at[3])
    resid_load = pltpu.make_async_copy(resid_ref, resid, load_sems.at[4])
    weight_loads = [
        pltpu.make_async_copy(ref, weights.at[at], load_sems.at[at])
        for at, ref in enumerate((gate_ref, up_ref, down_ref))
    ]
    own_load.start()
    greet(({"fsdp": right}, {"fsdp": left}, {"seq": core}, {"seq": far}))

    def cot_copies(step):
        return [
            pltpu.make_async_copy(
                cots_ref.at[
                    pl.ds(
                        pl.multiple_of(owner_of(step, side) * tokens + side * half, half), half
                    )
                ],
                cots.at[step % 2, sides[side][1]],
                cot_sems.at[step % 2, side],
            )
            for side in range(2)
        ]


    def row_copy(step, side):
        target, span = sides[side]
        return pltpu.make_async_remote_copy(
            src_ref=rows_all.at[step, span],
            dst_ref=rows_all.at[step + 1, span],
            send_sem=ring_send.at[side, step],
            recv_sem=ring_recv.at[side, step + 1],
            device_id={"fsdp": target},
            device_id_type=MESH,
        )

    def sum_span(side, sub):
        return pl.ds(side * half + sub * (half // 2), half // 2)

    def sum_copy(step, side, sub):
        target, span = sides[side][0], sum_span(side, sub)
        return pltpu.make_async_remote_copy(
            src_ref=backs.at[step, span],
            dst_ref=sums_in.at[step, span],
            send_sem=sum_send.at[side, sub, step],
            recv_sem=sum_recv.at[side, sub, step],
            device_id={"fsdp": target},
            device_id_type=MESH,
        )

    def sum_step(step):
        for sub in range(2):
            for side in range(2):
                span = sum_span(side, sub)
                if step >= 2:
                    sum_copy(step - 1, side, sub).wait_recv()
                    backs[step, span] = (
                        backs[step, span].astype(jnp.float32)
                        + sums_in[step - 1, span].astype(jnp.float32)
                    ).astype(jnp.bfloat16)
                sum_copy(step, side, sub).start()

    def out_copy(step, side):
        at = pl.multiple_of(owner_of(step, side) * tokens + side * half, half)
        return pltpu.make_async_copy(
            outs.at[step % 2, sides[side][1]], outs_ref.at[pl.ds(at, half)], out_sems.at[side, step]
        )

    def elementwise(step, span):
        rows = rows_all[step]
        gate = matmul(rows, weights[0, span, :], NT)
        up = matmul(rows, weights[1, span, :], NT)
        grad_hidden = matmul(cots[step % 2], weights[2, span, :], NT)
        sigmoid = jax.nn.sigmoid(gate)
        activated = gate * sigmoid
        hid[:, span] = (activated * up).astype(jnp.bfloat16)
        dgate[:, span] = (
            grad_hidden * up * sigmoid * (1.0 + gate * (1.0 - sigmoid))
        ).astype(jnp.bfloat16)
        dup[:, span] = (grad_hidden * activated).astype(jnp.bfloat16)

    own_load.wait()
    for side in range(2):
        row_copy(0, side).start()
    for load in weight_loads + cot_copies(0) + [resid_load]:
        load.start()

    @pl.loop(0, units // 16)
    def _(at):
        zeros = jnp.zeros((3, 16, width), jnp.float32)
        grads[:, pl.ds(pl.multiple_of(at * 16, 16), 16), :] = zeros

    for load in weight_loads:
        load.wait()

    @pl.loop(0, size)
    def _(step):
        slot = step % 2

        @pl.when(step >= 1)
        def _():
            for side in range(2):
                row_copy(step - 1, side).wait_recv()

        @pl.when((step >= 1) & (step < size - 1))
        def _():
            for side in range(2):
                row_copy(step, side).start()

        for load in cot_copies(step):
            load.wait()

        @pl.when(step < size - 1)
        def _():
            for load in cot_copies(step + 1):
                load.start()

        for_blocks(units, 256, functools.partial(elementwise, step))

        def back_part(span):
            backs[step, :, span] = (
                matmul(dgate[...], weights[0, :, span], NN)
                + matmul(dup[...], weights[1, :, span], NN)
            ).astype(jnp.bfloat16)

        for_blocks(width, 256, back_part)

        for when, at in IN_LOOP:

            @pl.when(step == when)
            def _():
                sum_step(at)

        @pl.when(step >= 2)
        def _():
            for side in range(2):
                out_copy(step - 2, side).wait()

        def out_part(span):
            outs[slot, :, span] = matmul(hid[...], weights[2, :, span], NN).astype(jnp.bfloat16)

        for_blocks(width, 256, out_part)
        for side in range(2):
            out_copy(step, side).start()

        def weight_part(span):
            rows, cot = rows_all[step, :, span], cots[slot, :, span]
            grads[0, :, span] += matmul(dgate[...], rows, TN)
            grads[1, :, span] += matmul(dup[...], rows, TN)
            grads[2, :, span] += matmul(hid[...], cot, TN)

        for_blocks(width, 256, weight_part)

    share = units // 2
    kept = pl.multiple_of((seq % 2) * share, 16)
    given = pl.multiple_of((1 - seq % 2) * share, 16)
    chunk = share // CHUNKS
    pl.semaphore_signal(swap_ready, inc=1, device_id={"seq": core}, device_id_type=MESH)

    def to_seq(source, target, sems, at, device):
        return pltpu.make_async_remote_copy(
            src_ref=source,
            dst_ref=target,
            send_sem=sems.at[0, at],
            recv_sem=sems.at[1, at],
            device_id={"seq": device},
            device_id_type=MESH,
        )

    swaps = [
        to_seq(
            weights.at[at, pl.ds(given, share)],
            weights.at[at, pl.ds(given, share)],
            swap_sems,
            at,
            core,
        )
        for at in range(3)
    ]
    waiting = [at for at in range(1, size) if at not in [pair[1] for pair in IN_LOOP]]
    sum_step(waiting[0])
    for at in range(3):

        @pl.loop(0, share // 16)
        def _(block):
            span = pl.ds(pl.multiple_of(given + block * 16, 16), 16)
            weights[at, span, :] = grads[at, span, :].astype(jnp.bfloat16)

        if at == 0:
            pl.semaphore_wait(swap_ready, 1)
        swaps[at].start()

    stores = []

    def kept_rows(at):
        return pl.ds(pl.multiple_of(kept + at * chunk, 16), chunk)

    far_copies = [
        to_seq(weights.at[0, kept_rows(at)], far_ref.at[kept_rows(at)], far_sems, at, far)
        for at in range(CHUNKS)
    ]
    def swap_finish(at):
        swaps[at].wait_recv()

        @pl.loop(0, share // 16)
        def _(block):
            span = pl.ds(pl.multiple_of(kept + block * 16, 16), 16)
            weights[at, span, :] = (
                grads[at, span, :] + weights[at, span, :].astype(jnp.float32)
            ).astype(jnp.bfloat16)

        done = weights.at[at, pl.ds(kept, share)]
        stores.append(
            pltpu.make_async_copy(done, sums_ref.at[at, pl.ds(kept, share)], load_sems.at[at])
        )
        if at == 0:
            for copy in far_copies:
                copy.start()
        stores[-1].start()

    cot_own = pltpu.make_async_copy(
        cots_ref.at[pl.ds(pl.multiple_of(me * tokens, tokens), tokens)],
        cots.at[0],
        load_sems.at[7],
    )
    cot_own.start()
    for turn, at in enumerate(waiting[1:]):
        sum_step(at)
        if turn < 3:
            swap_finish(turn)
    for turn in range(len(waiting) - 1, 3):
        swap_finish(turn)

    for side in range(2):
        for sub in range(2):
            sum_copy(size - 1, side, sub).wait_recv()
    grad_normed = backs[0].astype(jnp.float32) + sums_in[size - 1].astype(jnp.float32)
    resid_load.wait()
    inverse = inverse_of(resid[...])
    unit_rows = resid[...] * inverse
    gain_grad_ref[...] = jnp.sum(grad_normed * unit_rows, axis=0, keepdims=True)
    grad_unit = grad_normed * gain_ref[...]
    cot_own.wait()
    back_ref[...] = cots[0].astype(jnp.float32) + inverse * (
        grad_unit - unit_rows * jnp.mean(grad_unit * unit_rows, axis=-1, keepdims=True)
    )
    for side in range(2):
        out_copy(size - 2, side).wait()
        out_copy(size - 1, side).wait()

        @pl.loop(0, size - 1)
        def _(step):
            row_copy(step, side).wait_send()
            for sub in range(2):
                sum_copy(step + 1, side, sub).wait_send()

    for copy in swaps + far_copies:
        copy.wait_send()
    for copy in far_copies:
        copy.wait_recv()
    for store in stores:
        store.wait()


def mlp_ring(normed, resid, gain, cots, gate_weight, up_weight, down_weight):
    size = lax.axis_size("fsdp")
    tokens, width = normed.shape
    units = gate_weight.shape[0]
    anywhere = pl.BlockSpec(memory_space=pl.ANY)
    inside = pl.BlockSpec(memory_space=pltpu.VMEM)
    bf16, f32 = jnp.bfloat16, jnp.float32
    dma = pltpu.SemaphoreType.DMA
    return pl.pallas_call(
        functools.partial(mlp_kernel, size),
        out_shape=(
            jax.ShapeDtypeStruct((size * tokens, width), bf16),
            jax.ShapeDtypeStruct((tokens, width), f32),
            jax.ShapeDtypeStruct((1, width), f32),
            jax.ShapeDtypeStruct((3, units, width), bf16),
            jax.ShapeDtypeStruct((units, width), bf16),
        ),
        in_specs=[anywhere, anywhere, inside, anywhere, anywhere, anywhere, anywhere],
        out_specs=(anywhere, inside, inside, anywhere, anywhere),
        scratch_shapes=[
            pltpu.VMEM((size, tokens, width), bf16),
            pltpu.VMEM((2, tokens, width), bf16),
            pltpu.VMEM((3, units, width), bf16),
            pltpu.VMEM((3, units, width), f32),
            pltpu.VMEM((tokens, units), bf16),
            pltpu.VMEM((tokens, units), bf16),
            pltpu.VMEM((tokens, units), bf16),
            pltpu.VMEM((tokens, width), f32),
            pltpu.VMEM((size, tokens, width), bf16),
            pltpu.VMEM((size, tokens, width), bf16),
            pltpu.VMEM((2, tokens, width), bf16),
            dma((9,)),
            dma((2, 2)),
            dma((2, size)),
            dma((2, size)),
            dma((2, 2, size)),
            dma((2, 2, size)),
            dma((2, size)),
            dma((2, 3)),
            dma((2, CHUNKS)),
            pltpu.SemaphoreType.REGULAR,
        ],
        compiler_params=pltpu.CompilerParams(
            collective_id=0, has_side_effects=True, vmem_limit_bytes=VMEM_BYTES
        ),
        name="mlp_ring",
    )(normed, resid, gain, cots, gate_weight, up_weight, down_weight)


def attend_backward_kernel(
    size,
    heads_ref,
    attended_ref,
    log_ref,
    proj_ref,
    weight_ref,
    normed_ref,
    trig_ref,
    hidden_ref,
    resid_grad_ref,
    gain_ref,
    gain_grad_ref,
    resid_ref,
    outs_ref,
    units_in_ref,
    far_gate_in_ref,
    grad_in_ref,
    hidden_out_ref,
    small_ref,
    shards_ref,
    halves_ref,
    far_units_ref,
    units_ref,
    far_gate_ref,
    grads_all,
    grad_heads,
    grad_mixed,
    grad_keys,
    grad_values,
    grad_normed,
    term_qkv,
    term_out,
    out_columns,
    qkv_in,
    out_in,
    qkv_sum,
    out_sum,
    shard,
    shard_all,
    half_shard,
    half_all,
    out_own,
    out_recv,
    out_send,
    resid,
    seq_in,
    far_sum,
    small_in,
    load_sems,
    own_sems,
    out_sems,
    term_sems,
    column_sems,
    seq_sems,
    shard_sems,
    small_sems,
    unit_sems,
    pass_sems,
    share_sems,
    gate_sems,
    grad_sems,
):
    length = heads_ref.shape[0]
    tokens, width = hidden_ref.shape
    used = heads_ref.shape[1]
    own = attended_ref.shape[1]
    count = own // HEAD_DIM
    scale = HEAD_DIM**-0.5
    half = tokens // 2
    block = tokens
    depth = width // size
    chip_pieces = size // 2
    half_width = width // 2
    term_half = depth // 2
    units = units_ref.shape[1]
    f32, bf16 = jnp.float32, jnp.bfloat16
    me = lax.axis_index("fsdp")
    seq = lax.axis_index("seq")
    place = ring_place(me, size)
    right = ring_member((place + 1) % size, size)
    left = ring_member((place + size - 1) % size, size)
    core, far, diagonal = seq_partners(seq)
    rounds = size.bit_length() - 1
    mirrors = [me + (1 - 2 * ((me // 2**at) % 2)) * 2**at for at in range(rounds)]
    ring = ({"fsdp": right}, {"fsdp": left})

    def owner_of(step, side):
        return ring_member((place + size - step if side == 0 else place + step) % size, size)

    def remote(source, target, sems, at, device):
        return pltpu.make_async_remote_copy(
            src_ref=source,
            dst_ref=target,
            send_sem=sems.at[(0,) + at],
            recv_sem=sems.at[(1,) + at],
            device_id=device,
            device_id_type=MESH,
        )

    greet(
        ring
        + ({"seq": core}, {"seq": far})
        + tuple({"fsdp": mirror} for mirror in mirrors)
    )

    def own_load(step, side):
        at = pl.multiple_of(owner_of(step, side) * tokens + side * half, half)
        return pltpu.make_async_copy(
            outs_ref.at[pl.ds(at, half)],
            out_own.at[step % 2, pl.ds(side * half, half)],
            own_sems.at[step % 2, side],
        )

    def out_copy(step, side):
        span = pl.ds(side * half, half)
        return remote(
            out_send.at[step % 2, span], out_recv.at[step, span], out_sems, (side, step), ring[side]
        )

    def out_step(step):
        for side in range(2):
            own_load(step, side).wait()
            if step < size - 1:
                own_load(step + 1, side).start()
            if step >= 3:
                out_copy(step - 2, side).wait_send()
            if step >= 2:
                out_copy(step - 1, side).wait_recv()
        total = out_own[step % 2].astype(f32)
        if step >= 2:
            total += out_recv[step - 1].astype(f32)
        out_send[step % 2] = total.astype(bf16)
        for side in range(2):
            out_copy(step, side).start()

    resid_load = pltpu.make_async_copy(resid_ref, resid, load_sems.at[0])

    def out_finish():
        step = size
        for side in range(2):
            out_copy(step - 2, side).wait_send()
            out_copy(step - 1, side).wait_send()
            out_copy(step - 1, side).wait_recv()
        mine = pltpu.make_async_copy(
            outs_ref.at[pl.ds(pl.multiple_of(me * tokens, tokens), tokens)],
            out_own.at[0],
            load_sems.at[1],
        )
        mine.start()
        mine.wait()
        resid_load.wait()
        hidden_out_ref[...] = (
            resid[...] + out_own[0].astype(f32) + out_recv[size - 1].astype(f32)
        ).astype(bf16)

    share = units // 2
    piece = share // CHUNKS
    kept = (seq % 2) * share

    def unit_slice(ref, at):
        start = pl.multiple_of(kept + (at % CHUNKS) * piece, 16)
        return ref.at[at // CHUNKS, pl.ds(start, piece)]

    def unit_copy(at):
        return remote(
            unit_slice(units_ref, at + CHUNKS), unit_slice(far_units_ref, at), unit_sems, (at,), {"seq": far}
        )

    def unit_pass(at):
        part = unit_slice(far_units_ref, at)
        return remote(part, part, pass_sems, (at,), {"seq": core})

    def unit_share(at):
        part = unit_slice(units_ref, at)
        return remote(part, part, share_sems, (at,), {"seq": core})

    def gate_pass(at):
        part = far_gate_ref.at[pl.ds(pl.multiple_of(kept + at * piece, 16), piece)]
        return remote(part, part, gate_sems, (at,), {"seq": core})

    chunks = 2 * CHUNKS
    lag = 3
    turns = iter(range(chunks + lag))

    def pump():
        at = next(turns, chunks + lag)
        if at < chunks:
            unit_copy(at).start()
        if lag <= at < chunks + lag:
            unit_copy(at - lag).wait_recv()
            unit_pass(at - lag).start()

    def grad_copy(source, target, at):
        span = grads_all.at[source]
        return remote(span, span, grad_sems, (at,), {"seq": target})

    to_far_grads = grad_copy(seq, far, 0)
    to_core_grads = grad_copy(seq, core, 1)
    passed_grads = grad_copy(far, core, 2)
    grads_all[seq] = resid_grad_ref[...].astype(bf16)
    to_far_grads.start()
    to_core_grads.start()
    resid_load.start()
    for side in range(2):
        own_load(1, side).start()
    out_step(1)

    grad_keys[...] = jnp.zeros_like(grad_keys)
    grad_values[...] = jnp.zeros_like(grad_values)
    lane = lax.broadcasted_iota(jnp.int32, (block, HEAD_DIM), 1)
    keys = slice(own, own + HEAD_DIM)
    values = slice(own + HEAD_DIM, used)

    def attend_block(at_block):
        start = at_block * block
        span = slice(start, start + block)
        seen = slice(0, start + block)
        cosine, sine = turn_tables(trig_ref[span, :])
        grad_heads[span, :] = matmul(grads_all[at_block], proj_ref[...], NT).astype(bf16)

        @pl.loop(0, count)
        def _(at):
            head = pl.ds(pl.multiple_of(at * HEAD_DIM, HEAD_DIM), HEAD_DIM)
            query = heads_ref[span, head]
            grad = grad_heads[span, head]
            logs = jnp.sum(jnp.where(lane == at, log_ref[span, :], 0.0), axis=-1, keepdims=True)
            scores = causal(matmul(query, heads_ref[seen, keys], NT) * scale, start)
            probability = jnp.exp(scores - logs)
            grad_probs = matmul(grad, heads_ref[seen, values], NT)
            delta = jnp.sum(probability * grad_probs, axis=-1, keepdims=True)
            grad_scores = (probability * (grad_probs - delta)).astype(bf16)
            grad_query = matmul(grad_scores, heads_ref[seen, keys], NN) * scale
            grad_query = grad_query.astype(bf16).astype(f32)
            grad_mixed[span, head] = (
                grad_query * cosine + pltpu.roll(grad_query * sine, HEAD_DIM // 2, 1)
            ).astype(bf16)
            grad_keys[seen, :] += matmul(grad_scores, query, TN) * scale
            grad_values[seen, :] += matmul(probability.astype(bf16), grad, TN)

    @pl.loop(0, 4)
    def _(turn):
        @pl.when(turn == 1)
        def _():
            to_core_grads.wait_recv()

        @pl.when(turn == 2)
        def _():
            to_far_grads.wait_recv()
            passed_grads.start()
            unit_copy(0).start()

        @pl.when(turn == 3)
        def _():
            passed_grads.wait_recv()
            unit_copy(1).start()

        for late in range(3):

            @pl.when(turn == late + 1)
            def _():
                out_step(late + 2)

        for shared in range(3):
            unit_share(turn * 3 + shared).start()
        gate_pass(turn).start()
        at_block = ((seq // 2 + turn // 2) % 2) * 2 + (seq % 2 + turn % 2) % 2
        for at in range(4):

            @pl.when(at_block == at)
            def _():
                attend_block(at)

    next(turns)
    next(turns)
    for shared in range(12, 3 * CHUNKS):
        unit_share(shared).start()
    gate_pass(4).start()
    out_step(5)

    for start in range(0, length, block):
        span = slice(start, start + block)
        cosine, sine = turn_tables(trig_ref[span, :])
        part = grad_keys[span, :].astype(bf16).astype(f32)
        grad_mixed[span, keys] = (
            part * cosine + pltpu.roll(part * sine, HEAD_DIM // 2, 1)
        ).astype(bf16)
        grad_mixed[span, values] = grad_values[span, :].astype(bf16)

    def normed_part(span):
        grad_normed[:, span] = matmul(grad_mixed[...], weight_ref[span, :used], NT).astype(bf16)

    for_blocks(width, 256, normed_part)

    def block_rows(at):
        return grad_normed.at[pl.ds(pl.multiple_of(at * tokens, tokens), tokens)]

    to_core = [
        remote(block_rows(diagonal), seq_in.at[0], seq_sems, (0,), {"seq": core}),
        remote(block_rows(core), seq_in.at[1], seq_sems, (1,), {"seq": core}),
    ]
    to_far = remote(far_sum, seq_in.at[2], seq_sems, (2,), {"seq": far})
    for copy in to_core:
        copy.start()

    out_step(6)

    def out_term(span):
        term_out[:, span] = matmul(
            attended_ref[...], grads_all[:, :, span].reshape(length, span.size), TN
        ).astype(bf16)

    for_blocks(width, 256, out_term)
    my_row = pl.multiple_of((seq % 2) * own, 16)
    my_lane = pl.multiple_of((seq % 2) * half_width, 128)
    core_lane = pl.multiple_of((1 - seq % 2) * half_width, 128)
    columns = remote(
        term_out.at[:, pl.ds(core_lane, half_width)],
        out_columns.at[pl.ds(my_row, own)],
        column_sems,
        (0,),
        {"seq": core},
    )
    columns.start()
    out_columns[pl.ds(my_row, own), :] = term_out[:, pl.ds(my_lane, half_width)]

    def qkv_term(span):
        term_qkv[span, :] = matmul(normed_ref[:, span], grad_mixed[...], TN).astype(bf16)

    for_blocks(width, 256, qkv_term)
    to_core[0].wait_recv()
    far_sum[...] = (block_rows(far)[...].astype(f32) + seq_in[0].astype(f32)).astype(bf16)
    to_far.start()
    small_in[0] = jnp.zeros((8, width), f32)
    small_in[0, 1:2, :] = gain_grad_ref[...]
    bias = jnp.sum(grad_mixed[...].astype(f32), axis=0, keepdims=True)
    small_in[0, 2:3, pl.ds(pl.multiple_of(seq * own, 128), own)] = bias[:, :own]
    kv_lane = pl.multiple_of((seq // 2) * HEAD_DIM, HEAD_DIM)
    small_in[0, 3:4, pl.ds(kv_lane, HEAD_DIM)] = bias[:, keys]
    small_in[0, 3:4, pl.ds(kv_lane + KV_HEADS * HEAD_DIM, HEAD_DIM)] = bias[:, values]

    def term_copy(step, side):
        span = pl.ds(side * term_half, term_half)
        return remote(
            qkv_sum.at[step, span], qkv_in.at[step, span], term_sems, (0, side, step), ring[side]
        )

    def half_copy(step, side):
        span = pl.ds(side * term_half, term_half)
        return remote(
            out_sum.at[step, span], out_in.at[step, span], term_sems, (1, side, step), ring[side]
        )

    def here(owner):
        return owner // chip_pieces == seq // 2

    def half_rows(owner, side):
        start = (owner % chip_pieces) * depth + side * term_half
        return pl.ds(pl.multiple_of(start, 16), term_half)

    def term_step(step):
        for side in range(2):
            span = pl.ds(side * term_half, term_half)
            start = owner_of(step, side) * depth + side * term_half
            total = term_qkv[pl.ds(pl.multiple_of(start, 16), term_half), :].astype(f32)
            if step >= 2:
                term_copy(step - 1, side).wait_recv()
                total += qkv_in[step - 1, span, :].astype(f32)
            qkv_sum[step, span, :] = total.astype(bf16)
            term_copy(step, side).start()

    def half_step(step):
        for side in range(2):
            owner = owner_of(step, side)

            @pl.when(here(owner))
            def _():
                span = pl.ds(side * term_half, term_half)
                total = out_columns[half_rows(owner, side), :].astype(f32)
                if step >= 2:
                    half_copy(step - 1, side).wait_recv()
                    total += out_in[step - 1, span, :].astype(f32)
                out_sum[step, span, :] = total.astype(bf16)
                half_copy(step, side).start()

    def small_copy(at):
        device = ({"seq": core}, {"seq": far})[at] if at < 2 else {"fsdp": mirrors[at - 2]}
        return remote(small_in.at[2 * at], small_in.at[2 * at + 1], small_sems, (at,), device)

    def small_step(at):
        small_copy(at).wait_recv()
        small_in[2 * at + 2] = small_in[2 * at] + small_in[2 * at + 1]

    term_step(1)
    columns.wait_recv()
    half_step(1)
    term_step(2)
    half_step(2)
    to_core[1].wait_recv()
    to_far.wait_recv()
    rows = hidden_ref[...].astype(f32)
    inverse = lax.rsqrt(jnp.mean(rows * rows, axis=-1, keepdims=True) + norm_eps)
    unit_rows = rows * inverse
    grad_rows = (
        block_rows(seq)[...].astype(f32) + seq_in[1].astype(f32) + seq_in[2].astype(f32)
    )
    small_in[0, 0:1, :] = jnp.sum(grad_rows * unit_rows, axis=0, keepdims=True)
    small_copy(0).start()
    grad_unit = grad_rows * gain_ref[...]
    grad_in_ref[...] = resid_grad_ref[...] + inverse * (
        grad_unit - unit_rows * jnp.mean(grad_unit * unit_rows, axis=-1, keepdims=True)
    )
    pump()
    total_rounds = rounds + 2
    done = 0
    for step in range(3, size):
        term_step(step)
        half_step(step)
        if done < total_rounds:
            small_step(done)
            done += 1
            if done < total_rounds:
                small_copy(done).start()
        if step % 2:
            pump()
    while done < total_rounds:
        small_step(done)
        done += 1
        if done < total_rounds:
            small_copy(done).start()
    small_ref[...] = small_in[2 * total_rounds]
    source_chip = here(me)
    for side in range(2):
        span = pl.ds(side * term_half, term_half)
        start = me * depth + side * term_half
        term_copy(size - 1, side).wait_recv()
        shard[span, :] = (
            term_qkv[pl.ds(pl.multiple_of(start, 16), term_half), :].astype(f32)
            + qkv_in[size - 1, span, :].astype(f32)
        ).astype(bf16)

        @pl.when(source_chip)
        def _():
            half_copy(size - 1, side).wait_recv()
            half_shard[span, :] = (
                out_columns[half_rows(me, side), :].astype(f32)
                + out_in[size - 1, span, :].astype(f32)
            ).astype(bf16)

    def shard_copy(source, at, block_at, target):
        return remote(source, shard_all.at[block_at], shard_sems, (at,), {"seq": target})

    def half_move(source, at, target):
        return remote(source, half_all.at[seq % 2], shard_sems, (at,), {"seq": target})

    shard_far = shard_copy(shard, 0, seq, far)
    shard_core = shard_copy(shard, 1, seq, core)
    shard_pass = shard_copy(shard_all.at[far], 2, far, core)
    half_far = half_move(half_shard, 3, far)
    half_core = half_move(half_shard, 4, core)
    half_pass = half_move(half_all.at[seq % 2], 5, core)
    shard_far.start()
    shard_core.start()

    @pl.when(source_chip)
    def _():
        half_far.start()
        half_core.start()
        half_all[seq % 2] = half_shard[...]

    shard_all[seq] = shard[...]
    pump()
    out_step(size - 1)
    shard_far.wait_recv()
    shard_pass.start()

    @pl.when(jnp.logical_not(source_chip))
    def _():
        half_far.wait_recv()
        half_pass.start()

    out_finish()
    for _ in range(chunks + lag):
        pump()
    shard_core.wait_recv()
    shard_pass.wait_recv()
    shard_store = pltpu.make_async_copy(shard_all, shards_ref, load_sems.at[1])
    shard_store.start()

    @pl.when(source_chip)
    def _():
        half_core.wait_recv()
        half_core.wait_send()
        half_far.wait_send()

    @pl.when(jnp.logical_not(source_chip))
    def _():
        half_pass.wait_recv()
        half_pass.wait_send()

    half_store = pltpu.make_async_copy(half_all, halves_ref, load_sems.at[2])
    half_store.start()
    for step in range(1, size):
        for side in range(2):
            term_copy(step, side).wait_send()

            @pl.when(here(owner_of(step, side)))
            def _():
                half_copy(step, side).wait_send()

    for copy in [unit_share(at) for at in range(3 * CHUNKS)] + [
        gate_pass(at) for at in range(CHUNKS)
    ]:
        copy.wait_send()
        copy.wait_recv()
    for at in range(chunks):
        unit_pass(at).wait_recv()
        unit_copy(at).wait_send()
        unit_pass(at).wait_send()
    for at in range(total_rounds):
        small_copy(at).wait_send()
    for copy in to_core + [to_far, columns, shard_far, shard_core, shard_pass]:
        copy.wait_send()
    for copy in (to_far_grads, to_core_grads, passed_grads):
        copy.wait_send()
    shard_store.wait()
    half_store.wait()


def attend_group_backward(
    heads,
    attended,
    logs,
    proj,
    weight,
    normed,
    trig,
    hidden,
    resid_grad,
    gain,
    gain_grad,
    resid,
    outs,
    units,
    far_gate,
):
    size = lax.axis_size("fsdp")
    groups = lax.axis_size("seq")
    length = heads.shape[0]
    tokens, width = hidden.shape
    used = heads.shape[1]
    own = attended.shape[1]
    depth = width // size
    rounds = size.bit_length() + 1
    bf16, f32 = jnp.bfloat16, jnp.float32
    anywhere = pl.BlockSpec(memory_space=pl.ANY)
    inside = pl.BlockSpec(memory_space=pltpu.VMEM)
    dma = pltpu.SemaphoreType.DMA
    vmem = pltpu.VMEM
    return pl.pallas_call(
        functools.partial(attend_backward_kernel, size),
        out_shape=(
            jax.ShapeDtypeStruct((tokens, width), f32),
            jax.ShapeDtypeStruct((tokens, width), bf16),
            jax.ShapeDtypeStruct((8, width), f32),
            jax.ShapeDtypeStruct((groups, depth, used), bf16),
            jax.ShapeDtypeStruct((2, depth, width // 2), bf16),
            jax.ShapeDtypeStruct((2,) + units.shape[1:], bf16),
            jax.ShapeDtypeStruct(units.shape, bf16),
            jax.ShapeDtypeStruct(far_gate.shape, bf16),
        ),
        in_specs=[inside] * 11 + [anywhere] * 4,
        out_specs=(inside, inside, inside) + (anywhere,) * 5,
        input_output_aliases={13: 6, 14: 7},
        scratch_shapes=[
            vmem((groups, tokens, width), bf16),
            vmem((length, own), bf16),
            vmem((length, used), bf16),
            vmem((length, HEAD_DIM), f32),
            vmem((length, HEAD_DIM), f32),
            vmem((length, width), bf16),
            vmem((width, used), bf16),
            vmem((own, width), bf16),
            vmem((2 * own, width // 2), bf16),
            vmem((size, depth, used), bf16),
            vmem((size, depth, width // 2), bf16),
            vmem((size, depth, used), bf16),
            vmem((size, depth, width // 2), bf16),
            vmem((depth, used), bf16),
            vmem((groups, depth, used), bf16),
            vmem((depth, width // 2), bf16),
            vmem((2, depth, width // 2), bf16),
            vmem((2, tokens, width), bf16),
            vmem((size, tokens, width), bf16),
            vmem((2, tokens, width), bf16),
            vmem((tokens, width), f32),
            vmem((3, tokens, width), bf16),
            vmem((tokens, width), bf16),
            vmem((2 * rounds + 1, 8, width), f32),
            dma((3,)),
            dma((2, 2)),
            dma((2, 2, size)),
            dma((2, 2, 2, size)),
            dma((2, 1)),
            dma((2, 3)),
            dma((2, 6)),
            dma((2, rounds)),
            dma((2, 2 * CHUNKS)),
            dma((2, 2 * CHUNKS)),
            dma((2, 3 * CHUNKS)),
            dma((2, CHUNKS)),
            dma((2, 3)),
        ],
        compiler_params=pltpu.CompilerParams(
            collective_id=2, has_side_effects=True, vmem_limit_bytes=VMEM_BYTES
        ),
        name="attend_backward",
    )(
        heads,
        attended,
        logs,
        proj,
        weight,
        normed,
        trig,
        hidden,
        resid_grad,
        gain,
        gain_grad,
        resid,
        outs,
        units,
        far_gate,
    )


def kernels_fit(hidden_in, positions, attn_gain, qkv_weight, qkv_bias, out_weight, *rest):
    size, groups = lax.axis_size("fsdp"), lax.axis_size("seq")
    _, tokens, width = hidden_in.shape
    units = rest[1].shape[0]
    if groups != 4 or size != 8 or tokens % 256 or units % 160 or width % 512:
        return False
    if (width // size) % 32 or qkv_bias.shape[0] > 256 or KV_HEADS != 2:
        return False
    rows = tokens * width * (4 * size + 34)
    return rows + units * (18 * width + 6 * tokens) < 64_000_000


def group_columns(array, seq):
    width_query = HEADS * HEAD_DIM
    own = width_query // 4
    kv_head = seq // 2
    parts = (
        (seq * own, own),
        (width_query + kv_head * HEAD_DIM, HEAD_DIM),
        (width_query + (KV_HEADS + kv_head) * HEAD_DIM, HEAD_DIM),
    )
    return jnp.concatenate(
        [lax.dynamic_slice_in_dim(array, at, count, array.ndim - 1) for at, count in parts], -1
    )


def per_device_kernels(
    hidden_in,
    positions,
    attn_gain,
    qkv_weight,
    qkv_bias,
    out_weight,
    mlp_gain,
    gate_weight,
    up_weight,
    down_weight,
    cotangent,
):
    f32, bf16 = jnp.float32, jnp.bfloat16
    groups = lax.axis_size("seq")
    size = lax.axis_size("fsdp")
    seq = lax.axis_index("seq")
    _, tokens, width = hidden_in.shape
    length = tokens * groups
    own = width // groups
    used = own + 2 * HEAD_DIM
    cosine, sine = rope_tables(positions[0])
    half_dim = HEAD_DIM // 2
    trig = jnp.concatenate([cosine[:, :half_dim], sine[:, half_dim:]], axis=1)
    piece = jnp.concatenate(
        [
            group_columns(qkv_weight, seq),
            lax.dynamic_slice_in_dim(out_weight, seq * own, own, 1),
        ],
        axis=1,
    )
    small_width = 256
    small = jnp.stack(
        [
            jnp.pad(row, (0, small_width - row.shape[0]))
            for row in (attn_gain, mlp_gain, qkv_bias)
        ]
    )
    small = jnp.pad(small, ((0, 13), (0, 0)))
    (
        normed_one,
        heads,
        attended,
        logs,
        weight,
        proj,
        trig_all,
        gains,
        normed_two,
        residual,
        all_cots,
    ) = attend_group(hidden_in[0], trig, piece, small, cotangent[0], qkv_bias.shape[0])
    shard = width // size
    outs, grad_residual, term_gain_two, unit_sums, far_gate = mlp_ring(
        normed_two,
        residual,
        gains[1:2],
        all_cots.reshape(size * tokens, width),
        gate_weight,
        up_weight,
        down_weight,
    )
    (
        grad_rows,
        hidden_out,
        smalls,
        shards,
        halves,
        far_sums,
        unit_sums,
        far_gate,
    ) = attend_group_backward(
        heads,
        attended,
        logs,
        proj,
        weight,
        normed_one,
        trig_all.reshape(length, HEAD_DIM),
        hidden_in[0],
        grad_residual,
        gains[0:1],
        term_gain_two,
        residual,
        outs,
        unit_sums,
        far_gate,
    )
    shards = shards.astype(f32)
    keys = shards[:, :, own : own + HEAD_DIM]
    values = shards[:, :, own + HEAD_DIM :]
    grad_qkv = jnp.concatenate(
        [shards[at, :, :own] for at in range(groups)]
        + [part[2 * at] + part[2 * at + 1] for part in (keys, values) for at in range(KV_HEADS)],
        axis=1,
    )
    grad_out = jnp.concatenate([halves[0], halves[1]], axis=1).astype(f32)
    me = lax.axis_index("fsdp")
    bias_sums = jnp.concatenate([smalls[2], smalls[3, : 2 * KV_HEADS * HEAD_DIM]])
    bias_shard = qkv_bias.shape[0]
    return (
        hidden_out[None],
        grad_rows[None],
        lax.dynamic_slice_in_dim(smalls[0], me * shard, shard),
        grad_qkv,
        lax.dynamic_slice_in_dim(bias_sums, me * bias_shard, bias_shard),
        grad_out,
        lax.dynamic_slice_in_dim(smalls[1], me * shard, shard),
    ) + tuple(
        unit_sums[at].astype(f32) + part.astype(f32)
        for at, part in enumerate((far_gate, far_sums[0], far_sums[1]))
    )


def per_device_gathered(
    hidden_in,
    positions,
    attn_gain,
    qkv_weight,
    qkv_bias,
    out_weight,
    mlp_gain,
    gate_weight,
    up_weight,
    down_weight,
    cotangent,
):
    groups = lax.axis_size("seq")
    group_heads = HEADS // groups
    repeat = groups // KV_HEADS
    tokens = hidden_in.shape[1]
    width_query = HEADS * HEAD_DIM
    width_key = KV_HEADS * HEAD_DIM
    residual = hidden_in[0].astype(jnp.float32)
    cosine, sine = rope_tables(positions[0])
    gains_one, gains_two, qkv_full, bias_full, out_full = (
        lax.all_gather(attn_gain, "fsdp", axis=0, tiled=True),
        lax.all_gather(mlp_gain, "fsdp", axis=0, tiled=True),
        lax.all_gather(qkv_weight, "fsdp", axis=0, tiled=True),
        lax.all_gather(qkv_bias, "fsdp", axis=0, tiled=True),
        lax.all_gather(out_weight, "fsdp", axis=0, tiled=True),
    )
    gain_one = gains_one.astype(jnp.float32)
    gain_two = gains_two.astype(jnp.float32)
    unit_one, inverse_one, normed_one = norm_forward(residual, gain_one)
    qkv_mixed = jnp.dot(
        normed_one, qkv_full, preferred_element_type=jnp.float32
    ) + bias_full.astype(jnp.float32)
    query_part = qkv_mixed[:, :width_query].reshape(tokens, HEADS, HEAD_DIM)
    key_part = qkv_mixed[:, width_query : width_query + width_key].reshape(
        tokens, KV_HEADS, HEAD_DIM
    )
    value_part = qkv_mixed[:, width_query + width_key :].reshape(tokens, KV_HEADS, HEAD_DIM)
    queries = (
        rotate(query_part, cosine, sine)
        .astype(jnp.bfloat16)
        .reshape(tokens, groups, group_heads * HEAD_DIM)
    )
    keys_rep = jnp.repeat(rotate(key_part, cosine, sine).astype(jnp.bfloat16), repeat, axis=1)
    values_rep = jnp.repeat(value_part.astype(jnp.bfloat16), repeat, axis=1)
    head_queries, head_keys, head_values = (
        lax.all_to_all(queries, "seq", split_axis=1, concat_axis=0, tiled=True),
        lax.all_to_all(keys_rep, "seq", split_axis=1, concat_axis=0, tiled=True),
        lax.all_to_all(values_rep, "seq", split_axis=1, concat_axis=0, tiled=True),
    )
    head_queries = head_queries.reshape(-1, group_heads, HEAD_DIM)
    head_keys = head_keys.reshape(-1, HEAD_DIM)
    head_values = head_values.reshape(-1, HEAD_DIM)
    attended, log_totals = attend_forward(head_queries, head_keys, head_values)
    returned = lax.all_to_all(
        attended.reshape(-1, 1, group_heads * HEAD_DIM),
        "seq",
        split_axis=0,
        concat_axis=1,
        tiled=True,
    )
    attn_rows = returned.reshape(tokens, width_query)
    residual_two = residual + jnp.dot(attn_rows, out_full, preferred_element_type=jnp.float32)
    unit_two, inverse_two, normed_two = norm_forward(residual_two, gain_two)
    grad_output = cotangent[0].astype(jnp.float32)
    grad_mlp = grad_output.astype(jnp.bfloat16)
    all_rows = lax.all_gather(normed_two, "fsdp", axis=0, tiled=True)
    gate_pre = jnp.einsum("td,fd->tf", all_rows, gate_weight, preferred_element_type=jnp.float32)
    up_pre = jnp.einsum("td,fd->tf", all_rows, up_weight, preferred_element_type=jnp.float32)
    sigmoid_gate = jax.nn.sigmoid(gate_pre)
    activated = gate_pre * sigmoid_gate
    hidden = (activated * up_pre).astype(jnp.bfloat16)
    partial_out = jnp.dot(hidden, down_weight, preferred_element_type=jnp.float32)
    mlp_out = lax.psum_scatter(
        partial_out.astype(jnp.bfloat16), "fsdp", scatter_dimension=0, tiled=True
    ).astype(jnp.float32)
    all_grads = lax.all_gather(grad_mlp, "fsdp", axis=0, tiled=True)
    grad_hidden = jnp.einsum(
        "tm,fm->tf", all_grads, down_weight, preferred_element_type=jnp.float32
    )
    grad_gate = (
        grad_hidden * up_pre * sigmoid_gate * (1.0 + gate_pre * (1.0 - sigmoid_gate))
    ).astype(jnp.bfloat16)
    grad_up = (grad_hidden * activated).astype(jnp.bfloat16)
    partial_back = jnp.dot(grad_gate, gate_weight, preferred_element_type=jnp.float32) + jnp.dot(
        grad_up, up_weight, preferred_element_type=jnp.float32
    )
    grad_normed_two = lax.psum_scatter(partial_back, "fsdp", scatter_dimension=0, tiled=True)
    shard_gate = jnp.einsum("tf,td->fd", grad_gate, all_rows, preferred_element_type=jnp.float32)
    shard_up = jnp.einsum("tf,td->fd", grad_up, all_rows, preferred_element_type=jnp.float32)
    shard_down = jnp.einsum("tf,td->fd", hidden, all_grads, preferred_element_type=jnp.float32)
    hidden_out = (residual_two + mlp_out).astype(jnp.bfloat16)
    grad_norm_two, term_gain_two = norm_backward(grad_normed_two, unit_two, inverse_two, gain_two)
    grad_residual_two = grad_output + grad_norm_two
    grad_proj = grad_residual_two.astype(jnp.bfloat16)
    grad_attn_rows = jnp.einsum(
        "td,ed->te", grad_proj, out_full, preferred_element_type=jnp.float32
    ).astype(jnp.bfloat16)
    term_out = jnp.einsum("te,td->ed", attn_rows, grad_proj, preferred_element_type=jnp.float32)
    grad_heads = lax.all_to_all(
        grad_attn_rows.reshape(tokens, groups, group_heads * HEAD_DIM),
        "seq",
        split_axis=1,
        concat_axis=0,
        tiled=True,
    )
    grad_query, grad_keys, grad_values = attend_backward(
        head_queries,
        head_keys,
        head_values,
        log_totals,
        grad_heads.reshape(-1, group_heads, HEAD_DIM),
    )
    back_query, back_keys, back_values = (
        lax.all_to_all(
            grad_query.astype(jnp.bfloat16).reshape(-1, 1, group_heads * HEAD_DIM),
            "seq",
            split_axis=0,
            concat_axis=1,
            tiled=True,
        ),
        lax.all_to_all(
            grad_keys.astype(jnp.bfloat16)[:, None, :],
            "seq",
            split_axis=0,
            concat_axis=1,
            tiled=True,
        ),
        lax.all_to_all(
            grad_values.astype(jnp.bfloat16)[:, None, :],
            "seq",
            split_axis=0,
            concat_axis=1,
            tiled=True,
        ),
    )
    grad_query_rows = unrotate(
        back_query.reshape(tokens, HEADS, HEAD_DIM).astype(jnp.float32), cosine, sine
    )
    grad_key_rows = unrotate(
        jnp.sum(back_keys.astype(jnp.float32).reshape(tokens, KV_HEADS, repeat, HEAD_DIM), axis=2),
        cosine,
        sine,
    )
    grad_value_rows = jnp.sum(
        back_values.astype(jnp.float32).reshape(tokens, KV_HEADS, repeat, HEAD_DIM), axis=2
    )
    grad_mixed = jnp.concatenate(
        [
            grad_query_rows.reshape(tokens, width_query),
            grad_key_rows.reshape(tokens, width_key),
            grad_value_rows.reshape(tokens, width_key),
        ],
        axis=1,
    ).astype(jnp.bfloat16)
    term_qkv = jnp.einsum("td,tc->dc", normed_one, grad_mixed, preferred_element_type=jnp.float32)
    term_bias = jnp.sum(grad_mixed.astype(jnp.float32), axis=0)
    grad_normed_one = jnp.einsum(
        "tc,dc->td", grad_mixed, qkv_full, preferred_element_type=jnp.float32
    )
    grad_norm_one, term_gain_one = norm_backward(grad_normed_one, unit_one, inverse_one, gain_one)
    grad_rows = grad_residual_two + grad_norm_one
    shard_gain_one, shard_qkv, shard_bias, shard_out, shard_gain_two = (
        lax.psum_scatter(
            term_gain_one.astype(jnp.bfloat16), "fsdp", scatter_dimension=0, tiled=True
        ).astype(jnp.float32),
        lax.psum_scatter(
            term_qkv.astype(jnp.bfloat16), "fsdp", scatter_dimension=0, tiled=True
        ).astype(jnp.float32),
        lax.psum_scatter(
            term_bias.astype(jnp.bfloat16), "fsdp", scatter_dimension=0, tiled=True
        ).astype(jnp.float32),
        lax.psum_scatter(
            term_out.astype(jnp.bfloat16), "fsdp", scatter_dimension=0, tiled=True
        ).astype(jnp.float32),
        lax.psum_scatter(
            term_gain_two.astype(jnp.bfloat16), "fsdp", scatter_dimension=0, tiled=True
        ).astype(jnp.float32),
    )
    totals = (
        lax.psum(shard_gain_one.astype(jnp.bfloat16), "seq").astype(jnp.float32),
        lax.psum(shard_qkv.astype(jnp.bfloat16), "seq").astype(jnp.float32),
        lax.psum(shard_bias.astype(jnp.bfloat16), "seq").astype(jnp.float32),
        lax.psum(shard_out.astype(jnp.bfloat16), "seq").astype(jnp.float32),
        lax.psum(shard_gain_two.astype(jnp.bfloat16), "seq").astype(jnp.float32),
        lax.psum(shard_gate.astype(jnp.bfloat16), "seq").astype(jnp.float32),
        lax.psum(shard_up.astype(jnp.bfloat16), "seq").astype(jnp.float32),
        lax.psum(shard_down.astype(jnp.bfloat16), "seq").astype(jnp.float32),
    )
    return (
        hidden_out[None],
        grad_rows[None],
        totals[0],
        totals[1],
        totals[2],
        totals[3],
        totals[4],
        totals[5],
        totals[6],
        totals[7],
    )


def per_device(*arguments):
    return (per_device_kernels if kernels_fit(*arguments) else per_device_gathered)(*arguments)


def solution(mesh):
    placed = (
        P("fsdp", "seq", None),
        P("fsdp", "seq"),
        P("fsdp"),
        P("fsdp", None),
        P("fsdp"),
        P("fsdp", None),
        P("fsdp"),
        P("fsdp", None),
        P("fsdp", None),
        P("fsdp", None),
        P("fsdp", "seq", None),
    )
    return jax.shard_map(
        per_device,
        mesh=mesh,
        in_specs=placed,
        out_specs=(
            P("fsdp", "seq", None),
            P("fsdp", "seq", None),
            P("fsdp"),
            P("fsdp", None),
            P("fsdp"),
            P("fsdp", None),
            P("fsdp"),
            P("fsdp", None),
            P("fsdp", None),
            P("fsdp", None),
        ),
        check_vma=False,
    )
```

```python
import functools
import math

import jax
import jax.numpy as jnp
from jax import lax
from jax.experimental import pallas as pl
from jax.experimental.pallas import tpu as pltpu
from jax.sharding import PartitionSpec as P

HEADS = 12
KV_HEADS = 2
HEAD_DIM = 128


norm_eps = 1e-06
rope_base = 1000000.0


def rope_tables(position_row):
    half_dim = HEAD_DIM // 2
    frequency = jnp.exp(
        -(jnp.arange(half_dim, dtype=jnp.float32) * 2.0 / HEAD_DIM) * math.log(rope_base)
    )
    angles = position_row.astype(jnp.float32)[:, None] * frequency[None, :]
    angles = jnp.concatenate([angles, angles], axis=-1)
    return (jnp.cos(angles), jnp.sin(angles))


def rotate(values, cosine, sine):
    half_dim = values.shape[-1] // 2
    turned = jnp.concatenate([-values[..., half_dim:], values[..., :half_dim]], axis=-1)
    return values * cosine[:, None, :] + turned * sine[:, None, :]


def unrotate(grads_rot, cosine, sine):
    half_dim = grads_rot.shape[-1] // 2
    scaled = grads_rot * sine[:, None, :]
    return grads_rot * cosine[:, None, :] + jnp.concatenate(
        [scaled[..., half_dim:], -scaled[..., :half_dim]], axis=-1
    )


def norm_forward(values, gain):
    inverse = lax.rsqrt(jnp.mean(values * values, axis=-1, keepdims=True) + norm_eps)
    unit_rows = values * inverse
    return (unit_rows, inverse, (unit_rows * gain).astype(jnp.bfloat16))


def norm_backward(grad_normed, unit_rows, inverse, gain):
    grad_unit = grad_normed * gain
    grad_values = inverse * (
        grad_unit - unit_rows * jnp.mean(grad_unit * unit_rows, axis=-1, keepdims=True)
    )
    grad_gain = jnp.sum(grad_normed * unit_rows, axis=0)
    return (grad_values, grad_gain)


def masked_scores(queries, keys, block_start, block_rows):
    length = keys.shape[0]
    query_block = lax.dynamic_slice_in_dim(queries, block_start, block_rows, 0)
    scores = jnp.einsum(
        "bhd,ld->hbl", query_block, keys, preferred_element_type=jnp.float32
    ) * HEAD_DIM ** (-0.5)
    row_index = block_start + jnp.arange(block_rows)
    column_index = jnp.arange(length)
    allowed = column_index[None, :] <= row_index[:, None]
    return (query_block, jnp.where(allowed[None], scores, -1e30))


def attend_forward(queries, keys, values):
    length = keys.shape[0]
    block_rows = min(512, length)
    block_count = length // block_rows

    def one_block(block_start):
        query_block, scores = masked_scores(queries, keys, block_start, block_rows)
        row_max = jnp.max(scores, axis=-1, keepdims=True)
        exponent = jnp.exp(scores - row_max)
        row_total = jnp.sum(exponent, axis=-1, keepdims=True)
        probability = (exponent / row_total).astype(jnp.bfloat16)
        result = jnp.einsum("hbl,ld->bhd", probability, values, preferred_element_type=jnp.float32)
        return (result.astype(jnp.bfloat16), (row_max + jnp.log(row_total))[..., 0])

    results, log_totals = lax.map(one_block, jnp.arange(block_count) * block_rows)
    return (results.reshape(length, queries.shape[1], queries.shape[2]), log_totals)


def attend_backward(queries, keys, values, log_totals, grad_out):
    length = keys.shape[0]
    block_rows = min(512, length)
    block_count = length // block_rows
    score_scale = HEAD_DIM ** (-0.5)

    def one_block(running, inputs):
        grad_keys, grad_values = running
        block_start, log_block = inputs
        query_block, scores = masked_scores(queries, keys, block_start, block_rows)
        grad_block = lax.dynamic_slice_in_dim(grad_out, block_start, block_rows, 0)
        probability = jnp.exp(scores - log_block[..., None])
        grad_probs = jnp.einsum(
            "bhd,ld->hbl", grad_block, values, preferred_element_type=jnp.float32
        )
        row_delta = jnp.sum(probability * grad_probs, axis=-1, keepdims=True)
        grad_scores = (probability * (grad_probs - row_delta)).astype(jnp.bfloat16)
        grad_query = (
            jnp.einsum("hbl,ld->bhd", grad_scores, keys, preferred_element_type=jnp.float32)
            * score_scale
        )
        grad_keys = (
            grad_keys
            + jnp.einsum(
                "hbl,bhd->ld", grad_scores, query_block, preferred_element_type=jnp.float32
            )
            * score_scale
        )
        grad_values = grad_values + jnp.einsum(
            "hbl,bhd->ld",
            probability.astype(jnp.bfloat16),
            grad_block,
            preferred_element_type=jnp.float32,
        )
        return ((grad_keys, grad_values), grad_query)

    zero_rows = jnp.zeros((length, keys.shape[1]), jnp.float32)
    (grad_keys, grad_values), grad_query = lax.scan(
        one_block, (zero_rows, zero_rows), (jnp.arange(block_count) * block_rows, log_totals)
    )
    return (grad_query.reshape(queries.shape), grad_keys, grad_values)


MESH = pl.DeviceIdType.MESH
VMEM_BYTES = 67_000_000
NN = (((1,), (0,)), ((), ()))
NT = (((1,), (1,)), ((), ()))
TN = (((0,), (0,)), ((), ()))


def matmul(left, right, dims):
    return lax.dot_general(left, right, dims, preferred_element_type=jnp.float32)


def ring_place(index, size):
    side = index % 2
    return (index // 2) * (1 - side) + (size - 1 - index // 2) * side


def ring_member(place, size):
    side = place // (size // 2)
    return 2 * (place * (1 - side) + (size - 1 - place) * side) + side


def seq_partners(seq):
    core = seq + 1 - 2 * (seq % 2)
    far = (seq + 2) % 4
    return core, far, (core + 2) % 4


def greet(targets):
    barrier = pltpu.get_barrier_semaphore()
    for target in targets:
        pl.semaphore_signal(barrier, inc=1, device_id=target, device_id_type=MESH)
    pl.semaphore_wait(barrier, len(targets))


def for_blocks(width, block, body):
    for at in range(0, width, block):
        body(pl.ds(at, min(block, width - at)))


def loop_blocks(width, block, body):
    @pl.loop(0, width // block)
    def _(at):
        body(pl.ds(pl.multiple_of(at * block, block), block))


def turn_tables(trig):
    lane = lax.broadcasted_iota(jnp.int32, trig.shape, 1)
    swapped = pltpu.roll(trig, HEAD_DIM // 2, 1)
    first = lane < HEAD_DIM // 2
    return jnp.where(first, trig, swapped), jnp.where(first, -swapped, trig)


def head_columns(at):
    return slice(at * HEAD_DIM, (at + 1) * HEAD_DIM)


def causal(scores, start):
    rows = lax.broadcasted_iota(jnp.int32, scores.shape, 0) + start
    columns = lax.broadcasted_iota(jnp.int32, scores.shape, 1)
    return jnp.where(columns <= rows, scores, -1e30)


def inverse_of(values):
    return lax.rsqrt(jnp.mean(values * values, axis=-1, keepdims=True) + norm_eps)


def attend_forward_kernel(
    size,
    block,
    bias_share,
    rows_ref,
    trig_ref,
    piece_ref,
    small_ref,
    cot_ref,
    normed_out,
    heads_out,
    attended_out,
    log_out,
    piece_out,
    proj_out,
    trig_out,
    gains_out,
    normed_two_out,
    resid_out,
    cots_out,
    rows_all,
    trig_all,
    pieces,
    proj,
    smalls,
    cots,
    normed,
    heads,
    attended,
    logs,
    part,
    gains,
    bias,
    resid,
    seq_in,
    far_sum,
    normed_two,
    load_sems,
    store_sems,
    ring_sems,
    small_sems,
    cot_sems,
    cot_store_sems,
    seq_sems,
    sum_sems,
    proj_send,
    proj_recv,
):
    f32, bf16 = jnp.float32, jnp.bfloat16
    depth, joint = piece_ref.shape
    tokens, width = rows_ref.shape
    half = depth // 2
    cot_half = tokens // 2
    own = proj.shape[0]
    used = joint - own
    count = own // HEAD_DIM
    length = part.shape[0]
    per_group = own // depth
    scale = HEAD_DIM**-0.5
    me = lax.axis_index("fsdp")
    seq = lax.axis_index("seq")
    place = ring_place(me, size)
    right = ring_member((place + 1) % size, size)
    left = ring_member((place + size - 1) % size, size)
    core, far, diagonal = seq_partners(seq)
    ring = ({"fsdp": right}, {"fsdp": left})

    def remote(source, target, sems, at, device):
        return pltpu.make_async_remote_copy(
            src_ref=source,
            dst_ref=target,
            send_sem=sems.at[(0,) + at],
            recv_sem=sems.at[(1,) + at],
            device_id=device,
            device_id_type=MESH,
        )

    loads = [
        pltpu.make_async_copy(piece_ref, pieces.at[pl.ds(pl.multiple_of(me * depth, 16), depth)], load_sems.at[0]),
        pltpu.make_async_copy(trig_ref, trig_all.at[seq], load_sems.at[1]),
        pltpu.make_async_copy(rows_ref, rows_all.at[seq], load_sems.at[2]),
        pltpu.make_async_copy(small_ref, smalls.at[me], load_sems.at[3]),
        pltpu.make_async_copy(cot_ref, cots.at[me], load_sems.at[4]),
    ]
    for load in loads:
        load.start()
    greet(ring + ({"seq": core}, {"seq": far}, {"seq": diagonal}))

    def piece_of(step, side):
        return ring_member((place + size - step if side == 0 else place + step) % size, size)

    def ring_copy(step, side, sub):
        part_rows = half // 2
        start = piece_of(step, side) * depth + side * half + sub * part_rows
        span = pieces.at[pl.ds(pl.multiple_of(start, 16), part_rows)]
        return remote(span, span, ring_sems, (side, sub, step), ring[side])

    def small_copy(step):
        span = smalls.at[piece_of(step, 0)]
        return remote(span, span, small_sems, (step,), ring[0])

    def cot_copy(step, side, sub):
        part_rows = cot_half // 2
        start = side * cot_half + sub * part_rows
        span = cots.at[piece_of(step, side), pl.ds(start, part_rows)]
        return remote(span, span, cot_sems, (side, sub, step), ring[side])

    def cot_store(step, side):
        span = (piece_of(step, side), pl.ds(side * cot_half, cot_half))
        return pltpu.make_async_copy(
            cots.at[span], cots_out.at[span], cot_store_sems.at[side, step]
        )

    def seq_copy(which, block_at, target, at):
        span = (rows_all, trig_all)[which].at[block_at]
        return remote(span, span, seq_sems, (which, at), {"seq": target})

    def proj_part(step, side):
        at = piece_of(step, side)
        row = pl.multiple_of((at % per_group) * depth + side * half, 16)
        source = pieces.at[
            pl.ds(pl.multiple_of(at * depth + side * half, 16), half), pl.ds(used, own)
        ]
        target = proj.at[pl.ds(row, half), pl.ds(pl.multiple_of(seq * own, 128), own)]
        return at, at // per_group, source, target

    def proj_copy(step, side):
        at, owner, source, target = proj_part(step, side)
        return owner, pltpu.make_async_remote_copy(
            src_ref=source,
            dst_ref=target,
            send_sem=proj_send.at[side, step],
            recv_sem=proj_recv.at[seq, at % per_group, side],
            device_id={"seq": owner},
            device_id_type=MESH,
        )

    def proj_act(step, side, action):
        owner, copy = proj_copy(step, side)

        @pl.when(owner != seq)
        def _():
            if action == "start":
                copy.start()
            else:
                copy.wait_send()

        @pl.when(owner == seq)
        def _():
            _, _, source, target = proj_part(step, side)
            kept = pltpu.make_async_copy(source, target, proj_send.at[side, step])
            if action == "start":
                kept.start()
            else:
                kept.wait()

    stores = []

    def store(source, target):
        stores.append(pltpu.make_async_copy(source, target, store_sems.at[len(stores)]))
        stores[-1].start()

    def cot_pump(step):
        for sub in range(2):
            for side in range(2):
                if step >= 1:
                    cot_copy(step - 1, side, sub).wait_recv()
                if step < size - 1:
                    cot_copy(step, side, sub).start()
        for side in range(2):
            cot_store(step, side).start()

    loads[0].wait()
    for sub in range(2):
        for side in range(2):
            ring_copy(0, side, sub).start()
    loads[3].wait()
    small_copy(0).start()
    for which in (1, 0):
        loads[2 - which].wait()
        seq_copy(which, seq, far, 1).start()
        seq_copy(which, seq, core, 0).start()
    for side in range(2):
        proj_act(0, side, "start")
    loads[4].wait()

    for step in range(size - 1):
        for sub in range(2):
            for side in range(2):
                ring_copy(step, side, sub).wait_recv()
                if step < size - 2:
                    ring_copy(step + 1, side, sub).start()
        small_copy(step).wait_recv()
        if step < size - 2:
            small_copy(step + 1).start()
        if step == size - 3:
            cot_pump(0)
        for side in range(2):
            proj_act(step + 1, side, "start")
        if step == min(1, size - 2):
            for which in (1, 0):
                seq_copy(which, seq, far, 1).wait_recv()
                seq_copy(which, far, core, 2).start()

    gathered = jnp.zeros((8, width), f32)
    small_width = smalls.shape[2]
    for at in range(size):
        held = smalls[at].astype(f32)[0:8, :]
        lane = lax.broadcasted_iota(jnp.int32, held.shape, 1)
        wide = jnp.concatenate(
            [
                jnp.where(lane < depth, held, 0.0),
                jnp.zeros((8, width - small_width), f32),
            ],
            axis=1,
        )
        gathered += pltpu.roll(wide, at * depth, 1) if at else wide
        bias[:, at * bias_share : (at + 1) * bias_share] = held[:, :bias_share]
    gains[...] = gathered
    gain_one = gathered[0:1, :]
    gain_two = gathered[1:2, :]
    store(gains, gains_out)
    for which in (1, 0):
        seq_copy(which, seq, core, 0).wait_recv()
        seq_copy(which, far, core, 2).wait_recv()
    store(pieces, piece_out)
    store(trig_all, trig_out)

    width_query = count * HEAD_DIM * 4
    kv_lane = pl.multiple_of(width_query + (seq // 2) * HEAD_DIM, HEAD_DIM)
    value_lane = pl.multiple_of(kv_lane + KV_HEADS * HEAD_DIM, HEAD_DIM)
    own_bias = jnp.concatenate(
        [
            bias[2:3, pl.ds(pl.multiple_of(seq * own, HEAD_DIM), own)],
            bias[2:3, pl.ds(kv_lane, HEAD_DIM)],
            bias[2:3, pl.ds(value_lane, HEAD_DIM)],
        ],
        axis=1,
    )
    for at in range(length // block):
        span = slice(at * block, (at + 1) * block)
        rows = rows_all[at].astype(f32)
        normed[span, :] = (rows * inverse_of(rows) * gain_one).astype(bf16)
        mixed = matmul(normed[span, :], pieces[:, :used], NN) + own_bias
        cosine, sine = turn_tables(trig_all[at])
        for head in range(count + 1):
            turned = mixed[:, head_columns(head)]
            heads[span, head_columns(head)] = (
                turned * cosine + pltpu.roll(turned, HEAD_DIM // 2, 1) * sine
            ).astype(bf16)
        heads[span, head_columns(count + 1)] = mixed[:, head_columns(count + 1)].astype(bf16)
        if 2 * (at + 1) == length // block:
            cot_pump(1)
    store(normed, normed_out)
    store(heads, heads_out)

    for peer in (core, far, diagonal):
        for at in range(per_group):
            for side in range(2):
                pltpu.make_async_remote_copy(
                    src_ref=pieces.at[pl.ds(0, half), pl.ds(used, own)],
                    dst_ref=proj.at[pl.ds(0, half), pl.ds(0, own)],
                    send_sem=proj_send.at[side, 0],
                    recv_sem=proj_recv.at[peer, at, side],
                    device_id={"seq": peer},
                    device_id_type=MESH,
                ).wait_recv()
    for step in range(size):
        for side in range(2):
            proj_act(step, side, "wait")
    store(proj, proj_out)

    lane = lax.broadcasted_iota(jnp.int32, (block, HEAD_DIM), 1)
    for start in range(0, length, block):
        span = slice(start, start + block)
        seen = slice(0, start + block)
        logs[span, :] = jnp.zeros((block, HEAD_DIM), f32)

        @pl.loop(0, count)
        def _(at):
            head = pl.ds(pl.multiple_of(at * HEAD_DIM, HEAD_DIM), HEAD_DIM)
            scores = causal(
                matmul(heads[span, head], heads[seen, head_columns(count)], NT) * scale, start
            )
            top = jnp.max(scores, axis=-1, keepdims=True)
            exponent = jnp.exp(scores - top)
            total = jnp.sum(exponent, axis=-1, keepdims=True)
            probability = (exponent / total).astype(bf16)
            attended[span, head] = matmul(
                probability, heads[seen, head_columns(count + 1)], NN
            ).astype(bf16)
            logs[span, :] = jnp.where(lane == at, top + jnp.log(total), logs[span, :])

        if 2 * (start + block) == length:
            cot_pump(2)
    store(attended, attended_out)
    store(logs, log_out)

    def out_part(span):
        part[:, span] = matmul(attended[...], proj[:, span], NN).astype(bf16)

    for_blocks(width, 512, out_part)

    def part_rows(at):
        return part.at[pl.ds(pl.multiple_of(at * tokens, tokens), tokens)]

    to_core = [
        remote(part_rows(diagonal), seq_in.at[0], sum_sems, (0,), {"seq": core}),
        remote(part_rows(core), seq_in.at[1], sum_sems, (1,), {"seq": core}),
    ]
    to_far = remote(far_sum, seq_in.at[2], sum_sems, (2,), {"seq": far})
    for copy in to_core:
        copy.start()
    cot_pump(3)
    to_core[0].wait_recv()
    far_sum[...] = (part_rows(far)[...].astype(f32) + seq_in[0].astype(f32)).astype(bf16)
    to_far.start()
    to_core[1].wait_recv()
    resid[...] = (
        part_rows(seq)[...].astype(f32) + seq_in[1].astype(f32) + rows_all[seq].astype(f32)
    )
    cot_pump(4)
    cot_pump(5)
    to_far.wait_recv()
    resid[...] += seq_in[2].astype(f32)
    store(resid, resid_out)
    normed_two[...] = (resid[...] * inverse_of(resid[...]) * gain_two).astype(bf16)
    store(normed_two, normed_two_out)
    for step in range(6, size):
        cot_pump(step)
    for step in range(size):
        for side in range(2):
            cot_store(step, side).wait()

    for step in range(size - 1):
        for side in range(2):
            for sub in range(2):
                ring_copy(step, side, sub).wait_send()
                cot_copy(step, side, sub).wait_send()
        small_copy(step).wait_send()
    for which in (1, 0):
        seq_copy(which, seq, core, 0).wait_send()
        seq_copy(which, seq, far, 1).wait_send()
        seq_copy(which, far, core, 2).wait_send()
    for copy in to_core + [to_far]:
        copy.wait_send()
    for copy in stores:
        copy.wait()


def attend_group(rows, trig, piece, small, cots, bias_share):
    size = lax.axis_size("fsdp")
    groups = lax.axis_size("seq")
    tokens, width = rows.shape
    depth, joint = piece.shape
    own = width // groups
    used = joint - own
    length = tokens * groups
    f32, bf16 = jnp.float32, jnp.bfloat16
    dma = pltpu.SemaphoreType.DMA
    anywhere = pl.BlockSpec(memory_space=pl.ANY)
    normed = ((length, width), bf16)
    heads = ((length, used), bf16)
    attended = ((length, own), bf16)
    logs = ((length, HEAD_DIM), f32)
    pieces = ((width, joint), bf16)
    proj = ((own, width), bf16)
    trig_all = ((groups,) + trig.shape, f32)
    gains = ((8, width), f32)
    rows_all = ((groups, tokens, width), bf16)
    own_rows = ((tokens, width), bf16)
    resid = ((tokens, width), f32)
    cots_all = ((size, tokens, width), bf16)
    outs = (
        normed, heads, attended, logs, pieces, proj, trig_all, gains, own_rows, resid, cots_all
    )
    held = (
        rows_all,
        trig_all,
        pieces,
        proj,
        ((size,) + small.shape, bf16),
        cots_all,
        normed,
        heads,
        attended,
        logs,
        normed,
        gains,
        ((8, size * bias_share), f32),
        resid,
        ((3, tokens, width), bf16),
        own_rows,
        own_rows,
    )
    return pl.pallas_call(
        functools.partial(attend_forward_kernel, size, tokens, bias_share),
        out_shape=tuple(jax.ShapeDtypeStruct(*shape) for shape in outs),
        in_specs=[anywhere] * 5,
        out_specs=(anywhere,) * len(outs),
        scratch_shapes=[pltpu.VMEM(*shape) for shape in held]
        + [
            dma((5,)),
            dma((len(outs),)),
            dma((2, 2, 2, size)),
            dma((2, size)),
            dma((2, 2, 2, size)),
            dma((2, size)),
            dma((2, 2, 3)),
            dma((2, 3)),
            dma((2, size)),
            dma((groups, own // depth, 2)),
        ],
        compiler_params=pltpu.CompilerParams(
            collective_id=1, has_side_effects=True, vmem_limit_bytes=VMEM_BYTES
        ),
        name="attend_forward",
    )(rows, trig, piece, small, cots)


CHUNKS = 5
IN_LOOP = ((2, 1), (4, 2), (6, 3))


def mlp_kernel(
    size,
    normed_ref,
    resid_ref,
    gain_ref,
    cots_ref,
    gate_ref,
    up_ref,
    down_ref,
    outs_ref,
    back_ref,
    gain_grad_ref,
    sums_ref,
    far_ref,
    rows_all,
    cots,
    weights,
    grads,
    hid,
    dgate,
    dup,
    resid,
    sums_in,
    backs,
    outs,
    load_sems,
    cot_sems,
    ring_send,
    ring_recv,
    sum_send,
    sum_recv,
    out_sems,
    swap_sems,
    far_sems,
    swap_ready,
):
    tokens, width = normed_ref.shape
    units = gate_ref.shape[0]
    half = tokens // 2
    me = lax.axis_index("fsdp")
    seq = lax.axis_index("seq")
    place = ring_place(me, size)
    right = ring_member((place + 1) % size, size)
    left = ring_member((place + size - 1) % size, size)
    core, far, diagonal = seq_partners(seq)
    sides = ((right, pl.ds(0, half)), (left, pl.ds(half, half)))

    def owner_of(step, side):
        return ring_member((place + size - step if side == 0 else place + step) % size, size)

    own_load = pltpu.make_async_copy(normed_ref, rows_all.at[0], load_sems.at[3])
    resid_load = pltpu.make_async_copy(resid_ref, resid, load_sems.at[4])
    weight_loads = [
        pltpu.make_async_copy(ref, weights.at[at], load_sems.at[at])
        for at, ref in enumerate((gate_ref, up_ref, down_ref))
    ]
    own_load.start()
    greet(({"fsdp": right}, {"fsdp": left}, {"seq": core}, {"seq": far}))

    def cot_copies(step):
        return [
            pltpu.make_async_copy(
                cots_ref.at[
                    pl.ds(
                        pl.multiple_of(owner_of(step, side) * tokens + side * half, half), half
                    )
                ],
                cots.at[step % 2, sides[side][1]],
                cot_sems.at[step % 2, side],
            )
            for side in range(2)
        ]


    def row_copy(step, side):
        target, span = sides[side]
        return pltpu.make_async_remote_copy(
            src_ref=rows_all.at[step, span],
            dst_ref=rows_all.at[step + 1, span],
            send_sem=ring_send.at[side, step],
            recv_sem=ring_recv.at[side, step + 1],
            device_id={"fsdp": target},
            device_id_type=MESH,
        )

    def sum_span(side, sub):
        return pl.ds(side * half + sub * (half // 2), half // 2)

    def sum_copy(step, side, sub):
        target, span = sides[side][0], sum_span(side, sub)
        return pltpu.make_async_remote_copy(
            src_ref=backs.at[step, span],
            dst_ref=sums_in.at[step, span],
            send_sem=sum_send.at[side, sub, step],
            recv_sem=sum_recv.at[side, sub, step],
            device_id={"fsdp": target},
            device_id_type=MESH,
        )

    def sum_step(step):
        for sub in range(2):
            for side in range(2):
                span = sum_span(side, sub)
                if step >= 2:
                    sum_copy(step - 1, side, sub).wait_recv()
                    backs[step, span] = (
                        backs[step, span].astype(jnp.float32)
                        + sums_in[step - 1, span].astype(jnp.float32)
                    ).astype(jnp.bfloat16)
                sum_copy(step, side, sub).start()

    def out_copy(step, side):
        at = pl.multiple_of(owner_of(step, side) * tokens + side * half, half)
        return pltpu.make_async_copy(
            outs.at[step % 2, sides[side][1]], outs_ref.at[pl.ds(at, half)], out_sems.at[side, step]
        )

    def elementwise(step, span):
        rows = rows_all[step]
        gate = matmul(rows, weights[0, span, :], NT)
        up = matmul(rows, weights[1, span, :], NT)
        grad_hidden = matmul(cots[step % 2], weights[2, span, :], NT)
        sigmoid = jax.nn.sigmoid(gate)
        activated = gate * sigmoid
        hid[:, span] = (activated * up).astype(jnp.bfloat16)
        dgate[:, span] = (
            grad_hidden * up * sigmoid * (1.0 + gate * (1.0 - sigmoid))
        ).astype(jnp.bfloat16)
        dup[:, span] = (grad_hidden * activated).astype(jnp.bfloat16)

    own_load.wait()
    for side in range(2):
        row_copy(0, side).start()
    for load in weight_loads + cot_copies(0) + [resid_load]:
        load.start()

    @pl.loop(0, units // 16)
    def _(at):
        zeros = jnp.zeros((3, 16, width), jnp.float32)
        grads[:, pl.ds(pl.multiple_of(at * 16, 16), 16), :] = zeros

    for load in weight_loads:
        load.wait()

    @pl.loop(0, size)
    def _(step):
        slot = step % 2

        @pl.when(step >= 1)
        def _():
            for side in range(2):
                row_copy(step - 1, side).wait_recv()

        @pl.when((step >= 1) & (step < size - 1))
        def _():
            for side in range(2):
                row_copy(step, side).start()

        for load in cot_copies(step):
            load.wait()

        @pl.when(step < size - 1)
        def _():
            for load in cot_copies(step + 1):
                load.start()

        for_blocks(units, 256, functools.partial(elementwise, step))

        def back_part(span):
            backs[step, :, span] = (
                matmul(dgate[...], weights[0, :, span], NN)
                + matmul(dup[...], weights[1, :, span], NN)
            ).astype(jnp.bfloat16)

        for_blocks(width, 256, back_part)

        for when, at in IN_LOOP:

            @pl.when(step == when)
            def _():
                sum_step(at)

        @pl.when(step >= 2)
        def _():
            for side in range(2):
                out_copy(step - 2, side).wait()

        def out_part(span):
            outs[slot, :, span] = matmul(hid[...], weights[2, :, span], NN).astype(jnp.bfloat16)

        for_blocks(width, 256, out_part)
        for side in range(2):
            out_copy(step, side).start()

        def weight_part(span):
            rows, cot = rows_all[step, :, span], cots[slot, :, span]
            grads[0, :, span] += matmul(dgate[...], rows, TN)
            grads[1, :, span] += matmul(dup[...], rows, TN)
            grads[2, :, span] += matmul(hid[...], cot, TN)

        for_blocks(width, 256, weight_part)

    share = units // 2
    kept = pl.multiple_of((seq % 2) * share, 16)
    given = pl.multiple_of((1 - seq % 2) * share, 16)
    chunk = share // CHUNKS
    pl.semaphore_signal(swap_ready, inc=1, device_id={"seq": core}, device_id_type=MESH)

    def to_seq(source, target, sems, at, device):
        return pltpu.make_async_remote_copy(
            src_ref=source,
            dst_ref=target,
            send_sem=sems.at[0, at],
            recv_sem=sems.at[1, at],
            device_id={"seq": device},
            device_id_type=MESH,
        )

    swaps = [
        to_seq(
            weights.at[at, pl.ds(given, share)],
            weights.at[at, pl.ds(given, share)],
            swap_sems,
            at,
            core,
        )
        for at in range(3)
    ]
    waiting = [at for at in range(1, size) if at not in [pair[1] for pair in IN_LOOP]]
    sum_step(waiting[0])
    for at in range(3):

        @pl.loop(0, share // 16)
        def _(block):
            span = pl.ds(pl.multiple_of(given + block * 16, 16), 16)
            weights[at, span, :] = grads[at, span, :].astype(jnp.bfloat16)

        if at == 0:
            pl.semaphore_wait(swap_ready, 1)
        swaps[at].start()

    stores = []

    def kept_rows(at):
        return pl.ds(pl.multiple_of(kept + at * chunk, 16), chunk)

    far_copies = [
        to_seq(weights.at[0, kept_rows(at)], far_ref.at[kept_rows(at)], far_sems, at, far)
        for at in range(CHUNKS)
    ]
    def swap_finish(at):
        swaps[at].wait_recv()

        @pl.loop(0, share // 16)
        def _(block):
            span = pl.ds(pl.multiple_of(kept + block * 16, 16), 16)
            weights[at, span, :] = (
                grads[at, span, :] + weights[at, span, :].astype(jnp.float32)
            ).astype(jnp.bfloat16)

        done = weights.at[at, pl.ds(kept, share)]
        stores.append(
            pltpu.make_async_copy(done, sums_ref.at[at, pl.ds(kept, share)], load_sems.at[at])
        )
        if at == 0:
            for copy in far_copies:
                copy.start()
        stores[-1].start()

    cot_own = pltpu.make_async_copy(
        cots_ref.at[pl.ds(pl.multiple_of(me * tokens, tokens), tokens)],
        cots.at[0],
        load_sems.at[7],
    )
    cot_own.start()
    for turn, at in enumerate(waiting[1:]):
        sum_step(at)
        if turn < 3:
            swap_finish(turn)
    for turn in range(len(waiting) - 1, 3):
        swap_finish(turn)

    for side in range(2):
        for sub in range(2):
            sum_copy(size - 1, side, sub).wait_recv()
    grad_normed = backs[0].astype(jnp.float32) + sums_in[size - 1].astype(jnp.float32)
    resid_load.wait()
    inverse = inverse_of(resid[...])
    unit_rows = resid[...] * inverse
    gain_grad_ref[...] = jnp.sum(grad_normed * unit_rows, axis=0, keepdims=True)
    grad_unit = grad_normed * gain_ref[...]
    cot_own.wait()
    back_ref[...] = cots[0].astype(jnp.float32) + inverse * (
        grad_unit - unit_rows * jnp.mean(grad_unit * unit_rows, axis=-1, keepdims=True)
    )
    for side in range(2):
        out_copy(size - 2, side).wait()
        out_copy(size - 1, side).wait()

        @pl.loop(0, size - 1)
        def _(step):
            row_copy(step, side).wait_send()
            for sub in range(2):
                sum_copy(step + 1, side, sub).wait_send()

    for copy in swaps + far_copies:
        copy.wait_send()
    for copy in far_copies:
        copy.wait_recv()
    for store in stores:
        store.wait()


def mlp_ring(normed, resid, gain, cots, gate_weight, up_weight, down_weight):
    size = lax.axis_size("fsdp")
    tokens, width = normed.shape
    units = gate_weight.shape[0]
    anywhere = pl.BlockSpec(memory_space=pl.ANY)
    inside = pl.BlockSpec(memory_space=pltpu.VMEM)
    bf16, f32 = jnp.bfloat16, jnp.float32
    dma = pltpu.SemaphoreType.DMA
    return pl.pallas_call(
        functools.partial(mlp_kernel, size),
        out_shape=(
            jax.ShapeDtypeStruct((size * tokens, width), bf16),
            jax.ShapeDtypeStruct((tokens, width), f32),
            jax.ShapeDtypeStruct((1, width), f32),
            jax.ShapeDtypeStruct((3, units, width), bf16),
            jax.ShapeDtypeStruct((units, width), bf16),
        ),
        in_specs=[anywhere, anywhere, inside, anywhere, anywhere, anywhere, anywhere],
        out_specs=(anywhere, inside, inside, anywhere, anywhere),
        scratch_shapes=[
            pltpu.VMEM((size, tokens, width), bf16),
            pltpu.VMEM((2, tokens, width), bf16),
            pltpu.VMEM((3, units, width), bf16),
            pltpu.VMEM((3, units, width), f32),
            pltpu.VMEM((tokens, units), bf16),
            pltpu.VMEM((tokens, units), bf16),
            pltpu.VMEM((tokens, units), bf16),
            pltpu.VMEM((tokens, width), f32),
            pltpu.VMEM((size, tokens, width), bf16),
            pltpu.VMEM((size, tokens, width), bf16),
            pltpu.VMEM((2, tokens, width), bf16),
            dma((9,)),
            dma((2, 2)),
            dma((2, size)),
            dma((2, size)),
            dma((2, 2, size)),
            dma((2, 2, size)),
            dma((2, size)),
            dma((2, 3)),
            dma((2, CHUNKS)),
            pltpu.SemaphoreType.REGULAR,
        ],
        compiler_params=pltpu.CompilerParams(
            collective_id=0, has_side_effects=True, vmem_limit_bytes=VMEM_BYTES
        ),
        name="mlp_ring",
    )(normed, resid, gain, cots, gate_weight, up_weight, down_weight)


def attend_backward_kernel(
    size,
    heads_ref,
    attended_ref,
    log_ref,
    proj_ref,
    weight_ref,
    normed_ref,
    trig_ref,
    hidden_ref,
    resid_grad_ref,
    gain_ref,
    gain_grad_ref,
    resid_ref,
    outs_ref,
    units_in_ref,
    far_gate_in_ref,
    grad_in_ref,
    hidden_out_ref,
    small_ref,
    shards_ref,
    halves_ref,
    far_units_ref,
    units_ref,
    far_gate_ref,
    grads_all,
    grad_heads,
    grad_mixed,
    grad_keys,
    grad_values,
    grad_normed,
    term_qkv,
    term_out,
    out_columns,
    qkv_in,
    out_in,
    qkv_sum,
    out_sum,
    shard,
    shard_all,
    half_shard,
    half_all,
    out_own,
    out_recv,
    out_send,
    resid,
    seq_in,
    far_sum,
    small_in,
    load_sems,
    own_sems,
    out_sems,
    term_sems,
    column_sems,
    seq_sems,
    shard_sems,
    small_sems,
    unit_sems,
    pass_sems,
    share_sems,
    gate_sems,
    grad_sems,
):
    length = heads_ref.shape[0]
    tokens, width = hidden_ref.shape
    used = heads_ref.shape[1]
    own = attended_ref.shape[1]
    count = own // HEAD_DIM
    scale = HEAD_DIM**-0.5
    half = tokens // 2
    block = tokens
    depth = width // size
    chip_pieces = size // 2
    half_width = width // 2
    term_half = depth // 2
    units = units_ref.shape[1]
    f32, bf16 = jnp.float32, jnp.bfloat16
    me = lax.axis_index("fsdp")
    seq = lax.axis_index("seq")
    place = ring_place(me, size)
    right = ring_member((place + 1) % size, size)
    left = ring_member((place + size - 1) % size, size)
    core, far, diagonal = seq_partners(seq)
    rounds = size.bit_length() - 1
    mirrors = [me + (1 - 2 * ((me // 2**at) % 2)) * 2**at for at in range(rounds)]
    ring = ({"fsdp": right}, {"fsdp": left})

    def owner_of(step, side):
        return ring_member((place + size - step if side == 0 else place + step) % size, size)

    def remote(source, target, sems, at, device):
        return pltpu.make_async_remote_copy(
            src_ref=source,
            dst_ref=target,
            send_sem=sems.at[(0,) + at],
            recv_sem=sems.at[(1,) + at],
            device_id=device,
            device_id_type=MESH,
        )

    greet(
        ring
        + ({"seq": core}, {"seq": far})
        + tuple({"fsdp": mirror} for mirror in mirrors)
    )

    def own_load(step, side):
        at = pl.multiple_of(owner_of(step, side) * tokens + side * half, half)
        return pltpu.make_async_copy(
            outs_ref.at[pl.ds(at, half)],
            out_own.at[step % 2, pl.ds(side * half, half)],
            own_sems.at[step % 2, side],
        )

    def out_copy(step, side):
        span = pl.ds(side * half, half)
        return remote(
            out_send.at[step % 2, span], out_recv.at[step, span], out_sems, (side, step), ring[side]
        )

    def out_step(step):
        for side in range(2):
            own_load(step, side).wait()
            if step < size - 1:
                own_load(step + 1, side).start()
            if step >= 3:
                out_copy(step - 2, side).wait_send()
            if step >= 2:
                out_copy(step - 1, side).wait_recv()
        total = out_own[step % 2].astype(f32)
        if step >= 2:
            total += out_recv[step - 1].astype(f32)
        out_send[step % 2] = total.astype(bf16)
        for side in range(2):
            out_copy(step, side).start()

    resid_load = pltpu.make_async_copy(resid_ref, resid, load_sems.at[0])

    def out_finish():
        step = size
        for side in range(2):
            out_copy(step - 2, side).wait_send()
            out_copy(step - 1, side).wait_send()
            out_copy(step - 1, side).wait_recv()
        mine = pltpu.make_async_copy(
            outs_ref.at[pl.ds(pl.multiple_of(me * tokens, tokens), tokens)],
            out_own.at[0],
            load_sems.at[1],
        )
        mine.start()
        mine.wait()
        resid_load.wait()
        hidden_out_ref[...] = (
            resid[...] + out_own[0].astype(f32) + out_recv[size - 1].astype(f32)
        ).astype(bf16)

    share = units // 2
    piece = share // CHUNKS
    kept = (seq % 2) * share

    def unit_slice(ref, at):
        start = pl.multiple_of(kept + (at % CHUNKS) * piece, 16)
        return ref.at[at // CHUNKS, pl.ds(start, piece)]

    def unit_copy(at):
        return remote(
            unit_slice(units_ref, at + CHUNKS), unit_slice(far_units_ref, at), unit_sems, (at,), {"seq": far}
        )

    def unit_pass(at):
        part = unit_slice(far_units_ref, at)
        return remote(part, part, pass_sems, (at,), {"seq": core})

    def unit_share(at):
        part = unit_slice(units_ref, at)
        return remote(part, part, share_sems, (at,), {"seq": core})

    def gate_pass(at):
        part = far_gate_ref.at[pl.ds(pl.multiple_of(kept + at * piece, 16), piece)]
        return remote(part, part, gate_sems, (at,), {"seq": core})

    chunks = 2 * CHUNKS
    starts, passes = iter(range(chunks)), iter(range(chunks))

    def send_units(number):
        for _ in range(number):
            unit_copy(next(starts)).start()

    def pass_units(number):
        for _ in range(number):
            at = next(passes)
            unit_copy(at).wait_recv()
            unit_pass(at).start()

    def grad_copy(source, target, at):
        span = grads_all.at[source]
        return remote(span, span, grad_sems, (at,), {"seq": target})

    to_far_grads = grad_copy(seq, far, 0)
    to_core_grads = grad_copy(seq, core, 1)
    passed_grads = grad_copy(far, core, 2)
    grads_all[seq] = resid_grad_ref[...].astype(bf16)
    to_far_grads.start()
    to_core_grads.start()
    resid_load.start()
    for side in range(2):
        own_load(1, side).start()
    out_step(1)

    grad_keys[...] = jnp.zeros_like(grad_keys)
    grad_values[...] = jnp.zeros_like(grad_values)
    lane = lax.broadcasted_iota(jnp.int32, (block, HEAD_DIM), 1)
    keys = slice(own, own + HEAD_DIM)
    values = slice(own + HEAD_DIM, used)

    def attend_block(at_block):
        start = at_block * block
        span = slice(start, start + block)
        seen = slice(0, start + block)
        cosine, sine = turn_tables(trig_ref[span, :])
        grad_heads[span, :] = matmul(grads_all[at_block], proj_ref[...], NT).astype(bf16)

        @pl.loop(0, count)
        def _(at):
            head = pl.ds(pl.multiple_of(at * HEAD_DIM, HEAD_DIM), HEAD_DIM)
            query = heads_ref[span, head]
            grad = grad_heads[span, head]
            logs = jnp.sum(jnp.where(lane == at, log_ref[span, :], 0.0), axis=-1, keepdims=True)
            scores = causal(matmul(query, heads_ref[seen, keys], NT) * scale, start)
            probability = jnp.exp(scores - logs)
            grad_probs = matmul(grad, heads_ref[seen, values], NT)
            delta = jnp.sum(probability * grad_probs, axis=-1, keepdims=True)
            grad_scores = (probability * (grad_probs - delta)).astype(bf16)
            grad_query = matmul(grad_scores, heads_ref[seen, keys], NN) * scale
            grad_query = grad_query.astype(bf16).astype(f32)
            grad_mixed[span, head] = (
                grad_query * cosine + pltpu.roll(grad_query * sine, HEAD_DIM // 2, 1)
            ).astype(bf16)
            grad_keys[seen, :] += matmul(grad_scores, query, TN) * scale
            grad_values[seen, :] += matmul(probability.astype(bf16), grad, TN)

    @pl.loop(0, 4)
    def _(turn):
        @pl.when(turn == 1)
        def _():
            to_core_grads.wait_recv()

        @pl.when(turn == 2)
        def _():
            to_far_grads.wait_recv()
            passed_grads.start()
            unit_copy(0).start()

        @pl.when(turn == 3)
        def _():
            passed_grads.wait_recv()
            unit_copy(1).start()

        @pl.when(turn == 2)
        def _():
            out_step(2)

        for shared in range(3):
            unit_share(turn * 3 + shared).start()
        gate_pass(turn).start()
        at_block = ((seq // 2 + turn // 2) % 2) * 2 + (seq % 2 + turn % 2) % 2
        for at in range(4):

            @pl.when(at_block == at)
            def _():
                attend_block(at)

    next(starts)
    next(starts)
    send_units(1)
    for shared in range(12, 3 * CHUNKS):
        unit_share(shared).start()
    gate_pass(4).start()
    out_step(3)

    for start in range(0, length, block):
        span = slice(start, start + block)
        cosine, sine = turn_tables(trig_ref[span, :])
        part = grad_keys[span, :].astype(bf16).astype(f32)
        grad_mixed[span, keys] = (
            part * cosine + pltpu.roll(part * sine, HEAD_DIM // 2, 1)
        ).astype(bf16)
        grad_mixed[span, values] = grad_values[span, :].astype(bf16)

    def normed_part(span):
        grad_normed[:, span] = matmul(grad_mixed[...], weight_ref[span, :used], NT).astype(bf16)

    loop_blocks(width, 256, normed_part)

    def block_rows(at):
        return grad_normed.at[pl.ds(pl.multiple_of(at * tokens, tokens), tokens)]

    to_core = [
        remote(block_rows(diagonal), seq_in.at[0], seq_sems, (0,), {"seq": core}),
        remote(block_rows(core), seq_in.at[1], seq_sems, (1,), {"seq": core}),
    ]
    to_far = remote(far_sum, seq_in.at[2], seq_sems, (2,), {"seq": far})
    for copy in to_core:
        copy.start()

    def out_term(span):
        term_out[:, span] = matmul(
            attended_ref[...], grads_all[:, :, span].reshape(length, span.size), TN
        ).astype(bf16)

    loop_blocks(width, 256, out_term)
    my_row = pl.multiple_of((seq % 2) * own, 16)
    my_lane = pl.multiple_of((seq % 2) * half_width, 128)
    core_lane = pl.multiple_of((1 - seq % 2) * half_width, 128)
    columns = remote(
        term_out.at[:, pl.ds(core_lane, half_width)],
        out_columns.at[pl.ds(my_row, own)],
        column_sems,
        (0,),
        {"seq": core},
    )
    columns.start()
    out_columns[pl.ds(my_row, own), :] = term_out[:, pl.ds(my_lane, half_width)]

    def qkv_term(span):
        term_qkv[span, :] = matmul(normed_ref[:, span], grad_mixed[...], TN).astype(bf16)

    loop_blocks(width, 256, qkv_term)
    to_core[0].wait_recv()
    far_sum[...] = (block_rows(far)[...].astype(f32) + seq_in[0].astype(f32)).astype(bf16)
    to_far.start()
    out_step(4)
    small_in[0] = jnp.zeros((8, width), f32)
    small_in[0, 1:2, :] = gain_grad_ref[...]
    bias = jnp.sum(grad_mixed[...].astype(f32), axis=0, keepdims=True)
    small_in[0, 2:3, pl.ds(pl.multiple_of(seq * own, 128), own)] = bias[:, :own]
    kv_lane = pl.multiple_of((seq // 2) * HEAD_DIM, HEAD_DIM)
    small_in[0, 3:4, pl.ds(kv_lane, HEAD_DIM)] = bias[:, keys]
    small_in[0, 3:4, pl.ds(kv_lane + KV_HEADS * HEAD_DIM, HEAD_DIM)] = bias[:, values]

    def term_copy(step, side):
        span = pl.ds(side * term_half, term_half)
        return remote(
            qkv_sum.at[step, span], qkv_in.at[step, span], term_sems, (0, side, step), ring[side]
        )

    def half_copy(step, side):
        span = pl.ds(side * term_half, term_half)
        return remote(
            out_sum.at[step, span], out_in.at[step, span], term_sems, (1, side, step), ring[side]
        )

    def here(owner):
        return owner // chip_pieces == seq // 2

    def half_rows(owner, side):
        start = (owner % chip_pieces) * depth + side * term_half
        return pl.ds(pl.multiple_of(start, 16), term_half)

    def term_step(step):
        for side in range(2):
            span = pl.ds(side * term_half, term_half)
            start = owner_of(step, side) * depth + side * term_half
            total = term_qkv[pl.ds(pl.multiple_of(start, 16), term_half), :].astype(f32)
            if step >= 2:
                term_copy(step - 1, side).wait_recv()
                total += qkv_in[step - 1, span, :].astype(f32)
            qkv_sum[step, span, :] = total.astype(bf16)
            term_copy(step, side).start()

    def half_step(step):
        for side in range(2):
            owner = owner_of(step, side)

            @pl.when(here(owner))
            def _():
                span = pl.ds(side * term_half, term_half)
                total = out_columns[half_rows(owner, side), :].astype(f32)
                if step >= 2:
                    half_copy(step - 1, side).wait_recv()
                    total += out_in[step - 1, span, :].astype(f32)
                out_sum[step, span, :] = total.astype(bf16)
                half_copy(step, side).start()

    def small_copy(at):
        device = ({"seq": core}, {"seq": far})[at] if at < 2 else {"fsdp": mirrors[at - 2]}
        return remote(small_in.at[2 * at], small_in.at[2 * at + 1], small_sems, (at,), device)

    def small_step(at):
        small_copy(at).wait_recv()
        small_in[2 * at + 2] = small_in[2 * at] + small_in[2 * at + 1]

    term_step(1)
    columns.wait_recv()
    half_step(1)
    term_step(2)
    half_step(2)
    out_step(5)
    to_core[1].wait_recv()
    to_far.wait_recv()
    rows = hidden_ref[...].astype(f32)
    inverse = lax.rsqrt(jnp.mean(rows * rows, axis=-1, keepdims=True) + norm_eps)
    unit_rows = rows * inverse
    grad_rows = (
        block_rows(seq)[...].astype(f32) + seq_in[1].astype(f32) + seq_in[2].astype(f32)
    )
    small_in[0, 0:1, :] = jnp.sum(grad_rows * unit_rows, axis=0, keepdims=True)
    small_copy(0).start()
    grad_unit = grad_rows * gain_ref[...]
    grad_in_ref[...] = resid_grad_ref[...] + inverse * (
        grad_unit - unit_rows * jnp.mean(grad_unit * unit_rows, axis=-1, keepdims=True)
    )
    total_rounds = rounds + 2
    small_step(0)
    small_copy(1).start()
    done = 1
    send_units(3)
    for step in range(3, size):
        term_step(step)
        half_step(step)
        if done < total_rounds:
            small_step(done)
            done += 1
            if done < total_rounds:
                small_copy(done).start()
        if step == 4:
            send_units(2)
        if step % 2 == 0:
            pass_units(2)
    while done < total_rounds:
        small_step(done)
        done += 1
        if done < total_rounds:
            small_copy(done).start()
    small_ref[...] = small_in[2 * total_rounds]
    source_chip = here(me)
    for side in range(2):
        span = pl.ds(side * term_half, term_half)
        start = me * depth + side * term_half
        term_copy(size - 1, side).wait_recv()
        shard[span, :] = (
            term_qkv[pl.ds(pl.multiple_of(start, 16), term_half), :].astype(f32)
            + qkv_in[size - 1, span, :].astype(f32)
        ).astype(bf16)

        @pl.when(source_chip)
        def _():
            half_copy(size - 1, side).wait_recv()
            half_shard[span, :] = (
                out_columns[half_rows(me, side), :].astype(f32)
                + out_in[size - 1, span, :].astype(f32)
            ).astype(bf16)

    def shard_copy(source, at, block_at, target):
        return remote(source, shard_all.at[block_at], shard_sems, (at,), {"seq": target})

    def half_move(source, at, target):
        return remote(source, half_all.at[seq % 2], shard_sems, (at,), {"seq": target})

    shard_far = shard_copy(shard, 0, seq, far)
    shard_core = shard_copy(shard, 1, seq, core)
    shard_pass = shard_copy(shard_all.at[far], 2, far, core)
    half_far = half_move(half_shard, 3, far)
    half_core = half_move(half_shard, 4, core)
    half_pass = half_move(half_all.at[seq % 2], 5, core)
    shard_far.start()
    shard_core.start()

    @pl.when(source_chip)
    def _():
        half_far.start()
        half_core.start()
        half_all[seq % 2] = half_shard[...]

    send_units(2)
    shard_all[seq] = shard[...]
    out_step(6)
    shard_far.wait_recv()
    shard_pass.start()

    @pl.when(jnp.logical_not(source_chip))
    def _():
        half_far.wait_recv()
        half_pass.start()

    pass_units(3)
    out_step(7)
    pass_units(3)
    out_finish()
    shard_core.wait_recv()
    shard_pass.wait_recv()
    shard_store = pltpu.make_async_copy(shard_all, shards_ref, load_sems.at[1])
    shard_store.start()

    @pl.when(source_chip)
    def _():
        half_core.wait_recv()
        half_core.wait_send()
        half_far.wait_send()

    @pl.when(jnp.logical_not(source_chip))
    def _():
        half_pass.wait_recv()
        half_pass.wait_send()

    half_store = pltpu.make_async_copy(half_all, halves_ref, load_sems.at[2])
    half_store.start()
    for step in range(1, size):
        for side in range(2):
            term_copy(step, side).wait_send()

            @pl.when(here(owner_of(step, side)))
            def _():
                half_copy(step, side).wait_send()

    for copy in [unit_share(at) for at in range(3 * CHUNKS)] + [
        gate_pass(at) for at in range(CHUNKS)
    ]:
        copy.wait_send()
        copy.wait_recv()
    for at in range(chunks):
        unit_pass(at).wait_recv()
        unit_copy(at).wait_send()
        unit_pass(at).wait_send()
    for at in range(total_rounds):
        small_copy(at).wait_send()
    for copy in to_core + [to_far, columns, shard_far, shard_core, shard_pass]:
        copy.wait_send()
    for copy in (to_far_grads, to_core_grads, passed_grads):
        copy.wait_send()
    shard_store.wait()
    half_store.wait()


def attend_group_backward(
    heads,
    attended,
    logs,
    proj,
    weight,
    normed,
    trig,
    hidden,
    resid_grad,
    gain,
    gain_grad,
    resid,
    outs,
    units,
    far_gate,
):
    size = lax.axis_size("fsdp")
    groups = lax.axis_size("seq")
    length = heads.shape[0]
    tokens, width = hidden.shape
    used = heads.shape[1]
    own = attended.shape[1]
    depth = width // size
    rounds = size.bit_length() + 1
    bf16, f32 = jnp.bfloat16, jnp.float32
    anywhere = pl.BlockSpec(memory_space=pl.ANY)
    inside = pl.BlockSpec(memory_space=pltpu.VMEM)
    dma = pltpu.SemaphoreType.DMA
    vmem = pltpu.VMEM
    return pl.pallas_call(
        functools.partial(attend_backward_kernel, size),
        out_shape=(
            jax.ShapeDtypeStruct((tokens, width), f32),
            jax.ShapeDtypeStruct((tokens, width), bf16),
            jax.ShapeDtypeStruct((8, width), f32),
            jax.ShapeDtypeStruct((groups, depth, used), bf16),
            jax.ShapeDtypeStruct((2, depth, width // 2), bf16),
            jax.ShapeDtypeStruct((2,) + units.shape[1:], bf16),
            jax.ShapeDtypeStruct(units.shape, bf16),
            jax.ShapeDtypeStruct(far_gate.shape, bf16),
        ),
        in_specs=[inside] * 11 + [anywhere] * 4,
        out_specs=(inside, inside, inside) + (anywhere,) * 5,
        input_output_aliases={13: 6, 14: 7},
        scratch_shapes=[
            vmem((groups, tokens, width), bf16),
            vmem((length, own), bf16),
            vmem((length, used), bf16),
            vmem((length, HEAD_DIM), f32),
            vmem((length, HEAD_DIM), f32),
            vmem((length, width), bf16),
            vmem((width, used), bf16),
            vmem((own, width), bf16),
            vmem((2 * own, width // 2), bf16),
            vmem((size, depth, used), bf16),
            vmem((size, depth, width // 2), bf16),
            vmem((size, depth, used), bf16),
            vmem((size, depth, width // 2), bf16),
            vmem((depth, used), bf16),
            vmem((groups, depth, used), bf16),
            vmem((depth, width // 2), bf16),
            vmem((2, depth, width // 2), bf16),
            vmem((2, tokens, width), bf16),
            vmem((size, tokens, width), bf16),
            vmem((2, tokens, width), bf16),
            vmem((tokens, width), f32),
            vmem((3, tokens, width), bf16),
            vmem((tokens, width), bf16),
            vmem((2 * rounds + 1, 8, width), f32),
            dma((3,)),
            dma((2, 2)),
            dma((2, 2, size)),
            dma((2, 2, 2, size)),
            dma((2, 1)),
            dma((2, 3)),
            dma((2, 6)),
            dma((2, rounds)),
            dma((2, 2 * CHUNKS)),
            dma((2, 2 * CHUNKS)),
            dma((2, 3 * CHUNKS)),
            dma((2, CHUNKS)),
            dma((2, 3)),
        ],
        compiler_params=pltpu.CompilerParams(
            collective_id=2, has_side_effects=True, vmem_limit_bytes=VMEM_BYTES
        ),
        name="attend_backward",
    )(
        heads,
        attended,
        logs,
        proj,
        weight,
        normed,
        trig,
        hidden,
        resid_grad,
        gain,
        gain_grad,
        resid,
        outs,
        units,
        far_gate,
    )


def finish_kernel(
    sums_ref,
    far_gate_ref,
    far_ref,
    grad_in_ref,
    hidden_ref,
    shards_ref,
    halves_ref,
    gate_out,
    up_out,
    down_out,
    grad_in_out,
    hidden_out,
    qkv_out,
    proj_out,
):
    f32 = jnp.float32
    gate_out[...] = sums_ref[0].astype(f32) + far_gate_ref[...].astype(f32)
    up_out[...] = sums_ref[1].astype(f32) + far_ref[0].astype(f32)
    down_out[...] = sums_ref[2].astype(f32) + far_ref[1].astype(f32)
    grad_in_out[...] = grad_in_ref[...]
    hidden_out[...] = hidden_ref[...]
    groups, _, used = shards_ref.shape
    own = used - 2 * HEAD_DIM
    for at in range(groups):
        qkv_out[:, at * own : (at + 1) * own] = shards_ref[at, :, :own].astype(f32)
    for which in range(2):
        lanes = slice(own + which * HEAD_DIM, own + (which + 1) * HEAD_DIM)
        for head in range(KV_HEADS):
            at = groups * own + (which * KV_HEADS + head) * HEAD_DIM
            qkv_out[:, at : at + HEAD_DIM] = shards_ref[2 * head, :, lanes].astype(
                f32
            ) + shards_ref[2 * head + 1, :, lanes].astype(f32)
    half = halves_ref.shape[2]
    for which in range(2):
        proj_out[:, which * half : (which + 1) * half] = halves_ref[which].astype(f32)


def finish_totals(unit_sums, far_gate, far_sums, grad_in, hidden, shards, halves):
    f32, bf16 = jnp.float32, jnp.bfloat16
    _, units, width = unit_sums.shape
    groups, depth, used = shards.shape
    joint = groups * (used - 2 * HEAD_DIM) + 2 * KV_HEADS * HEAD_DIM
    tokens = grad_in.shape[0]
    steps, few = 10, 8

    def spec(*dims, many=False):
        lead = len(dims) - 2
        return pl.BlockSpec(
            dims,
            lambda at: (0,) * lead + (at if many else jnp.minimum(at, few - 1), 0),
        )

    rows = units // steps
    return pl.pallas_call(
        finish_kernel,
        grid=(steps,),
        out_shape=(
            jax.ShapeDtypeStruct((units, width), f32),
            jax.ShapeDtypeStruct((units, width), f32),
            jax.ShapeDtypeStruct((units, width), f32),
            jax.ShapeDtypeStruct((tokens, width), f32),
            jax.ShapeDtypeStruct((tokens, width), bf16),
            jax.ShapeDtypeStruct((depth, joint), f32),
            jax.ShapeDtypeStruct((depth, width), f32),
        ),
        in_specs=[
            spec(3, rows, width, many=True),
            spec(rows, width, many=True),
            spec(2, rows, width, many=True),
            spec(tokens // few, width),
            spec(tokens // few, width),
            spec(groups, depth // few, used),
            spec(2, depth // few, width // 2),
        ],
        out_specs=(
            spec(rows, width, many=True),
            spec(rows, width, many=True),
            spec(rows, width, many=True),
            spec(tokens // few, width),
            spec(tokens // few, width),
            spec(depth // few, joint),
            spec(depth // few, width),
        ),
        compiler_params=pltpu.CompilerParams(vmem_limit_bytes=VMEM_BYTES),
        name="finish_totals",
    )(unit_sums, far_gate, far_sums, grad_in, hidden, shards, halves)


def kernels_fit(hidden_in, positions, attn_gain, qkv_weight, qkv_bias, out_weight, *rest):
    size, groups = lax.axis_size("fsdp"), lax.axis_size("seq")
    _, tokens, width = hidden_in.shape
    units = rest[1].shape[0]
    if groups != 4 or size != 8 or tokens % 256 or units % 160 or width % 512:
        return False
    if (width // size) % 32 or qkv_bias.shape[0] > 256 or KV_HEADS != 2:
        return False
    rows = tokens * width * (4 * size + 34)
    return rows + units * (18 * width + 6 * tokens) < 64_000_000


def group_columns(array, seq):
    width_query = HEADS * HEAD_DIM
    own = width_query // 4
    kv_head = seq // 2
    parts = (
        (seq * own, own),
        (width_query + kv_head * HEAD_DIM, HEAD_DIM),
        (width_query + (KV_HEADS + kv_head) * HEAD_DIM, HEAD_DIM),
    )
    return jnp.concatenate(
        [lax.dynamic_slice_in_dim(array, at, count, array.ndim - 1) for at, count in parts], -1
    )


def per_device_kernels(
    hidden_in,
    positions,
    attn_gain,
    qkv_weight,
    qkv_bias,
    out_weight,
    mlp_gain,
    gate_weight,
    up_weight,
    down_weight,
    cotangent,
):
    f32, bf16 = jnp.float32, jnp.bfloat16
    groups = lax.axis_size("seq")
    size = lax.axis_size("fsdp")
    seq = lax.axis_index("seq")
    _, tokens, width = hidden_in.shape
    length = tokens * groups
    own = width // groups
    used = own + 2 * HEAD_DIM
    cosine, sine = rope_tables(positions[0])
    half_dim = HEAD_DIM // 2
    trig = jnp.concatenate([cosine[:, :half_dim], sine[:, half_dim:]], axis=1)
    piece = jnp.concatenate(
        [
            group_columns(qkv_weight, seq),
            lax.dynamic_slice_in_dim(out_weight, seq * own, own, 1),
        ],
        axis=1,
    )
    small_width = 256
    small = jnp.stack(
        [
            jnp.pad(row, (0, small_width - row.shape[0]))
            for row in (attn_gain, mlp_gain, qkv_bias)
        ]
    )
    small = jnp.pad(small, ((0, 13), (0, 0)))
    (
        normed_one,
        heads,
        attended,
        logs,
        weight,
        proj,
        trig_all,
        gains,
        normed_two,
        residual,
        all_cots,
    ) = attend_group(hidden_in[0], trig, piece, small, cotangent[0], qkv_bias.shape[0])
    shard = width // size
    outs, grad_residual, term_gain_two, unit_sums, far_gate = mlp_ring(
        normed_two,
        residual,
        gains[1:2],
        all_cots.reshape(size * tokens, width),
        gate_weight,
        up_weight,
        down_weight,
    )
    (
        grad_rows,
        hidden_out,
        smalls,
        shards,
        halves,
        far_sums,
        unit_sums,
        far_gate,
    ) = attend_group_backward(
        heads,
        attended,
        logs,
        proj,
        weight,
        normed_one,
        trig_all.reshape(length, HEAD_DIM),
        hidden_in[0],
        grad_residual,
        gains[0:1],
        term_gain_two,
        residual,
        outs,
        unit_sums,
        far_gate,
    )
    grad_gate, grad_up, grad_down, grad_rows, hidden_out, grad_qkv, grad_out = finish_totals(
        unit_sums, far_gate, far_sums, grad_rows, hidden_out, shards, halves
    )
    me = lax.axis_index("fsdp")
    bias_sums = jnp.concatenate([smalls[2], smalls[3, : 2 * KV_HEADS * HEAD_DIM]])
    bias_shard = qkv_bias.shape[0]
    return (
        hidden_out[None],
        grad_rows[None],
        lax.dynamic_slice_in_dim(smalls[0], me * shard, shard),
        grad_qkv,
        lax.dynamic_slice_in_dim(bias_sums, me * bias_shard, bias_shard),
        grad_out,
        lax.dynamic_slice_in_dim(smalls[1], me * shard, shard),
        grad_gate,
        grad_up,
        grad_down,
    )


def per_device_gathered(
    hidden_in,
    positions,
    attn_gain,
    qkv_weight,
    qkv_bias,
    out_weight,
    mlp_gain,
    gate_weight,
    up_weight,
    down_weight,
    cotangent,
):
    groups = lax.axis_size("seq")
    group_heads = HEADS // groups
    repeat = groups // KV_HEADS
    tokens = hidden_in.shape[1]
    width_query = HEADS * HEAD_DIM
    width_key = KV_HEADS * HEAD_DIM
    residual = hidden_in[0].astype(jnp.float32)
    cosine, sine = rope_tables(positions[0])
    gains_one, gains_two, qkv_full, bias_full, out_full = (
        lax.all_gather(attn_gain, "fsdp", axis=0, tiled=True),
        lax.all_gather(mlp_gain, "fsdp", axis=0, tiled=True),
        lax.all_gather(qkv_weight, "fsdp", axis=0, tiled=True),
        lax.all_gather(qkv_bias, "fsdp", axis=0, tiled=True),
        lax.all_gather(out_weight, "fsdp", axis=0, tiled=True),
    )
    gain_one = gains_one.astype(jnp.float32)
    gain_two = gains_two.astype(jnp.float32)
    unit_one, inverse_one, normed_one = norm_forward(residual, gain_one)
    qkv_mixed = jnp.dot(
        normed_one, qkv_full, preferred_element_type=jnp.float32
    ) + bias_full.astype(jnp.float32)
    query_part = qkv_mixed[:, :width_query].reshape(tokens, HEADS, HEAD_DIM)
    key_part = qkv_mixed[:, width_query : width_query + width_key].reshape(
        tokens, KV_HEADS, HEAD_DIM
    )
    value_part = qkv_mixed[:, width_query + width_key :].reshape(tokens, KV_HEADS, HEAD_DIM)
    queries = (
        rotate(query_part, cosine, sine)
        .astype(jnp.bfloat16)
        .reshape(tokens, groups, group_heads * HEAD_DIM)
    )
    keys_rep = jnp.repeat(rotate(key_part, cosine, sine).astype(jnp.bfloat16), repeat, axis=1)
    values_rep = jnp.repeat(value_part.astype(jnp.bfloat16), repeat, axis=1)
    head_queries, head_keys, head_values = (
        lax.all_to_all(queries, "seq", split_axis=1, concat_axis=0, tiled=True),
        lax.all_to_all(keys_rep, "seq", split_axis=1, concat_axis=0, tiled=True),
        lax.all_to_all(values_rep, "seq", split_axis=1, concat_axis=0, tiled=True),
    )
    head_queries = head_queries.reshape(-1, group_heads, HEAD_DIM)
    head_keys = head_keys.reshape(-1, HEAD_DIM)
    head_values = head_values.reshape(-1, HEAD_DIM)
    attended, log_totals = attend_forward(head_queries, head_keys, head_values)
    returned = lax.all_to_all(
        attended.reshape(-1, 1, group_heads * HEAD_DIM),
        "seq",
        split_axis=0,
        concat_axis=1,
        tiled=True,
    )
    attn_rows = returned.reshape(tokens, width_query)
    residual_two = residual + jnp.dot(attn_rows, out_full, preferred_element_type=jnp.float32)
    unit_two, inverse_two, normed_two = norm_forward(residual_two, gain_two)
    grad_output = cotangent[0].astype(jnp.float32)
    grad_mlp = grad_output.astype(jnp.bfloat16)
    all_rows = lax.all_gather(normed_two, "fsdp", axis=0, tiled=True)
    gate_pre = jnp.einsum("td,fd->tf", all_rows, gate_weight, preferred_element_type=jnp.float32)
    up_pre = jnp.einsum("td,fd->tf", all_rows, up_weight, preferred_element_type=jnp.float32)
    sigmoid_gate = jax.nn.sigmoid(gate_pre)
    activated = gate_pre * sigmoid_gate
    hidden = (activated * up_pre).astype(jnp.bfloat16)
    partial_out = jnp.dot(hidden, down_weight, preferred_element_type=jnp.float32)
    mlp_out = lax.psum_scatter(
        partial_out.astype(jnp.bfloat16), "fsdp", scatter_dimension=0, tiled=True
    ).astype(jnp.float32)
    all_grads = lax.all_gather(grad_mlp, "fsdp", axis=0, tiled=True)
    grad_hidden = jnp.einsum(
        "tm,fm->tf", all_grads, down_weight, preferred_element_type=jnp.float32
    )
    grad_gate = (
        grad_hidden * up_pre * sigmoid_gate * (1.0 + gate_pre * (1.0 - sigmoid_gate))
    ).astype(jnp.bfloat16)
    grad_up = (grad_hidden * activated).astype(jnp.bfloat16)
    partial_back = jnp.dot(grad_gate, gate_weight, preferred_element_type=jnp.float32) + jnp.dot(
        grad_up, up_weight, preferred_element_type=jnp.float32
    )
    grad_normed_two = lax.psum_scatter(partial_back, "fsdp", scatter_dimension=0, tiled=True)
    shard_gate = jnp.einsum("tf,td->fd", grad_gate, all_rows, preferred_element_type=jnp.float32)
    shard_up = jnp.einsum("tf,td->fd", grad_up, all_rows, preferred_element_type=jnp.float32)
    shard_down = jnp.einsum("tf,td->fd", hidden, all_grads, preferred_element_type=jnp.float32)
    hidden_out = (residual_two + mlp_out).astype(jnp.bfloat16)
    grad_norm_two, term_gain_two = norm_backward(grad_normed_two, unit_two, inverse_two, gain_two)
    grad_residual_two = grad_output + grad_norm_two
    grad_proj = grad_residual_two.astype(jnp.bfloat16)
    grad_attn_rows = jnp.einsum(
        "td,ed->te", grad_proj, out_full, preferred_element_type=jnp.float32
    ).astype(jnp.bfloat16)
    term_out = jnp.einsum("te,td->ed", attn_rows, grad_proj, preferred_element_type=jnp.float32)
    grad_heads = lax.all_to_all(
        grad_attn_rows.reshape(tokens, groups, group_heads * HEAD_DIM),
        "seq",
        split_axis=1,
        concat_axis=0,
        tiled=True,
    )
    grad_query, grad_keys, grad_values = attend_backward(
        head_queries,
        head_keys,
        head_values,
        log_totals,
        grad_heads.reshape(-1, group_heads, HEAD_DIM),
    )
    back_query, back_keys, back_values = (
        lax.all_to_all(
            grad_query.astype(jnp.bfloat16).reshape(-1, 1, group_heads * HEAD_DIM),
            "seq",
            split_axis=0,
            concat_axis=1,
            tiled=True,
        ),
        lax.all_to_all(
            grad_keys.astype(jnp.bfloat16)[:, None, :],
            "seq",
            split_axis=0,
            concat_axis=1,
            tiled=True,
        ),
        lax.all_to_all(
            grad_values.astype(jnp.bfloat16)[:, None, :],
            "seq",
            split_axis=0,
            concat_axis=1,
            tiled=True,
        ),
    )
    grad_query_rows = unrotate(
        back_query.reshape(tokens, HEADS, HEAD_DIM).astype(jnp.float32), cosine, sine
    )
    grad_key_rows = unrotate(
        jnp.sum(back_keys.astype(jnp.float32).reshape(tokens, KV_HEADS, repeat, HEAD_DIM), axis=2),
        cosine,
        sine,
    )
    grad_value_rows = jnp.sum(
        back_values.astype(jnp.float32).reshape(tokens, KV_HEADS, repeat, HEAD_DIM), axis=2
    )
    grad_mixed = jnp.concatenate(
        [
            grad_query_rows.reshape(tokens, width_query),
            grad_key_rows.reshape(tokens, width_key),
            grad_value_rows.reshape(tokens, width_key),
        ],
        axis=1,
    ).astype(jnp.bfloat16)
    term_qkv = jnp.einsum("td,tc->dc", normed_one, grad_mixed, preferred_element_type=jnp.float32)
    term_bias = jnp.sum(grad_mixed.astype(jnp.float32), axis=0)
    grad_normed_one = jnp.einsum(
        "tc,dc->td", grad_mixed, qkv_full, preferred_element_type=jnp.float32
    )
    grad_norm_one, term_gain_one = norm_backward(grad_normed_one, unit_one, inverse_one, gain_one)
    grad_rows = grad_residual_two + grad_norm_one
    shard_gain_one, shard_qkv, shard_bias, shard_out, shard_gain_two = (
        lax.psum_scatter(
            term_gain_one.astype(jnp.bfloat16), "fsdp", scatter_dimension=0, tiled=True
        ).astype(jnp.float32),
        lax.psum_scatter(
            term_qkv.astype(jnp.bfloat16), "fsdp", scatter_dimension=0, tiled=True
        ).astype(jnp.float32),
        lax.psum_scatter(
            term_bias.astype(jnp.bfloat16), "fsdp", scatter_dimension=0, tiled=True
        ).astype(jnp.float32),
        lax.psum_scatter(
            term_out.astype(jnp.bfloat16), "fsdp", scatter_dimension=0, tiled=True
        ).astype(jnp.float32),
        lax.psum_scatter(
            term_gain_two.astype(jnp.bfloat16), "fsdp", scatter_dimension=0, tiled=True
        ).astype(jnp.float32),
    )
    totals = (
        lax.psum(shard_gain_one.astype(jnp.bfloat16), "seq").astype(jnp.float32),
        lax.psum(shard_qkv.astype(jnp.bfloat16), "seq").astype(jnp.float32),
        lax.psum(shard_bias.astype(jnp.bfloat16), "seq").astype(jnp.float32),
        lax.psum(shard_out.astype(jnp.bfloat16), "seq").astype(jnp.float32),
        lax.psum(shard_gain_two.astype(jnp.bfloat16), "seq").astype(jnp.float32),
        lax.psum(shard_gate.astype(jnp.bfloat16), "seq").astype(jnp.float32),
        lax.psum(shard_up.astype(jnp.bfloat16), "seq").astype(jnp.float32),
        lax.psum(shard_down.astype(jnp.bfloat16), "seq").astype(jnp.float32),
    )
    return (
        hidden_out[None],
        grad_rows[None],
        totals[0],
        totals[1],
        totals[2],
        totals[3],
        totals[4],
        totals[5],
        totals[6],
        totals[7],
    )


def per_device(*arguments):
    return (per_device_kernels if kernels_fit(*arguments) else per_device_gathered)(*arguments)


def solution(mesh):
    placed = (
        P("fsdp", "seq", None),
        P("fsdp", "seq"),
        P("fsdp"),
        P("fsdp", None),
        P("fsdp"),
        P("fsdp", None),
        P("fsdp"),
        P("fsdp", None),
        P("fsdp", None),
        P("fsdp", None),
        P("fsdp", "seq", None),
    )
    return jax.shard_map(
        per_device,
        mesh=mesh,
        in_specs=placed,
        out_specs=(
            P("fsdp", "seq", None),
            P("fsdp", "seq", None),
            P("fsdp"),
            P("fsdp", None),
            P("fsdp"),
            P("fsdp", None),
            P("fsdp"),
            P("fsdp", None),
            P("fsdp", None),
            P("fsdp", None),
        ),
        check_vma=False,
    )
```

```python
import functools
import math

import jax
import jax.numpy as jnp
from jax import lax
from jax.experimental import pallas as pl
from jax.experimental.pallas import tpu as pltpu
from jax.sharding import PartitionSpec as P

HEADS = 12
KV_HEADS = 2
HEAD_DIM = 128


norm_eps = 1e-06
rope_base = 1000000.0


def rope_tables(position_row):
    half_dim = HEAD_DIM // 2
    frequency = jnp.exp(
        -(jnp.arange(half_dim, dtype=jnp.float32) * 2.0 / HEAD_DIM) * math.log(rope_base)
    )
    angles = position_row.astype(jnp.float32)[:, None] * frequency[None, :]
    angles = jnp.concatenate([angles, angles], axis=-1)
    return (jnp.cos(angles), jnp.sin(angles))


def rotate(values, cosine, sine):
    half_dim = values.shape[-1] // 2
    turned = jnp.concatenate([-values[..., half_dim:], values[..., :half_dim]], axis=-1)
    return values * cosine[:, None, :] + turned * sine[:, None, :]


def unrotate(grads_rot, cosine, sine):
    half_dim = grads_rot.shape[-1] // 2
    scaled = grads_rot * sine[:, None, :]
    return grads_rot * cosine[:, None, :] + jnp.concatenate(
        [scaled[..., half_dim:], -scaled[..., :half_dim]], axis=-1
    )


def norm_forward(values, gain):
    inverse = lax.rsqrt(jnp.mean(values * values, axis=-1, keepdims=True) + norm_eps)
    unit_rows = values * inverse
    return (unit_rows, inverse, (unit_rows * gain).astype(jnp.bfloat16))


def norm_backward(grad_normed, unit_rows, inverse, gain):
    grad_unit = grad_normed * gain
    grad_values = inverse * (
        grad_unit - unit_rows * jnp.mean(grad_unit * unit_rows, axis=-1, keepdims=True)
    )
    grad_gain = jnp.sum(grad_normed * unit_rows, axis=0)
    return (grad_values, grad_gain)


def masked_scores(queries, keys, block_start, block_rows):
    length = keys.shape[0]
    query_block = lax.dynamic_slice_in_dim(queries, block_start, block_rows, 0)
    scores = jnp.einsum(
        "bhd,ld->hbl", query_block, keys, preferred_element_type=jnp.float32
    ) * HEAD_DIM ** (-0.5)
    row_index = block_start + jnp.arange(block_rows)
    column_index = jnp.arange(length)
    allowed = column_index[None, :] <= row_index[:, None]
    return (query_block, jnp.where(allowed[None], scores, -1e30))


def attend_forward(queries, keys, values):
    length = keys.shape[0]
    block_rows = min(512, length)
    block_count = length // block_rows

    def one_block(block_start):
        query_block, scores = masked_scores(queries, keys, block_start, block_rows)
        row_max = jnp.max(scores, axis=-1, keepdims=True)
        exponent = jnp.exp(scores - row_max)
        row_total = jnp.sum(exponent, axis=-1, keepdims=True)
        probability = (exponent / row_total).astype(jnp.bfloat16)
        result = jnp.einsum("hbl,ld->bhd", probability, values, preferred_element_type=jnp.float32)
        return (result.astype(jnp.bfloat16), (row_max + jnp.log(row_total))[..., 0])

    results, log_totals = lax.map(one_block, jnp.arange(block_count) * block_rows)
    return (results.reshape(length, queries.shape[1], queries.shape[2]), log_totals)


def attend_backward(queries, keys, values, log_totals, grad_out):
    length = keys.shape[0]
    block_rows = min(512, length)
    block_count = length // block_rows
    score_scale = HEAD_DIM ** (-0.5)

    def one_block(running, inputs):
        grad_keys, grad_values = running
        block_start, log_block = inputs
        query_block, scores = masked_scores(queries, keys, block_start, block_rows)
        grad_block = lax.dynamic_slice_in_dim(grad_out, block_start, block_rows, 0)
        probability = jnp.exp(scores - log_block[..., None])
        grad_probs = jnp.einsum(
            "bhd,ld->hbl", grad_block, values, preferred_element_type=jnp.float32
        )
        row_delta = jnp.sum(probability * grad_probs, axis=-1, keepdims=True)
        grad_scores = (probability * (grad_probs - row_delta)).astype(jnp.bfloat16)
        grad_query = (
            jnp.einsum("hbl,ld->bhd", grad_scores, keys, preferred_element_type=jnp.float32)
            * score_scale
        )
        grad_keys = (
            grad_keys
            + jnp.einsum(
                "hbl,bhd->ld", grad_scores, query_block, preferred_element_type=jnp.float32
            )
            * score_scale
        )
        grad_values = grad_values + jnp.einsum(
            "hbl,bhd->ld",
            probability.astype(jnp.bfloat16),
            grad_block,
            preferred_element_type=jnp.float32,
        )
        return ((grad_keys, grad_values), grad_query)

    zero_rows = jnp.zeros((length, keys.shape[1]), jnp.float32)
    (grad_keys, grad_values), grad_query = lax.scan(
        one_block, (zero_rows, zero_rows), (jnp.arange(block_count) * block_rows, log_totals)
    )
    return (grad_query.reshape(queries.shape), grad_keys, grad_values)


MESH = pl.DeviceIdType.MESH
VMEM_BYTES = 67_000_000
NN = (((1,), (0,)), ((), ()))
NT = (((1,), (1,)), ((), ()))
TN = (((0,), (0,)), ((), ()))


def matmul(left, right, dims):
    return lax.dot_general(left, right, dims, preferred_element_type=jnp.float32)


def ring_place(index, size):
    side = index % 2
    return (index // 2) * (1 - side) + (size - 1 - index // 2) * side


def ring_member(place, size):
    side = place // (size // 2)
    return 2 * (place * (1 - side) + (size - 1 - place) * side) + side


def seq_partners(seq):
    core = seq + 1 - 2 * (seq % 2)
    far = (seq + 2) % 4
    return core, far, (core + 2) % 4


def greet(targets):
    barrier = pltpu.get_barrier_semaphore()
    for target in targets:
        pl.semaphore_signal(barrier, inc=1, device_id=target, device_id_type=MESH)
    pl.semaphore_wait(barrier, len(targets))


def for_blocks(width, block, body):
    for at in range(0, width, block):
        body(pl.ds(at, min(block, width - at)))


def loop_blocks(width, block, body):
    @pl.loop(0, width // block)
    def _(at):
        body(pl.ds(pl.multiple_of(at * block, block), block))


def turn_tables(trig):
    lane = lax.broadcasted_iota(jnp.int32, trig.shape, 1)
    swapped = pltpu.roll(trig, HEAD_DIM // 2, 1)
    first = lane < HEAD_DIM // 2
    return jnp.where(first, trig, swapped), jnp.where(first, -swapped, trig)


def head_columns(at):
    return slice(at * HEAD_DIM, (at + 1) * HEAD_DIM)


def causal(scores, start):
    rows = lax.broadcasted_iota(jnp.int32, scores.shape, 0) + start
    columns = lax.broadcasted_iota(jnp.int32, scores.shape, 1)
    return jnp.where(columns <= rows, scores, -1e30)


def inverse_of(values):
    return lax.rsqrt(jnp.mean(values * values, axis=-1, keepdims=True) + norm_eps)


def attend_forward_kernel(
    size,
    block,
    bias_share,
    rows_ref,
    trig_ref,
    qkv_ref,
    proj_ref,
    small_ref,
    cot_ref,
    normed_out,
    heads_out,
    attended_out,
    log_out,
    piece_out,
    proj_out,
    trig_out,
    gains_out,
    normed_two_out,
    resid_out,
    cots_out,
    rows_all,
    trig_all,
    pieces,
    proj,
    smalls,
    cots,
    normed,
    heads,
    attended,
    logs,
    part,
    gains,
    bias,
    resid,
    seq_in,
    far_sum,
    normed_two,
    load_sems,
    column_sems,
    store_sems,
    ring_sems,
    small_sems,
    cot_sems,
    cot_store_sems,
    seq_sems,
    sum_sems,
    proj_send,
    proj_recv,
):
    f32, bf16 = jnp.float32, jnp.bfloat16
    depth = qkv_ref.shape[0]
    tokens, width = rows_ref.shape
    half = depth // 2
    cot_half = tokens // 2
    own = proj.shape[0]
    used = own + 2 * HEAD_DIM
    count = own // HEAD_DIM
    length = part.shape[0]
    per_group = own // depth
    scale = HEAD_DIM**-0.5
    me = lax.axis_index("fsdp")
    seq = lax.axis_index("seq")
    place = ring_place(me, size)
    right = ring_member((place + 1) % size, size)
    left = ring_member((place + size - 1) % size, size)
    core, far, diagonal = seq_partners(seq)
    ring = ({"fsdp": right}, {"fsdp": left})

    def remote(source, target, sems, at, device):
        return pltpu.make_async_remote_copy(
            src_ref=source,
            dst_ref=target,
            send_sem=sems.at[(0,) + at],
            recv_sem=sems.at[(1,) + at],
            device_id=device,
            device_id_type=MESH,
        )

    width_query = 4 * own
    own_lane = pl.multiple_of(seq * own, HEAD_DIM)
    kv_lane = pl.multiple_of(width_query + (seq // 2) * HEAD_DIM, HEAD_DIM)
    value_lane = pl.multiple_of(kv_lane + KV_HEADS * HEAD_DIM, HEAD_DIM)
    my_rows = pl.ds(pl.multiple_of(me * depth, 16), depth)
    column_loads = [
        pltpu.make_async_copy(
            source.at[:, pl.ds(lane_at, lanes)],
            pieces.at[my_rows, pl.ds(target, lanes)],
            column_sems.at[at],
        )
        for at, (source, lane_at, target, lanes) in enumerate(
            (
                (qkv_ref, own_lane, 0, own),
                (qkv_ref, kv_lane, own, HEAD_DIM),
                (qkv_ref, value_lane, own + HEAD_DIM, HEAD_DIM),
                (proj_ref, own_lane, used, own),
            )
        )
    ]
    loads = [
        pltpu.make_async_copy(trig_ref, trig_all.at[seq], load_sems.at[0]),
        pltpu.make_async_copy(rows_ref, rows_all.at[seq], load_sems.at[1]),
        pltpu.make_async_copy(cot_ref, cots.at[me], load_sems.at[2]),
    ]
    for load in column_loads + loads:
        load.start()
    smalls[me] = jnp.zeros(smalls.shape[1:], f32)
    for at in range(3):
        smalls[me, at : at + 1, :] = small_ref[:, at * 256 : (at + 1) * 256]
    greet(ring + ({"seq": core}, {"seq": far}, {"seq": diagonal}))

    def piece_of(step, side):
        return ring_member((place + size - step if side == 0 else place + step) % size, size)

    def ring_copy(step, side, sub):
        part_rows = half // 2
        start = piece_of(step, side) * depth + side * half + sub * part_rows
        span = pieces.at[pl.ds(pl.multiple_of(start, 16), part_rows)]
        return remote(span, span, ring_sems, (side, sub, step), ring[side])

    def small_copy(step):
        span = smalls.at[piece_of(step, 0)]
        return remote(span, span, small_sems, (step,), ring[0])

    def cot_copy(step, side, sub):
        part_rows = cot_half // 2
        start = side * cot_half + sub * part_rows
        span = cots.at[piece_of(step, side), pl.ds(start, part_rows)]
        return remote(span, span, cot_sems, (side, sub, step), ring[side])

    def cot_store(step, side):
        span = (piece_of(step, side), pl.ds(side * cot_half, cot_half))
        return pltpu.make_async_copy(
            cots.at[span], cots_out.at[span], cot_store_sems.at[side, step]
        )

    def seq_copy(which, block_at, target, at):
        span = (rows_all, trig_all)[which].at[block_at]
        return remote(span, span, seq_sems, (which, at), {"seq": target})

    def proj_part(step, side):
        at = piece_of(step, side)
        row = pl.multiple_of((at % per_group) * depth + side * half, 16)
        source = pieces.at[
            pl.ds(pl.multiple_of(at * depth + side * half, 16), half), pl.ds(used, own)
        ]
        target = proj.at[pl.ds(row, half), pl.ds(pl.multiple_of(seq * own, 128), own)]
        return at, at // per_group, source, target

    def proj_copy(step, side):
        at, owner, source, target = proj_part(step, side)
        return owner, pltpu.make_async_remote_copy(
            src_ref=source,
            dst_ref=target,
            send_sem=proj_send.at[side, step],
            recv_sem=proj_recv.at[seq, at % per_group, side],
            device_id={"seq": owner},
            device_id_type=MESH,
        )

    def proj_act(step, side, action):
        owner, copy = proj_copy(step, side)

        @pl.when(owner != seq)
        def _():
            if action == "start":
                copy.start()
            else:
                copy.wait_send()

        @pl.when(owner == seq)
        def _():
            _, _, source, target = proj_part(step, side)
            kept = pltpu.make_async_copy(source, target, proj_send.at[side, step])
            if action == "start":
                kept.start()
            else:
                kept.wait()

    stores = []

    def store(source, target):
        stores.append(pltpu.make_async_copy(source, target, store_sems.at[len(stores)]))
        stores[-1].start()

    def cot_pump(step):
        for sub in range(2):
            for side in range(2):
                if step >= 1:
                    cot_copy(step - 1, side, sub).wait_recv()
                if step < size - 1:
                    cot_copy(step, side, sub).start()
        for side in range(2):
            cot_store(step, side).start()

    for load in column_loads:
        load.wait()
    for sub in range(2):
        for side in range(2):
            ring_copy(0, side, sub).start()
    small_copy(0).start()
    for which in (1, 0):
        loads[1 - which].wait()
        seq_copy(which, seq, far, 1).start()
        seq_copy(which, seq, core, 0).start()
    for side in range(2):
        proj_act(0, side, "start")
    loads[2].wait()

    for step in range(size - 1):
        for sub in range(2):
            for side in range(2):
                ring_copy(step, side, sub).wait_recv()
                if step < size - 2:
                    ring_copy(step + 1, side, sub).start()
        small_copy(step).wait_recv()
        if step < size - 2:
            small_copy(step + 1).start()
        if step == size - 3:
            cot_pump(0)
        for side in range(2):
            proj_act(step + 1, side, "start")
        if step == min(1, size - 2):
            for which in (1, 0):
                seq_copy(which, seq, far, 1).wait_recv()
                seq_copy(which, far, core, 2).start()

    gathered = jnp.zeros((8, width), f32)
    small_width = smalls.shape[2]
    for at in range(size):
        held = smalls[at]
        lane = lax.broadcasted_iota(jnp.int32, held.shape, 1)
        wide = jnp.concatenate(
            [
                jnp.where(lane < depth, held, 0.0),
                jnp.zeros((8, width - small_width), f32),
            ],
            axis=1,
        )
        gathered += pltpu.roll(wide, at * depth, 1) if at else wide
        bias[:, at * bias_share : (at + 1) * bias_share] = held[:, :bias_share]
    gains[...] = gathered
    gain_one = gathered[0:1, :]
    gain_two = gathered[1:2, :]
    store(gains, gains_out)
    for which in (1, 0):
        seq_copy(which, seq, core, 0).wait_recv()
        seq_copy(which, far, core, 2).wait_recv()
    store(pieces, piece_out)
    store(trig_all, trig_out)

    own_bias = jnp.concatenate(
        [
            bias[2:3, pl.ds(own_lane, own)],
            bias[2:3, pl.ds(kv_lane, HEAD_DIM)],
            bias[2:3, pl.ds(value_lane, HEAD_DIM)],
        ],
        axis=1,
    )
    for at in range(length // block):
        span = slice(at * block, (at + 1) * block)
        rows = rows_all[at].astype(f32)
        normed[span, :] = (rows * inverse_of(rows) * gain_one).astype(bf16)
        mixed = matmul(normed[span, :], pieces[:, :used], NN) + own_bias
        cosine, sine = turn_tables(trig_all[at])
        for head in range(count + 1):
            turned = mixed[:, head_columns(head)]
            heads[span, head_columns(head)] = (
                turned * cosine + pltpu.roll(turned, HEAD_DIM // 2, 1) * sine
            ).astype(bf16)
        heads[span, head_columns(count + 1)] = mixed[:, head_columns(count + 1)].astype(bf16)
        if 2 * (at + 1) == length // block:
            cot_pump(1)
    store(normed, normed_out)
    store(heads, heads_out)

    for peer in (core, far, diagonal):
        for at in range(per_group):
            for side in range(2):
                pltpu.make_async_remote_copy(
                    src_ref=pieces.at[pl.ds(0, half), pl.ds(used, own)],
                    dst_ref=proj.at[pl.ds(0, half), pl.ds(0, own)],
                    send_sem=proj_send.at[side, 0],
                    recv_sem=proj_recv.at[peer, at, side],
                    device_id={"seq": peer},
                    device_id_type=MESH,
                ).wait_recv()
    for step in range(size):
        for side in range(2):
            proj_act(step, side, "wait")
    store(proj, proj_out)

    lane = lax.broadcasted_iota(jnp.int32, (block, HEAD_DIM), 1)
    for start in range(0, length, block):
        span = slice(start, start + block)
        seen = slice(0, start + block)
        logs[span, :] = jnp.zeros((block, HEAD_DIM), f32)

        @pl.loop(0, count)
        def _(at):
            head = pl.ds(pl.multiple_of(at * HEAD_DIM, HEAD_DIM), HEAD_DIM)
            scores = causal(
                matmul(heads[span, head], heads[seen, head_columns(count)], NT) * scale, start
            )
            top = jnp.max(scores, axis=-1, keepdims=True)
            exponent = jnp.exp(scores - top)
            total = jnp.sum(exponent, axis=-1, keepdims=True)
            probability = (exponent / total).astype(bf16)
            attended[span, head] = matmul(
                probability, heads[seen, head_columns(count + 1)], NN
            ).astype(bf16)
            logs[span, :] = jnp.where(lane == at, top + jnp.log(total), logs[span, :])

        if 2 * (start + block) == length:
            cot_pump(2)
    store(attended, attended_out)
    store(logs, log_out)

    def out_part(span):
        part[:, span] = matmul(attended[...], proj[:, span], NN).astype(bf16)

    for_blocks(width, 512, out_part)

    def part_rows(at):
        return part.at[pl.ds(pl.multiple_of(at * tokens, tokens), tokens)]

    to_core = [
        remote(part_rows(diagonal), seq_in.at[0], sum_sems, (0,), {"seq": core}),
        remote(part_rows(core), seq_in.at[1], sum_sems, (1,), {"seq": core}),
    ]
    to_far = remote(far_sum, seq_in.at[2], sum_sems, (2,), {"seq": far})
    for copy in to_core:
        copy.start()
    cot_pump(3)
    to_core[0].wait_recv()
    far_sum[...] = (part_rows(far)[...].astype(f32) + seq_in[0].astype(f32)).astype(bf16)
    to_far.start()
    to_core[1].wait_recv()
    resid[...] = (
        part_rows(seq)[...].astype(f32) + seq_in[1].astype(f32) + rows_all[seq].astype(f32)
    )
    cot_pump(4)
    cot_pump(5)
    to_far.wait_recv()
    resid[...] += seq_in[2].astype(f32)
    store(resid, resid_out)
    normed_two[...] = (resid[...] * inverse_of(resid[...]) * gain_two).astype(bf16)
    store(normed_two, normed_two_out)
    for step in range(6, size):
        cot_pump(step)
    for step in range(size):
        for side in range(2):
            cot_store(step, side).wait()

    for step in range(size - 1):
        for side in range(2):
            for sub in range(2):
                ring_copy(step, side, sub).wait_send()
                cot_copy(step, side, sub).wait_send()
        small_copy(step).wait_send()
    for which in (1, 0):
        seq_copy(which, seq, core, 0).wait_send()
        seq_copy(which, seq, far, 1).wait_send()
        seq_copy(which, far, core, 2).wait_send()
    for copy in to_core + [to_far]:
        copy.wait_send()
    for copy in stores:
        copy.wait()


def attend_group(rows, trig, qkv_weight, out_weight, small, bias_share, cots):
    size = lax.axis_size("fsdp")
    groups = lax.axis_size("seq")
    tokens, width = rows.shape
    depth = qkv_weight.shape[0]
    own = width // groups
    used = own + 2 * HEAD_DIM
    joint = used + own
    length = tokens * groups
    f32, bf16 = jnp.float32, jnp.bfloat16
    dma = pltpu.SemaphoreType.DMA
    anywhere = pl.BlockSpec(memory_space=pl.ANY)
    normed = ((length, width), bf16)
    heads = ((length, used), bf16)
    attended = ((length, own), bf16)
    logs = ((length, HEAD_DIM), f32)
    pieces = ((width, joint), bf16)
    proj = ((own, width), bf16)
    trig_all = ((groups,) + trig.shape, f32)
    gains = ((8, width), f32)
    rows_all = ((groups, tokens, width), bf16)
    own_rows = ((tokens, width), bf16)
    resid = ((tokens, width), f32)
    cots_all = ((size, tokens, width), bf16)
    outs = (
        normed, heads, attended, logs, pieces, proj, trig_all, gains, own_rows, resid, cots_all
    )
    held = (
        rows_all,
        trig_all,
        pieces,
        proj,
        ((size, 8, 256), f32),
        cots_all,
        normed,
        heads,
        attended,
        logs,
        normed,
        gains,
        ((8, size * bias_share), f32),
        resid,
        ((3, tokens, width), bf16),
        own_rows,
        own_rows,
    )
    return pl.pallas_call(
        functools.partial(attend_forward_kernel, size, tokens, bias_share),
        out_shape=tuple(jax.ShapeDtypeStruct(*shape) for shape in outs),
        in_specs=[anywhere] * 4 + [pl.BlockSpec(memory_space=pltpu.VMEM), anywhere],
        out_specs=(anywhere,) * len(outs),
        scratch_shapes=[pltpu.VMEM(*shape) for shape in held]
        + [
            dma((3,)),
            dma((4,)),
            dma((len(outs),)),
            dma((2, 2, 2, size)),
            dma((2, size)),
            dma((2, 2, 2, size)),
            dma((2, size)),
            dma((2, 2, 3)),
            dma((2, 3)),
            dma((2, size)),
            dma((groups, own // depth, 2)),
        ],
        compiler_params=pltpu.CompilerParams(
            collective_id=1, has_side_effects=True, vmem_limit_bytes=VMEM_BYTES
        ),
        name="attend_forward",
    )(
        rows,
        trig,
        qkv_weight,
        out_weight,
        small,
        cots,
    )


CHUNKS = 5
IN_LOOP = ((2, 1), (4, 2), (6, 3))


def mlp_kernel(
    size,
    normed_ref,
    resid_ref,
    gain_ref,
    cots_ref,
    gate_ref,
    up_ref,
    down_ref,
    outs_ref,
    back_ref,
    gain_grad_ref,
    sums_ref,
    far_ref,
    rows_all,
    cots,
    weights,
    grads,
    hid,
    dgate,
    dup,
    resid,
    sums_in,
    backs,
    outs,
    load_sems,
    cot_sems,
    ring_send,
    ring_recv,
    sum_send,
    sum_recv,
    out_sems,
    swap_sems,
    far_sems,
    swap_ready,
):
    tokens, width = normed_ref.shape
    units = gate_ref.shape[0]
    half = tokens // 2
    me = lax.axis_index("fsdp")
    seq = lax.axis_index("seq")
    place = ring_place(me, size)
    right = ring_member((place + 1) % size, size)
    left = ring_member((place + size - 1) % size, size)
    core, far, diagonal = seq_partners(seq)
    sides = ((right, pl.ds(0, half)), (left, pl.ds(half, half)))

    def owner_of(step, side):
        return ring_member((place + size - step if side == 0 else place + step) % size, size)

    own_load = pltpu.make_async_copy(normed_ref, rows_all.at[0], load_sems.at[3])
    resid_load = pltpu.make_async_copy(resid_ref, resid, load_sems.at[4])
    weight_loads = [
        pltpu.make_async_copy(ref, weights.at[at], load_sems.at[at])
        for at, ref in enumerate((gate_ref, up_ref, down_ref))
    ]
    own_load.start()
    greet(({"fsdp": right}, {"fsdp": left}, {"seq": core}, {"seq": far}))

    def cot_copies(step):
        return [
            pltpu.make_async_copy(
                cots_ref.at[
                    pl.ds(
                        pl.multiple_of(owner_of(step, side) * tokens + side * half, half), half
                    )
                ],
                cots.at[step % 2, sides[side][1]],
                cot_sems.at[step % 2, side],
            )
            for side in range(2)
        ]


    def row_copy(step, side):
        target, span = sides[side]
        return pltpu.make_async_remote_copy(
            src_ref=rows_all.at[step, span],
            dst_ref=rows_all.at[step + 1, span],
            send_sem=ring_send.at[side, step],
            recv_sem=ring_recv.at[side, step + 1],
            device_id={"fsdp": target},
            device_id_type=MESH,
        )

    def sum_span(side, sub):
        return pl.ds(side * half + sub * (half // 2), half // 2)

    def sum_copy(step, side, sub):
        target, span = sides[side][0], sum_span(side, sub)
        return pltpu.make_async_remote_copy(
            src_ref=backs.at[step, span],
            dst_ref=sums_in.at[step, span],
            send_sem=sum_send.at[side, sub, step],
            recv_sem=sum_recv.at[side, sub, step],
            device_id={"fsdp": target},
            device_id_type=MESH,
        )

    def sum_step(step):
        for sub in range(2):
            for side in range(2):
                span = sum_span(side, sub)
                if step >= 2:
                    sum_copy(step - 1, side, sub).wait_recv()
                    backs[step, span] = (
                        backs[step, span].astype(jnp.float32)
                        + sums_in[step - 1, span].astype(jnp.float32)
                    ).astype(jnp.bfloat16)
                sum_copy(step, side, sub).start()

    def out_copy(step, side):
        at = pl.multiple_of(owner_of(step, side) * tokens + side * half, half)
        return pltpu.make_async_copy(
            outs.at[step % 2, sides[side][1]], outs_ref.at[pl.ds(at, half)], out_sems.at[side, step]
        )

    def elementwise(step, span):
        rows = rows_all[step]
        gate = matmul(rows, weights[0, span, :], NT)
        up = matmul(rows, weights[1, span, :], NT)
        grad_hidden = matmul(cots[step % 2], weights[2, span, :], NT)
        sigmoid = jax.nn.sigmoid(gate)
        activated = gate * sigmoid
        hid[:, span] = (activated * up).astype(jnp.bfloat16)
        dgate[:, span] = (
            grad_hidden * up * sigmoid * (1.0 + gate * (1.0 - sigmoid))
        ).astype(jnp.bfloat16)
        dup[:, span] = (grad_hidden * activated).astype(jnp.bfloat16)

    own_load.wait()
    for side in range(2):
        row_copy(0, side).start()
    for load in weight_loads + cot_copies(0) + [resid_load]:
        load.start()

    @pl.loop(0, units // 16)
    def _(at):
        zeros = jnp.zeros((3, 16, width), jnp.float32)
        grads[:, pl.ds(pl.multiple_of(at * 16, 16), 16), :] = zeros

    for load in weight_loads:
        load.wait()

    @pl.loop(0, size)
    def _(step):
        slot = step % 2

        @pl.when(step >= 1)
        def _():
            for side in range(2):
                row_copy(step - 1, side).wait_recv()

        @pl.when((step >= 1) & (step < size - 1))
        def _():
            for side in range(2):
                row_copy(step, side).start()

        for load in cot_copies(step):
            load.wait()

        @pl.when(step < size - 1)
        def _():
            for load in cot_copies(step + 1):
                load.start()

        for_blocks(units, 256, functools.partial(elementwise, step))

        def back_part(span):
            backs[step, :, span] = (
                matmul(dgate[...], weights[0, :, span], NN)
                + matmul(dup[...], weights[1, :, span], NN)
            ).astype(jnp.bfloat16)

        for_blocks(width, 256, back_part)

        for when, at in IN_LOOP:

            @pl.when(step == when)
            def _():
                sum_step(at)

        @pl.when(step >= 2)
        def _():
            for side in range(2):
                out_copy(step - 2, side).wait()

        def out_part(span):
            outs[slot, :, span] = matmul(hid[...], weights[2, :, span], NN).astype(jnp.bfloat16)

        for_blocks(width, 256, out_part)
        for side in range(2):
            out_copy(step, side).start()

        def weight_part(span):
            rows, cot = rows_all[step, :, span], cots[slot, :, span]
            grads[0, :, span] += matmul(dgate[...], rows, TN)
            grads[1, :, span] += matmul(dup[...], rows, TN)
            grads[2, :, span] += matmul(hid[...], cot, TN)

        for_blocks(width, 256, weight_part)

    share = units // 2
    kept = pl.multiple_of((seq % 2) * share, 16)
    given = pl.multiple_of((1 - seq % 2) * share, 16)
    chunk = share // CHUNKS
    pl.semaphore_signal(swap_ready, inc=1, device_id={"seq": core}, device_id_type=MESH)

    def to_seq(source, target, sems, at, device):
        return pltpu.make_async_remote_copy(
            src_ref=source,
            dst_ref=target,
            send_sem=sems.at[0, at],
            recv_sem=sems.at[1, at],
            device_id={"seq": device},
            device_id_type=MESH,
        )

    swaps = [
        to_seq(
            weights.at[at, pl.ds(given, share)],
            weights.at[at, pl.ds(given, share)],
            swap_sems,
            at,
            core,
        )
        for at in range(3)
    ]
    waiting = [at for at in range(1, size) if at not in [pair[1] for pair in IN_LOOP]]
    sum_step(waiting[0])
    for at in range(3):

        @pl.loop(0, share // 16)
        def _(block):
            span = pl.ds(pl.multiple_of(given + block * 16, 16), 16)
            weights[at, span, :] = grads[at, span, :].astype(jnp.bfloat16)

        if at == 0:
            pl.semaphore_wait(swap_ready, 1)
        swaps[at].start()

    stores = []

    def kept_rows(at):
        return pl.ds(pl.multiple_of(kept + at * chunk, 16), chunk)

    far_copies = [
        to_seq(weights.at[0, kept_rows(at)], far_ref.at[kept_rows(at)], far_sems, at, far)
        for at in range(CHUNKS)
    ]
    def swap_finish(at):
        swaps[at].wait_recv()

        @pl.loop(0, share // 16)
        def _(block):
            span = pl.ds(pl.multiple_of(kept + block * 16, 16), 16)
            weights[at, span, :] = (
                grads[at, span, :] + weights[at, span, :].astype(jnp.float32)
            ).astype(jnp.bfloat16)

        done = weights.at[at, pl.ds(kept, share)]
        stores.append(
            pltpu.make_async_copy(done, sums_ref.at[at, pl.ds(kept, share)], load_sems.at[at])
        )
        if at == 0:
            for copy in far_copies:
                copy.start()
        stores[-1].start()

    cot_own = pltpu.make_async_copy(
        cots_ref.at[pl.ds(pl.multiple_of(me * tokens, tokens), tokens)],
        cots.at[0],
        load_sems.at[7],
    )
    cot_own.start()
    for turn, at in enumerate(waiting[1:]):
        sum_step(at)
        if turn < 3:
            swap_finish(turn)
    for turn in range(len(waiting) - 1, 3):
        swap_finish(turn)

    for side in range(2):
        for sub in range(2):
            sum_copy(size - 1, side, sub).wait_recv()
    grad_normed = backs[0].astype(jnp.float32) + sums_in[size - 1].astype(jnp.float32)
    resid_load.wait()
    inverse = inverse_of(resid[...])
    unit_rows = resid[...] * inverse
    gain_grad_ref[...] = jnp.sum(grad_normed * unit_rows, axis=0, keepdims=True)
    grad_unit = grad_normed * gain_ref[1:2, :]
    cot_own.wait()
    back_ref[...] = cots[0].astype(jnp.float32) + inverse * (
        grad_unit - unit_rows * jnp.mean(grad_unit * unit_rows, axis=-1, keepdims=True)
    )
    for side in range(2):
        out_copy(size - 2, side).wait()
        out_copy(size - 1, side).wait()

        @pl.loop(0, size - 1)
        def _(step):
            row_copy(step, side).wait_send()
            for sub in range(2):
                sum_copy(step + 1, side, sub).wait_send()

    for copy in swaps + far_copies:
        copy.wait_send()
    for copy in far_copies:
        copy.wait_recv()
    for store in stores:
        store.wait()


def mlp_ring(normed, resid, gain, cots, gate_weight, up_weight, down_weight):
    size = lax.axis_size("fsdp")
    tokens, width = normed.shape
    units = gate_weight.shape[0]
    anywhere = pl.BlockSpec(memory_space=pl.ANY)
    inside = pl.BlockSpec(memory_space=pltpu.VMEM)
    bf16, f32 = jnp.bfloat16, jnp.float32
    dma = pltpu.SemaphoreType.DMA
    return pl.pallas_call(
        functools.partial(mlp_kernel, size),
        out_shape=(
            jax.ShapeDtypeStruct((size * tokens, width), bf16),
            jax.ShapeDtypeStruct((tokens, width), f32),
            jax.ShapeDtypeStruct((1, width), f32),
            jax.ShapeDtypeStruct((3, units, width), bf16),
            jax.ShapeDtypeStruct((units, width), bf16),
        ),
        in_specs=[anywhere, anywhere, inside, anywhere, anywhere, anywhere, anywhere],
        out_specs=(anywhere, inside, inside, anywhere, anywhere),
        scratch_shapes=[
            pltpu.VMEM((size, tokens, width), bf16),
            pltpu.VMEM((2, tokens, width), bf16),
            pltpu.VMEM((3, units, width), bf16),
            pltpu.VMEM((3, units, width), f32),
            pltpu.VMEM((tokens, units), bf16),
            pltpu.VMEM((tokens, units), bf16),
            pltpu.VMEM((tokens, units), bf16),
            pltpu.VMEM((tokens, width), f32),
            pltpu.VMEM((size, tokens, width), bf16),
            pltpu.VMEM((size, tokens, width), bf16),
            pltpu.VMEM((2, tokens, width), bf16),
            dma((9,)),
            dma((2, 2)),
            dma((2, size)),
            dma((2, size)),
            dma((2, 2, size)),
            dma((2, 2, size)),
            dma((2, size)),
            dma((2, 3)),
            dma((2, CHUNKS)),
            pltpu.SemaphoreType.REGULAR,
        ],
        compiler_params=pltpu.CompilerParams(
            collective_id=0, has_side_effects=True, vmem_limit_bytes=VMEM_BYTES
        ),
        name="mlp_ring",
    )(normed, resid, gain, cots, gate_weight, up_weight, down_weight)


def attend_backward_kernel(
    size,
    heads_ref,
    attended_ref,
    log_ref,
    proj_ref,
    weight_ref,
    normed_ref,
    trig_ref,
    hidden_ref,
    resid_grad_ref,
    gain_ref,
    gain_grad_ref,
    resid_ref,
    outs_ref,
    units_in_ref,
    far_gate_in_ref,
    grad_in_ref,
    hidden_out_ref,
    small_ref,
    shards_ref,
    halves_ref,
    far_units_ref,
    units_ref,
    far_gate_ref,
    grads_all,
    grad_heads,
    grad_mixed,
    grad_keys,
    grad_values,
    grad_normed,
    term_qkv,
    term_out,
    out_columns,
    qkv_in,
    out_in,
    qkv_sum,
    out_sum,
    shard,
    shard_all,
    half_shard,
    half_all,
    out_own,
    out_recv,
    out_send,
    resid,
    seq_in,
    far_sum,
    small_in,
    load_sems,
    own_sems,
    out_sems,
    term_sems,
    column_sems,
    seq_sems,
    shard_sems,
    small_sems,
    unit_sems,
    pass_sems,
    share_sems,
    gate_sems,
    grad_sems,
):
    length = heads_ref.shape[0]
    tokens, width = hidden_ref.shape
    used = heads_ref.shape[1]
    own = attended_ref.shape[1]
    count = own // HEAD_DIM
    scale = HEAD_DIM**-0.5
    half = tokens // 2
    block = tokens
    depth = width // size
    chip_pieces = size // 2
    half_width = width // 2
    term_half = depth // 2
    units = units_ref.shape[1]
    f32, bf16 = jnp.float32, jnp.bfloat16
    me = lax.axis_index("fsdp")
    seq = lax.axis_index("seq")
    place = ring_place(me, size)
    right = ring_member((place + 1) % size, size)
    left = ring_member((place + size - 1) % size, size)
    core, far, diagonal = seq_partners(seq)
    rounds = size.bit_length() - 1
    mirrors = [me + (1 - 2 * ((me // 2**at) % 2)) * 2**at for at in range(rounds)]
    ring = ({"fsdp": right}, {"fsdp": left})

    def owner_of(step, side):
        return ring_member((place + size - step if side == 0 else place + step) % size, size)

    def remote(source, target, sems, at, device):
        return pltpu.make_async_remote_copy(
            src_ref=source,
            dst_ref=target,
            send_sem=sems.at[(0,) + at],
            recv_sem=sems.at[(1,) + at],
            device_id=device,
            device_id_type=MESH,
        )

    greet(
        ring
        + ({"seq": core}, {"seq": far})
        + tuple({"fsdp": mirror} for mirror in mirrors)
    )

    def own_load(step, side):
        at = pl.multiple_of(owner_of(step, side) * tokens + side * half, half)
        return pltpu.make_async_copy(
            outs_ref.at[pl.ds(at, half)],
            out_own.at[step % 2, pl.ds(side * half, half)],
            own_sems.at[step % 2, side],
        )

    def out_copy(step, side):
        span = pl.ds(side * half, half)
        return remote(
            out_send.at[step % 2, span], out_recv.at[step, span], out_sems, (side, step), ring[side]
        )

    def out_step(step):
        for side in range(2):
            own_load(step, side).wait()
            if step < size - 1:
                own_load(step + 1, side).start()
            if step >= 3:
                out_copy(step - 2, side).wait_send()
            if step >= 2:
                out_copy(step - 1, side).wait_recv()
        total = out_own[step % 2].astype(f32)
        if step >= 2:
            total += out_recv[step - 1].astype(f32)
        out_send[step % 2] = total.astype(bf16)
        for side in range(2):
            out_copy(step, side).start()

    resid_load = pltpu.make_async_copy(resid_ref, resid, load_sems.at[0])

    def out_finish():
        step = size
        for side in range(2):
            out_copy(step - 2, side).wait_send()
            out_copy(step - 1, side).wait_send()
            out_copy(step - 1, side).wait_recv()
        mine = pltpu.make_async_copy(
            outs_ref.at[pl.ds(pl.multiple_of(me * tokens, tokens), tokens)],
            out_own.at[0],
            load_sems.at[1],
        )
        mine.start()
        mine.wait()
        resid_load.wait()
        hidden_out_ref[...] = (
            resid[...] + out_own[0].astype(f32) + out_recv[size - 1].astype(f32)
        ).astype(bf16)

    share = units // 2
    piece = share // CHUNKS
    kept = (seq % 2) * share

    def unit_slice(ref, at):
        start = pl.multiple_of(kept + (at % CHUNKS) * piece, 16)
        return ref.at[at // CHUNKS, pl.ds(start, piece)]

    def unit_copy(at):
        return remote(
            unit_slice(units_ref, at + CHUNKS), unit_slice(far_units_ref, at), unit_sems, (at,), {"seq": far}
        )

    def unit_pass(at):
        part = unit_slice(far_units_ref, at)
        return remote(part, part, pass_sems, (at,), {"seq": core})

    def unit_share(at):
        part = unit_slice(units_ref, at)
        return remote(part, part, share_sems, (at,), {"seq": core})

    def gate_pass(at):
        part = far_gate_ref.at[pl.ds(pl.multiple_of(kept + at * piece, 16), piece)]
        return remote(part, part, gate_sems, (at,), {"seq": core})

    chunks = 2 * CHUNKS
    starts, passes = iter(range(chunks)), iter(range(chunks))

    def send_units(number):
        for _ in range(number):
            unit_copy(next(starts)).start()

    def pass_units(number):
        for _ in range(number):
            at = next(passes)
            unit_copy(at).wait_recv()
            unit_pass(at).start()

    def grad_copy(source, target, at):
        span = grads_all.at[source]
        return remote(span, span, grad_sems, (at,), {"seq": target})

    to_far_grads = grad_copy(seq, far, 0)
    to_core_grads = grad_copy(seq, core, 1)
    passed_grads = grad_copy(far, core, 2)
    grads_all[seq] = resid_grad_ref[...].astype(bf16)
    to_far_grads.start()
    to_core_grads.start()
    resid_load.start()
    for side in range(2):
        own_load(1, side).start()
    out_step(1)

    grad_keys[...] = jnp.zeros_like(grad_keys)
    grad_values[...] = jnp.zeros_like(grad_values)
    lane = lax.broadcasted_iota(jnp.int32, (block, HEAD_DIM), 1)
    keys = slice(own, own + HEAD_DIM)
    values = slice(own + HEAD_DIM, used)

    def attend_block(at_block):
        start = at_block * block
        span = slice(start, start + block)
        seen = slice(0, start + block)
        cosine, sine = turn_tables(trig_ref[span, :])
        grad_heads[span, :] = matmul(grads_all[at_block], proj_ref[...], NT).astype(bf16)

        @pl.loop(0, count)
        def _(at):
            head = pl.ds(pl.multiple_of(at * HEAD_DIM, HEAD_DIM), HEAD_DIM)
            query = heads_ref[span, head]
            grad = grad_heads[span, head]
            logs = jnp.sum(jnp.where(lane == at, log_ref[span, :], 0.0), axis=-1, keepdims=True)
            scores = causal(matmul(query, heads_ref[seen, keys], NT) * scale, start)
            probability = jnp.exp(scores - logs)
            grad_probs = matmul(grad, heads_ref[seen, values], NT)
            delta = jnp.sum(probability * grad_probs, axis=-1, keepdims=True)
            grad_scores = (probability * (grad_probs - delta)).astype(bf16)
            grad_query = matmul(grad_scores, heads_ref[seen, keys], NN) * scale
            grad_query = grad_query.astype(bf16).astype(f32)
            grad_mixed[span, head] = (
                grad_query * cosine + pltpu.roll(grad_query * sine, HEAD_DIM // 2, 1)
            ).astype(bf16)
            grad_keys[seen, :] += matmul(grad_scores, query, TN) * scale
            grad_values[seen, :] += matmul(probability.astype(bf16), grad, TN)

    @pl.loop(0, 4)
    def _(turn):
        @pl.when(turn == 1)
        def _():
            to_core_grads.wait_recv()

        @pl.when(turn == 2)
        def _():
            to_far_grads.wait_recv()
            passed_grads.start()
            unit_copy(0).start()

        @pl.when(turn == 3)
        def _():
            passed_grads.wait_recv()
            unit_copy(1).start()

        @pl.when(turn == 2)
        def _():
            out_step(2)

        for shared in range(3):
            unit_share(turn * 3 + shared).start()
        gate_pass(turn).start()
        at_block = ((seq // 2 + turn // 2) % 2) * 2 + (seq % 2 + turn % 2) % 2
        for at in range(4):

            @pl.when(at_block == at)
            def _():
                attend_block(at)

    next(starts)
    next(starts)
    send_units(1)
    for shared in range(12, 3 * CHUNKS):
        unit_share(shared).start()
    gate_pass(4).start()
    out_step(3)

    for start in range(0, length, block):
        span = slice(start, start + block)
        cosine, sine = turn_tables(trig_ref[span, :])
        part = grad_keys[span, :].astype(bf16).astype(f32)
        grad_mixed[span, keys] = (
            part * cosine + pltpu.roll(part * sine, HEAD_DIM // 2, 1)
        ).astype(bf16)
        grad_mixed[span, values] = grad_values[span, :].astype(bf16)

    def normed_part(span):
        grad_normed[:, span] = matmul(grad_mixed[...], weight_ref[span, :used], NT).astype(bf16)

    loop_blocks(width, 256, normed_part)

    def block_rows(at):
        return grad_normed.at[pl.ds(pl.multiple_of(at * tokens, tokens), tokens)]

    to_core = [
        remote(block_rows(diagonal), seq_in.at[0], seq_sems, (0,), {"seq": core}),
        remote(block_rows(core), seq_in.at[1], seq_sems, (1,), {"seq": core}),
    ]
    to_far = remote(far_sum, seq_in.at[2], seq_sems, (2,), {"seq": far})
    for copy in to_core:
        copy.start()

    def out_term(span):
        term_out[:, span] = matmul(
            attended_ref[...], grads_all[:, :, span].reshape(length, span.size), TN
        ).astype(bf16)

    loop_blocks(width, 256, out_term)
    my_row = pl.multiple_of((seq % 2) * own, 16)
    my_lane = pl.multiple_of((seq % 2) * half_width, 128)
    core_lane = pl.multiple_of((1 - seq % 2) * half_width, 128)
    columns = remote(
        term_out.at[:, pl.ds(core_lane, half_width)],
        out_columns.at[pl.ds(my_row, own)],
        column_sems,
        (0,),
        {"seq": core},
    )
    columns.start()
    out_columns[pl.ds(my_row, own), :] = term_out[:, pl.ds(my_lane, half_width)]

    def qkv_term(span):
        term_qkv[span, :] = matmul(normed_ref[:, span], grad_mixed[...], TN).astype(bf16)

    loop_blocks(width, 256, qkv_term)
    to_core[0].wait_recv()
    far_sum[...] = (block_rows(far)[...].astype(f32) + seq_in[0].astype(f32)).astype(bf16)
    to_far.start()
    out_step(4)
    small_in[0] = jnp.zeros((8, width), f32)
    small_in[0, 1:2, :] = gain_grad_ref[...]
    bias = jnp.sum(grad_mixed[...].astype(f32), axis=0, keepdims=True)
    small_in[0, 2:3, pl.ds(pl.multiple_of(seq * own, 128), own)] = bias[:, :own]
    kv_lane = pl.multiple_of((seq // 2) * HEAD_DIM, HEAD_DIM)
    small_in[0, 3:4, pl.ds(kv_lane, HEAD_DIM)] = bias[:, keys]
    small_in[0, 3:4, pl.ds(kv_lane + KV_HEADS * HEAD_DIM, HEAD_DIM)] = bias[:, values]

    def term_copy(step, side):
        span = pl.ds(side * term_half, term_half)
        return remote(
            qkv_sum.at[step, span], qkv_in.at[step, span], term_sems, (0, side, step), ring[side]
        )

    def half_copy(step, side):
        span = pl.ds(side * term_half, term_half)
        return remote(
            out_sum.at[step, span], out_in.at[step, span], term_sems, (1, side, step), ring[side]
        )

    def here(owner):
        return owner // chip_pieces == seq // 2

    def half_rows(owner, side):
        start = (owner % chip_pieces) * depth + side * term_half
        return pl.ds(pl.multiple_of(start, 16), term_half)

    def term_step(step):
        for side in range(2):
            span = pl.ds(side * term_half, term_half)
            start = owner_of(step, side) * depth + side * term_half
            total = term_qkv[pl.ds(pl.multiple_of(start, 16), term_half), :].astype(f32)
            if step >= 2:
                term_copy(step - 1, side).wait_recv()
                total += qkv_in[step - 1, span, :].astype(f32)
            qkv_sum[step, span, :] = total.astype(bf16)
            term_copy(step, side).start()

    def half_step(step):
        for side in range(2):
            owner = owner_of(step, side)

            @pl.when(here(owner))
            def _():
                span = pl.ds(side * term_half, term_half)
                total = out_columns[half_rows(owner, side), :].astype(f32)
                if step >= 2:
                    half_copy(step - 1, side).wait_recv()
                    total += out_in[step - 1, span, :].astype(f32)
                out_sum[step, span, :] = total.astype(bf16)
                half_copy(step, side).start()

    def small_copy(at):
        device = ({"seq": core}, {"seq": far})[at] if at < 2 else {"fsdp": mirrors[at - 2]}
        return remote(small_in.at[2 * at], small_in.at[2 * at + 1], small_sems, (at,), device)

    def small_step(at):
        small_copy(at).wait_recv()
        small_in[2 * at + 2] = small_in[2 * at] + small_in[2 * at + 1]

    term_step(1)
    columns.wait_recv()
    half_step(1)
    term_step(2)
    half_step(2)
    out_step(5)
    to_core[1].wait_recv()
    send_units(1)
    to_far.wait_recv()
    rows = hidden_ref[...].astype(f32)
    inverse = lax.rsqrt(jnp.mean(rows * rows, axis=-1, keepdims=True) + norm_eps)
    unit_rows = rows * inverse
    grad_rows = (
        block_rows(seq)[...].astype(f32) + seq_in[1].astype(f32) + seq_in[2].astype(f32)
    )
    small_in[0, 0:1, :] = jnp.sum(grad_rows * unit_rows, axis=0, keepdims=True)
    small_copy(0).start()
    grad_unit = grad_rows * gain_ref[0:1, :]
    grad_in_ref[...] = resid_grad_ref[...] + inverse * (
        grad_unit - unit_rows * jnp.mean(grad_unit * unit_rows, axis=-1, keepdims=True)
    )
    total_rounds = rounds + 2
    small_step(0)
    small_copy(1).start()
    done = 1
    send_units(2)
    for step in range(3, size):
        term_step(step)
        half_step(step)
        if done < total_rounds:
            small_step(done)
            done += 1
            if done < total_rounds:
                small_copy(done).start()
        if step == 4:
            send_units(2)
        if step % 2 == 0:
            pass_units(2)
    while done < total_rounds:
        small_step(done)
        done += 1
        if done < total_rounds:
            small_copy(done).start()
    small_ref[...] = small_in[2 * total_rounds]
    source_chip = here(me)
    for side in range(2):
        span = pl.ds(side * term_half, term_half)
        start = me * depth + side * term_half
        term_copy(size - 1, side).wait_recv()
        shard[span, :] = (
            term_qkv[pl.ds(pl.multiple_of(start, 16), term_half), :].astype(f32)
            + qkv_in[size - 1, span, :].astype(f32)
        ).astype(bf16)

        @pl.when(source_chip)
        def _():
            half_copy(size - 1, side).wait_recv()
            half_shard[span, :] = (
                out_columns[half_rows(me, side), :].astype(f32)
                + out_in[size - 1, span, :].astype(f32)
            ).astype(bf16)

    def shard_copy(source, at, block_at, target):
        return remote(source, shard_all.at[block_at], shard_sems, (at,), {"seq": target})

    def half_move(source, at, target):
        return remote(source, half_all.at[seq % 2], shard_sems, (at,), {"seq": target})

    shard_far = shard_copy(shard, 0, seq, far)
    shard_core = shard_copy(shard, 1, seq, core)
    shard_pass = shard_copy(shard_all.at[far], 2, far, core)
    half_far = half_move(half_shard, 3, far)
    half_core = half_move(half_shard, 4, core)
    half_pass = half_move(half_all.at[seq % 2], 5, core)
    shard_far.start()
    shard_core.start()

    @pl.when(source_chip)
    def _():
        half_far.start()
        half_core.start()
        half_all[seq % 2] = half_shard[...]

    send_units(2)
    shard_all[seq] = shard[...]
    out_step(6)
    shard_far.wait_recv()
    shard_pass.start()

    @pl.when(jnp.logical_not(source_chip))
    def _():
        half_far.wait_recv()
        half_pass.start()

    pass_units(3)
    out_step(7)
    pass_units(3)
    out_finish()
    shard_core.wait_recv()
    shard_pass.wait_recv()
    shard_store = pltpu.make_async_copy(shard_all, shards_ref, load_sems.at[1])
    shard_store.start()

    @pl.when(source_chip)
    def _():
        half_core.wait_recv()
        half_core.wait_send()
        half_far.wait_send()

    @pl.when(jnp.logical_not(source_chip))
    def _():
        half_pass.wait_recv()
        half_pass.wait_send()

    half_store = pltpu.make_async_copy(half_all, halves_ref, load_sems.at[2])
    half_store.start()
    for step in range(1, size):
        for side in range(2):
            term_copy(step, side).wait_send()

            @pl.when(here(owner_of(step, side)))
            def _():
                half_copy(step, side).wait_send()

    for copy in [unit_share(at) for at in range(3 * CHUNKS)] + [
        gate_pass(at) for at in range(CHUNKS)
    ]:
        copy.wait_send()
        copy.wait_recv()
    for at in range(chunks):
        unit_pass(at).wait_recv()
        unit_copy(at).wait_send()
        unit_pass(at).wait_send()
    for at in range(total_rounds):
        small_copy(at).wait_send()
    for copy in to_core + [to_far, columns, shard_far, shard_core, shard_pass]:
        copy.wait_send()
    for copy in (to_far_grads, to_core_grads, passed_grads):
        copy.wait_send()
    shard_store.wait()
    half_store.wait()


def attend_group_backward(
    heads,
    attended,
    logs,
    proj,
    weight,
    normed,
    trig,
    hidden,
    resid_grad,
    gain,
    gain_grad,
    resid,
    outs,
    units,
    far_gate,
):
    size = lax.axis_size("fsdp")
    groups = lax.axis_size("seq")
    length = heads.shape[0]
    tokens, width = hidden.shape
    used = heads.shape[1]
    own = attended.shape[1]
    depth = width // size
    rounds = size.bit_length() + 1
    bf16, f32 = jnp.bfloat16, jnp.float32
    anywhere = pl.BlockSpec(memory_space=pl.ANY)
    inside = pl.BlockSpec(memory_space=pltpu.VMEM)
    dma = pltpu.SemaphoreType.DMA
    vmem = pltpu.VMEM
    return pl.pallas_call(
        functools.partial(attend_backward_kernel, size),
        out_shape=(
            jax.ShapeDtypeStruct((tokens, width), f32),
            jax.ShapeDtypeStruct((tokens, width), bf16),
            jax.ShapeDtypeStruct((8, width), f32),
            jax.ShapeDtypeStruct((groups, depth, used), bf16),
            jax.ShapeDtypeStruct((2, depth, width // 2), bf16),
            jax.ShapeDtypeStruct((2,) + units.shape[1:], bf16),
            jax.ShapeDtypeStruct(units.shape, bf16),
            jax.ShapeDtypeStruct(far_gate.shape, bf16),
        ),
        in_specs=[inside] * 11 + [anywhere] * 4,
        out_specs=(inside, inside, inside) + (anywhere,) * 5,
        input_output_aliases={13: 6, 14: 7},
        scratch_shapes=[
            vmem((groups, tokens, width), bf16),
            vmem((length, own), bf16),
            vmem((length, used), bf16),
            vmem((length, HEAD_DIM), f32),
            vmem((length, HEAD_DIM), f32),
            vmem((length, width), bf16),
            vmem((width, used), bf16),
            vmem((own, width), bf16),
            vmem((2 * own, width // 2), bf16),
            vmem((size, depth, used), bf16),
            vmem((size, depth, width // 2), bf16),
            vmem((size, depth, used), bf16),
            vmem((size, depth, width // 2), bf16),
            vmem((depth, used), bf16),
            vmem((groups, depth, used), bf16),
            vmem((depth, width // 2), bf16),
            vmem((2, depth, width // 2), bf16),
            vmem((2, tokens, width), bf16),
            vmem((size, tokens, width), bf16),
            vmem((2, tokens, width), bf16),
            vmem((tokens, width), f32),
            vmem((3, tokens, width), bf16),
            vmem((tokens, width), bf16),
            vmem((2 * rounds + 1, 8, width), f32),
            dma((3,)),
            dma((2, 2)),
            dma((2, 2, size)),
            dma((2, 2, 2, size)),
            dma((2, 1)),
            dma((2, 3)),
            dma((2, 6)),
            dma((2, rounds)),
            dma((2, 2 * CHUNKS)),
            dma((2, 2 * CHUNKS)),
            dma((2, 3 * CHUNKS)),
            dma((2, CHUNKS)),
            dma((2, 3)),
        ],
        compiler_params=pltpu.CompilerParams(
            collective_id=2, has_side_effects=True, vmem_limit_bytes=VMEM_BYTES
        ),
        name="attend_backward",
    )(
        heads,
        attended,
        logs,
        proj,
        weight,
        normed,
        trig,
        hidden,
        resid_grad,
        gain,
        gain_grad,
        resid,
        outs,
        units,
        far_gate,
    )


def finish_kernel(
    sums_ref,
    far_gate_ref,
    far_ref,
    grad_in_ref,
    hidden_ref,
    shards_ref,
    halves_ref,
    gate_out,
    up_out,
    down_out,
    grad_in_out,
    hidden_out,
    qkv_out,
    proj_out,
):
    f32 = jnp.float32
    gate_out[...] = sums_ref[0].astype(f32) + far_gate_ref[...].astype(f32)
    up_out[...] = sums_ref[1].astype(f32) + far_ref[0].astype(f32)
    down_out[...] = sums_ref[2].astype(f32) + far_ref[1].astype(f32)
    grad_in_out[...] = grad_in_ref[...]
    hidden_out[...] = hidden_ref[...]
    groups, _, used = shards_ref.shape
    own = used - 2 * HEAD_DIM
    for at in range(groups):
        qkv_out[:, at * own : (at + 1) * own] = shards_ref[at, :, :own].astype(f32)
    for which in range(2):
        lanes = slice(own + which * HEAD_DIM, own + (which + 1) * HEAD_DIM)
        for head in range(KV_HEADS):
            at = groups * own + (which * KV_HEADS + head) * HEAD_DIM
            qkv_out[:, at : at + HEAD_DIM] = shards_ref[2 * head, :, lanes].astype(
                f32
            ) + shards_ref[2 * head + 1, :, lanes].astype(f32)
    half = halves_ref.shape[2]
    for which in range(2):
        proj_out[:, which * half : (which + 1) * half] = halves_ref[which].astype(f32)


def finish_totals(unit_sums, far_gate, far_sums, grad_in, hidden, shards, halves):
    f32, bf16 = jnp.float32, jnp.bfloat16
    _, units, width = unit_sums.shape
    groups, depth, used = shards.shape
    joint = groups * (used - 2 * HEAD_DIM) + 2 * KV_HEADS * HEAD_DIM
    tokens = grad_in.shape[0]
    steps, few = 5, 4

    def spec(*dims, many=False):
        lead = len(dims) - 2
        return pl.BlockSpec(
            dims,
            lambda at: (0,) * lead + (at if many else jnp.minimum(at, few - 1), 0),
        )

    rows = units // steps
    return pl.pallas_call(
        finish_kernel,
        grid=(steps,),
        out_shape=(
            jax.ShapeDtypeStruct((units, width), f32),
            jax.ShapeDtypeStruct((units, width), f32),
            jax.ShapeDtypeStruct((units, width), f32),
            jax.ShapeDtypeStruct((tokens, width), f32),
            jax.ShapeDtypeStruct((tokens, width), bf16),
            jax.ShapeDtypeStruct((depth, joint), f32),
            jax.ShapeDtypeStruct((depth, width), f32),
        ),
        in_specs=[
            spec(3, rows, width, many=True),
            spec(rows, width, many=True),
            spec(2, rows, width, many=True),
            spec(tokens // few, width),
            spec(tokens // few, width),
            spec(groups, depth // few, used),
            spec(2, depth // few, width // 2),
        ],
        out_specs=(
            spec(rows, width, many=True),
            spec(rows, width, many=True),
            spec(rows, width, many=True),
            spec(tokens // few, width),
            spec(tokens // few, width),
            spec(depth // few, joint),
            spec(depth // few, width),
        ),
        compiler_params=pltpu.CompilerParams(vmem_limit_bytes=VMEM_BYTES),
        name="finish_totals",
    )(unit_sums, far_gate, far_sums, grad_in, hidden, shards, halves)


def kernels_fit(hidden_in, positions, attn_gain, qkv_weight, qkv_bias, out_weight, *rest):
    size, groups = lax.axis_size("fsdp"), lax.axis_size("seq")
    _, tokens, width = hidden_in.shape
    units = rest[1].shape[0]
    if groups != 4 or size != 8 or tokens % 256 or units % 160 or width % 512:
        return False
    if (width // size) % 32 or qkv_bias.shape[0] > 256 or KV_HEADS != 2:
        return False
    rows = tokens * width * (4 * size + 34)
    return rows + units * (18 * width + 6 * tokens) < 64_000_000


def per_device_kernels(
    hidden_in,
    positions,
    attn_gain,
    qkv_weight,
    qkv_bias,
    out_weight,
    mlp_gain,
    gate_weight,
    up_weight,
    down_weight,
    cotangent,
):
    f32, bf16 = jnp.float32, jnp.bfloat16
    groups = lax.axis_size("seq")
    size = lax.axis_size("fsdp")
    _, tokens, width = hidden_in.shape
    length = tokens * groups
    lane = jnp.arange(HEAD_DIM)
    frequency = jnp.exp(
        -((lane % (HEAD_DIM // 2)).astype(f32) * 2.0 / HEAD_DIM) * math.log(rope_base)
    )
    angles = positions[0].astype(f32)[:, None] * frequency[None, :]
    trig = jnp.where(lane[None, :] < HEAD_DIM // 2, jnp.cos(angles), jnp.sin(angles))
    small = jnp.concatenate(
        [
            jnp.pad(row.astype(f32), (0, 256 - row.shape[0]))
            for row in (attn_gain, mlp_gain, qkv_bias)
        ]
    )[None]
    (
        normed_one,
        heads,
        attended,
        logs,
        weight,
        proj,
        trig_all,
        gains,
        normed_two,
        residual,
        all_cots,
    ) = attend_group(
        hidden_in[0], trig, qkv_weight, out_weight, small, qkv_bias.shape[0], cotangent[0]
    )
    shard = width // size
    outs, grad_residual, term_gain_two, unit_sums, far_gate = mlp_ring(
        normed_two,
        residual,
        gains,
        all_cots.reshape(size * tokens, width),
        gate_weight,
        up_weight,
        down_weight,
    )
    (
        grad_rows,
        hidden_out,
        smalls,
        shards,
        halves,
        far_sums,
        unit_sums,
        far_gate,
    ) = attend_group_backward(
        heads,
        attended,
        logs,
        proj,
        weight,
        normed_one,
        trig_all.reshape(length, HEAD_DIM),
        hidden_in[0],
        grad_residual,
        gains,
        term_gain_two,
        residual,
        outs,
        unit_sums,
        far_gate,
    )
    grad_gate, grad_up, grad_down, grad_rows, hidden_out, grad_qkv, grad_out = finish_totals(
        unit_sums, far_gate, far_sums, grad_rows, hidden_out, shards, halves
    )
    me = lax.axis_index("fsdp")
    bias_sums = jnp.concatenate([smalls[2], smalls[3, : 2 * KV_HEADS * HEAD_DIM]])
    bias_shard = qkv_bias.shape[0]
    return (
        hidden_out[None],
        grad_rows[None],
        lax.dynamic_slice_in_dim(smalls[0], me * shard, shard),
        grad_qkv,
        lax.dynamic_slice_in_dim(bias_sums, me * bias_shard, bias_shard),
        grad_out,
        lax.dynamic_slice_in_dim(smalls[1], me * shard, shard),
        grad_gate,
        grad_up,
        grad_down,
    )


def per_device_gathered(
    hidden_in,
    positions,
    attn_gain,
    qkv_weight,
    qkv_bias,
    out_weight,
    mlp_gain,
    gate_weight,
    up_weight,
    down_weight,
    cotangent,
):
    groups = lax.axis_size("seq")
    group_heads = HEADS // groups
    repeat = groups // KV_HEADS
    tokens = hidden_in.shape[1]
    width_query = HEADS * HEAD_DIM
    width_key = KV_HEADS * HEAD_DIM
    residual = hidden_in[0].astype(jnp.float32)
    cosine, sine = rope_tables(positions[0])
    gains_one, gains_two, qkv_full, bias_full, out_full = (
        lax.all_gather(attn_gain, "fsdp", axis=0, tiled=True),
        lax.all_gather(mlp_gain, "fsdp", axis=0, tiled=True),
        lax.all_gather(qkv_weight, "fsdp", axis=0, tiled=True),
        lax.all_gather(qkv_bias, "fsdp", axis=0, tiled=True),
        lax.all_gather(out_weight, "fsdp", axis=0, tiled=True),
    )
    gain_one = gains_one.astype(jnp.float32)
    gain_two = gains_two.astype(jnp.float32)
    unit_one, inverse_one, normed_one = norm_forward(residual, gain_one)
    qkv_mixed = jnp.dot(
        normed_one, qkv_full, preferred_element_type=jnp.float32
    ) + bias_full.astype(jnp.float32)
    query_part = qkv_mixed[:, :width_query].reshape(tokens, HEADS, HEAD_DIM)
    key_part = qkv_mixed[:, width_query : width_query + width_key].reshape(
        tokens, KV_HEADS, HEAD_DIM
    )
    value_part = qkv_mixed[:, width_query + width_key :].reshape(tokens, KV_HEADS, HEAD_DIM)
    queries = (
        rotate(query_part, cosine, sine)
        .astype(jnp.bfloat16)
        .reshape(tokens, groups, group_heads * HEAD_DIM)
    )
    keys_rep = jnp.repeat(rotate(key_part, cosine, sine).astype(jnp.bfloat16), repeat, axis=1)
    values_rep = jnp.repeat(value_part.astype(jnp.bfloat16), repeat, axis=1)
    head_queries, head_keys, head_values = (
        lax.all_to_all(queries, "seq", split_axis=1, concat_axis=0, tiled=True),
        lax.all_to_all(keys_rep, "seq", split_axis=1, concat_axis=0, tiled=True),
        lax.all_to_all(values_rep, "seq", split_axis=1, concat_axis=0, tiled=True),
    )
    head_queries = head_queries.reshape(-1, group_heads, HEAD_DIM)
    head_keys = head_keys.reshape(-1, HEAD_DIM)
    head_values = head_values.reshape(-1, HEAD_DIM)
    attended, log_totals = attend_forward(head_queries, head_keys, head_values)
    returned = lax.all_to_all(
        attended.reshape(-1, 1, group_heads * HEAD_DIM),
        "seq",
        split_axis=0,
        concat_axis=1,
        tiled=True,
    )
    attn_rows = returned.reshape(tokens, width_query)
    residual_two = residual + jnp.dot(attn_rows, out_full, preferred_element_type=jnp.float32)
    unit_two, inverse_two, normed_two = norm_forward(residual_two, gain_two)
    grad_output = cotangent[0].astype(jnp.float32)
    grad_mlp = grad_output.astype(jnp.bfloat16)
    all_rows = lax.all_gather(normed_two, "fsdp", axis=0, tiled=True)
    gate_pre = jnp.einsum("td,fd->tf", all_rows, gate_weight, preferred_element_type=jnp.float32)
    up_pre = jnp.einsum("td,fd->tf", all_rows, up_weight, preferred_element_type=jnp.float32)
    sigmoid_gate = jax.nn.sigmoid(gate_pre)
    activated = gate_pre * sigmoid_gate
    hidden = (activated * up_pre).astype(jnp.bfloat16)
    partial_out = jnp.dot(hidden, down_weight, preferred_element_type=jnp.float32)
    mlp_out = lax.psum_scatter(
        partial_out.astype(jnp.bfloat16), "fsdp", scatter_dimension=0, tiled=True
    ).astype(jnp.float32)
    all_grads = lax.all_gather(grad_mlp, "fsdp", axis=0, tiled=True)
    grad_hidden = jnp.einsum(
        "tm,fm->tf", all_grads, down_weight, preferred_element_type=jnp.float32
    )
    grad_gate = (
        grad_hidden * up_pre * sigmoid_gate * (1.0 + gate_pre * (1.0 - sigmoid_gate))
    ).astype(jnp.bfloat16)
    grad_up = (grad_hidden * activated).astype(jnp.bfloat16)
    partial_back = jnp.dot(grad_gate, gate_weight, preferred_element_type=jnp.float32) + jnp.dot(
        grad_up, up_weight, preferred_element_type=jnp.float32
    )
    grad_normed_two = lax.psum_scatter(partial_back, "fsdp", scatter_dimension=0, tiled=True)
    shard_gate = jnp.einsum("tf,td->fd", grad_gate, all_rows, preferred_element_type=jnp.float32)
    shard_up = jnp.einsum("tf,td->fd", grad_up, all_rows, preferred_element_type=jnp.float32)
    shard_down = jnp.einsum("tf,td->fd", hidden, all_grads, preferred_element_type=jnp.float32)
    hidden_out = (residual_two + mlp_out).astype(jnp.bfloat16)
    grad_norm_two, term_gain_two = norm_backward(grad_normed_two, unit_two, inverse_two, gain_two)
    grad_residual_two = grad_output + grad_norm_two
    grad_proj = grad_residual_two.astype(jnp.bfloat16)
    grad_attn_rows = jnp.einsum(
        "td,ed->te", grad_proj, out_full, preferred_element_type=jnp.float32
    ).astype(jnp.bfloat16)
    term_out = jnp.einsum("te,td->ed", attn_rows, grad_proj, preferred_element_type=jnp.float32)
    grad_heads = lax.all_to_all(
        grad_attn_rows.reshape(tokens, groups, group_heads * HEAD_DIM),
        "seq",
        split_axis=1,
        concat_axis=0,
        tiled=True,
    )
    grad_query, grad_keys, grad_values = attend_backward(
        head_queries,
        head_keys,
        head_values,
        log_totals,
        grad_heads.reshape(-1, group_heads, HEAD_DIM),
    )
    back_query, back_keys, back_values = (
        lax.all_to_all(
            grad_query.astype(jnp.bfloat16).reshape(-1, 1, group_heads * HEAD_DIM),
            "seq",
            split_axis=0,
            concat_axis=1,
            tiled=True,
        ),
        lax.all_to_all(
            grad_keys.astype(jnp.bfloat16)[:, None, :],
            "seq",
            split_axis=0,
            concat_axis=1,
            tiled=True,
        ),
        lax.all_to_all(
            grad_values.astype(jnp.bfloat16)[:, None, :],
            "seq",
            split_axis=0,
            concat_axis=1,
            tiled=True,
        ),
    )
    grad_query_rows = unrotate(
        back_query.reshape(tokens, HEADS, HEAD_DIM).astype(jnp.float32), cosine, sine
    )
    grad_key_rows = unrotate(
        jnp.sum(back_keys.astype(jnp.float32).reshape(tokens, KV_HEADS, repeat, HEAD_DIM), axis=2),
        cosine,
        sine,
    )
    grad_value_rows = jnp.sum(
        back_values.astype(jnp.float32).reshape(tokens, KV_HEADS, repeat, HEAD_DIM), axis=2
    )
    grad_mixed = jnp.concatenate(
        [
            grad_query_rows.reshape(tokens, width_query),
            grad_key_rows.reshape(tokens, width_key),
            grad_value_rows.reshape(tokens, width_key),
        ],
        axis=1,
    ).astype(jnp.bfloat16)
    term_qkv = jnp.einsum("td,tc->dc", normed_one, grad_mixed, preferred_element_type=jnp.float32)
    term_bias = jnp.sum(grad_mixed.astype(jnp.float32), axis=0)
    grad_normed_one = jnp.einsum(
        "tc,dc->td", grad_mixed, qkv_full, preferred_element_type=jnp.float32
    )
    grad_norm_one, term_gain_one = norm_backward(grad_normed_one, unit_one, inverse_one, gain_one)
    grad_rows = grad_residual_two + grad_norm_one
    shard_gain_one, shard_qkv, shard_bias, shard_out, shard_gain_two = (
        lax.psum_scatter(
            term_gain_one.astype(jnp.bfloat16), "fsdp", scatter_dimension=0, tiled=True
        ).astype(jnp.float32),
        lax.psum_scatter(
            term_qkv.astype(jnp.bfloat16), "fsdp", scatter_dimension=0, tiled=True
        ).astype(jnp.float32),
        lax.psum_scatter(
            term_bias.astype(jnp.bfloat16), "fsdp", scatter_dimension=0, tiled=True
        ).astype(jnp.float32),
        lax.psum_scatter(
            term_out.astype(jnp.bfloat16), "fsdp", scatter_dimension=0, tiled=True
        ).astype(jnp.float32),
        lax.psum_scatter(
            term_gain_two.astype(jnp.bfloat16), "fsdp", scatter_dimension=0, tiled=True
        ).astype(jnp.float32),
    )
    totals = (
        lax.psum(shard_gain_one.astype(jnp.bfloat16), "seq").astype(jnp.float32),
        lax.psum(shard_qkv.astype(jnp.bfloat16), "seq").astype(jnp.float32),
        lax.psum(shard_bias.astype(jnp.bfloat16), "seq").astype(jnp.float32),
        lax.psum(shard_out.astype(jnp.bfloat16), "seq").astype(jnp.float32),
        lax.psum(shard_gain_two.astype(jnp.bfloat16), "seq").astype(jnp.float32),
        lax.psum(shard_gate.astype(jnp.bfloat16), "seq").astype(jnp.float32),
        lax.psum(shard_up.astype(jnp.bfloat16), "seq").astype(jnp.float32),
        lax.psum(shard_down.astype(jnp.bfloat16), "seq").astype(jnp.float32),
    )
    return (
        hidden_out[None],
        grad_rows[None],
        totals[0],
        totals[1],
        totals[2],
        totals[3],
        totals[4],
        totals[5],
        totals[6],
        totals[7],
    )


def per_device(*arguments):
    return (per_device_kernels if kernels_fit(*arguments) else per_device_gathered)(*arguments)


def solution(mesh):
    placed = (
        P("fsdp", "seq", None),
        P("fsdp", "seq"),
        P("fsdp"),
        P("fsdp", None),
        P("fsdp"),
        P("fsdp", None),
        P("fsdp"),
        P("fsdp", None),
        P("fsdp", None),
        P("fsdp", None),
        P("fsdp", "seq", None),
    )
    return jax.shard_map(
        per_device,
        mesh=mesh,
        in_specs=placed,
        out_specs=(
            P("fsdp", "seq", None),
            P("fsdp", "seq", None),
            P("fsdp"),
            P("fsdp", None),
            P("fsdp"),
            P("fsdp", None),
            P("fsdp"),
            P("fsdp", None),
            P("fsdp", None),
            P("fsdp", None),
        ),
        check_vma=False,
    )
```

```python
import functools
import math

import jax
import jax.numpy as jnp
from jax import lax
from jax.experimental import pallas as pl
from jax.experimental.pallas import tpu as pltpu
from jax.sharding import PartitionSpec as P

HEADS = 12
KV_HEADS = 2
HEAD_DIM = 128


norm_eps = 1e-06
rope_base = 1000000.0


def rope_tables(position_row):
    half_dim = HEAD_DIM // 2
    frequency = jnp.exp(
        -(jnp.arange(half_dim, dtype=jnp.float32) * 2.0 / HEAD_DIM) * math.log(rope_base)
    )
    angles = position_row.astype(jnp.float32)[:, None] * frequency[None, :]
    angles = jnp.concatenate([angles, angles], axis=-1)
    return (jnp.cos(angles), jnp.sin(angles))


def rotate(values, cosine, sine):
    half_dim = values.shape[-1] // 2
    turned = jnp.concatenate([-values[..., half_dim:], values[..., :half_dim]], axis=-1)
    return values * cosine[:, None, :] + turned * sine[:, None, :]


def unrotate(grads_rot, cosine, sine):
    half_dim = grads_rot.shape[-1] // 2
    scaled = grads_rot * sine[:, None, :]
    return grads_rot * cosine[:, None, :] + jnp.concatenate(
        [scaled[..., half_dim:], -scaled[..., :half_dim]], axis=-1
    )


def norm_forward(values, gain):
    inverse = lax.rsqrt(jnp.mean(values * values, axis=-1, keepdims=True) + norm_eps)
    unit_rows = values * inverse
    return (unit_rows, inverse, (unit_rows * gain).astype(jnp.bfloat16))


def norm_backward(grad_normed, unit_rows, inverse, gain):
    grad_unit = grad_normed * gain
    grad_values = inverse * (
        grad_unit - unit_rows * jnp.mean(grad_unit * unit_rows, axis=-1, keepdims=True)
    )
    grad_gain = jnp.sum(grad_normed * unit_rows, axis=0)
    return (grad_values, grad_gain)


def masked_scores(queries, keys, block_start, block_rows):
    length = keys.shape[0]
    query_block = lax.dynamic_slice_in_dim(queries, block_start, block_rows, 0)
    scores = jnp.einsum(
        "bhd,ld->hbl", query_block, keys, preferred_element_type=jnp.float32
    ) * HEAD_DIM ** (-0.5)
    row_index = block_start + jnp.arange(block_rows)
    column_index = jnp.arange(length)
    allowed = column_index[None, :] <= row_index[:, None]
    return (query_block, jnp.where(allowed[None], scores, -1e30))


def attend_forward(queries, keys, values):
    length = keys.shape[0]
    block_rows = min(512, length)
    block_count = length // block_rows

    def one_block(block_start):
        query_block, scores = masked_scores(queries, keys, block_start, block_rows)
        row_max = jnp.max(scores, axis=-1, keepdims=True)
        exponent = jnp.exp(scores - row_max)
        row_total = jnp.sum(exponent, axis=-1, keepdims=True)
        probability = (exponent / row_total).astype(jnp.bfloat16)
        result = jnp.einsum("hbl,ld->bhd", probability, values, preferred_element_type=jnp.float32)
        return (result.astype(jnp.bfloat16), (row_max + jnp.log(row_total))[..., 0])

    results, log_totals = lax.map(one_block, jnp.arange(block_count) * block_rows)
    return (results.reshape(length, queries.shape[1], queries.shape[2]), log_totals)


def attend_backward(queries, keys, values, log_totals, grad_out):
    length = keys.shape[0]
    block_rows = min(512, length)
    block_count = length // block_rows
    score_scale = HEAD_DIM ** (-0.5)

    def one_block(running, inputs):
        grad_keys, grad_values = running
        block_start, log_block = inputs
        query_block, scores = masked_scores(queries, keys, block_start, block_rows)
        grad_block = lax.dynamic_slice_in_dim(grad_out, block_start, block_rows, 0)
        probability = jnp.exp(scores - log_block[..., None])
        grad_probs = jnp.einsum(
            "bhd,ld->hbl", grad_block, values, preferred_element_type=jnp.float32
        )
        row_delta = jnp.sum(probability * grad_probs, axis=-1, keepdims=True)
        grad_scores = (probability * (grad_probs - row_delta)).astype(jnp.bfloat16)
        grad_query = (
            jnp.einsum("hbl,ld->bhd", grad_scores, keys, preferred_element_type=jnp.float32)
            * score_scale
        )
        grad_keys = (
            grad_keys
            + jnp.einsum(
                "hbl,bhd->ld", grad_scores, query_block, preferred_element_type=jnp.float32
            )
            * score_scale
        )
        grad_values = grad_values + jnp.einsum(
            "hbl,bhd->ld",
            probability.astype(jnp.bfloat16),
            grad_block,
            preferred_element_type=jnp.float32,
        )
        return ((grad_keys, grad_values), grad_query)

    zero_rows = jnp.zeros((length, keys.shape[1]), jnp.float32)
    (grad_keys, grad_values), grad_query = lax.scan(
        one_block, (zero_rows, zero_rows), (jnp.arange(block_count) * block_rows, log_totals)
    )
    return (grad_query.reshape(queries.shape), grad_keys, grad_values)


MESH = pl.DeviceIdType.MESH
VMEM_BYTES = 67_000_000
NN = (((1,), (0,)), ((), ()))
NT = (((1,), (1,)), ((), ()))
TN = (((0,), (0,)), ((), ()))


def matmul(left, right, dims):
    return lax.dot_general(left, right, dims, preferred_element_type=jnp.float32)


def ring_place(index, size):
    side = index % 2
    return (index // 2) * (1 - side) + (size - 1 - index // 2) * side


def ring_member(place, size):
    side = place // (size // 2)
    return 2 * (place * (1 - side) + (size - 1 - place) * side) + side


def seq_partners(seq):
    core = seq + 1 - 2 * (seq % 2)
    far = (seq + 2) % 4
    return core, far, (core + 2) % 4


def greet(targets):
    barrier = pltpu.get_barrier_semaphore()
    for target in targets:
        pl.semaphore_signal(barrier, inc=1, device_id=target, device_id_type=MESH)
    pl.semaphore_wait(barrier, len(targets))


def for_blocks(width, block, body):
    for at in range(0, width, block):
        body(pl.ds(at, min(block, width - at)))


def loop_blocks(width, block, body):
    @pl.loop(0, width // block)
    def _(at):
        body(pl.ds(pl.multiple_of(at * block, block), block))


def turn_tables(trig):
    lane = lax.broadcasted_iota(jnp.int32, trig.shape, 1)
    swapped = pltpu.roll(trig, HEAD_DIM // 2, 1)
    first = lane < HEAD_DIM // 2
    return jnp.where(first, trig, swapped), jnp.where(first, -swapped, trig)


def head_columns(at):
    return slice(at * HEAD_DIM, (at + 1) * HEAD_DIM)


def causal(scores, start):
    rows = lax.broadcasted_iota(jnp.int32, scores.shape, 0) + start
    columns = lax.broadcasted_iota(jnp.int32, scores.shape, 1)
    return jnp.where(columns <= rows, scores, -1e30)


def inverse_of(values):
    return lax.rsqrt(jnp.mean(values * values, axis=-1, keepdims=True) + norm_eps)


def attend_forward_kernel(
    size,
    block,
    bias_share,
    rows_ref,
    trig_ref,
    qkv_ref,
    proj_ref,
    small_ref,
    cot_ref,
    normed_out,
    heads_out,
    attended_out,
    log_out,
    piece_out,
    proj_out,
    trig_out,
    gains_out,
    normed_two_out,
    resid_out,
    cots_out,
    rows_all,
    trig_all,
    pieces,
    proj,
    smalls,
    cots,
    normed,
    heads,
    attended,
    logs,
    part,
    gains,
    bias,
    resid,
    seq_in,
    far_sum,
    normed_two,
    load_sems,
    column_sems,
    store_sems,
    ring_sems,
    small_sems,
    cot_sems,
    cot_store_sems,
    seq_sems,
    sum_sems,
    proj_send,
    proj_recv,
):
    f32, bf16 = jnp.float32, jnp.bfloat16
    depth = qkv_ref.shape[0]
    tokens, width = rows_ref.shape
    half = depth // 2
    cot_half = tokens // 2
    own = proj.shape[0]
    used = own + 2 * HEAD_DIM
    count = own // HEAD_DIM
    length = part.shape[0]
    per_group = own // depth
    scale = HEAD_DIM**-0.5
    me = lax.axis_index("fsdp")
    seq = lax.axis_index("seq")
    place = ring_place(me, size)
    right = ring_member((place + 1) % size, size)
    left = ring_member((place + size - 1) % size, size)
    core, far, diagonal = seq_partners(seq)
    ring = ({"fsdp": right}, {"fsdp": left})

    def remote(source, target, sems, at, device):
        return pltpu.make_async_remote_copy(
            src_ref=source,
            dst_ref=target,
            send_sem=sems.at[(0,) + at],
            recv_sem=sems.at[(1,) + at],
            device_id=device,
            device_id_type=MESH,
        )

    width_query = 4 * own
    own_lane = pl.multiple_of(seq * own, HEAD_DIM)
    kv_lane = pl.multiple_of(width_query + (seq // 2) * HEAD_DIM, HEAD_DIM)
    value_lane = pl.multiple_of(kv_lane + KV_HEADS * HEAD_DIM, HEAD_DIM)
    my_rows = pl.ds(pl.multiple_of(me * depth, 16), depth)
    column_loads = [
        pltpu.make_async_copy(
            source.at[:, pl.ds(lane_at, lanes)],
            pieces.at[my_rows, pl.ds(target, lanes)],
            column_sems.at[at],
        )
        for at, (source, lane_at, target, lanes) in enumerate(
            (
                (qkv_ref, own_lane, 0, own),
                (qkv_ref, kv_lane, own, HEAD_DIM),
                (qkv_ref, value_lane, own + HEAD_DIM, HEAD_DIM),
                (proj_ref, own_lane, used, own),
            )
        )
    ]
    loads = [
        pltpu.make_async_copy(trig_ref, trig_all.at[seq], load_sems.at[0]),
        pltpu.make_async_copy(rows_ref, rows_all.at[seq], load_sems.at[1]),
        pltpu.make_async_copy(cot_ref, cots.at[me], load_sems.at[2]),
    ]
    for load in column_loads + loads:
        load.start()
    smalls[me] = jnp.zeros(smalls.shape[1:], f32)
    for at in range(3):
        smalls[me, at : at + 1, :] = small_ref[:, at * 256 : (at + 1) * 256]
    greet(ring + ({"seq": core}, {"seq": far}, {"seq": diagonal}))

    def piece_of(step, side):
        return ring_member((place + size - step if side == 0 else place + step) % size, size)

    def ring_copy(step, side, sub):
        part_rows = half // 2
        start = piece_of(step, side) * depth + side * half + sub * part_rows
        span = pieces.at[pl.ds(pl.multiple_of(start, 16), part_rows)]
        return remote(span, span, ring_sems, (side, sub, step), ring[side])

    def small_copy(step):
        span = smalls.at[piece_of(step, 0)]
        return remote(span, span, small_sems, (step,), ring[0])

    def cot_copy(step, side, sub):
        part_rows = cot_half // 2
        start = side * cot_half + sub * part_rows
        span = cots.at[piece_of(step, side), pl.ds(start, part_rows)]
        return remote(span, span, cot_sems, (side, sub, step), ring[side])

    def cot_store(step, side):
        span = (piece_of(step, side), pl.ds(side * cot_half, cot_half))
        return pltpu.make_async_copy(
            cots.at[span], cots_out.at[span], cot_store_sems.at[side, step]
        )

    def seq_copy(which, block_at, target, at):
        span = (rows_all, trig_all)[which].at[block_at]
        return remote(span, span, seq_sems, (which, at), {"seq": target})

    def proj_part(step, side):
        at = piece_of(step, side)
        row = pl.multiple_of((at % per_group) * depth + side * half, 16)
        source = pieces.at[
            pl.ds(pl.multiple_of(at * depth + side * half, 16), half), pl.ds(used, own)
        ]
        target = proj.at[pl.ds(row, half), pl.ds(pl.multiple_of(seq * own, 128), own)]
        return at, at // per_group, source, target

    def proj_copy(step, side):
        at, owner, source, target = proj_part(step, side)
        return owner, pltpu.make_async_remote_copy(
            src_ref=source,
            dst_ref=target,
            send_sem=proj_send.at[side, step],
            recv_sem=proj_recv.at[seq, at % per_group, side],
            device_id={"seq": owner},
            device_id_type=MESH,
        )

    def proj_act(step, side, action):
        owner, copy = proj_copy(step, side)

        @pl.when(owner != seq)
        def _():
            if action == "start":
                copy.start()
            else:
                copy.wait_send()

        @pl.when(owner == seq)
        def _():
            _, _, source, target = proj_part(step, side)
            kept = pltpu.make_async_copy(source, target, proj_send.at[side, step])
            if action == "start":
                kept.start()
            else:
                kept.wait()

    stores = []

    def store(source, target):
        stores.append(pltpu.make_async_copy(source, target, store_sems.at[len(stores)]))
        stores[-1].start()

    def cot_pump(step):
        for sub in range(2):
            for side in range(2):
                if step >= 1:
                    cot_copy(step - 1, side, sub).wait_recv()
                if step < size - 1:
                    cot_copy(step, side, sub).start()
        for side in range(2):
            cot_store(step, side).start()

    for load in column_loads:
        load.wait()
    for sub in range(2):
        for side in range(2):
            ring_copy(0, side, sub).start()
    small_copy(0).start()
    for which in (1, 0):
        loads[1 - which].wait()
        seq_copy(which, seq, far, 1).start()
        seq_copy(which, seq, core, 0).start()
    for side in range(2):
        proj_act(0, side, "start")
    loads[2].wait()

    for step in range(size - 1):
        for sub in range(2):
            for side in range(2):
                ring_copy(step, side, sub).wait_recv()
                if step < size - 2:
                    ring_copy(step + 1, side, sub).start()
        small_copy(step).wait_recv()
        if step < size - 2:
            small_copy(step + 1).start()
        if step == 1:
            cot_pump(0)
        for side in range(2):
            proj_act(step + 1, side, "start")
        if step == min(1, size - 2):
            for which in (1, 0):
                seq_copy(which, seq, far, 1).wait_recv()
                seq_copy(which, far, core, 2).start()

    gathered = jnp.zeros((8, width), f32)
    small_width = smalls.shape[2]
    for at in range(size):
        held = smalls[at]
        lane = lax.broadcasted_iota(jnp.int32, held.shape, 1)
        wide = jnp.concatenate(
            [
                jnp.where(lane < depth, held, 0.0),
                jnp.zeros((8, width - small_width), f32),
            ],
            axis=1,
        )
        gathered += pltpu.roll(wide, at * depth, 1) if at else wide
        bias[:, at * bias_share : (at + 1) * bias_share] = held[:, :bias_share]
    gains[...] = gathered
    gain_one = gathered[0:1, :]
    gain_two = gathered[1:2, :]
    store(gains, gains_out)
    for which in (1, 0):
        seq_copy(which, seq, core, 0).wait_recv()
        seq_copy(which, far, core, 2).wait_recv()
    store(pieces, piece_out)
    store(trig_all, trig_out)

    own_bias = jnp.concatenate(
        [
            bias[2:3, pl.ds(own_lane, own)],
            bias[2:3, pl.ds(kv_lane, HEAD_DIM)],
            bias[2:3, pl.ds(value_lane, HEAD_DIM)],
        ],
        axis=1,
    )
    for at in range(length // block):
        span = slice(at * block, (at + 1) * block)
        rows = rows_all[at].astype(f32)
        normed[span, :] = (rows * inverse_of(rows) * gain_one).astype(bf16)
        mixed = matmul(normed[span, :], pieces[:, :used], NN) + own_bias
        cosine, sine = turn_tables(trig_all[at])
        for head in range(count + 1):
            turned = mixed[:, head_columns(head)]
            heads[span, head_columns(head)] = (
                turned * cosine + pltpu.roll(turned, HEAD_DIM // 2, 1) * sine
            ).astype(bf16)
        heads[span, head_columns(count + 1)] = mixed[:, head_columns(count + 1)].astype(bf16)
        if at == 0:
            cot_pump(1)
    store(normed, normed_out)
    store(heads, heads_out)

    for peer in (core, far, diagonal):
        for at in range(per_group):
            for side in range(2):
                pltpu.make_async_remote_copy(
                    src_ref=pieces.at[pl.ds(0, half), pl.ds(used, own)],
                    dst_ref=proj.at[pl.ds(0, half), pl.ds(0, own)],
                    send_sem=proj_send.at[side, 0],
                    recv_sem=proj_recv.at[peer, at, side],
                    device_id={"seq": peer},
                    device_id_type=MESH,
                ).wait_recv()
    for step in range(size):
        for side in range(2):
            proj_act(step, side, "wait")
    store(proj, proj_out)

    lane = lax.broadcasted_iota(jnp.int32, (block, HEAD_DIM), 1)
    for start in range(0, length, block):
        span = slice(start, start + block)
        seen = slice(0, start + block)
        logs[span, :] = jnp.zeros((block, HEAD_DIM), f32)

        @pl.loop(0, count)
        def _(at):
            head = pl.ds(pl.multiple_of(at * HEAD_DIM, HEAD_DIM), HEAD_DIM)
            scores = causal(
                matmul(heads[span, head], heads[seen, head_columns(count)], NT) * scale, start
            )
            top = jnp.max(scores, axis=-1, keepdims=True)
            exponent = jnp.exp(scores - top)
            total = jnp.sum(exponent, axis=-1, keepdims=True)
            probability = (exponent / total).astype(bf16)
            attended[span, head] = matmul(
                probability, heads[seen, head_columns(count + 1)], NN
            ).astype(bf16)
            logs[span, :] = jnp.where(lane == at, top + jnp.log(total), logs[span, :])

        if 2 * (start + block) == length:
            cot_pump(2)
    store(attended, attended_out)
    store(logs, log_out)

    def out_part(span):
        part[:, span] = matmul(attended[...], proj[:, span], NN).astype(bf16)

    for_blocks(width, 512, out_part)

    def part_rows(at):
        return part.at[pl.ds(pl.multiple_of(at * tokens, tokens), tokens)]

    to_core = [
        remote(part_rows(diagonal), seq_in.at[0], sum_sems, (0,), {"seq": core}),
        remote(part_rows(core), seq_in.at[1], sum_sems, (1,), {"seq": core}),
    ]
    to_far = remote(far_sum, seq_in.at[2], sum_sems, (2,), {"seq": far})
    for copy in to_core:
        copy.start()
    cot_pump(3)
    to_core[0].wait_recv()
    far_sum[...] = (part_rows(far)[...].astype(f32) + seq_in[0].astype(f32)).astype(bf16)
    to_far.start()
    to_core[1].wait_recv()
    resid[...] = (
        part_rows(seq)[...].astype(f32) + seq_in[1].astype(f32) + rows_all[seq].astype(f32)
    )
    cot_pump(4)
    cot_pump(5)
    to_far.wait_recv()
    resid[...] += seq_in[2].astype(f32)
    store(resid, resid_out)
    normed_two[...] = (resid[...] * inverse_of(resid[...]) * gain_two).astype(bf16)
    store(normed_two, normed_two_out)
    for step in range(6, size):
        cot_pump(step)
    for step in range(size):
        for side in range(2):
            cot_store(step, side).wait()

    for step in range(size - 1):
        for side in range(2):
            for sub in range(2):
                ring_copy(step, side, sub).wait_send()
                cot_copy(step, side, sub).wait_send()
        small_copy(step).wait_send()
    for which in (1, 0):
        seq_copy(which, seq, core, 0).wait_send()
        seq_copy(which, seq, far, 1).wait_send()
        seq_copy(which, far, core, 2).wait_send()
    for copy in to_core + [to_far]:
        copy.wait_send()
    for copy in stores:
        copy.wait()


def attend_group(rows, trig, qkv_weight, out_weight, small, bias_share, cots):
    size = lax.axis_size("fsdp")
    groups = lax.axis_size("seq")
    tokens, width = rows.shape
    depth = qkv_weight.shape[0]
    own = width // groups
    used = own + 2 * HEAD_DIM
    joint = used + own
    length = tokens * groups
    f32, bf16 = jnp.float32, jnp.bfloat16
    dma = pltpu.SemaphoreType.DMA
    anywhere = pl.BlockSpec(memory_space=pl.ANY)
    normed = ((length, width), bf16)
    heads = ((length, used), bf16)
    attended = ((length, own), bf16)
    logs = ((length, HEAD_DIM), f32)
    pieces = ((width, joint), bf16)
    proj = ((own, width), bf16)
    trig_all = ((groups,) + trig.shape, f32)
    gains = ((8, width), f32)
    rows_all = ((groups, tokens, width), bf16)
    own_rows = ((tokens, width), bf16)
    resid = ((tokens, width), f32)
    cots_all = ((size, tokens, width), bf16)
    outs = (
        normed, heads, attended, logs, pieces, proj, trig_all, gains, own_rows, resid, cots_all
    )
    held = (
        rows_all,
        trig_all,
        pieces,
        proj,
        ((size, 8, 256), f32),
        cots_all,
        normed,
        heads,
        attended,
        logs,
        normed,
        gains,
        ((8, size * bias_share), f32),
        resid,
        ((3, tokens, width), bf16),
        own_rows,
        own_rows,
    )
    return pl.pallas_call(
        functools.partial(attend_forward_kernel, size, tokens, bias_share),
        out_shape=tuple(jax.ShapeDtypeStruct(*shape) for shape in outs),
        in_specs=[anywhere] * 4 + [pl.BlockSpec(memory_space=pltpu.VMEM), anywhere],
        out_specs=(anywhere,) * len(outs),
        scratch_shapes=[pltpu.VMEM(*shape) for shape in held]
        + [
            dma((3,)),
            dma((4,)),
            dma((len(outs),)),
            dma((2, 2, 2, size)),
            dma((2, size)),
            dma((2, 2, 2, size)),
            dma((2, size)),
            dma((2, 2, 3)),
            dma((2, 3)),
            dma((2, size)),
            dma((groups, own // depth, 2)),
        ],
        compiler_params=pltpu.CompilerParams(
            collective_id=1, has_side_effects=True, vmem_limit_bytes=VMEM_BYTES
        ),
        name="attend_forward",
    )(
        rows,
        trig,
        qkv_weight,
        out_weight,
        small,
        cots,
    )


CHUNKS = 5
IN_LOOP = ((2, 1), (4, 2), (6, 3))


def mlp_kernel(
    size,
    normed_ref,
    resid_ref,
    gain_ref,
    cots_ref,
    gate_ref,
    up_ref,
    down_ref,
    outs_ref,
    back_ref,
    gain_grad_ref,
    sums_ref,
    far_ref,
    rows_all,
    cots,
    weights,
    grads,
    hid,
    dgate,
    dup,
    resid,
    sums_in,
    backs,
    outs,
    load_sems,
    cot_sems,
    ring_send,
    ring_recv,
    sum_send,
    sum_recv,
    out_sems,
    swap_sems,
    far_sems,
    swap_ready,
):
    tokens, width = normed_ref.shape
    units = gate_ref.shape[0]
    half = tokens // 2
    me = lax.axis_index("fsdp")
    seq = lax.axis_index("seq")
    place = ring_place(me, size)
    right = ring_member((place + 1) % size, size)
    left = ring_member((place + size - 1) % size, size)
    core, far, diagonal = seq_partners(seq)
    sides = ((right, pl.ds(0, half)), (left, pl.ds(half, half)))

    def owner_of(step, side):
        return ring_member((place + size - step if side == 0 else place + step) % size, size)

    own_load = pltpu.make_async_copy(normed_ref, rows_all.at[0], load_sems.at[3])
    resid_load = pltpu.make_async_copy(resid_ref, resid, load_sems.at[4])
    weight_loads = [
        pltpu.make_async_copy(ref, weights.at[at], load_sems.at[at])
        for at, ref in enumerate((gate_ref, up_ref, down_ref))
    ]
    own_load.start()
    greet(({"fsdp": right}, {"fsdp": left}, {"seq": core}, {"seq": far}))

    def cot_copies(step):
        return [
            pltpu.make_async_copy(
                cots_ref.at[
                    pl.ds(
                        pl.multiple_of(owner_of(step, side) * tokens + side * half, half), half
                    )
                ],
                cots.at[step % 2, sides[side][1]],
                cot_sems.at[step % 2, side],
            )
            for side in range(2)
        ]


    def row_copy(step, side):
        target, span = sides[side]
        return pltpu.make_async_remote_copy(
            src_ref=rows_all.at[step, span],
            dst_ref=rows_all.at[step + 1, span],
            send_sem=ring_send.at[side, step],
            recv_sem=ring_recv.at[side, step + 1],
            device_id={"fsdp": target},
            device_id_type=MESH,
        )

    def sum_span(side, sub):
        return pl.ds(side * half + sub * (half // 2), half // 2)

    def sum_copy(step, side, sub):
        target, span = sides[side][0], sum_span(side, sub)
        return pltpu.make_async_remote_copy(
            src_ref=backs.at[step, span],
            dst_ref=sums_in.at[step, span],
            send_sem=sum_send.at[side, sub, step],
            recv_sem=sum_recv.at[side, sub, step],
            device_id={"fsdp": target},
            device_id_type=MESH,
        )

    def sum_step(step):
        for sub in range(2):
            for side in range(2):
                span = sum_span(side, sub)
                if step >= 2:
                    sum_copy(step - 1, side, sub).wait_recv()
                    backs[step, span] = (
                        backs[step, span].astype(jnp.float32)
                        + sums_in[step - 1, span].astype(jnp.float32)
                    ).astype(jnp.bfloat16)
                sum_copy(step, side, sub).start()

    def out_copy(step, side):
        at = pl.multiple_of(owner_of(step, side) * tokens + side * half, half)
        return pltpu.make_async_copy(
            outs.at[step % 2, sides[side][1]], outs_ref.at[pl.ds(at, half)], out_sems.at[side, step]
        )

    def elementwise(step, span):
        rows = rows_all[step]
        gate = matmul(rows, weights[0, span, :], NT)
        up = matmul(rows, weights[1, span, :], NT)
        grad_hidden = matmul(cots[step % 2], weights[2, span, :], NT)
        sigmoid = jax.nn.sigmoid(gate)
        activated = gate * sigmoid
        hid[:, span] = (activated * up).astype(jnp.bfloat16)
        dgate[:, span] = (
            grad_hidden * up * sigmoid * (1.0 + gate * (1.0 - sigmoid))
        ).astype(jnp.bfloat16)
        dup[:, span] = (grad_hidden * activated).astype(jnp.bfloat16)

    own_load.wait()
    for side in range(2):
        row_copy(0, side).start()
    for load in weight_loads + cot_copies(0) + [resid_load]:
        load.start()

    @pl.loop(0, units // 16)
    def _(at):
        zeros = jnp.zeros((3, 16, width), jnp.float32)
        grads[:, pl.ds(pl.multiple_of(at * 16, 16), 16), :] = zeros

    for load in weight_loads:
        load.wait()

    @pl.loop(0, size)
    def _(step):
        slot = step % 2

        @pl.when(step >= 1)
        def _():
            for side in range(2):
                row_copy(step - 1, side).wait_recv()

        @pl.when((step >= 1) & (step < size - 1))
        def _():
            for side in range(2):
                row_copy(step, side).start()

        for load in cot_copies(step):
            load.wait()

        @pl.when(step < size - 1)
        def _():
            for load in cot_copies(step + 1):
                load.start()

        for_blocks(units, 256, functools.partial(elementwise, step))

        def back_part(span):
            backs[step, :, span] = (
                matmul(dgate[...], weights[0, :, span], NN)
                + matmul(dup[...], weights[1, :, span], NN)
            ).astype(jnp.bfloat16)

        for_blocks(width, 256, back_part)

        for when, at in IN_LOOP:

            @pl.when(step == when)
            def _():
                sum_step(at)

        @pl.when(step >= 2)
        def _():
            for side in range(2):
                out_copy(step - 2, side).wait()

        def out_part(span):
            outs[slot, :, span] = matmul(hid[...], weights[2, :, span], NN).astype(jnp.bfloat16)

        for_blocks(width, 256, out_part)
        for side in range(2):
            out_copy(step, side).start()

        def weight_part(span):
            rows, cot = rows_all[step, :, span], cots[slot, :, span]
            grads[0, :, span] += matmul(dgate[...], rows, TN)
            grads[1, :, span] += matmul(dup[...], rows, TN)
            grads[2, :, span] += matmul(hid[...], cot, TN)

        for_blocks(width, 256, weight_part)

    share = units // 2
    kept = pl.multiple_of((seq % 2) * share, 16)
    given = pl.multiple_of((1 - seq % 2) * share, 16)
    chunk = share // CHUNKS
    pl.semaphore_signal(swap_ready, inc=1, device_id={"seq": core}, device_id_type=MESH)

    def to_seq(source, target, sems, at, device):
        return pltpu.make_async_remote_copy(
            src_ref=source,
            dst_ref=target,
            send_sem=sems.at[0, at],
            recv_sem=sems.at[1, at],
            device_id={"seq": device},
            device_id_type=MESH,
        )

    swaps = [
        to_seq(
            weights.at[at, pl.ds(given, share)],
            weights.at[at, pl.ds(given, share)],
            swap_sems,
            at,
            core,
        )
        for at in range(3)
    ]
    waiting = [at for at in range(1, size) if at not in [pair[1] for pair in IN_LOOP]]
    sum_step(waiting[0])
    for at in range(3):

        @pl.loop(0, share // 16)
        def _(block):
            span = pl.ds(pl.multiple_of(given + block * 16, 16), 16)
            weights[at, span, :] = grads[at, span, :].astype(jnp.bfloat16)

        if at == 0:
            pl.semaphore_wait(swap_ready, 1)
        swaps[at].start()

    stores = []

    def kept_rows(at):
        return pl.ds(pl.multiple_of(kept + at * chunk, 16), chunk)

    far_copies = [
        to_seq(weights.at[0, kept_rows(at)], far_ref.at[kept_rows(at)], far_sems, at, far)
        for at in range(CHUNKS)
    ]
    def swap_finish(at):
        swaps[at].wait_recv()

        @pl.loop(0, share // 16)
        def _(block):
            span = pl.ds(pl.multiple_of(kept + block * 16, 16), 16)
            weights[at, span, :] = (
                grads[at, span, :] + weights[at, span, :].astype(jnp.float32)
            ).astype(jnp.bfloat16)

        done = weights.at[at, pl.ds(kept, share)]
        stores.append(
            pltpu.make_async_copy(done, sums_ref.at[at, pl.ds(kept, share)], load_sems.at[at])
        )
        if at == 0:
            for copy in far_copies:
                copy.start()
        stores[-1].start()

    cot_own = pltpu.make_async_copy(
        cots_ref.at[pl.ds(pl.multiple_of(me * tokens, tokens), tokens)],
        cots.at[0],
        load_sems.at[7],
    )
    cot_own.start()
    for turn, at in enumerate(waiting[1:]):
        sum_step(at)
        if turn < 3:
            swap_finish(turn)
    for turn in range(len(waiting) - 1, 3):
        swap_finish(turn)

    for side in range(2):
        for sub in range(2):
            sum_copy(size - 1, side, sub).wait_recv()
    grad_normed = backs[0].astype(jnp.float32) + sums_in[size - 1].astype(jnp.float32)
    resid_load.wait()
    inverse = inverse_of(resid[...])
    unit_rows = resid[...] * inverse
    gain_grad_ref[...] = jnp.sum(grad_normed * unit_rows, axis=0, keepdims=True)
    grad_unit = grad_normed * gain_ref[1:2, :]
    cot_own.wait()
    back_ref[...] = cots[0].astype(jnp.float32) + inverse * (
        grad_unit - unit_rows * jnp.mean(grad_unit * unit_rows, axis=-1, keepdims=True)
    )
    for side in range(2):
        out_copy(size - 2, side).wait()
        out_copy(size - 1, side).wait()

        @pl.loop(0, size - 1)
        def _(step):
            row_copy(step, side).wait_send()
            for sub in range(2):
                sum_copy(step + 1, side, sub).wait_send()

    for copy in swaps + far_copies:
        copy.wait_send()
    for copy in far_copies:
        copy.wait_recv()
    for store in stores:
        store.wait()


def mlp_ring(normed, resid, gain, cots, gate_weight, up_weight, down_weight):
    size = lax.axis_size("fsdp")
    tokens, width = normed.shape
    units = gate_weight.shape[0]
    anywhere = pl.BlockSpec(memory_space=pl.ANY)
    inside = pl.BlockSpec(memory_space=pltpu.VMEM)
    bf16, f32 = jnp.bfloat16, jnp.float32
    dma = pltpu.SemaphoreType.DMA
    return pl.pallas_call(
        functools.partial(mlp_kernel, size),
        out_shape=(
            jax.ShapeDtypeStruct((size * tokens, width), bf16),
            jax.ShapeDtypeStruct((tokens, width), f32),
            jax.ShapeDtypeStruct((1, width), f32),
            jax.ShapeDtypeStruct((3, units, width), bf16),
            jax.ShapeDtypeStruct((units, width), bf16),
        ),
        in_specs=[anywhere, anywhere, inside, anywhere, anywhere, anywhere, anywhere],
        out_specs=(anywhere, inside, inside, anywhere, anywhere),
        scratch_shapes=[
            pltpu.VMEM((size, tokens, width), bf16),
            pltpu.VMEM((2, tokens, width), bf16),
            pltpu.VMEM((3, units, width), bf16),
            pltpu.VMEM((3, units, width), f32),
            pltpu.VMEM((tokens, units), bf16),
            pltpu.VMEM((tokens, units), bf16),
            pltpu.VMEM((tokens, units), bf16),
            pltpu.VMEM((tokens, width), f32),
            pltpu.VMEM((size, tokens, width), bf16),
            pltpu.VMEM((size, tokens, width), bf16),
            pltpu.VMEM((2, tokens, width), bf16),
            dma((9,)),
            dma((2, 2)),
            dma((2, size)),
            dma((2, size)),
            dma((2, 2, size)),
            dma((2, 2, size)),
            dma((2, size)),
            dma((2, 3)),
            dma((2, CHUNKS)),
            pltpu.SemaphoreType.REGULAR,
        ],
        compiler_params=pltpu.CompilerParams(
            collective_id=0, has_side_effects=True, vmem_limit_bytes=VMEM_BYTES
        ),
        name="mlp_ring",
    )(normed, resid, gain, cots, gate_weight, up_weight, down_weight)


def attend_backward_kernel(
    size,
    heads_ref,
    attended_ref,
    log_ref,
    proj_ref,
    weight_ref,
    normed_ref,
    trig_ref,
    hidden_ref,
    resid_grad_ref,
    gain_ref,
    gain_grad_ref,
    resid_ref,
    outs_ref,
    units_in_ref,
    far_gate_in_ref,
    grad_in_ref,
    hidden_out_ref,
    small_ref,
    shards_ref,
    halves_ref,
    far_units_ref,
    units_ref,
    far_gate_ref,
    grads_all,
    grad_heads,
    grad_mixed,
    grad_keys,
    grad_values,
    grad_normed,
    term_qkv,
    term_out,
    out_columns,
    qkv_in,
    out_in,
    qkv_sum,
    out_sum,
    shard,
    shard_all,
    half_shard,
    half_all,
    out_own,
    out_recv,
    out_send,
    resid,
    seq_in,
    far_sum,
    small_in,
    load_sems,
    own_sems,
    out_sems,
    term_sems,
    column_sems,
    seq_sems,
    shard_sems,
    small_sems,
    unit_sems,
    pass_sems,
    share_sems,
    gate_sems,
    grad_sems,
):
    length = heads_ref.shape[0]
    tokens, width = hidden_ref.shape
    used = heads_ref.shape[1]
    own = attended_ref.shape[1]
    count = own // HEAD_DIM
    scale = HEAD_DIM**-0.5
    half = tokens // 2
    block = tokens
    depth = width // size
    chip_pieces = size // 2
    half_width = width // 2
    term_half = depth // 2
    units = units_ref.shape[1]
    f32, bf16 = jnp.float32, jnp.bfloat16
    me = lax.axis_index("fsdp")
    seq = lax.axis_index("seq")
    place = ring_place(me, size)
    right = ring_member((place + 1) % size, size)
    left = ring_member((place + size - 1) % size, size)
    core, far, diagonal = seq_partners(seq)
    rounds = size.bit_length() - 1
    mirrors = [me + (1 - 2 * ((me // 2**at) % 2)) * 2**at for at in range(rounds)]
    ring = ({"fsdp": right}, {"fsdp": left})

    def owner_of(step, side):
        return ring_member((place + size - step if side == 0 else place + step) % size, size)

    def remote(source, target, sems, at, device):
        return pltpu.make_async_remote_copy(
            src_ref=source,
            dst_ref=target,
            send_sem=sems.at[(0,) + at],
            recv_sem=sems.at[(1,) + at],
            device_id=device,
            device_id_type=MESH,
        )

    greet(
        ring
        + ({"seq": core}, {"seq": far})
        + tuple({"fsdp": mirror} for mirror in mirrors)
    )

    def own_load(step, side):
        at = pl.multiple_of(owner_of(step, side) * tokens + side * half, half)
        return pltpu.make_async_copy(
            outs_ref.at[pl.ds(at, half)],
            out_own.at[step % 2, pl.ds(side * half, half)],
            own_sems.at[step % 2, side],
        )

    def out_copy(step, side):
        span = pl.ds(side * half, half)
        return remote(
            out_send.at[step % 2, span], out_recv.at[step, span], out_sems, (side, step), ring[side]
        )

    def out_step(step):
        for side in range(2):
            own_load(step, side).wait()
            if step < size - 1:
                own_load(step + 1, side).start()
            if step >= 3:
                out_copy(step - 2, side).wait_send()
            if step >= 2:
                out_copy(step - 1, side).wait_recv()
        total = out_own[step % 2].astype(f32)
        if step >= 2:
            total += out_recv[step - 1].astype(f32)
        out_send[step % 2] = total.astype(bf16)
        for side in range(2):
            out_copy(step, side).start()

    resid_load = pltpu.make_async_copy(resid_ref, resid, load_sems.at[0])

    def out_finish():
        step = size
        for side in range(2):
            out_copy(step - 2, side).wait_send()
            out_copy(step - 1, side).wait_send()
            out_copy(step - 1, side).wait_recv()
        mine = pltpu.make_async_copy(
            outs_ref.at[pl.ds(pl.multiple_of(me * tokens, tokens), tokens)],
            out_own.at[0],
            load_sems.at[1],
        )
        mine.start()
        mine.wait()
        resid_load.wait()
        hidden_out_ref[...] = (
            resid[...] + out_own[0].astype(f32) + out_recv[size - 1].astype(f32)
        ).astype(bf16)

    share = units // 2
    piece = share // CHUNKS
    kept = (seq % 2) * share

    def unit_slice(ref, at):
        start = pl.multiple_of(kept + (at % CHUNKS) * piece, 16)
        return ref.at[at // CHUNKS, pl.ds(start, piece)]

    def unit_copy(at):
        return remote(
            unit_slice(units_ref, at + CHUNKS), unit_slice(far_units_ref, at), unit_sems, (at,), {"seq": far}
        )

    def unit_pass(at):
        part = unit_slice(far_units_ref, at)
        return remote(part, part, pass_sems, (at,), {"seq": core})

    def unit_share(at):
        part = unit_slice(units_ref, at)
        return remote(part, part, share_sems, (at,), {"seq": core})

    def gate_pass(at):
        part = far_gate_ref.at[pl.ds(pl.multiple_of(kept + at * piece, 16), piece)]
        return remote(part, part, gate_sems, (at,), {"seq": core})

    chunks = 2 * CHUNKS
    starts, passes = iter(range(chunks)), iter(range(chunks))

    def send_units(number):
        for _ in range(number):
            unit_copy(next(starts)).start()

    def pass_units(number):
        for _ in range(number):
            at = next(passes)
            unit_copy(at).wait_recv()
            unit_pass(at).start()

    def grad_copy(source, target, at):
        span = grads_all.at[source]
        return remote(span, span, grad_sems, (at,), {"seq": target})

    to_far_grads = grad_copy(seq, far, 0)
    to_core_grads = grad_copy(seq, core, 1)
    passed_grads = grad_copy(far, core, 2)
    grads_all[seq] = resid_grad_ref[...].astype(bf16)
    to_far_grads.start()
    to_core_grads.start()
    resid_load.start()
    for side in range(2):
        own_load(1, side).start()
    out_step(1)

    grad_keys[...] = jnp.zeros_like(grad_keys)
    grad_values[...] = jnp.zeros_like(grad_values)
    lane = lax.broadcasted_iota(jnp.int32, (block, HEAD_DIM), 1)
    keys = slice(own, own + HEAD_DIM)
    values = slice(own + HEAD_DIM, used)

    def attend_block(at_block):
        start = at_block * block
        span = slice(start, start + block)
        seen = slice(0, start + block)
        cosine, sine = turn_tables(trig_ref[span, :])
        grad_heads[span, :] = matmul(grads_all[at_block], proj_ref[...], NT).astype(bf16)

        @pl.loop(0, count)
        def _(at):
            head = pl.ds(pl.multiple_of(at * HEAD_DIM, HEAD_DIM), HEAD_DIM)
            query = heads_ref[span, head]
            grad = grad_heads[span, head]
            logs = jnp.sum(jnp.where(lane == at, log_ref[span, :], 0.0), axis=-1, keepdims=True)
            scores = causal(matmul(query, heads_ref[seen, keys], NT) * scale, start)
            probability = jnp.exp(scores - logs)
            grad_probs = matmul(grad, heads_ref[seen, values], NT)
            delta = jnp.sum(probability * grad_probs, axis=-1, keepdims=True)
            grad_scores = (probability * (grad_probs - delta)).astype(bf16)
            grad_query = matmul(grad_scores, heads_ref[seen, keys], NN) * scale
            grad_query = grad_query.astype(bf16).astype(f32)
            grad_mixed[span, head] = (
                grad_query * cosine + pltpu.roll(grad_query * sine, HEAD_DIM // 2, 1)
            ).astype(bf16)
            grad_keys[seen, :] += matmul(grad_scores, query, TN) * scale
            grad_values[seen, :] += matmul(probability.astype(bf16), grad, TN)

    @pl.loop(0, 4)
    def _(turn):
        @pl.when(turn == 1)
        def _():
            to_core_grads.wait_recv()

        @pl.when(turn == 2)
        def _():
            to_far_grads.wait_recv()
            passed_grads.start()
            unit_copy(0).start()

        @pl.when(turn == 3)
        def _():
            passed_grads.wait_recv()
            unit_copy(1).start()

        @pl.when(turn == 2)
        def _():
            out_step(2)

        for shared in range(3):
            unit_share(turn * 3 + shared).start()
        gate_pass(turn).start()
        at_block = ((seq // 2 + turn // 2) % 2) * 2 + (seq % 2 + turn % 2) % 2
        for at in range(4):

            @pl.when(at_block == at)
            def _():
                attend_block(at)

    next(starts)
    next(starts)
    send_units(1)
    for shared in range(12, 3 * CHUNKS):
        unit_share(shared).start()
    gate_pass(4).start()
    out_step(3)

    for start in range(0, length, block):
        span = slice(start, start + block)
        cosine, sine = turn_tables(trig_ref[span, :])
        part = grad_keys[span, :].astype(bf16).astype(f32)
        grad_mixed[span, keys] = (
            part * cosine + pltpu.roll(part * sine, HEAD_DIM // 2, 1)
        ).astype(bf16)
        grad_mixed[span, values] = grad_values[span, :].astype(bf16)

    def normed_part(span):
        grad_normed[:, span] = matmul(grad_mixed[...], weight_ref[span, :used], NT).astype(bf16)

    loop_blocks(width, 256, normed_part)

    def block_rows(at):
        return grad_normed.at[pl.ds(pl.multiple_of(at * tokens, tokens), tokens)]

    to_core = [
        remote(block_rows(diagonal), seq_in.at[0], seq_sems, (0,), {"seq": core}),
        remote(block_rows(core), seq_in.at[1], seq_sems, (1,), {"seq": core}),
    ]
    to_far = remote(far_sum, seq_in.at[2], seq_sems, (2,), {"seq": far})
    for copy in to_core:
        copy.start()

    def out_term(span):
        term_out[:, span] = matmul(
            attended_ref[...], grads_all[:, :, span].reshape(length, span.size), TN
        ).astype(bf16)

    loop_blocks(width, 256, out_term)
    my_row = pl.multiple_of((seq % 2) * own, 16)
    my_lane = pl.multiple_of((seq % 2) * half_width, 128)
    core_lane = pl.multiple_of((1 - seq % 2) * half_width, 128)
    columns = remote(
        term_out.at[:, pl.ds(core_lane, half_width)],
        out_columns.at[pl.ds(my_row, own)],
        column_sems,
        (0,),
        {"seq": core},
    )
    columns.start()
    out_columns[pl.ds(my_row, own), :] = term_out[:, pl.ds(my_lane, half_width)]

    def qkv_term(span):
        term_qkv[span, :] = matmul(normed_ref[:, span], grad_mixed[...], TN).astype(bf16)

    loop_blocks(width, 256, qkv_term)
    to_core[0].wait_recv()
    far_sum[...] = (block_rows(far)[...].astype(f32) + seq_in[0].astype(f32)).astype(bf16)
    to_far.start()
    out_step(4)
    small_in[0] = jnp.zeros((8, width), f32)
    small_in[0, 1:2, :] = gain_grad_ref[...]
    bias = jnp.sum(grad_mixed[...].astype(f32), axis=0, keepdims=True)
    small_in[0, 2:3, pl.ds(pl.multiple_of(seq * own, 128), own)] = bias[:, :own]
    kv_lane = pl.multiple_of((seq // 2) * HEAD_DIM, HEAD_DIM)
    small_in[0, 3:4, pl.ds(kv_lane, HEAD_DIM)] = bias[:, keys]
    small_in[0, 3:4, pl.ds(kv_lane + KV_HEADS * HEAD_DIM, HEAD_DIM)] = bias[:, values]

    def term_copy(step, side):
        span = pl.ds(side * term_half, term_half)
        return remote(
            qkv_sum.at[step, span], qkv_in.at[step, span], term_sems, (0, side, step), ring[side]
        )

    def half_copy(step, side):
        span = pl.ds(side * term_half, term_half)
        return remote(
            out_sum.at[step, span], out_in.at[step, span], term_sems, (1, side, step), ring[side]
        )

    def here(owner):
        return owner // chip_pieces == seq // 2

    def half_rows(owner, side):
        start = (owner % chip_pieces) * depth + side * term_half
        return pl.ds(pl.multiple_of(start, 16), term_half)

    def term_step(step):
        for side in range(2):
            span = pl.ds(side * term_half, term_half)
            start = owner_of(step, side) * depth + side * term_half
            total = term_qkv[pl.ds(pl.multiple_of(start, 16), term_half), :].astype(f32)
            if step >= 2:
                term_copy(step - 1, side).wait_recv()
                total += qkv_in[step - 1, span, :].astype(f32)
            qkv_sum[step, span, :] = total.astype(bf16)
            term_copy(step, side).start()

    def half_step(step):
        for side in range(2):
            owner = owner_of(step, side)

            @pl.when(here(owner))
            def _():
                span = pl.ds(side * term_half, term_half)
                total = out_columns[half_rows(owner, side), :].astype(f32)
                if step >= 2:
                    half_copy(step - 1, side).wait_recv()
                    total += out_in[step - 1, span, :].astype(f32)
                out_sum[step, span, :] = total.astype(bf16)
                half_copy(step, side).start()

    def small_copy(at):
        device = ({"seq": core}, {"seq": far})[at] if at < 2 else {"fsdp": mirrors[at - 2]}
        return remote(small_in.at[2 * at], small_in.at[2 * at + 1], small_sems, (at,), device)

    def small_step(at):
        small_copy(at).wait_recv()
        small_in[2 * at + 2] = small_in[2 * at] + small_in[2 * at + 1]

    term_step(1)
    columns.wait_recv()
    half_step(1)
    term_step(2)
    half_step(2)
    out_step(5)
    to_core[1].wait_recv()
    send_units(1)
    to_far.wait_recv()
    rows = hidden_ref[...].astype(f32)
    inverse = lax.rsqrt(jnp.mean(rows * rows, axis=-1, keepdims=True) + norm_eps)
    unit_rows = rows * inverse
    grad_rows = (
        block_rows(seq)[...].astype(f32) + seq_in[1].astype(f32) + seq_in[2].astype(f32)
    )
    small_in[0, 0:1, :] = jnp.sum(grad_rows * unit_rows, axis=0, keepdims=True)
    small_copy(0).start()
    grad_unit = grad_rows * gain_ref[0:1, :]
    grad_in_ref[...] = resid_grad_ref[...] + inverse * (
        grad_unit - unit_rows * jnp.mean(grad_unit * unit_rows, axis=-1, keepdims=True)
    )
    total_rounds = rounds + 2
    small_step(0)
    small_copy(1).start()
    done = 1
    send_units(2)
    for step in range(3, size):
        term_step(step)
        half_step(step)
        if done < total_rounds:
            small_step(done)
            done += 1
            if done < total_rounds:
                small_copy(done).start()
        if step == 4:
            send_units(2)
        if step % 2 == 0:
            pass_units(2)
    while done < total_rounds:
        small_step(done)
        done += 1
        if done < total_rounds:
            small_copy(done).start()
    small_ref[...] = small_in[2 * total_rounds]
    source_chip = here(me)
    for side in range(2):
        span = pl.ds(side * term_half, term_half)
        start = me * depth + side * term_half
        term_copy(size - 1, side).wait_recv()
        shard[span, :] = (
            term_qkv[pl.ds(pl.multiple_of(start, 16), term_half), :].astype(f32)
            + qkv_in[size - 1, span, :].astype(f32)
        ).astype(bf16)

        @pl.when(source_chip)
        def _():
            half_copy(size - 1, side).wait_recv()
            half_shard[span, :] = (
                out_columns[half_rows(me, side), :].astype(f32)
                + out_in[size - 1, span, :].astype(f32)
            ).astype(bf16)

    def shard_copy(source, at, block_at, target):
        return remote(source, shard_all.at[block_at], shard_sems, (at,), {"seq": target})

    def half_move(source, at, target):
        return remote(source, half_all.at[seq % 2], shard_sems, (at,), {"seq": target})

    shard_far = shard_copy(shard, 0, seq, far)
    shard_core = shard_copy(shard, 1, seq, core)
    shard_pass = shard_copy(shard_all.at[far], 2, far, core)
    half_far = half_move(half_shard, 3, far)
    half_core = half_move(half_shard, 4, core)
    half_pass = half_move(half_all.at[seq % 2], 5, core)
    shard_far.start()
    shard_core.start()

    @pl.when(source_chip)
    def _():
        half_far.start()
        half_core.start()
        half_all[seq % 2] = half_shard[...]

    send_units(2)
    shard_all[seq] = shard[...]
    out_step(6)
    shard_far.wait_recv()
    shard_pass.start()

    @pl.when(jnp.logical_not(source_chip))
    def _():
        half_far.wait_recv()
        half_pass.start()

    pass_units(3)
    out_step(7)
    pass_units(3)
    out_finish()
    shard_core.wait_recv()
    shard_pass.wait_recv()
    shard_store = pltpu.make_async_copy(shard_all, shards_ref, load_sems.at[1])
    shard_store.start()

    @pl.when(source_chip)
    def _():
        half_core.wait_recv()
        half_core.wait_send()
        half_far.wait_send()

    @pl.when(jnp.logical_not(source_chip))
    def _():
        half_pass.wait_recv()
        half_pass.wait_send()

    half_store = pltpu.make_async_copy(half_all, halves_ref, load_sems.at[2])
    half_store.start()
    for step in range(1, size):
        for side in range(2):
            term_copy(step, side).wait_send()

            @pl.when(here(owner_of(step, side)))
            def _():
                half_copy(step, side).wait_send()

    for copy in [unit_share(at) for at in range(3 * CHUNKS)] + [
        gate_pass(at) for at in range(CHUNKS)
    ]:
        copy.wait_send()
        copy.wait_recv()
    for at in range(chunks):
        unit_pass(at).wait_recv()
        unit_copy(at).wait_send()
        unit_pass(at).wait_send()
    for at in range(total_rounds):
        small_copy(at).wait_send()
    for copy in to_core + [to_far, columns, shard_far, shard_core, shard_pass]:
        copy.wait_send()
    for copy in (to_far_grads, to_core_grads, passed_grads):
        copy.wait_send()
    shard_store.wait()
    half_store.wait()


def attend_group_backward(
    heads,
    attended,
    logs,
    proj,
    weight,
    normed,
    trig,
    hidden,
    resid_grad,
    gain,
    gain_grad,
    resid,
    outs,
    units,
    far_gate,
):
    size = lax.axis_size("fsdp")
    groups = lax.axis_size("seq")
    length = heads.shape[0]
    tokens, width = hidden.shape
    used = heads.shape[1]
    own = attended.shape[1]
    depth = width // size
    rounds = size.bit_length() + 1
    bf16, f32 = jnp.bfloat16, jnp.float32
    anywhere = pl.BlockSpec(memory_space=pl.ANY)
    inside = pl.BlockSpec(memory_space=pltpu.VMEM)
    dma = pltpu.SemaphoreType.DMA
    vmem = pltpu.VMEM
    return pl.pallas_call(
        functools.partial(attend_backward_kernel, size),
        out_shape=(
            jax.ShapeDtypeStruct((tokens, width), f32),
            jax.ShapeDtypeStruct((tokens, width), bf16),
            jax.ShapeDtypeStruct((8, width), f32),
            jax.ShapeDtypeStruct((groups, depth, used), bf16),
            jax.ShapeDtypeStruct((2, depth, width // 2), bf16),
            jax.ShapeDtypeStruct((2,) + units.shape[1:], bf16),
            jax.ShapeDtypeStruct(units.shape, bf16),
            jax.ShapeDtypeStruct(far_gate.shape, bf16),
        ),
        in_specs=[inside] * 11 + [anywhere] * 4,
        out_specs=(inside, inside, inside) + (anywhere,) * 5,
        input_output_aliases={13: 6, 14: 7},
        scratch_shapes=[
            vmem((groups, tokens, width), bf16),
            vmem((length, own), bf16),
            vmem((length, used), bf16),
            vmem((length, HEAD_DIM), f32),
            vmem((length, HEAD_DIM), f32),
            vmem((length, width), bf16),
            vmem((width, used), bf16),
            vmem((own, width), bf16),
            vmem((2 * own, width // 2), bf16),
            vmem((size, depth, used), bf16),
            vmem((size, depth, width // 2), bf16),
            vmem((size, depth, used), bf16),
            vmem((size, depth, width // 2), bf16),
            vmem((depth, used), bf16),
            vmem((groups, depth, used), bf16),
            vmem((depth, width // 2), bf16),
            vmem((2, depth, width // 2), bf16),
            vmem((2, tokens, width), bf16),
            vmem((size, tokens, width), bf16),
            vmem((2, tokens, width), bf16),
            vmem((tokens, width), f32),
            vmem((3, tokens, width), bf16),
            vmem((tokens, width), bf16),
            vmem((2 * rounds + 1, 8, width), f32),
            dma((3,)),
            dma((2, 2)),
            dma((2, 2, size)),
            dma((2, 2, 2, size)),
            dma((2, 1)),
            dma((2, 3)),
            dma((2, 6)),
            dma((2, rounds)),
            dma((2, 2 * CHUNKS)),
            dma((2, 2 * CHUNKS)),
            dma((2, 3 * CHUNKS)),
            dma((2, CHUNKS)),
            dma((2, 3)),
        ],
        compiler_params=pltpu.CompilerParams(
            collective_id=2, has_side_effects=True, vmem_limit_bytes=VMEM_BYTES
        ),
        name="attend_backward",
    )(
        heads,
        attended,
        logs,
        proj,
        weight,
        normed,
        trig,
        hidden,
        resid_grad,
        gain,
        gain_grad,
        resid,
        outs,
        units,
        far_gate,
    )


def finish_kernel(
    sums_ref,
    far_gate_ref,
    far_ref,
    grad_in_ref,
    hidden_ref,
    shards_ref,
    halves_ref,
    gate_out,
    up_out,
    down_out,
    grad_in_out,
    hidden_out,
    qkv_out,
    proj_out,
):
    f32 = jnp.float32
    gate_out[...] = sums_ref[0].astype(f32) + far_gate_ref[...].astype(f32)
    up_out[...] = sums_ref[1].astype(f32) + far_ref[0].astype(f32)
    down_out[...] = sums_ref[2].astype(f32) + far_ref[1].astype(f32)
    grad_in_out[...] = grad_in_ref[...]
    hidden_out[...] = hidden_ref[...]
    groups, _, used = shards_ref.shape
    own = used - 2 * HEAD_DIM
    for at in range(groups):
        qkv_out[:, at * own : (at + 1) * own] = shards_ref[at, :, :own].astype(f32)
    for which in range(2):
        lanes = slice(own + which * HEAD_DIM, own + (which + 1) * HEAD_DIM)
        for head in range(KV_HEADS):
            at = groups * own + (which * KV_HEADS + head) * HEAD_DIM
            qkv_out[:, at : at + HEAD_DIM] = shards_ref[2 * head, :, lanes].astype(
                f32
            ) + shards_ref[2 * head + 1, :, lanes].astype(f32)
    half = halves_ref.shape[2]
    for which in range(2):
        proj_out[:, which * half : (which + 1) * half] = halves_ref[which].astype(f32)


def finish_totals(unit_sums, far_gate, far_sums, grad_in, hidden, shards, halves):
    f32, bf16 = jnp.float32, jnp.bfloat16
    _, units, width = unit_sums.shape
    groups, depth, used = shards.shape
    joint = groups * (used - 2 * HEAD_DIM) + 2 * KV_HEADS * HEAD_DIM
    tokens = grad_in.shape[0]
    steps, few = 5, 4

    def spec(*dims, many=False):
        lead = len(dims) - 2
        return pl.BlockSpec(
            dims,
            lambda at: (0,) * lead + (at if many else jnp.minimum(at, few - 1), 0),
        )

    rows = units // steps
    return pl.pallas_call(
        finish_kernel,
        grid=(steps,),
        out_shape=(
            jax.ShapeDtypeStruct((units, width), f32),
            jax.ShapeDtypeStruct((units, width), f32),
            jax.ShapeDtypeStruct((units, width), f32),
            jax.ShapeDtypeStruct((tokens, width), f32),
            jax.ShapeDtypeStruct((tokens, width), bf16),
            jax.ShapeDtypeStruct((depth, joint), f32),
            jax.ShapeDtypeStruct((depth, width), f32),
        ),
        in_specs=[
            spec(3, rows, width, many=True),
            spec(rows, width, many=True),
            spec(2, rows, width, many=True),
            spec(tokens // few, width),
            spec(tokens // few, width),
            spec(groups, depth // few, used),
            spec(2, depth // few, width // 2),
        ],
        out_specs=(
            spec(rows, width, many=True),
            spec(rows, width, many=True),
            spec(rows, width, many=True),
            spec(tokens // few, width),
            spec(tokens // few, width),
            spec(depth // few, joint),
            spec(depth // few, width),
        ),
        compiler_params=pltpu.CompilerParams(vmem_limit_bytes=VMEM_BYTES),
        name="finish_totals",
    )(unit_sums, far_gate, far_sums, grad_in, hidden, shards, halves)


def kernels_fit(hidden_in, positions, attn_gain, qkv_weight, qkv_bias, out_weight, *rest):
    size, groups = lax.axis_size("fsdp"), lax.axis_size("seq")
    _, tokens, width = hidden_in.shape
    units = rest[1].shape[0]
    if groups != 4 or size != 8 or tokens % 256 or units % 160 or width % 512:
        return False
    if (width // size) % 32 or qkv_bias.shape[0] > 256 or KV_HEADS != 2:
        return False
    rows = tokens * width * (4 * size + 34)
    return rows + units * (18 * width + 6 * tokens) < 64_000_000


def per_device_kernels(
    hidden_in,
    positions,
    attn_gain,
    qkv_weight,
    qkv_bias,
    out_weight,
    mlp_gain,
    gate_weight,
    up_weight,
    down_weight,
    cotangent,
):
    f32, bf16 = jnp.float32, jnp.bfloat16
    groups = lax.axis_size("seq")
    size = lax.axis_size("fsdp")
    _, tokens, width = hidden_in.shape
    length = tokens * groups
    lane = jnp.arange(HEAD_DIM)
    frequency = jnp.exp(
        -((lane % (HEAD_DIM // 2)).astype(f32) * 2.0 / HEAD_DIM) * math.log(rope_base)
    )
    angles = positions[0].astype(f32)[:, None] * frequency[None, :]
    trig = jnp.where(lane[None, :] < HEAD_DIM // 2, jnp.cos(angles), jnp.sin(angles))
    small = jnp.concatenate(
        [
            jnp.pad(row.astype(f32), (0, 256 - row.shape[0]))
            for row in (attn_gain, mlp_gain, qkv_bias)
        ]
    )[None]
    (
        normed_one,
        heads,
        attended,
        logs,
        weight,
        proj,
        trig_all,
        gains,
        normed_two,
        residual,
        all_cots,
    ) = attend_group(
        hidden_in[0], trig, qkv_weight, out_weight, small, qkv_bias.shape[0], cotangent[0]
    )
    shard = width // size
    outs, grad_residual, term_gain_two, unit_sums, far_gate = mlp_ring(
        normed_two,
        residual,
        gains,
        all_cots.reshape(size * tokens, width),
        gate_weight,
        up_weight,
        down_weight,
    )
    (
        grad_rows,
        hidden_out,
        smalls,
        shards,
        halves,
        far_sums,
        unit_sums,
        far_gate,
    ) = attend_group_backward(
        heads,
        attended,
        logs,
        proj,
        weight,
        normed_one,
        trig_all.reshape(length, HEAD_DIM),
        hidden_in[0],
        grad_residual,
        gains,
        term_gain_two,
        residual,
        outs,
        unit_sums,
        far_gate,
    )
    grad_gate, grad_up, grad_down, grad_rows, hidden_out, grad_qkv, grad_out = finish_totals(
        unit_sums, far_gate, far_sums, grad_rows, hidden_out, shards, halves
    )
    me = lax.axis_index("fsdp")
    bias_sums = jnp.concatenate([smalls[2], smalls[3, : 2 * KV_HEADS * HEAD_DIM]])
    bias_shard = qkv_bias.shape[0]
    return (
        hidden_out[None],
        grad_rows[None],
        lax.dynamic_slice_in_dim(smalls[0], me * shard, shard),
        grad_qkv,
        lax.dynamic_slice_in_dim(bias_sums, me * bias_shard, bias_shard),
        grad_out,
        lax.dynamic_slice_in_dim(smalls[1], me * shard, shard),
        grad_gate,
        grad_up,
        grad_down,
    )


def per_device_gathered(
    hidden_in,
    positions,
    attn_gain,
    qkv_weight,
    qkv_bias,
    out_weight,
    mlp_gain,
    gate_weight,
    up_weight,
    down_weight,
    cotangent,
):
    groups = lax.axis_size("seq")
    group_heads = HEADS // groups
    repeat = groups // KV_HEADS
    tokens = hidden_in.shape[1]
    width_query = HEADS * HEAD_DIM
    width_key = KV_HEADS * HEAD_DIM
    residual = hidden_in[0].astype(jnp.float32)
    cosine, sine = rope_tables(positions[0])
    gains_one, gains_two, qkv_full, bias_full, out_full = (
        lax.all_gather(attn_gain, "fsdp", axis=0, tiled=True),
        lax.all_gather(mlp_gain, "fsdp", axis=0, tiled=True),
        lax.all_gather(qkv_weight, "fsdp", axis=0, tiled=True),
        lax.all_gather(qkv_bias, "fsdp", axis=0, tiled=True),
        lax.all_gather(out_weight, "fsdp", axis=0, tiled=True),
    )
    gain_one = gains_one.astype(jnp.float32)
    gain_two = gains_two.astype(jnp.float32)
    unit_one, inverse_one, normed_one = norm_forward(residual, gain_one)
    qkv_mixed = jnp.dot(
        normed_one, qkv_full, preferred_element_type=jnp.float32
    ) + bias_full.astype(jnp.float32)
    query_part = qkv_mixed[:, :width_query].reshape(tokens, HEADS, HEAD_DIM)
    key_part = qkv_mixed[:, width_query : width_query + width_key].reshape(
        tokens, KV_HEADS, HEAD_DIM
    )
    value_part = qkv_mixed[:, width_query + width_key :].reshape(tokens, KV_HEADS, HEAD_DIM)
    queries = (
        rotate(query_part, cosine, sine)
        .astype(jnp.bfloat16)
        .reshape(tokens, groups, group_heads * HEAD_DIM)
    )
    keys_rep = jnp.repeat(rotate(key_part, cosine, sine).astype(jnp.bfloat16), repeat, axis=1)
    values_rep = jnp.repeat(value_part.astype(jnp.bfloat16), repeat, axis=1)
    head_queries, head_keys, head_values = (
        lax.all_to_all(queries, "seq", split_axis=1, concat_axis=0, tiled=True),
        lax.all_to_all(keys_rep, "seq", split_axis=1, concat_axis=0, tiled=True),
        lax.all_to_all(values_rep, "seq", split_axis=1, concat_axis=0, tiled=True),
    )
    head_queries = head_queries.reshape(-1, group_heads, HEAD_DIM)
    head_keys = head_keys.reshape(-1, HEAD_DIM)
    head_values = head_values.reshape(-1, HEAD_DIM)
    attended, log_totals = attend_forward(head_queries, head_keys, head_values)
    returned = lax.all_to_all(
        attended.reshape(-1, 1, group_heads * HEAD_DIM),
        "seq",
        split_axis=0,
        concat_axis=1,
        tiled=True,
    )
    attn_rows = returned.reshape(tokens, width_query)
    residual_two = residual + jnp.dot(attn_rows, out_full, preferred_element_type=jnp.float32)
    unit_two, inverse_two, normed_two = norm_forward(residual_two, gain_two)
    grad_output = cotangent[0].astype(jnp.float32)
    grad_mlp = grad_output.astype(jnp.bfloat16)
    all_rows = lax.all_gather(normed_two, "fsdp", axis=0, tiled=True)
    gate_pre = jnp.einsum("td,fd->tf", all_rows, gate_weight, preferred_element_type=jnp.float32)
    up_pre = jnp.einsum("td,fd->tf", all_rows, up_weight, preferred_element_type=jnp.float32)
    sigmoid_gate = jax.nn.sigmoid(gate_pre)
    activated = gate_pre * sigmoid_gate
    hidden = (activated * up_pre).astype(jnp.bfloat16)
    partial_out = jnp.dot(hidden, down_weight, preferred_element_type=jnp.float32)
    mlp_out = lax.psum_scatter(
        partial_out.astype(jnp.bfloat16), "fsdp", scatter_dimension=0, tiled=True
    ).astype(jnp.float32)
    all_grads = lax.all_gather(grad_mlp, "fsdp", axis=0, tiled=True)
    grad_hidden = jnp.einsum(
        "tm,fm->tf", all_grads, down_weight, preferred_element_type=jnp.float32
    )
    grad_gate = (
        grad_hidden * up_pre * sigmoid_gate * (1.0 + gate_pre * (1.0 - sigmoid_gate))
    ).astype(jnp.bfloat16)
    grad_up = (grad_hidden * activated).astype(jnp.bfloat16)
    partial_back = jnp.dot(grad_gate, gate_weight, preferred_element_type=jnp.float32) + jnp.dot(
        grad_up, up_weight, preferred_element_type=jnp.float32
    )
    grad_normed_two = lax.psum_scatter(partial_back, "fsdp", scatter_dimension=0, tiled=True)
    shard_gate = jnp.einsum("tf,td->fd", grad_gate, all_rows, preferred_element_type=jnp.float32)
    shard_up = jnp.einsum("tf,td->fd", grad_up, all_rows, preferred_element_type=jnp.float32)
    shard_down = jnp.einsum("tf,td->fd", hidden, all_grads, preferred_element_type=jnp.float32)
    hidden_out = (residual_two + mlp_out).astype(jnp.bfloat16)
    grad_norm_two, term_gain_two = norm_backward(grad_normed_two, unit_two, inverse_two, gain_two)
    grad_residual_two = grad_output + grad_norm_two
    grad_proj = grad_residual_two.astype(jnp.bfloat16)
    grad_attn_rows = jnp.einsum(
        "td,ed->te", grad_proj, out_full, preferred_element_type=jnp.float32
    ).astype(jnp.bfloat16)
    term_out = jnp.einsum("te,td->ed", attn_rows, grad_proj, preferred_element_type=jnp.float32)
    grad_heads = lax.all_to_all(
        grad_attn_rows.reshape(tokens, groups, group_heads * HEAD_DIM),
        "seq",
        split_axis=1,
        concat_axis=0,
        tiled=True,
    )
    grad_query, grad_keys, grad_values = attend_backward(
        head_queries,
        head_keys,
        head_values,
        log_totals,
        grad_heads.reshape(-1, group_heads, HEAD_DIM),
    )
    back_query, back_keys, back_values = (
        lax.all_to_all(
            grad_query.astype(jnp.bfloat16).reshape(-1, 1, group_heads * HEAD_DIM),
            "seq",
            split_axis=0,
            concat_axis=1,
            tiled=True,
        ),
        lax.all_to_all(
            grad_keys.astype(jnp.bfloat16)[:, None, :],
            "seq",
            split_axis=0,
            concat_axis=1,
            tiled=True,
        ),
        lax.all_to_all(
            grad_values.astype(jnp.bfloat16)[:, None, :],
            "seq",
            split_axis=0,
            concat_axis=1,
            tiled=True,
        ),
    )
    grad_query_rows = unrotate(
        back_query.reshape(tokens, HEADS, HEAD_DIM).astype(jnp.float32), cosine, sine
    )
    grad_key_rows = unrotate(
        jnp.sum(back_keys.astype(jnp.float32).reshape(tokens, KV_HEADS, repeat, HEAD_DIM), axis=2),
        cosine,
        sine,
    )
    grad_value_rows = jnp.sum(
        back_values.astype(jnp.float32).reshape(tokens, KV_HEADS, repeat, HEAD_DIM), axis=2
    )
    grad_mixed = jnp.concatenate(
        [
            grad_query_rows.reshape(tokens, width_query),
            grad_key_rows.reshape(tokens, width_key),
            grad_value_rows.reshape(tokens, width_key),
        ],
        axis=1,
    ).astype(jnp.bfloat16)
    term_qkv = jnp.einsum("td,tc->dc", normed_one, grad_mixed, preferred_element_type=jnp.float32)
    term_bias = jnp.sum(grad_mixed.astype(jnp.float32), axis=0)
    grad_normed_one = jnp.einsum(
        "tc,dc->td", grad_mixed, qkv_full, preferred_element_type=jnp.float32
    )
    grad_norm_one, term_gain_one = norm_backward(grad_normed_one, unit_one, inverse_one, gain_one)
    grad_rows = grad_residual_two + grad_norm_one
    shard_gain_one, shard_qkv, shard_bias, shard_out, shard_gain_two = (
        lax.psum_scatter(
            term_gain_one.astype(jnp.bfloat16), "fsdp", scatter_dimension=0, tiled=True
        ).astype(jnp.float32),
        lax.psum_scatter(
            term_qkv.astype(jnp.bfloat16), "fsdp", scatter_dimension=0, tiled=True
        ).astype(jnp.float32),
        lax.psum_scatter(
            term_bias.astype(jnp.bfloat16), "fsdp", scatter_dimension=0, tiled=True
        ).astype(jnp.float32),
        lax.psum_scatter(
            term_out.astype(jnp.bfloat16), "fsdp", scatter_dimension=0, tiled=True
        ).astype(jnp.float32),
        lax.psum_scatter(
            term_gain_two.astype(jnp.bfloat16), "fsdp", scatter_dimension=0, tiled=True
        ).astype(jnp.float32),
    )
    totals = (
        lax.psum(shard_gain_one.astype(jnp.bfloat16), "seq").astype(jnp.float32),
        lax.psum(shard_qkv.astype(jnp.bfloat16), "seq").astype(jnp.float32),
        lax.psum(shard_bias.astype(jnp.bfloat16), "seq").astype(jnp.float32),
        lax.psum(shard_out.astype(jnp.bfloat16), "seq").astype(jnp.float32),
        lax.psum(shard_gain_two.astype(jnp.bfloat16), "seq").astype(jnp.float32),
        lax.psum(shard_gate.astype(jnp.bfloat16), "seq").astype(jnp.float32),
        lax.psum(shard_up.astype(jnp.bfloat16), "seq").astype(jnp.float32),
        lax.psum(shard_down.astype(jnp.bfloat16), "seq").astype(jnp.float32),
    )
    return (
        hidden_out[None],
        grad_rows[None],
        totals[0],
        totals[1],
        totals[2],
        totals[3],
        totals[4],
        totals[5],
        totals[6],
        totals[7],
    )


def per_device(*arguments):
    return (per_device_kernels if kernels_fit(*arguments) else per_device_gathered)(*arguments)


def solution(mesh):
    placed = (
        P("fsdp", "seq", None),
        P("fsdp", "seq"),
        P("fsdp"),
        P("fsdp", None),
        P("fsdp"),
        P("fsdp", None),
        P("fsdp"),
        P("fsdp", None),
        P("fsdp", None),
        P("fsdp", None),
        P("fsdp", "seq", None),
    )
    return jax.shard_map(
        per_device,
        mesh=mesh,
        in_specs=placed,
        out_specs=(
            P("fsdp", "seq", None),
            P("fsdp", "seq", None),
            P("fsdp"),
            P("fsdp", None),
            P("fsdp"),
            P("fsdp", None),
            P("fsdp"),
            P("fsdp", None),
            P("fsdp", None),
            P("fsdp", None),
        ),
        check_vma=False,
    )
```

```python
import functools
import math

import jax
import jax.numpy as jnp
from jax import lax
from jax.experimental import pallas as pl
from jax.experimental.pallas import tpu as pltpu
from jax.sharding import PartitionSpec as P

HEADS = 12
KV_HEADS = 2
HEAD_DIM = 128


norm_eps = 1e-06
rope_base = 1000000.0


def rope_tables(position_row):
    half_dim = HEAD_DIM // 2
    frequency = jnp.exp(
        -(jnp.arange(half_dim, dtype=jnp.float32) * 2.0 / HEAD_DIM) * math.log(rope_base)
    )
    angles = position_row.astype(jnp.float32)[:, None] * frequency[None, :]
    angles = jnp.concatenate([angles, angles], axis=-1)
    return (jnp.cos(angles), jnp.sin(angles))


def rotate(values, cosine, sine):
    half_dim = values.shape[-1] // 2
    turned = jnp.concatenate([-values[..., half_dim:], values[..., :half_dim]], axis=-1)
    return values * cosine[:, None, :] + turned * sine[:, None, :]


def unrotate(grads_rot, cosine, sine):
    half_dim = grads_rot.shape[-1] // 2
    scaled = grads_rot * sine[:, None, :]
    return grads_rot * cosine[:, None, :] + jnp.concatenate(
        [scaled[..., half_dim:], -scaled[..., :half_dim]], axis=-1
    )


def norm_forward(values, gain):
    inverse = lax.rsqrt(jnp.mean(values * values, axis=-1, keepdims=True) + norm_eps)
    unit_rows = values * inverse
    return (unit_rows, inverse, (unit_rows * gain).astype(jnp.bfloat16))


def norm_backward(grad_normed, unit_rows, inverse, gain):
    grad_unit = grad_normed * gain
    grad_values = inverse * (
        grad_unit - unit_rows * jnp.mean(grad_unit * unit_rows, axis=-1, keepdims=True)
    )
    grad_gain = jnp.sum(grad_normed * unit_rows, axis=0)
    return (grad_values, grad_gain)


def masked_scores(queries, keys, block_start, block_rows):
    length = keys.shape[0]
    query_block = lax.dynamic_slice_in_dim(queries, block_start, block_rows, 0)
    scores = jnp.einsum(
        "bhd,ld->hbl", query_block, keys, preferred_element_type=jnp.float32
    ) * HEAD_DIM ** (-0.5)
    row_index = block_start + jnp.arange(block_rows)
    column_index = jnp.arange(length)
    allowed = column_index[None, :] <= row_index[:, None]
    return (query_block, jnp.where(allowed[None], scores, -1e30))


def attend_forward(queries, keys, values):
    length = keys.shape[0]
    block_rows = min(512, length)
    block_count = length // block_rows

    def one_block(block_start):
        query_block, scores = masked_scores(queries, keys, block_start, block_rows)
        row_max = jnp.max(scores, axis=-1, keepdims=True)
        exponent = jnp.exp(scores - row_max)
        row_total = jnp.sum(exponent, axis=-1, keepdims=True)
        probability = (exponent / row_total).astype(jnp.bfloat16)
        result = jnp.einsum("hbl,ld->bhd", probability, values, preferred_element_type=jnp.float32)
        return (result.astype(jnp.bfloat16), (row_max + jnp.log(row_total))[..., 0])

    results, log_totals = lax.map(one_block, jnp.arange(block_count) * block_rows)
    return (results.reshape(length, queries.shape[1], queries.shape[2]), log_totals)


def attend_backward(queries, keys, values, log_totals, grad_out):
    length = keys.shape[0]
    block_rows = min(512, length)
    block_count = length // block_rows
    score_scale = HEAD_DIM ** (-0.5)

    def one_block(running, inputs):
        grad_keys, grad_values = running
        block_start, log_block = inputs
        query_block, scores = masked_scores(queries, keys, block_start, block_rows)
        grad_block = lax.dynamic_slice_in_dim(grad_out, block_start, block_rows, 0)
        probability = jnp.exp(scores - log_block[..., None])
        grad_probs = jnp.einsum(
            "bhd,ld->hbl", grad_block, values, preferred_element_type=jnp.float32
        )
        row_delta = jnp.sum(probability * grad_probs, axis=-1, keepdims=True)
        grad_scores = (probability * (grad_probs - row_delta)).astype(jnp.bfloat16)
        grad_query = (
            jnp.einsum("hbl,ld->bhd", grad_scores, keys, preferred_element_type=jnp.float32)
            * score_scale
        )
        grad_keys = (
            grad_keys
            + jnp.einsum(
                "hbl,bhd->ld", grad_scores, query_block, preferred_element_type=jnp.float32
            )
            * score_scale
        )
        grad_values = grad_values + jnp.einsum(
            "hbl,bhd->ld",
            probability.astype(jnp.bfloat16),
            grad_block,
            preferred_element_type=jnp.float32,
        )
        return ((grad_keys, grad_values), grad_query)

    zero_rows = jnp.zeros((length, keys.shape[1]), jnp.float32)
    (grad_keys, grad_values), grad_query = lax.scan(
        one_block, (zero_rows, zero_rows), (jnp.arange(block_count) * block_rows, log_totals)
    )
    return (grad_query.reshape(queries.shape), grad_keys, grad_values)


MESH = pl.DeviceIdType.MESH
VMEM_BYTES = 67_000_000
NN = (((1,), (0,)), ((), ()))
NT = (((1,), (1,)), ((), ()))
TN = (((0,), (0,)), ((), ()))


def matmul(left, right, dims):
    return lax.dot_general(left, right, dims, preferred_element_type=jnp.float32)


def ring_place(index, size):
    side = index % 2
    return (index // 2) * (1 - side) + (size - 1 - index // 2) * side


def ring_member(place, size):
    side = place // (size // 2)
    return 2 * (place * (1 - side) + (size - 1 - place) * side) + side


def seq_partners(seq):
    core = seq + 1 - 2 * (seq % 2)
    far = (seq + 2) % 4
    return core, far, (core + 2) % 4


def greet(targets):
    barrier = pltpu.get_barrier_semaphore()
    for target in targets:
        pl.semaphore_signal(barrier, inc=1, device_id=target, device_id_type=MESH)
    pl.semaphore_wait(barrier, len(targets))


def for_blocks(width, block, body):
    for at in range(0, width, block):
        body(pl.ds(at, min(block, width - at)))


def loop_blocks(width, block, body):
    @pl.loop(0, width // block)
    def _(at):
        body(pl.ds(pl.multiple_of(at * block, block), block))


def turn_tables(trig):
    lane = lax.broadcasted_iota(jnp.int32, trig.shape, 1)
    swapped = pltpu.roll(trig, HEAD_DIM // 2, 1)
    first = lane < HEAD_DIM // 2
    return jnp.where(first, trig, swapped), jnp.where(first, -swapped, trig)


def head_columns(at):
    return slice(at * HEAD_DIM, (at + 1) * HEAD_DIM)


def causal(scores, start):
    rows = lax.broadcasted_iota(jnp.int32, scores.shape, 0) + start
    columns = lax.broadcasted_iota(jnp.int32, scores.shape, 1)
    return jnp.where(columns <= rows, scores, -1e30)


def inverse_of(values):
    return lax.rsqrt(jnp.mean(values * values, axis=-1, keepdims=True) + norm_eps)


def attend_forward_kernel(
    size,
    block,
    bias_share,
    rows_ref,
    trig_ref,
    qkv_ref,
    proj_ref,
    small_ref,
    cot_ref,
    normed_out,
    heads_out,
    attended_out,
    log_out,
    piece_out,
    proj_out,
    trig_out,
    gains_out,
    normed_two_out,
    resid_out,
    cots_out,
    rows_all,
    trig_all,
    pieces,
    proj,
    smalls,
    cots,
    normed,
    heads,
    attended,
    logs,
    part,
    gains,
    bias,
    resid,
    seq_in,
    far_sum,
    normed_two,
    load_sems,
    column_sems,
    store_sems,
    ring_sems,
    small_sems,
    cot_sems,
    cot_store_sems,
    seq_sems,
    sum_sems,
    proj_send,
    proj_recv,
):
    f32, bf16 = jnp.float32, jnp.bfloat16
    depth = qkv_ref.shape[0]
    tokens, width = rows_ref.shape
    half = depth // 2
    cot_half = tokens // 2
    own = proj.shape[0]
    used = own + 2 * HEAD_DIM
    count = own // HEAD_DIM
    length = part.shape[0]
    per_group = own // depth
    scale = HEAD_DIM**-0.5
    me = lax.axis_index("fsdp")
    seq = lax.axis_index("seq")
    place = ring_place(me, size)
    right = ring_member((place + 1) % size, size)
    left = ring_member((place + size - 1) % size, size)
    core, far, diagonal = seq_partners(seq)
    ring = ({"fsdp": right}, {"fsdp": left})

    def remote(source, target, sems, at, device):
        return pltpu.make_async_remote_copy(
            src_ref=source,
            dst_ref=target,
            send_sem=sems.at[(0,) + at],
            recv_sem=sems.at[(1,) + at],
            device_id=device,
            device_id_type=MESH,
        )

    width_query = 4 * own
    own_lane = pl.multiple_of(seq * own, HEAD_DIM)
    kv_lane = pl.multiple_of(width_query + (seq // 2) * HEAD_DIM, HEAD_DIM)
    value_lane = pl.multiple_of(kv_lane + KV_HEADS * HEAD_DIM, HEAD_DIM)
    my_rows = pl.ds(pl.multiple_of(me * depth, 16), depth)
    column_loads = [
        pltpu.make_async_copy(
            source.at[:, pl.ds(lane_at, lanes)],
            pieces.at[my_rows, pl.ds(target, lanes)],
            column_sems.at[at],
        )
        for at, (source, lane_at, target, lanes) in enumerate(
            (
                (qkv_ref, own_lane, 0, own),
                (qkv_ref, kv_lane, own, HEAD_DIM),
                (qkv_ref, value_lane, own + HEAD_DIM, HEAD_DIM),
                (proj_ref, own_lane, used, own),
            )
        )
    ]
    loads = [
        pltpu.make_async_copy(trig_ref, trig_all.at[seq], load_sems.at[0]),
        pltpu.make_async_copy(rows_ref, rows_all.at[seq], load_sems.at[1]),
        pltpu.make_async_copy(cot_ref, cots.at[me], load_sems.at[2]),
    ]
    for load in column_loads + loads:
        load.start()
    smalls[me] = jnp.zeros(smalls.shape[1:], f32)
    for at in range(3):
        smalls[me, at : at + 1, :] = small_ref[:, at * 256 : (at + 1) * 256]
    greet(ring + ({"seq": core}, {"seq": far}, {"seq": diagonal}))

    def piece_of(step, side):
        return ring_member((place + size - step if side == 0 else place + step) % size, size)

    def ring_copy(step, side, sub):
        part_rows = half // 2
        start = piece_of(step, side) * depth + side * half + sub * part_rows
        span = pieces.at[pl.ds(pl.multiple_of(start, 16), part_rows)]
        return remote(span, span, ring_sems, (side, sub, step), ring[side])

    def small_copy(step):
        span = smalls.at[piece_of(step, 0)]
        return remote(span, span, small_sems, (step,), ring[0])

    def cot_copy(step, side, sub):
        part_rows = cot_half // 2
        start = side * cot_half + sub * part_rows
        span = cots.at[piece_of(step, side), pl.ds(start, part_rows)]
        return remote(span, span, cot_sems, (side, sub, step), ring[side])

    def cot_store(step, side):
        span = (piece_of(step, side), pl.ds(side * cot_half, cot_half))
        return pltpu.make_async_copy(
            cots.at[span], cots_out.at[span], cot_store_sems.at[side, step]
        )

    def seq_copy(which, block_at, target, at):
        span = (rows_all, trig_all)[which].at[block_at]
        return remote(span, span, seq_sems, (which, at), {"seq": target})

    def proj_part(step, side):
        at = piece_of(step, side)
        row = pl.multiple_of((at % per_group) * depth + side * half, 16)
        source = pieces.at[
            pl.ds(pl.multiple_of(at * depth + side * half, 16), half), pl.ds(used, own)
        ]
        target = proj.at[pl.ds(row, half), pl.ds(pl.multiple_of(seq * own, 128), own)]
        return at, at // per_group, source, target

    def proj_copy(step, side):
        at, owner, source, target = proj_part(step, side)
        return owner, pltpu.make_async_remote_copy(
            src_ref=source,
            dst_ref=target,
            send_sem=proj_send.at[side, step],
            recv_sem=proj_recv.at[seq, at % per_group, side],
            device_id={"seq": owner},
            device_id_type=MESH,
        )

    def proj_act(step, side, action):
        owner, copy = proj_copy(step, side)

        @pl.when(owner != seq)
        def _():
            if action == "start":
                copy.start()
            else:
                copy.wait_send()

        @pl.when(owner == seq)
        def _():
            _, _, source, target = proj_part(step, side)
            kept = pltpu.make_async_copy(source, target, proj_send.at[side, step])
            if action == "start":
                kept.start()
            else:
                kept.wait()

    stores = []

    def store(source, target):
        stores.append(pltpu.make_async_copy(source, target, store_sems.at[len(stores)]))
        stores[-1].start()

    def cot_pump(step):
        for sub in range(2):
            for side in range(2):
                if step >= 1:
                    cot_copy(step - 1, side, sub).wait_recv()
                if step < size - 1:
                    cot_copy(step, side, sub).start()
        for side in range(2):
            cot_store(step, side).start()

    for load in column_loads:
        load.wait()
    for sub in range(2):
        for side in range(2):
            ring_copy(0, side, sub).start()
    small_copy(0).start()
    for which in (1, 0):
        loads[1 - which].wait()
        seq_copy(which, seq, far, 1).start()
        seq_copy(which, seq, core, 0).start()
    for side in range(2):
        proj_act(0, side, "start")
    loads[2].wait()

    for step in range(size - 1):
        for sub in range(2):
            for side in range(2):
                ring_copy(step, side, sub).wait_recv()
                if step < size - 2:
                    ring_copy(step + 1, side, sub).start()
        small_copy(step).wait_recv()
        if step < size - 2:
            small_copy(step + 1).start()
        if step == 1:
            cot_pump(0)
        for side in range(2):
            proj_act(step + 1, side, "start")
        if step == min(1, size - 2):
            for which in (1, 0):
                seq_copy(which, seq, far, 1).wait_recv()
                seq_copy(which, far, core, 2).start()

    gathered = jnp.zeros((8, width), f32)
    small_width = smalls.shape[2]
    for at in range(size):
        held = smalls[at]
        lane = lax.broadcasted_iota(jnp.int32, held.shape, 1)
        wide = jnp.concatenate(
            [
                jnp.where(lane < depth, held, 0.0),
                jnp.zeros((8, width - small_width), f32),
            ],
            axis=1,
        )
        gathered += pltpu.roll(wide, at * depth, 1) if at else wide
        bias[:, at * bias_share : (at + 1) * bias_share] = held[:, :bias_share]
    gains[...] = gathered
    gain_one = gathered[0:1, :]
    gain_two = gathered[1:2, :]
    store(gains, gains_out)
    for which in (1, 0):
        seq_copy(which, seq, core, 0).wait_recv()
        seq_copy(which, far, core, 2).wait_recv()
    store(pieces, piece_out)
    store(trig_all, trig_out)

    own_bias = jnp.concatenate(
        [
            bias[2:3, pl.ds(own_lane, own)],
            bias[2:3, pl.ds(kv_lane, HEAD_DIM)],
            bias[2:3, pl.ds(value_lane, HEAD_DIM)],
        ],
        axis=1,
    )
    for at in range(length // block):
        span = slice(at * block, (at + 1) * block)
        rows = rows_all[at].astype(f32)
        normed[span, :] = (rows * inverse_of(rows) * gain_one).astype(bf16)
        mixed = matmul(normed[span, :], pieces[:, :used], NN) + own_bias
        cosine, sine = turn_tables(trig_all[at])
        for head in range(count + 1):
            turned = mixed[:, head_columns(head)]
            heads[span, head_columns(head)] = (
                turned * cosine + pltpu.roll(turned, HEAD_DIM // 2, 1) * sine
            ).astype(bf16)
        heads[span, head_columns(count + 1)] = mixed[:, head_columns(count + 1)].astype(bf16)
        if at == 0:
            cot_pump(1)
    store(normed, normed_out)
    store(heads, heads_out)

    for peer in (core, far, diagonal):
        for at in range(per_group):
            for side in range(2):
                pltpu.make_async_remote_copy(
                    src_ref=pieces.at[pl.ds(0, half), pl.ds(used, own)],
                    dst_ref=proj.at[pl.ds(0, half), pl.ds(0, own)],
                    send_sem=proj_send.at[side, 0],
                    recv_sem=proj_recv.at[peer, at, side],
                    device_id={"seq": peer},
                    device_id_type=MESH,
                ).wait_recv()
    for step in range(size):
        for side in range(2):
            proj_act(step, side, "wait")
    store(proj, proj_out)

    lane = lax.broadcasted_iota(jnp.int32, (block, HEAD_DIM), 1)
    for start in range(0, length, block):
        span = slice(start, start + block)
        seen = slice(0, start + block)
        logs[span, :] = jnp.zeros((block, HEAD_DIM), f32)

        @pl.loop(0, count)
        def _(at):
            head = pl.ds(pl.multiple_of(at * HEAD_DIM, HEAD_DIM), HEAD_DIM)
            scores = causal(
                matmul(heads[span, head], heads[seen, head_columns(count)], NT) * scale, start
            )
            top = jnp.max(scores, axis=-1, keepdims=True)
            exponent = jnp.exp(scores - top)
            total = jnp.sum(exponent, axis=-1, keepdims=True)
            probability = (exponent / total).astype(bf16)
            attended[span, head] = matmul(
                probability, heads[seen, head_columns(count + 1)], NN
            ).astype(bf16)
            logs[span, :] = jnp.where(lane == at, top + jnp.log(total), logs[span, :])

        if 2 * (start + block) == length:
            cot_pump(2)
    store(attended, attended_out)
    store(logs, log_out)

    def out_part(span):
        part[:, span] = matmul(attended[...], proj[:, span], NN).astype(bf16)

    for_blocks(width, 512, out_part)

    def part_rows(at):
        return part.at[pl.ds(pl.multiple_of(at * tokens, tokens), tokens)]

    to_core = [
        remote(part_rows(diagonal), seq_in.at[0], sum_sems, (0,), {"seq": core}),
        remote(part_rows(core), seq_in.at[1], sum_sems, (1,), {"seq": core}),
    ]
    to_far = remote(far_sum, seq_in.at[2], sum_sems, (2,), {"seq": far})
    for copy in to_core:
        copy.start()
    cot_pump(3)
    to_core[0].wait_recv()
    far_sum[...] = (part_rows(far)[...].astype(f32) + seq_in[0].astype(f32)).astype(bf16)
    to_far.start()
    to_core[1].wait_recv()
    resid[...] = (
        part_rows(seq)[...].astype(f32) + seq_in[1].astype(f32) + rows_all[seq].astype(f32)
    )
    cot_pump(4)
    cot_pump(5)
    to_far.wait_recv()
    resid[...] += seq_in[2].astype(f32)
    store(resid, resid_out)
    normed_two[...] = (resid[...] * inverse_of(resid[...]) * gain_two).astype(bf16)
    store(normed_two, normed_two_out)
    for step in range(6, size):
        cot_pump(step)
    for step in range(size):
        for side in range(2):
            cot_store(step, side).wait()

    for step in range(size - 1):
        for side in range(2):
            for sub in range(2):
                ring_copy(step, side, sub).wait_send()
                cot_copy(step, side, sub).wait_send()
        small_copy(step).wait_send()
    for which in (1, 0):
        seq_copy(which, seq, core, 0).wait_send()
        seq_copy(which, seq, far, 1).wait_send()
        seq_copy(which, far, core, 2).wait_send()
    for copy in to_core + [to_far]:
        copy.wait_send()
    for copy in stores:
        copy.wait()


def attend_group(rows, trig, qkv_weight, out_weight, small, bias_share, cots):
    size = lax.axis_size("fsdp")
    groups = lax.axis_size("seq")
    tokens, width = rows.shape
    depth = qkv_weight.shape[0]
    own = width // groups
    used = own + 2 * HEAD_DIM
    joint = used + own
    length = tokens * groups
    f32, bf16 = jnp.float32, jnp.bfloat16
    dma = pltpu.SemaphoreType.DMA
    anywhere = pl.BlockSpec(memory_space=pl.ANY)
    normed = ((length, width), bf16)
    heads = ((length, used), bf16)
    attended = ((length, own), bf16)
    logs = ((length, HEAD_DIM), f32)
    pieces = ((width, joint), bf16)
    proj = ((own, width), bf16)
    trig_all = ((groups,) + trig.shape, f32)
    gains = ((8, width), f32)
    rows_all = ((groups, tokens, width), bf16)
    own_rows = ((tokens, width), bf16)
    resid = ((tokens, width), f32)
    cots_all = ((size, tokens, width), bf16)
    outs = (
        normed, heads, attended, logs, pieces, proj, trig_all, gains, own_rows, resid, cots_all
    )
    held = (
        rows_all,
        trig_all,
        pieces,
        proj,
        ((size, 8, 256), f32),
        cots_all,
        normed,
        heads,
        attended,
        logs,
        normed,
        gains,
        ((8, size * bias_share), f32),
        resid,
        ((3, tokens, width), bf16),
        own_rows,
        own_rows,
    )
    return pl.pallas_call(
        functools.partial(attend_forward_kernel, size, tokens, bias_share),
        out_shape=tuple(jax.ShapeDtypeStruct(*shape) for shape in outs),
        in_specs=[anywhere] * 4 + [pl.BlockSpec(memory_space=pltpu.VMEM), anywhere],
        out_specs=(anywhere,) * len(outs),
        scratch_shapes=[pltpu.VMEM(*shape) for shape in held]
        + [
            dma((3,)),
            dma((4,)),
            dma((len(outs),)),
            dma((2, 2, 2, size)),
            dma((2, size)),
            dma((2, 2, 2, size)),
            dma((2, size)),
            dma((2, 2, 3)),
            dma((2, 3)),
            dma((2, size)),
            dma((groups, own // depth, 2)),
        ],
        compiler_params=pltpu.CompilerParams(
            collective_id=1, has_side_effects=True, vmem_limit_bytes=VMEM_BYTES
        ),
        name="attend_forward",
    )(
        rows,
        trig,
        qkv_weight,
        out_weight,
        small,
        cots,
    )


CHUNKS = 5
IN_LOOP = ((2, 1), (4, 2), (6, 3))


def mlp_kernel(
    size,
    normed_ref,
    resid_ref,
    gain_ref,
    cots_ref,
    gate_ref,
    up_ref,
    down_ref,
    outs_ref,
    back_ref,
    gain_grad_ref,
    sums_ref,
    far_ref,
    rows_all,
    cots,
    weights,
    grads,
    hid,
    dgate,
    dup,
    resid,
    sums_in,
    backs,
    outs,
    load_sems,
    cot_sems,
    ring_send,
    ring_recv,
    sum_send,
    sum_recv,
    out_sems,
    swap_sems,
    far_sems,
    swap_ready,
):
    tokens, width = normed_ref.shape
    units = gate_ref.shape[0]
    half = tokens // 2
    me = lax.axis_index("fsdp")
    seq = lax.axis_index("seq")
    place = ring_place(me, size)
    right = ring_member((place + 1) % size, size)
    left = ring_member((place + size - 1) % size, size)
    core, far, diagonal = seq_partners(seq)
    sides = ((right, pl.ds(0, half)), (left, pl.ds(half, half)))

    def owner_of(step, side):
        return ring_member((place + size - step if side == 0 else place + step) % size, size)

    own_load = pltpu.make_async_copy(normed_ref, rows_all.at[0], load_sems.at[3])
    resid_load = pltpu.make_async_copy(resid_ref, resid, load_sems.at[4])
    weight_loads = [
        pltpu.make_async_copy(ref, weights.at[at], load_sems.at[at])
        for at, ref in enumerate((gate_ref, up_ref, down_ref))
    ]
    own_load.start()
    greet(({"fsdp": right}, {"fsdp": left}, {"seq": core}, {"seq": far}))

    def cot_copies(step):
        return [
            pltpu.make_async_copy(
                cots_ref.at[
                    pl.ds(
                        pl.multiple_of(owner_of(step, side) * tokens + side * half, half), half
                    )
                ],
                cots.at[step % 2, sides[side][1]],
                cot_sems.at[step % 2, side],
            )
            for side in range(2)
        ]


    def row_copy(step, side):
        target, span = sides[side]
        return pltpu.make_async_remote_copy(
            src_ref=rows_all.at[step, span],
            dst_ref=rows_all.at[step + 1, span],
            send_sem=ring_send.at[side, step],
            recv_sem=ring_recv.at[side, step + 1],
            device_id={"fsdp": target},
            device_id_type=MESH,
        )

    def sum_span(side, sub):
        return pl.ds(side * half + sub * (half // 2), half // 2)

    def sum_copy(step, side, sub):
        target, span = sides[side][0], sum_span(side, sub)
        return pltpu.make_async_remote_copy(
            src_ref=backs.at[step, span],
            dst_ref=sums_in.at[step, span],
            send_sem=sum_send.at[side, sub, step],
            recv_sem=sum_recv.at[side, sub, step],
            device_id={"fsdp": target},
            device_id_type=MESH,
        )

    def sum_step(step):
        for sub in range(2):
            for side in range(2):
                span = sum_span(side, sub)
                if step >= 2:
                    sum_copy(step - 1, side, sub).wait_recv()
                    backs[step, span] = (
                        backs[step, span].astype(jnp.float32)
                        + sums_in[step - 1, span].astype(jnp.float32)
                    ).astype(jnp.bfloat16)
                sum_copy(step, side, sub).start()

    def out_copy(step, side):
        at = pl.multiple_of(owner_of(step, side) * tokens + side * half, half)
        return pltpu.make_async_copy(
            outs.at[step % 2, sides[side][1]], outs_ref.at[pl.ds(at, half)], out_sems.at[side, step]
        )

    def elementwise(step, span):
        rows = rows_all[step]
        gate = matmul(rows, weights[0, span, :], NT)
        up = matmul(rows, weights[1, span, :], NT)
        grad_hidden = matmul(cots[step % 2], weights[2, span, :], NT)
        sigmoid = jax.nn.sigmoid(gate)
        activated = gate * sigmoid
        hid[:, span] = (activated * up).astype(jnp.bfloat16)
        dgate[:, span] = (
            grad_hidden * up * sigmoid * (1.0 + gate * (1.0 - sigmoid))
        ).astype(jnp.bfloat16)
        dup[:, span] = (grad_hidden * activated).astype(jnp.bfloat16)

    own_load.wait()
    for side in range(2):
        row_copy(0, side).start()
    for load in weight_loads + cot_copies(0) + [resid_load]:
        load.start()

    @pl.loop(0, units // 16)
    def _(at):
        zeros = jnp.zeros((3, 16, width), jnp.float32)
        grads[:, pl.ds(pl.multiple_of(at * 16, 16), 16), :] = zeros

    for load in weight_loads:
        load.wait()

    @pl.loop(0, size)
    def _(step):
        slot = step % 2

        @pl.when(step >= 1)
        def _():
            for side in range(2):
                row_copy(step - 1, side).wait_recv()

        @pl.when((step >= 1) & (step < size - 1))
        def _():
            for side in range(2):
                row_copy(step, side).start()

        for load in cot_copies(step):
            load.wait()

        @pl.when(step < size - 1)
        def _():
            for load in cot_copies(step + 1):
                load.start()

        for_blocks(units, 256, functools.partial(elementwise, step))

        def back_part(span):
            backs[step, :, span] = (
                matmul(dgate[...], weights[0, :, span], NN)
                + matmul(dup[...], weights[1, :, span], NN)
            ).astype(jnp.bfloat16)

        for_blocks(width, 256, back_part)

        for when, at in IN_LOOP:

            @pl.when(step == when)
            def _():
                sum_step(at)

        @pl.when(step >= 2)
        def _():
            for side in range(2):
                out_copy(step - 2, side).wait()

        def out_part(span):
            outs[slot, :, span] = matmul(hid[...], weights[2, :, span], NN).astype(jnp.bfloat16)

        for_blocks(width, 256, out_part)
        for side in range(2):
            out_copy(step, side).start()

        def weight_part(span):
            rows, cot = rows_all[step, :, span], cots[slot, :, span]
            grads[0, :, span] += matmul(dgate[...], rows, TN)
            grads[1, :, span] += matmul(dup[...], rows, TN)
            grads[2, :, span] += matmul(hid[...], cot, TN)

        for_blocks(width, 256, weight_part)

    share = units // 2
    kept = pl.multiple_of((seq % 2) * share, 16)
    given = pl.multiple_of((1 - seq % 2) * share, 16)
    chunk = share // CHUNKS
    pl.semaphore_signal(swap_ready, inc=1, device_id={"seq": core}, device_id_type=MESH)

    def to_seq(source, target, sems, at, device):
        return pltpu.make_async_remote_copy(
            src_ref=source,
            dst_ref=target,
            send_sem=sems.at[0, at],
            recv_sem=sems.at[1, at],
            device_id={"seq": device},
            device_id_type=MESH,
        )

    swaps = [
        to_seq(
            weights.at[at, pl.ds(given, share)],
            weights.at[at, pl.ds(given, share)],
            swap_sems,
            at,
            core,
        )
        for at in range(3)
    ]
    waiting = [at for at in range(1, size) if at not in [pair[1] for pair in IN_LOOP]]
    sum_step(waiting[0])
    for at in range(3):

        @pl.loop(0, share // 16)
        def _(block):
            span = pl.ds(pl.multiple_of(given + block * 16, 16), 16)
            weights[at, span, :] = grads[at, span, :].astype(jnp.bfloat16)

        if at == 0:
            pl.semaphore_wait(swap_ready, 1)
        swaps[at].start()

    stores = []

    def kept_rows(at):
        return pl.ds(pl.multiple_of(kept + at * chunk, 16), chunk)

    far_copies = [
        to_seq(weights.at[0, kept_rows(at)], far_ref.at[kept_rows(at)], far_sems, at, far)
        for at in range(CHUNKS)
    ]
    def swap_finish(at):
        swaps[at].wait_recv()

        @pl.loop(0, share // 16)
        def _(block):
            span = pl.ds(pl.multiple_of(kept + block * 16, 16), 16)
            weights[at, span, :] = (
                grads[at, span, :] + weights[at, span, :].astype(jnp.float32)
            ).astype(jnp.bfloat16)

        done = weights.at[at, pl.ds(kept, share)]
        stores.append(
            pltpu.make_async_copy(done, sums_ref.at[at, pl.ds(kept, share)], load_sems.at[at])
        )
        if at == 0:
            for copy in far_copies:
                copy.start()
        stores[-1].start()

    cot_own = pltpu.make_async_copy(
        cots_ref.at[pl.ds(pl.multiple_of(me * tokens, tokens), tokens)],
        cots.at[0],
        load_sems.at[7],
    )
    cot_own.start()
    for turn, at in enumerate(waiting[1:]):
        sum_step(at)
        if turn < 3:
            swap_finish(turn)
    for turn in range(len(waiting) - 1, 3):
        swap_finish(turn)

    for side in range(2):
        for sub in range(2):
            sum_copy(size - 1, side, sub).wait_recv()
    grad_normed = backs[0].astype(jnp.float32) + sums_in[size - 1].astype(jnp.float32)
    resid_load.wait()
    inverse = inverse_of(resid[...])
    unit_rows = resid[...] * inverse
    gain_grad_ref[...] = jnp.sum(grad_normed * unit_rows, axis=0, keepdims=True)
    grad_unit = grad_normed * gain_ref[1:2, :]
    cot_own.wait()
    back_ref[...] = cots[0].astype(jnp.float32) + inverse * (
        grad_unit - unit_rows * jnp.mean(grad_unit * unit_rows, axis=-1, keepdims=True)
    )
    for side in range(2):
        out_copy(size - 2, side).wait()
        out_copy(size - 1, side).wait()

        @pl.loop(0, size - 1)
        def _(step):
            row_copy(step, side).wait_send()
            for sub in range(2):
                sum_copy(step + 1, side, sub).wait_send()

    for copy in swaps + far_copies:
        copy.wait_send()
    for copy in far_copies:
        copy.wait_recv()
    for store in stores:
        store.wait()


def mlp_ring(normed, resid, gain, cots, gate_weight, up_weight, down_weight):
    size = lax.axis_size("fsdp")
    tokens, width = normed.shape
    units = gate_weight.shape[0]
    anywhere = pl.BlockSpec(memory_space=pl.ANY)
    inside = pl.BlockSpec(memory_space=pltpu.VMEM)
    bf16, f32 = jnp.bfloat16, jnp.float32
    dma = pltpu.SemaphoreType.DMA
    return pl.pallas_call(
        functools.partial(mlp_kernel, size),
        out_shape=(
            jax.ShapeDtypeStruct((size * tokens, width), bf16),
            jax.ShapeDtypeStruct((tokens, width), f32),
            jax.ShapeDtypeStruct((1, width), f32),
            jax.ShapeDtypeStruct((3, units, width), bf16),
            jax.ShapeDtypeStruct((units, width), bf16),
        ),
        in_specs=[anywhere, anywhere, inside, anywhere, anywhere, anywhere, anywhere],
        out_specs=(anywhere, inside, inside, anywhere, anywhere),
        scratch_shapes=[
            pltpu.VMEM((size, tokens, width), bf16),
            pltpu.VMEM((2, tokens, width), bf16),
            pltpu.VMEM((3, units, width), bf16),
            pltpu.VMEM((3, units, width), f32),
            pltpu.VMEM((tokens, units), bf16),
            pltpu.VMEM((tokens, units), bf16),
            pltpu.VMEM((tokens, units), bf16),
            pltpu.VMEM((tokens, width), f32),
            pltpu.VMEM((size, tokens, width), bf16),
            pltpu.VMEM((size, tokens, width), bf16),
            pltpu.VMEM((2, tokens, width), bf16),
            dma((9,)),
            dma((2, 2)),
            dma((2, size)),
            dma((2, size)),
            dma((2, 2, size)),
            dma((2, 2, size)),
            dma((2, size)),
            dma((2, 3)),
            dma((2, CHUNKS)),
            pltpu.SemaphoreType.REGULAR,
        ],
        compiler_params=pltpu.CompilerParams(
            collective_id=0, has_side_effects=True, vmem_limit_bytes=VMEM_BYTES
        ),
        name="mlp_ring",
    )(normed, resid, gain, cots, gate_weight, up_weight, down_weight)


def attend_backward_kernel(
    size,
    heads_ref,
    attended_ref,
    log_ref,
    proj_ref,
    weight_ref,
    normed_ref,
    trig_ref,
    hidden_ref,
    resid_grad_ref,
    gain_ref,
    gain_grad_ref,
    resid_ref,
    outs_ref,
    units_in_ref,
    far_gate_in_ref,
    grad_in_ref,
    hidden_out_ref,
    small_ref,
    shards_ref,
    halves_ref,
    far_units_ref,
    units_ref,
    far_gate_ref,
    grads_all,
    grad_heads,
    grad_mixed,
    grad_keys,
    grad_values,
    grad_normed,
    term_qkv,
    term_out,
    out_columns,
    qkv_in,
    out_in,
    qkv_sum,
    out_sum,
    shard,
    shard_all,
    half_shard,
    half_all,
    out_own,
    out_recv,
    out_send,
    resid,
    seq_in,
    far_sum,
    small_in,
    load_sems,
    own_sems,
    out_sems,
    term_sems,
    column_sems,
    seq_sems,
    shard_sems,
    small_sems,
    unit_sems,
    pass_sems,
    share_sems,
    gate_sems,
    grad_sems,
):
    length = heads_ref.shape[0]
    tokens, width = hidden_ref.shape
    used = heads_ref.shape[1]
    own = attended_ref.shape[1]
    count = own // HEAD_DIM
    scale = HEAD_DIM**-0.5
    half = tokens // 2
    block = tokens
    depth = width // size
    chip_pieces = size // 2
    half_width = width // 2
    term_half = depth // 2
    units = units_ref.shape[1]
    f32, bf16 = jnp.float32, jnp.bfloat16
    me = lax.axis_index("fsdp")
    seq = lax.axis_index("seq")
    place = ring_place(me, size)
    right = ring_member((place + 1) % size, size)
    left = ring_member((place + size - 1) % size, size)
    core, far, diagonal = seq_partners(seq)
    rounds = size.bit_length() - 1
    mirrors = [me + (1 - 2 * ((me // 2**at) % 2)) * 2**at for at in range(rounds)]
    ring = ({"fsdp": right}, {"fsdp": left})

    def owner_of(step, side):
        return ring_member((place + size - step if side == 0 else place + step) % size, size)

    def remote(source, target, sems, at, device):
        return pltpu.make_async_remote_copy(
            src_ref=source,
            dst_ref=target,
            send_sem=sems.at[(0,) + at],
            recv_sem=sems.at[(1,) + at],
            device_id=device,
            device_id_type=MESH,
        )

    greet(
        ring
        + ({"seq": core}, {"seq": far})
        + tuple({"fsdp": mirror} for mirror in mirrors)
    )

    def own_load(step, side):
        at = pl.multiple_of(owner_of(step, side) * tokens + side * half, half)
        return pltpu.make_async_copy(
            outs_ref.at[pl.ds(at, half)],
            out_own.at[step % 2, pl.ds(side * half, half)],
            own_sems.at[step % 2, side],
        )

    def out_copy(step, side):
        span = pl.ds(side * half, half)
        return remote(
            out_send.at[step % 2, span], out_recv.at[step, span], out_sems, (side, step), ring[side]
        )

    def out_step(step):
        for side in range(2):
            own_load(step, side).wait()
            if step < size - 1:
                own_load(step + 1, side).start()
            if step >= 3:
                out_copy(step - 2, side).wait_send()
            if step >= 2:
                out_copy(step - 1, side).wait_recv()
        total = out_own[step % 2].astype(f32)
        if step >= 2:
            total += out_recv[step - 1].astype(f32)
        out_send[step % 2] = total.astype(bf16)
        for side in range(2):
            out_copy(step, side).start()

    resid_load = pltpu.make_async_copy(resid_ref, resid, load_sems.at[0])

    def out_finish():
        step = size
        for side in range(2):
            out_copy(step - 2, side).wait_send()
            out_copy(step - 1, side).wait_send()
            out_copy(step - 1, side).wait_recv()
        mine = pltpu.make_async_copy(
            outs_ref.at[pl.ds(pl.multiple_of(me * tokens, tokens), tokens)],
            out_own.at[0],
            load_sems.at[1],
        )
        mine.start()
        mine.wait()
        resid_load.wait()
        hidden_out_ref[...] = (
            resid[...] + out_own[0].astype(f32) + out_recv[size - 1].astype(f32)
        ).astype(bf16)

    share = units // 2
    piece = share // CHUNKS
    kept = (seq % 2) * share

    def unit_slice(ref, at):
        start = pl.multiple_of(kept + (at % CHUNKS) * piece, 16)
        return ref.at[at // CHUNKS, pl.ds(start, piece)]

    def unit_copy(at):
        return remote(
            unit_slice(units_ref, at + CHUNKS), unit_slice(far_units_ref, at), unit_sems, (at,), {"seq": far}
        )

    def unit_pass(at):
        part = unit_slice(far_units_ref, at)
        return remote(part, part, pass_sems, (at,), {"seq": core})

    def unit_share(at):
        part = unit_slice(units_ref, at)
        return remote(part, part, share_sems, (at,), {"seq": core})

    def gate_pass(at):
        part = far_gate_ref.at[pl.ds(pl.multiple_of(kept + at * piece, 16), piece)]
        return remote(part, part, gate_sems, (at,), {"seq": core})

    chunks = 2 * CHUNKS
    starts, passes = iter(range(chunks)), iter(range(chunks))

    def send_units(number):
        for _ in range(number):
            unit_copy(next(starts)).start()

    def pass_units(number):
        for _ in range(number):
            at = next(passes)
            unit_copy(at).wait_recv()
            unit_pass(at).start()

    def grad_copy(source, target, at):
        span = grads_all.at[source]
        return remote(span, span, grad_sems, (at,), {"seq": target})

    to_far_grads = grad_copy(seq, far, 0)
    to_core_grads = grad_copy(seq, core, 1)
    passed_grads = grad_copy(far, core, 2)
    grads_all[seq] = resid_grad_ref[...].astype(bf16)
    to_far_grads.start()
    to_core_grads.start()
    resid_load.start()
    for side in range(2):
        own_load(1, side).start()
    out_step(1)

    grad_keys[...] = jnp.zeros_like(grad_keys)
    grad_values[...] = jnp.zeros_like(grad_values)
    lane = lax.broadcasted_iota(jnp.int32, (block, HEAD_DIM), 1)
    keys = slice(own, own + HEAD_DIM)
    values = slice(own + HEAD_DIM, used)

    def attend_block(at_block):
        start = at_block * block
        span = slice(start, start + block)
        seen = slice(0, start + block)
        cosine, sine = turn_tables(trig_ref[span, :])
        grad_heads[span, :] = matmul(grads_all[at_block], proj_ref[...], NT).astype(bf16)

        @pl.loop(0, count)
        def _(at):
            head = pl.ds(pl.multiple_of(at * HEAD_DIM, HEAD_DIM), HEAD_DIM)
            query = heads_ref[span, head]
            grad = grad_heads[span, head]
            logs = jnp.sum(jnp.where(lane == at, log_ref[span, :], 0.0), axis=-1, keepdims=True)
            scores = causal(matmul(query, heads_ref[seen, keys], NT) * scale, start)
            probability = jnp.exp(scores - logs)
            grad_probs = matmul(grad, heads_ref[seen, values], NT)
            delta = jnp.sum(probability * grad_probs, axis=-1, keepdims=True)
            grad_scores = (probability * (grad_probs - delta)).astype(bf16)
            grad_query = matmul(grad_scores, heads_ref[seen, keys], NN) * scale
            grad_query = grad_query.astype(bf16).astype(f32)
            grad_mixed[span, head] = (
                grad_query * cosine + pltpu.roll(grad_query * sine, HEAD_DIM // 2, 1)
            ).astype(bf16)
            grad_keys[seen, :] += matmul(grad_scores, query, TN) * scale
            grad_values[seen, :] += matmul(probability.astype(bf16), grad, TN)

    @pl.loop(0, 4)
    def _(turn):
        @pl.when(turn == 1)
        def _():
            to_core_grads.wait_recv()

        @pl.when(turn == 2)
        def _():
            to_far_grads.wait_recv()
            passed_grads.start()
            unit_copy(0).start()

        @pl.when(turn == 3)
        def _():
            passed_grads.wait_recv()
            unit_copy(1).start()

        @pl.when(turn == 2)
        def _():
            out_step(2)

        for shared in range(3):
            unit_share(turn * 3 + shared).start()
        gate_pass(turn).start()
        at_block = ((seq // 2 + turn // 2) % 2) * 2 + (seq % 2 + turn % 2) % 2
        for at in range(4):

            @pl.when(at_block == at)
            def _():
                attend_block(at)

    next(starts)
    next(starts)
    send_units(1)
    for shared in range(12, 3 * CHUNKS):
        unit_share(shared).start()
    gate_pass(4).start()
    out_step(3)

    for start in range(0, length, block):
        span = slice(start, start + block)
        cosine, sine = turn_tables(trig_ref[span, :])
        part = grad_keys[span, :].astype(bf16).astype(f32)
        grad_mixed[span, keys] = (
            part * cosine + pltpu.roll(part * sine, HEAD_DIM // 2, 1)
        ).astype(bf16)
        grad_mixed[span, values] = grad_values[span, :].astype(bf16)

    def normed_part(span):
        grad_normed[:, span] = matmul(grad_mixed[...], weight_ref[span, :used], NT).astype(bf16)

    loop_blocks(width, 256, normed_part)

    def block_rows(at):
        return grad_normed.at[pl.ds(pl.multiple_of(at * tokens, tokens), tokens)]

    to_core = [
        remote(block_rows(diagonal), seq_in.at[0], seq_sems, (0,), {"seq": core}),
        remote(block_rows(core), seq_in.at[1], seq_sems, (1,), {"seq": core}),
    ]
    to_far = remote(far_sum, seq_in.at[2], seq_sems, (2,), {"seq": far})
    for copy in to_core:
        copy.start()

    def out_term(span):
        term_out[:, span] = matmul(
            attended_ref[...], grads_all[:, :, span].reshape(length, span.size), TN
        ).astype(bf16)

    loop_blocks(width, 256, out_term)
    my_row = pl.multiple_of((seq % 2) * own, 16)
    my_lane = pl.multiple_of((seq % 2) * half_width, 128)
    core_lane = pl.multiple_of((1 - seq % 2) * half_width, 128)
    columns = remote(
        term_out.at[:, pl.ds(core_lane, half_width)],
        out_columns.at[pl.ds(my_row, own)],
        column_sems,
        (0,),
        {"seq": core},
    )
    columns.start()
    out_columns[pl.ds(my_row, own), :] = term_out[:, pl.ds(my_lane, half_width)]

    def qkv_term(span):
        term_qkv[span, :] = matmul(normed_ref[:, span], grad_mixed[...], TN).astype(bf16)

    loop_blocks(width, 256, qkv_term)
    to_core[0].wait_recv()
    far_sum[...] = (block_rows(far)[...].astype(f32) + seq_in[0].astype(f32)).astype(bf16)
    to_far.start()
    out_step(4)
    small_in[0] = jnp.zeros((8, width), f32)
    small_in[0, 1:2, :] = gain_grad_ref[...]
    bias = jnp.sum(grad_mixed[...].astype(f32), axis=0, keepdims=True)
    small_in[0, 2:3, pl.ds(pl.multiple_of(seq * own, 128), own)] = bias[:, :own]
    kv_lane = pl.multiple_of((seq // 2) * HEAD_DIM, HEAD_DIM)
    small_in[0, 3:4, pl.ds(kv_lane, HEAD_DIM)] = bias[:, keys]
    small_in[0, 3:4, pl.ds(kv_lane + KV_HEADS * HEAD_DIM, HEAD_DIM)] = bias[:, values]

    def term_copy(step, side):
        span = pl.ds(side * term_half, term_half)
        return remote(
            qkv_sum.at[step, span], qkv_in.at[step, span], term_sems, (0, side, step), ring[side]
        )

    def half_copy(step, side):
        span = pl.ds(side * term_half, term_half)
        return remote(
            out_sum.at[step, span], out_in.at[step, span], term_sems, (1, side, step), ring[side]
        )

    def here(owner):
        return owner // chip_pieces == seq // 2

    def half_rows(owner, side):
        start = (owner % chip_pieces) * depth + side * term_half
        return pl.ds(pl.multiple_of(start, 16), term_half)

    def term_step(step):
        for side in range(2):
            span = pl.ds(side * term_half, term_half)
            start = owner_of(step, side) * depth + side * term_half
            total = term_qkv[pl.ds(pl.multiple_of(start, 16), term_half), :].astype(f32)
            if step >= 2:
                term_copy(step - 1, side).wait_recv()
                total += qkv_in[step - 1, span, :].astype(f32)
            qkv_sum[step, span, :] = total.astype(bf16)
            term_copy(step, side).start()

    def half_step(step):
        for side in range(2):
            owner = owner_of(step, side)

            @pl.when(here(owner))
            def _():
                span = pl.ds(side * term_half, term_half)
                total = out_columns[half_rows(owner, side), :].astype(f32)
                if step >= 2:
                    half_copy(step - 1, side).wait_recv()
                    total += out_in[step - 1, span, :].astype(f32)
                out_sum[step, span, :] = total.astype(bf16)
                half_copy(step, side).start()

    def small_copy(at):
        device = ({"seq": core}, {"seq": far})[at] if at < 2 else {"fsdp": mirrors[at - 2]}
        return remote(small_in.at[2 * at], small_in.at[2 * at + 1], small_sems, (at,), device)

    def small_step(at):
        small_copy(at).wait_recv()
        small_in[2 * at + 2] = small_in[2 * at] + small_in[2 * at + 1]

    term_step(1)
    columns.wait_recv()
    half_step(1)
    term_step(2)
    half_step(2)
    out_step(5)
    to_core[1].wait_recv()
    send_units(1)
    to_far.wait_recv()
    rows = hidden_ref[...].astype(f32)
    inverse = lax.rsqrt(jnp.mean(rows * rows, axis=-1, keepdims=True) + norm_eps)
    unit_rows = rows * inverse
    grad_rows = (
        block_rows(seq)[...].astype(f32) + seq_in[1].astype(f32) + seq_in[2].astype(f32)
    )
    small_in[0, 0:1, :] = jnp.sum(grad_rows * unit_rows, axis=0, keepdims=True)
    small_copy(0).start()
    grad_unit = grad_rows * gain_ref[0:1, :]
    grad_in_ref[...] = resid_grad_ref[...] + inverse * (
        grad_unit - unit_rows * jnp.mean(grad_unit * unit_rows, axis=-1, keepdims=True)
    )
    total_rounds = rounds + 2
    small_step(0)
    small_copy(1).start()
    done = 1
    send_units(2)
    for step in range(3, size):
        term_step(step)
        half_step(step)
        if done < total_rounds:
            small_step(done)
            done += 1
            if done < total_rounds:
                small_copy(done).start()
        if step == 4:
            send_units(2)
        if step % 2 == 0:
            pass_units(2)
    while done < total_rounds:
        small_step(done)
        done += 1
        if done < total_rounds:
            small_copy(done).start()
    small_ref[...] = small_in[2 * total_rounds]
    source_chip = here(me)
    for side in range(2):
        span = pl.ds(side * term_half, term_half)
        start = me * depth + side * term_half
        term_copy(size - 1, side).wait_recv()
        shard[span, :] = (
            term_qkv[pl.ds(pl.multiple_of(start, 16), term_half), :].astype(f32)
            + qkv_in[size - 1, span, :].astype(f32)
        ).astype(bf16)

        @pl.when(source_chip)
        def _():
            half_copy(size - 1, side).wait_recv()
            half_shard[span, :] = (
                out_columns[half_rows(me, side), :].astype(f32)
                + out_in[size - 1, span, :].astype(f32)
            ).astype(bf16)

    def shard_copy(source, at, block_at, target):
        return remote(source, shard_all.at[block_at], shard_sems, (at,), {"seq": target})

    def half_move(source, at, target):
        return remote(source, half_all.at[seq % 2], shard_sems, (at,), {"seq": target})

    shard_far = shard_copy(shard, 0, seq, far)
    shard_core = shard_copy(shard, 1, seq, core)
    shard_pass = shard_copy(shard_all.at[far], 2, far, core)
    half_far = half_move(half_shard, 3, far)
    half_core = half_move(half_shard, 4, core)
    half_pass = half_move(half_all.at[seq % 2], 5, core)
    shard_far.start()
    shard_core.start()

    @pl.when(source_chip)
    def _():
        half_far.start()
        half_core.start()
        half_all[seq % 2] = half_shard[...]

    send_units(2)
    shard_all[seq] = shard[...]
    out_step(6)
    shard_far.wait_recv()
    shard_pass.start()

    @pl.when(jnp.logical_not(source_chip))
    def _():
        half_far.wait_recv()
        half_pass.start()

    pass_units(3)
    out_step(7)
    pass_units(3)
    out_finish()
    shard_core.wait_recv()
    shard_pass.wait_recv()
    shard_store = pltpu.make_async_copy(shard_all, shards_ref, load_sems.at[1])
    shard_store.start()

    @pl.when(source_chip)
    def _():
        half_core.wait_recv()
        half_core.wait_send()
        half_far.wait_send()

    @pl.when(jnp.logical_not(source_chip))
    def _():
        half_pass.wait_recv()
        half_pass.wait_send()

    half_store = pltpu.make_async_copy(half_all, halves_ref, load_sems.at[2])
    half_store.start()
    for step in range(1, size):
        for side in range(2):
            term_copy(step, side).wait_send()

            @pl.when(here(owner_of(step, side)))
            def _():
                half_copy(step, side).wait_send()

    for copy in [unit_share(at) for at in range(3 * CHUNKS)] + [
        gate_pass(at) for at in range(CHUNKS)
    ]:
        copy.wait_send()
        copy.wait_recv()
    for at in range(chunks):
        unit_pass(at).wait_recv()
        unit_copy(at).wait_send()
        unit_pass(at).wait_send()
    for at in range(total_rounds):
        small_copy(at).wait_send()
    for copy in to_core + [to_far, columns, shard_far, shard_core, shard_pass]:
        copy.wait_send()
    for copy in (to_far_grads, to_core_grads, passed_grads):
        copy.wait_send()
    shard_store.wait()
    half_store.wait()


def attend_group_backward(
    heads,
    attended,
    logs,
    proj,
    weight,
    normed,
    trig,
    hidden,
    resid_grad,
    gain,
    gain_grad,
    resid,
    outs,
    units,
    far_gate,
):
    size = lax.axis_size("fsdp")
    groups = lax.axis_size("seq")
    length = heads.shape[0]
    tokens, width = hidden.shape
    used = heads.shape[1]
    own = attended.shape[1]
    depth = width // size
    rounds = size.bit_length() + 1
    bf16, f32 = jnp.bfloat16, jnp.float32
    anywhere = pl.BlockSpec(memory_space=pl.ANY)
    inside = pl.BlockSpec(memory_space=pltpu.VMEM)
    dma = pltpu.SemaphoreType.DMA
    vmem = pltpu.VMEM
    return pl.pallas_call(
        functools.partial(attend_backward_kernel, size),
        out_shape=(
            jax.ShapeDtypeStruct((tokens, width), f32),
            jax.ShapeDtypeStruct((tokens, width), bf16),
            jax.ShapeDtypeStruct((8, width), f32),
            jax.ShapeDtypeStruct((groups, depth, used), bf16),
            jax.ShapeDtypeStruct((2, depth, width // 2), bf16),
            jax.ShapeDtypeStruct((2,) + units.shape[1:], bf16),
            jax.ShapeDtypeStruct(units.shape, bf16),
            jax.ShapeDtypeStruct(far_gate.shape, bf16),
        ),
        in_specs=[inside] * 11 + [anywhere] * 4,
        out_specs=(inside, inside, inside) + (anywhere,) * 5,
        input_output_aliases={13: 6, 14: 7},
        scratch_shapes=[
            vmem((groups, tokens, width), bf16),
            vmem((length, own), bf16),
            vmem((length, used), bf16),
            vmem((length, HEAD_DIM), f32),
            vmem((length, HEAD_DIM), f32),
            vmem((length, width), bf16),
            vmem((width, used), bf16),
            vmem((own, width), bf16),
            vmem((2 * own, width // 2), bf16),
            vmem((size, depth, used), bf16),
            vmem((size, depth, width // 2), bf16),
            vmem((size, depth, used), bf16),
            vmem((size, depth, width // 2), bf16),
            vmem((depth, used), bf16),
            vmem((groups, depth, used), bf16),
            vmem((depth, width // 2), bf16),
            vmem((2, depth, width // 2), bf16),
            vmem((2, tokens, width), bf16),
            vmem((size, tokens, width), bf16),
            vmem((2, tokens, width), bf16),
            vmem((tokens, width), f32),
            vmem((3, tokens, width), bf16),
            vmem((tokens, width), bf16),
            vmem((2 * rounds + 1, 8, width), f32),
            dma((3,)),
            dma((2, 2)),
            dma((2, 2, size)),
            dma((2, 2, 2, size)),
            dma((2, 1)),
            dma((2, 3)),
            dma((2, 6)),
            dma((2, rounds)),
            dma((2, 2 * CHUNKS)),
            dma((2, 2 * CHUNKS)),
            dma((2, 3 * CHUNKS)),
            dma((2, CHUNKS)),
            dma((2, 3)),
        ],
        compiler_params=pltpu.CompilerParams(
            collective_id=2, has_side_effects=True, vmem_limit_bytes=VMEM_BYTES
        ),
        name="attend_backward",
    )(
        heads,
        attended,
        logs,
        proj,
        weight,
        normed,
        trig,
        hidden,
        resid_grad,
        gain,
        gain_grad,
        resid,
        outs,
        units,
        far_gate,
    )


def finish_kernel(
    sums_ref,
    far_gate_ref,
    far_ref,
    grad_in_ref,
    hidden_ref,
    shards_ref,
    halves_ref,
    gate_out,
    up_out,
    down_out,
    grad_in_out,
    hidden_out,
    qkv_out,
    proj_out,
):
    f32 = jnp.float32
    gate_out[...] = sums_ref[0].astype(f32) + far_gate_ref[...].astype(f32)
    up_out[...] = sums_ref[1].astype(f32) + far_ref[0].astype(f32)
    down_out[...] = sums_ref[2].astype(f32) + far_ref[1].astype(f32)
    grad_in_out[...] = grad_in_ref[...]
    hidden_out[...] = hidden_ref[...]
    groups, _, used = shards_ref.shape
    own = used - 2 * HEAD_DIM
    for at in range(groups):
        qkv_out[:, at * own : (at + 1) * own] = shards_ref[at, :, :own].astype(f32)
    for which in range(2):
        lanes = slice(own + which * HEAD_DIM, own + (which + 1) * HEAD_DIM)
        for head in range(KV_HEADS):
            at = groups * own + (which * KV_HEADS + head) * HEAD_DIM
            qkv_out[:, at : at + HEAD_DIM] = shards_ref[2 * head, :, lanes].astype(
                f32
            ) + shards_ref[2 * head + 1, :, lanes].astype(f32)
    half = halves_ref.shape[2]
    for which in range(2):
        proj_out[:, which * half : (which + 1) * half] = halves_ref[which].astype(f32)


def finish_totals(unit_sums, far_gate, far_sums, grad_in, hidden, shards, halves):
    f32, bf16 = jnp.float32, jnp.bfloat16
    _, units, width = unit_sums.shape
    groups, depth, used = shards.shape
    joint = groups * (used - 2 * HEAD_DIM) + 2 * KV_HEADS * HEAD_DIM
    tokens = grad_in.shape[0]
    steps, few = 4, 4

    def spec(*dims, many=False):
        lead = len(dims) - 2
        return pl.BlockSpec(
            dims,
            lambda at: (0,) * lead + (at if many else jnp.minimum(at, few - 1), 0),
        )

    rows = units // steps
    return pl.pallas_call(
        finish_kernel,
        grid=(steps,),
        out_shape=(
            jax.ShapeDtypeStruct((units, width), f32),
            jax.ShapeDtypeStruct((units, width), f32),
            jax.ShapeDtypeStruct((units, width), f32),
            jax.ShapeDtypeStruct((tokens, width), f32),
            jax.ShapeDtypeStruct((tokens, width), bf16),
            jax.ShapeDtypeStruct((depth, joint), f32),
            jax.ShapeDtypeStruct((depth, width), f32),
        ),
        in_specs=[
            spec(3, rows, width, many=True),
            spec(rows, width, many=True),
            spec(2, rows, width, many=True),
            spec(tokens // few, width),
            spec(tokens // few, width),
            spec(groups, depth // few, used),
            spec(2, depth // few, width // 2),
        ],
        out_specs=(
            spec(rows, width, many=True),
            spec(rows, width, many=True),
            spec(rows, width, many=True),
            spec(tokens // few, width),
            spec(tokens // few, width),
            spec(depth // few, joint),
            spec(depth // few, width),
        ),
        compiler_params=pltpu.CompilerParams(vmem_limit_bytes=VMEM_BYTES),
        name="finish_totals",
    )(unit_sums, far_gate, far_sums, grad_in, hidden, shards, halves)


def kernels_fit(hidden_in, positions, attn_gain, qkv_weight, qkv_bias, out_weight, *rest):
    size, groups = lax.axis_size("fsdp"), lax.axis_size("seq")
    _, tokens, width = hidden_in.shape
    units = rest[1].shape[0]
    if groups != 4 or size != 8 or tokens % 256 or units % 160 or width % 512:
        return False
    if (width // size) % 32 or qkv_bias.shape[0] > 256 or KV_HEADS != 2:
        return False
    rows = tokens * width * (4 * size + 34)
    return rows + units * (18 * width + 6 * tokens) < 64_000_000


def per_device_kernels(
    hidden_in,
    positions,
    attn_gain,
    qkv_weight,
    qkv_bias,
    out_weight,
    mlp_gain,
    gate_weight,
    up_weight,
    down_weight,
    cotangent,
):
    f32, bf16 = jnp.float32, jnp.bfloat16
    groups = lax.axis_size("seq")
    size = lax.axis_size("fsdp")
    _, tokens, width = hidden_in.shape
    length = tokens * groups
    lane = jnp.arange(HEAD_DIM)
    frequency = jnp.exp(
        -((lane % (HEAD_DIM // 2)).astype(f32) * 2.0 / HEAD_DIM) * math.log(rope_base)
    )
    angles = positions[0].astype(f32)[:, None] * frequency[None, :]
    trig = jnp.where(lane[None, :] < HEAD_DIM // 2, jnp.cos(angles), jnp.sin(angles))
    small = jnp.concatenate(
        [
            jnp.pad(row.astype(f32), (0, 256 - row.shape[0]))
            for row in (attn_gain, mlp_gain, qkv_bias)
        ]
    )[None]
    (
        normed_one,
        heads,
        attended,
        logs,
        weight,
        proj,
        trig_all,
        gains,
        normed_two,
        residual,
        all_cots,
    ) = attend_group(
        hidden_in[0], trig, qkv_weight, out_weight, small, qkv_bias.shape[0], cotangent[0]
    )
    shard = width // size
    outs, grad_residual, term_gain_two, unit_sums, far_gate = mlp_ring(
        normed_two,
        residual,
        gains,
        all_cots.reshape(size * tokens, width),
        gate_weight,
        up_weight,
        down_weight,
    )
    (
        grad_rows,
        hidden_out,
        smalls,
        shards,
        halves,
        far_sums,
        unit_sums,
        far_gate,
    ) = attend_group_backward(
        heads,
        attended,
        logs,
        proj,
        weight,
        normed_one,
        trig_all.reshape(length, HEAD_DIM),
        hidden_in[0],
        grad_residual,
        gains,
        term_gain_two,
        residual,
        outs,
        unit_sums,
        far_gate,
    )
    grad_gate, grad_up, grad_down, grad_rows, hidden_out, grad_qkv, grad_out = finish_totals(
        unit_sums, far_gate, far_sums, grad_rows, hidden_out, shards, halves
    )
    me = lax.axis_index("fsdp")
    bias_sums = jnp.concatenate([smalls[2], smalls[3, : 2 * KV_HEADS * HEAD_DIM]])
    bias_shard = qkv_bias.shape[0]
    return (
        hidden_out[None],
        grad_rows[None],
        lax.dynamic_slice_in_dim(smalls[0], me * shard, shard),
        grad_qkv,
        lax.dynamic_slice_in_dim(bias_sums, me * bias_shard, bias_shard),
        grad_out,
        lax.dynamic_slice_in_dim(smalls[1], me * shard, shard),
        grad_gate,
        grad_up,
        grad_down,
    )


def per_device_gathered(
    hidden_in,
    positions,
    attn_gain,
    qkv_weight,
    qkv_bias,
    out_weight,
    mlp_gain,
    gate_weight,
    up_weight,
    down_weight,
    cotangent,
):
    groups = lax.axis_size("seq")
    group_heads = HEADS // groups
    repeat = groups // KV_HEADS
    tokens = hidden_in.shape[1]
    width_query = HEADS * HEAD_DIM
    width_key = KV_HEADS * HEAD_DIM
    residual = hidden_in[0].astype(jnp.float32)
    cosine, sine = rope_tables(positions[0])
    gains_one, gains_two, qkv_full, bias_full, out_full = (
        lax.all_gather(attn_gain, "fsdp", axis=0, tiled=True),
        lax.all_gather(mlp_gain, "fsdp", axis=0, tiled=True),
        lax.all_gather(qkv_weight, "fsdp", axis=0, tiled=True),
        lax.all_gather(qkv_bias, "fsdp", axis=0, tiled=True),
        lax.all_gather(out_weight, "fsdp", axis=0, tiled=True),
    )
    gain_one = gains_one.astype(jnp.float32)
    gain_two = gains_two.astype(jnp.float32)
    unit_one, inverse_one, normed_one = norm_forward(residual, gain_one)
    qkv_mixed = jnp.dot(
        normed_one, qkv_full, preferred_element_type=jnp.float32
    ) + bias_full.astype(jnp.float32)
    query_part = qkv_mixed[:, :width_query].reshape(tokens, HEADS, HEAD_DIM)
    key_part = qkv_mixed[:, width_query : width_query + width_key].reshape(
        tokens, KV_HEADS, HEAD_DIM
    )
    value_part = qkv_mixed[:, width_query + width_key :].reshape(tokens, KV_HEADS, HEAD_DIM)
    queries = (
        rotate(query_part, cosine, sine)
        .astype(jnp.bfloat16)
        .reshape(tokens, groups, group_heads * HEAD_DIM)
    )
    keys_rep = jnp.repeat(rotate(key_part, cosine, sine).astype(jnp.bfloat16), repeat, axis=1)
    values_rep = jnp.repeat(value_part.astype(jnp.bfloat16), repeat, axis=1)
    head_queries, head_keys, head_values = (
        lax.all_to_all(queries, "seq", split_axis=1, concat_axis=0, tiled=True),
        lax.all_to_all(keys_rep, "seq", split_axis=1, concat_axis=0, tiled=True),
        lax.all_to_all(values_rep, "seq", split_axis=1, concat_axis=0, tiled=True),
    )
    head_queries = head_queries.reshape(-1, group_heads, HEAD_DIM)
    head_keys = head_keys.reshape(-1, HEAD_DIM)
    head_values = head_values.reshape(-1, HEAD_DIM)
    attended, log_totals = attend_forward(head_queries, head_keys, head_values)
    returned = lax.all_to_all(
        attended.reshape(-1, 1, group_heads * HEAD_DIM),
        "seq",
        split_axis=0,
        concat_axis=1,
        tiled=True,
    )
    attn_rows = returned.reshape(tokens, width_query)
    residual_two = residual + jnp.dot(attn_rows, out_full, preferred_element_type=jnp.float32)
    unit_two, inverse_two, normed_two = norm_forward(residual_two, gain_two)
    grad_output = cotangent[0].astype(jnp.float32)
    grad_mlp = grad_output.astype(jnp.bfloat16)
    all_rows = lax.all_gather(normed_two, "fsdp", axis=0, tiled=True)
    gate_pre = jnp.einsum("td,fd->tf", all_rows, gate_weight, preferred_element_type=jnp.float32)
    up_pre = jnp.einsum("td,fd->tf", all_rows, up_weight, preferred_element_type=jnp.float32)
    sigmoid_gate = jax.nn.sigmoid(gate_pre)
    activated = gate_pre * sigmoid_gate
    hidden = (activated * up_pre).astype(jnp.bfloat16)
    partial_out = jnp.dot(hidden, down_weight, preferred_element_type=jnp.float32)
    mlp_out = lax.psum_scatter(
        partial_out.astype(jnp.bfloat16), "fsdp", scatter_dimension=0, tiled=True
    ).astype(jnp.float32)
    all_grads = lax.all_gather(grad_mlp, "fsdp", axis=0, tiled=True)
    grad_hidden = jnp.einsum(
        "tm,fm->tf", all_grads, down_weight, preferred_element_type=jnp.float32
    )
    grad_gate = (
        grad_hidden * up_pre * sigmoid_gate * (1.0 + gate_pre * (1.0 - sigmoid_gate))
    ).astype(jnp.bfloat16)
    grad_up = (grad_hidden * activated).astype(jnp.bfloat16)
    partial_back = jnp.dot(grad_gate, gate_weight, preferred_element_type=jnp.float32) + jnp.dot(
        grad_up, up_weight, preferred_element_type=jnp.float32
    )
    grad_normed_two = lax.psum_scatter(partial_back, "fsdp", scatter_dimension=0, tiled=True)
    shard_gate = jnp.einsum("tf,td->fd", grad_gate, all_rows, preferred_element_type=jnp.float32)
    shard_up = jnp.einsum("tf,td->fd", grad_up, all_rows, preferred_element_type=jnp.float32)
    shard_down = jnp.einsum("tf,td->fd", hidden, all_grads, preferred_element_type=jnp.float32)
    hidden_out = (residual_two + mlp_out).astype(jnp.bfloat16)
    grad_norm_two, term_gain_two = norm_backward(grad_normed_two, unit_two, inverse_two, gain_two)
    grad_residual_two = grad_output + grad_norm_two
    grad_proj = grad_residual_two.astype(jnp.bfloat16)
    grad_attn_rows = jnp.einsum(
        "td,ed->te", grad_proj, out_full, preferred_element_type=jnp.float32
    ).astype(jnp.bfloat16)
    term_out = jnp.einsum("te,td->ed", attn_rows, grad_proj, preferred_element_type=jnp.float32)
    grad_heads = lax.all_to_all(
        grad_attn_rows.reshape(tokens, groups, group_heads * HEAD_DIM),
        "seq",
        split_axis=1,
        concat_axis=0,
        tiled=True,
    )
    grad_query, grad_keys, grad_values = attend_backward(
        head_queries,
        head_keys,
        head_values,
        log_totals,
        grad_heads.reshape(-1, group_heads, HEAD_DIM),
    )
    back_query, back_keys, back_values = (
        lax.all_to_all(
            grad_query.astype(jnp.bfloat16).reshape(-1, 1, group_heads * HEAD_DIM),
            "seq",
            split_axis=0,
            concat_axis=1,
            tiled=True,
        ),
        lax.all_to_all(
            grad_keys.astype(jnp.bfloat16)[:, None, :],
            "seq",
            split_axis=0,
            concat_axis=1,
            tiled=True,
        ),
        lax.all_to_all(
            grad_values.astype(jnp.bfloat16)[:, None, :],
            "seq",
            split_axis=0,
            concat_axis=1,
            tiled=True,
        ),
    )
    grad_query_rows = unrotate(
        back_query.reshape(tokens, HEADS, HEAD_DIM).astype(jnp.float32), cosine, sine
    )
    grad_key_rows = unrotate(
        jnp.sum(back_keys.astype(jnp.float32).reshape(tokens, KV_HEADS, repeat, HEAD_DIM), axis=2),
        cosine,
        sine,
    )
    grad_value_rows = jnp.sum(
        back_values.astype(jnp.float32).reshape(tokens, KV_HEADS, repeat, HEAD_DIM), axis=2
    )
    grad_mixed = jnp.concatenate(
        [
            grad_query_rows.reshape(tokens, width_query),
            grad_key_rows.reshape(tokens, width_key),
            grad_value_rows.reshape(tokens, width_key),
        ],
        axis=1,
    ).astype(jnp.bfloat16)
    term_qkv = jnp.einsum("td,tc->dc", normed_one, grad_mixed, preferred_element_type=jnp.float32)
    term_bias = jnp.sum(grad_mixed.astype(jnp.float32), axis=0)
    grad_normed_one = jnp.einsum(
        "tc,dc->td", grad_mixed, qkv_full, preferred_element_type=jnp.float32
    )
    grad_norm_one, term_gain_one = norm_backward(grad_normed_one, unit_one, inverse_one, gain_one)
    grad_rows = grad_residual_two + grad_norm_one
    shard_gain_one, shard_qkv, shard_bias, shard_out, shard_gain_two = (
        lax.psum_scatter(
            term_gain_one.astype(jnp.bfloat16), "fsdp", scatter_dimension=0, tiled=True
        ).astype(jnp.float32),
        lax.psum_scatter(
            term_qkv.astype(jnp.bfloat16), "fsdp", scatter_dimension=0, tiled=True
        ).astype(jnp.float32),
        lax.psum_scatter(
            term_bias.astype(jnp.bfloat16), "fsdp", scatter_dimension=0, tiled=True
        ).astype(jnp.float32),
        lax.psum_scatter(
            term_out.astype(jnp.bfloat16), "fsdp", scatter_dimension=0, tiled=True
        ).astype(jnp.float32),
        lax.psum_scatter(
            term_gain_two.astype(jnp.bfloat16), "fsdp", scatter_dimension=0, tiled=True
        ).astype(jnp.float32),
    )
    totals = (
        lax.psum(shard_gain_one.astype(jnp.bfloat16), "seq").astype(jnp.float32),
        lax.psum(shard_qkv.astype(jnp.bfloat16), "seq").astype(jnp.float32),
        lax.psum(shard_bias.astype(jnp.bfloat16), "seq").astype(jnp.float32),
        lax.psum(shard_out.astype(jnp.bfloat16), "seq").astype(jnp.float32),
        lax.psum(shard_gain_two.astype(jnp.bfloat16), "seq").astype(jnp.float32),
        lax.psum(shard_gate.astype(jnp.bfloat16), "seq").astype(jnp.float32),
        lax.psum(shard_up.astype(jnp.bfloat16), "seq").astype(jnp.float32),
        lax.psum(shard_down.astype(jnp.bfloat16), "seq").astype(jnp.float32),
    )
    return (
        hidden_out[None],
        grad_rows[None],
        totals[0],
        totals[1],
        totals[2],
        totals[3],
        totals[4],
        totals[5],
        totals[6],
        totals[7],
    )


def per_device(*arguments):
    return (per_device_kernels if kernels_fit(*arguments) else per_device_gathered)(*arguments)


def solution(mesh):
    placed = (
        P("fsdp", "seq", None),
        P("fsdp", "seq"),
        P("fsdp"),
        P("fsdp", None),
        P("fsdp"),
        P("fsdp", None),
        P("fsdp"),
        P("fsdp", None),
        P("fsdp", None),
        P("fsdp", None),
        P("fsdp", "seq", None),
    )
    return jax.shard_map(
        per_device,
        mesh=mesh,
        in_specs=placed,
        out_specs=(
            P("fsdp", "seq", None),
            P("fsdp", "seq", None),
            P("fsdp"),
            P("fsdp", None),
            P("fsdp"),
            P("fsdp", None),
            P("fsdp"),
            P("fsdp", None),
            P("fsdp", None),
            P("fsdp", None),
        ),
        check_vma=False,
    )
```

```python
import functools
import math

import jax
import jax.numpy as jnp
from jax import lax
from jax.experimental import pallas as pl
from jax.experimental.pallas import tpu as pltpu
from jax.sharding import PartitionSpec as P

HEADS = 12
KV_HEADS = 2
HEAD_DIM = 128


norm_eps = 1e-06
rope_base = 1000000.0


def rope_tables(position_row):
    half_dim = HEAD_DIM // 2
    frequency = jnp.exp(
        -(jnp.arange(half_dim, dtype=jnp.float32) * 2.0 / HEAD_DIM) * math.log(rope_base)
    )
    angles = position_row.astype(jnp.float32)[:, None] * frequency[None, :]
    angles = jnp.concatenate([angles, angles], axis=-1)
    return (jnp.cos(angles), jnp.sin(angles))


def rotate(values, cosine, sine):
    half_dim = values.shape[-1] // 2
    turned = jnp.concatenate([-values[..., half_dim:], values[..., :half_dim]], axis=-1)
    return values * cosine[:, None, :] + turned * sine[:, None, :]


def unrotate(grads_rot, cosine, sine):
    half_dim = grads_rot.shape[-1] // 2
    scaled = grads_rot * sine[:, None, :]
    return grads_rot * cosine[:, None, :] + jnp.concatenate(
        [scaled[..., half_dim:], -scaled[..., :half_dim]], axis=-1
    )


def norm_forward(values, gain):
    inverse = lax.rsqrt(jnp.mean(values * values, axis=-1, keepdims=True) + norm_eps)
    unit_rows = values * inverse
    return (unit_rows, inverse, (unit_rows * gain).astype(jnp.bfloat16))


def norm_backward(grad_normed, unit_rows, inverse, gain):
    grad_unit = grad_normed * gain
    grad_values = inverse * (
        grad_unit - unit_rows * jnp.mean(grad_unit * unit_rows, axis=-1, keepdims=True)
    )
    grad_gain = jnp.sum(grad_normed * unit_rows, axis=0)
    return (grad_values, grad_gain)


def masked_scores(queries, keys, block_start, block_rows):
    length = keys.shape[0]
    query_block = lax.dynamic_slice_in_dim(queries, block_start, block_rows, 0)
    scores = jnp.einsum(
        "bhd,ld->hbl", query_block, keys, preferred_element_type=jnp.float32
    ) * HEAD_DIM ** (-0.5)
    row_index = block_start + jnp.arange(block_rows)
    column_index = jnp.arange(length)
    allowed = column_index[None, :] <= row_index[:, None]
    return (query_block, jnp.where(allowed[None], scores, -1e30))


def attend_forward(queries, keys, values):
    length = keys.shape[0]
    block_rows = min(512, length)
    block_count = length // block_rows

    def one_block(block_start):
        query_block, scores = masked_scores(queries, keys, block_start, block_rows)
        row_max = jnp.max(scores, axis=-1, keepdims=True)
        exponent = jnp.exp(scores - row_max)
        row_total = jnp.sum(exponent, axis=-1, keepdims=True)
        probability = (exponent / row_total).astype(jnp.bfloat16)
        result = jnp.einsum("hbl,ld->bhd", probability, values, preferred_element_type=jnp.float32)
        return (result.astype(jnp.bfloat16), (row_max + jnp.log(row_total))[..., 0])

    results, log_totals = lax.map(one_block, jnp.arange(block_count) * block_rows)
    return (results.reshape(length, queries.shape[1], queries.shape[2]), log_totals)


def attend_backward(queries, keys, values, log_totals, grad_out):
    length = keys.shape[0]
    block_rows = min(512, length)
    block_count = length // block_rows
    score_scale = HEAD_DIM ** (-0.5)

    def one_block(running, inputs):
        grad_keys, grad_values = running
        block_start, log_block = inputs
        query_block, scores = masked_scores(queries, keys, block_start, block_rows)
        grad_block = lax.dynamic_slice_in_dim(grad_out, block_start, block_rows, 0)
        probability = jnp.exp(scores - log_block[..., None])
        grad_probs = jnp.einsum(
            "bhd,ld->hbl", grad_block, values, preferred_element_type=jnp.float32
        )
        row_delta = jnp.sum(probability * grad_probs, axis=-1, keepdims=True)
        grad_scores = (probability * (grad_probs - row_delta)).astype(jnp.bfloat16)
        grad_query = (
            jnp.einsum("hbl,ld->bhd", grad_scores, keys, preferred_element_type=jnp.float32)
            * score_scale
        )
        grad_keys = (
            grad_keys
            + jnp.einsum(
                "hbl,bhd->ld", grad_scores, query_block, preferred_element_type=jnp.float32
            )
            * score_scale
        )
        grad_values = grad_values + jnp.einsum(
            "hbl,bhd->ld",
            probability.astype(jnp.bfloat16),
            grad_block,
            preferred_element_type=jnp.float32,
        )
        return ((grad_keys, grad_values), grad_query)

    zero_rows = jnp.zeros((length, keys.shape[1]), jnp.float32)
    (grad_keys, grad_values), grad_query = lax.scan(
        one_block, (zero_rows, zero_rows), (jnp.arange(block_count) * block_rows, log_totals)
    )
    return (grad_query.reshape(queries.shape), grad_keys, grad_values)


MESH = pl.DeviceIdType.MESH
VMEM_BYTES = 67_000_000
NN = (((1,), (0,)), ((), ()))
NT = (((1,), (1,)), ((), ()))
TN = (((0,), (0,)), ((), ()))


def matmul(left, right, dims):
    return lax.dot_general(left, right, dims, preferred_element_type=jnp.float32)


def ring_place(index, size):
    side = index % 2
    return (index // 2) * (1 - side) + (size - 1 - index // 2) * side


def ring_member(place, size):
    side = place // (size // 2)
    return 2 * (place * (1 - side) + (size - 1 - place) * side) + side


def seq_partners(seq):
    core = seq + 1 - 2 * (seq % 2)
    far = (seq + 2) % 4
    return core, far, (core + 2) % 4


def greet(targets):
    barrier = pltpu.get_barrier_semaphore()
    for target in targets:
        pl.semaphore_signal(barrier, inc=1, device_id=target, device_id_type=MESH)
    pl.semaphore_wait(barrier, len(targets))


def for_blocks(width, block, body):
    for at in range(0, width, block):
        body(pl.ds(at, min(block, width - at)))


def loop_blocks(width, block, body):
    @pl.loop(0, width // block)
    def _(at):
        body(pl.ds(pl.multiple_of(at * block, block), block))


def turn_tables(trig):
    lane = lax.broadcasted_iota(jnp.int32, trig.shape, 1)
    swapped = pltpu.roll(trig, HEAD_DIM // 2, 1)
    first = lane < HEAD_DIM // 2
    return jnp.where(first, trig, swapped), jnp.where(first, -swapped, trig)


def head_columns(at):
    return slice(at * HEAD_DIM, (at + 1) * HEAD_DIM)


def causal(scores, start):
    rows = lax.broadcasted_iota(jnp.int32, scores.shape, 0) + start
    columns = lax.broadcasted_iota(jnp.int32, scores.shape, 1)
    return jnp.where(columns <= rows, scores, -1e30)


def inverse_of(values):
    return lax.rsqrt(jnp.mean(values * values, axis=-1, keepdims=True) + norm_eps)


def attend_forward_kernel(
    size,
    block,
    bias_share,
    rows_ref,
    trig_ref,
    qkv_ref,
    proj_ref,
    small_ref,
    cot_ref,
    normed_out,
    heads_out,
    attended_out,
    log_out,
    piece_out,
    proj_out,
    trig_out,
    gains_out,
    normed_two_out,
    resid_out,
    cots_out,
    rows_all,
    trig_all,
    pieces,
    proj,
    smalls,
    cots,
    normed,
    heads,
    attended,
    logs,
    part,
    gains,
    bias,
    resid,
    seq_in,
    far_sum,
    normed_two,
    load_sems,
    column_sems,
    store_sems,
    ring_sems,
    small_sems,
    cot_sems,
    cot_store_sems,
    seq_sems,
    sum_sems,
    proj_send,
    proj_recv,
):
    f32, bf16 = jnp.float32, jnp.bfloat16
    depth = qkv_ref.shape[0]
    tokens, width = rows_ref.shape
    half = depth // 2
    cot_half = tokens // 2
    own = proj.shape[0]
    used = own + 2 * HEAD_DIM
    count = own // HEAD_DIM
    length = part.shape[0]
    per_group = own // depth
    scale = HEAD_DIM**-0.5
    me = lax.axis_index("fsdp")
    seq = lax.axis_index("seq")
    place = ring_place(me, size)
    right = ring_member((place + 1) % size, size)
    left = ring_member((place + size - 1) % size, size)
    core, far, diagonal = seq_partners(seq)
    ring = ({"fsdp": right}, {"fsdp": left})

    def remote(source, target, sems, at, device):
        return pltpu.make_async_remote_copy(
            src_ref=source,
            dst_ref=target,
            send_sem=sems.at[(0,) + at],
            recv_sem=sems.at[(1,) + at],
            device_id=device,
            device_id_type=MESH,
        )

    width_query = 4 * own
    own_lane = pl.multiple_of(seq * own, HEAD_DIM)
    kv_lane = pl.multiple_of(width_query + (seq // 2) * HEAD_DIM, HEAD_DIM)
    value_lane = pl.multiple_of(kv_lane + KV_HEADS * HEAD_DIM, HEAD_DIM)
    my_rows = pl.ds(pl.multiple_of(me * depth, 16), depth)
    column_loads = [
        pltpu.make_async_copy(
            source.at[:, pl.ds(lane_at, lanes)],
            pieces.at[my_rows, pl.ds(target, lanes)],
            column_sems.at[at],
        )
        for at, (source, lane_at, target, lanes) in enumerate(
            (
                (qkv_ref, own_lane, 0, own),
                (qkv_ref, kv_lane, own, HEAD_DIM),
                (qkv_ref, value_lane, own + HEAD_DIM, HEAD_DIM),
                (proj_ref, own_lane, used, own),
            )
        )
    ]
    loads = [
        pltpu.make_async_copy(trig_ref, trig_all.at[seq], load_sems.at[0]),
        pltpu.make_async_copy(rows_ref, rows_all.at[seq], load_sems.at[1]),
        pltpu.make_async_copy(cot_ref, cots.at[me], load_sems.at[2]),
    ]
    for load in column_loads + loads:
        load.start()
    smalls[me] = jnp.zeros(smalls.shape[1:], f32)
    for at in range(3):
        smalls[me, at : at + 1, :] = small_ref[:, at * 256 : (at + 1) * 256]
    greet(ring + ({"seq": core}, {"seq": far}, {"seq": diagonal}))

    def piece_of(step, side):
        return ring_member((place + size - step if side == 0 else place + step) % size, size)

    def ring_copy(step, side, sub):
        part_rows = half // 2
        start = piece_of(step, side) * depth + side * half + sub * part_rows
        span = pieces.at[pl.ds(pl.multiple_of(start, 16), part_rows)]
        return remote(span, span, ring_sems, (side, sub, step), ring[side])

    def small_copy(step):
        span = smalls.at[piece_of(step, 0)]
        return remote(span, span, small_sems, (step,), ring[0])

    def cot_copy(step, side, sub):
        part_rows = cot_half // 2
        start = side * cot_half + sub * part_rows
        span = cots.at[piece_of(step, side), pl.ds(start, part_rows)]
        return remote(span, span, cot_sems, (side, sub, step), ring[side])

    def cot_store(step, side):
        span = (piece_of(step, side), pl.ds(side * cot_half, cot_half))
        return pltpu.make_async_copy(
            cots.at[span], cots_out.at[span], cot_store_sems.at[side, step]
        )

    def seq_copy(which, block_at, target, at):
        span = (rows_all, trig_all)[which].at[block_at]
        return remote(span, span, seq_sems, (which, at), {"seq": target})

    def proj_part(step, side):
        at = piece_of(step, side)
        row = pl.multiple_of((at % per_group) * depth + side * half, 16)
        source = pieces.at[
            pl.ds(pl.multiple_of(at * depth + side * half, 16), half), pl.ds(used, own)
        ]
        target = proj.at[pl.ds(row, half), pl.ds(pl.multiple_of(seq * own, 128), own)]
        return at, at // per_group, source, target

    def proj_copy(step, side):
        at, owner, source, target = proj_part(step, side)
        return owner, pltpu.make_async_remote_copy(
            src_ref=source,
            dst_ref=target,
            send_sem=proj_send.at[side, step],
            recv_sem=proj_recv.at[seq, at % per_group, side],
            device_id={"seq": owner},
            device_id_type=MESH,
        )

    def proj_act(step, side, action):
        owner, copy = proj_copy(step, side)

        @pl.when(owner != seq)
        def _():
            if action == "start":
                copy.start()
            else:
                copy.wait_send()

        @pl.when(owner == seq)
        def _():
            _, _, source, target = proj_part(step, side)
            kept = pltpu.make_async_copy(source, target, proj_send.at[side, step])
            if action == "start":
                kept.start()
            else:
                kept.wait()

    stores = []

    def store(source, target):
        stores.append(pltpu.make_async_copy(source, target, store_sems.at[len(stores)]))
        stores[-1].start()

    def cot_pump(step):
        for sub in range(2):
            for side in range(2):
                if step >= 1:
                    cot_copy(step - 1, side, sub).wait_recv()
                if step < size - 1:
                    cot_copy(step, side, sub).start()
        for side in range(2):
            cot_store(step, side).start()

    for load in column_loads:
        load.wait()
    for sub in range(2):
        for side in range(2):
            ring_copy(0, side, sub).start()
    small_copy(0).start()
    for which in (1, 0):
        loads[1 - which].wait()
        seq_copy(which, seq, far, 1).start()
        seq_copy(which, seq, core, 0).start()
    for side in range(2):
        proj_act(0, side, "start")
    loads[2].wait()

    for step in range(size - 1):
        for sub in range(2):
            for side in range(2):
                ring_copy(step, side, sub).wait_recv()
                if step < size - 2:
                    ring_copy(step + 1, side, sub).start()
        small_copy(step).wait_recv()
        if step < size - 2:
            small_copy(step + 1).start()
        if step == 1:
            cot_pump(0)
        for side in range(2):
            proj_act(step + 1, side, "start")
        if step == min(1, size - 2):
            for which in (1, 0):
                seq_copy(which, seq, far, 1).wait_recv()
                seq_copy(which, far, core, 2).start()

    gathered = jnp.zeros((8, width), f32)
    small_width = smalls.shape[2]
    for at in range(size):
        held = smalls[at]
        lane = lax.broadcasted_iota(jnp.int32, held.shape, 1)
        wide = jnp.concatenate(
            [
                jnp.where(lane < depth, held, 0.0),
                jnp.zeros((8, width - small_width), f32),
            ],
            axis=1,
        )
        gathered += pltpu.roll(wide, at * depth, 1) if at else wide
        bias[:, at * bias_share : (at + 1) * bias_share] = held[:, :bias_share]
    gains[...] = gathered
    gain_one = gathered[0:1, :]
    gain_two = gathered[1:2, :]
    store(gains, gains_out)
    for which in (1, 0):
        seq_copy(which, seq, core, 0).wait_recv()
        seq_copy(which, far, core, 2).wait_recv()
    store(pieces, piece_out)
    store(trig_all, trig_out)

    own_bias = jnp.concatenate(
        [
            bias[2:3, pl.ds(own_lane, own)],
            bias[2:3, pl.ds(kv_lane, HEAD_DIM)],
            bias[2:3, pl.ds(value_lane, HEAD_DIM)],
        ],
        axis=1,
    )
    for at in range(length // block):
        span = slice(at * block, (at + 1) * block)
        rows = rows_all[at].astype(f32)
        normed[span, :] = (rows * inverse_of(rows) * gain_one).astype(bf16)
        mixed = matmul(normed[span, :], pieces[:, :used], NN) + own_bias
        cosine, sine = turn_tables(trig_all[at])
        for head in range(count + 1):
            turned = mixed[:, head_columns(head)]
            heads[span, head_columns(head)] = (
                turned * cosine + pltpu.roll(turned, HEAD_DIM // 2, 1) * sine
            ).astype(bf16)
        heads[span, head_columns(count + 1)] = mixed[:, head_columns(count + 1)].astype(bf16)
        if at == 0:
            cot_pump(1)
    store(normed, normed_out)
    store(heads, heads_out)

    for peer in (core, far, diagonal):
        for at in range(per_group):
            for side in range(2):
                pltpu.make_async_remote_copy(
                    src_ref=pieces.at[pl.ds(0, half), pl.ds(used, own)],
                    dst_ref=proj.at[pl.ds(0, half), pl.ds(0, own)],
                    send_sem=proj_send.at[side, 0],
                    recv_sem=proj_recv.at[peer, at, side],
                    device_id={"seq": peer},
                    device_id_type=MESH,
                ).wait_recv()
    for step in range(size):
        for side in range(2):
            proj_act(step, side, "wait")
    store(proj, proj_out)

    lane = lax.broadcasted_iota(jnp.int32, (block, HEAD_DIM), 1)
    for start in range(0, length, block):
        span = slice(start, start + block)
        seen = slice(0, start + block)
        logs[span, :] = jnp.zeros((block, HEAD_DIM), f32)

        @pl.loop(0, count)
        def _(at):
            head = pl.ds(pl.multiple_of(at * HEAD_DIM, HEAD_DIM), HEAD_DIM)
            scores = causal(
                matmul(heads[span, head], heads[seen, head_columns(count)], NT) * scale, start
            )
            top = jnp.max(scores, axis=-1, keepdims=True)
            exponent = jnp.exp(scores - top)
            total = jnp.sum(exponent, axis=-1, keepdims=True)
            probability = (exponent / total).astype(bf16)
            attended[span, head] = matmul(
                probability, heads[seen, head_columns(count + 1)], NN
            ).astype(bf16)
            logs[span, :] = jnp.where(lane == at, top + jnp.log(total), logs[span, :])

        if 2 * (start + block) == length:
            cot_pump(2)
    store(attended, attended_out)
    store(logs, log_out)

    def out_part(span):
        part[:, span] = matmul(attended[...], proj[:, span], NN).astype(bf16)

    for_blocks(width, 512, out_part)

    def part_rows(at):
        return part.at[pl.ds(pl.multiple_of(at * tokens, tokens), tokens)]

    to_core = [
        remote(part_rows(diagonal), seq_in.at[0], sum_sems, (0,), {"seq": core}),
        remote(part_rows(core), seq_in.at[1], sum_sems, (1,), {"seq": core}),
    ]
    to_far = remote(far_sum, seq_in.at[2], sum_sems, (2,), {"seq": far})
    for copy in to_core:
        copy.start()
    cot_pump(3)
    to_core[0].wait_recv()
    far_sum[...] = (part_rows(far)[...].astype(f32) + seq_in[0].astype(f32)).astype(bf16)
    to_far.start()
    to_core[1].wait_recv()
    resid[...] = (
        part_rows(seq)[...].astype(f32) + seq_in[1].astype(f32) + rows_all[seq].astype(f32)
    )
    cot_pump(4)
    cot_pump(5)
    to_far.wait_recv()
    resid[...] += seq_in[2].astype(f32)
    store(resid, resid_out)
    normed_two[...] = (resid[...] * inverse_of(resid[...]) * gain_two).astype(bf16)
    store(normed_two, normed_two_out)
    for step in range(6, size):
        cot_pump(step)
    for step in range(size):
        for side in range(2):
            cot_store(step, side).wait()

    for step in range(size - 1):
        for side in range(2):
            for sub in range(2):
                ring_copy(step, side, sub).wait_send()
                cot_copy(step, side, sub).wait_send()
        small_copy(step).wait_send()
    for which in (1, 0):
        seq_copy(which, seq, core, 0).wait_send()
        seq_copy(which, seq, far, 1).wait_send()
        seq_copy(which, far, core, 2).wait_send()
    for copy in to_core + [to_far]:
        copy.wait_send()
    for copy in stores:
        copy.wait()


def attend_group(rows, trig, qkv_weight, out_weight, small, bias_share, cots):
    size = lax.axis_size("fsdp")
    groups = lax.axis_size("seq")
    tokens, width = rows.shape
    depth = qkv_weight.shape[0]
    own = width // groups
    used = own + 2 * HEAD_DIM
    joint = used + own
    length = tokens * groups
    f32, bf16 = jnp.float32, jnp.bfloat16
    dma = pltpu.SemaphoreType.DMA
    anywhere = pl.BlockSpec(memory_space=pl.ANY)
    normed = ((length, width), bf16)
    heads = ((length, used), bf16)
    attended = ((length, own), bf16)
    logs = ((length, HEAD_DIM), f32)
    pieces = ((width, joint), bf16)
    proj = ((own, width), bf16)
    trig_all = ((groups,) + trig.shape, f32)
    gains = ((8, width), f32)
    rows_all = ((groups, tokens, width), bf16)
    own_rows = ((tokens, width), bf16)
    resid = ((tokens, width), f32)
    cots_all = ((size, tokens, width), bf16)
    outs = (
        normed, heads, attended, logs, pieces, proj, trig_all, gains, own_rows, resid, cots_all
    )
    held = (
        rows_all,
        trig_all,
        pieces,
        proj,
        ((size, 8, 256), f32),
        cots_all,
        normed,
        heads,
        attended,
        logs,
        normed,
        gains,
        ((8, size * bias_share), f32),
        resid,
        ((3, tokens, width), bf16),
        own_rows,
        own_rows,
    )
    return pl.pallas_call(
        functools.partial(attend_forward_kernel, size, tokens, bias_share),
        out_shape=tuple(jax.ShapeDtypeStruct(*shape) for shape in outs),
        in_specs=[anywhere] * 4 + [pl.BlockSpec(memory_space=pltpu.VMEM), anywhere],
        out_specs=(anywhere,) * len(outs),
        scratch_shapes=[pltpu.VMEM(*shape) for shape in held]
        + [
            dma((3,)),
            dma((4,)),
            dma((len(outs),)),
            dma((2, 2, 2, size)),
            dma((2, size)),
            dma((2, 2, 2, size)),
            dma((2, size)),
            dma((2, 2, 3)),
            dma((2, 3)),
            dma((2, size)),
            dma((groups, own // depth, 2)),
        ],
        compiler_params=pltpu.CompilerParams(
            collective_id=1, has_side_effects=True, vmem_limit_bytes=VMEM_BYTES
        ),
        name="attend_forward",
    )(
        rows,
        trig,
        qkv_weight,
        out_weight,
        small,
        cots,
    )


CHUNKS = 5
IN_LOOP = ((2, 1), (4, 2), (6, 3))


def mlp_kernel(
    size,
    normed_ref,
    resid_ref,
    gain_ref,
    cots_ref,
    gate_ref,
    up_ref,
    down_ref,
    outs_ref,
    back_ref,
    gain_grad_ref,
    sums_ref,
    far_ref,
    rows_all,
    cots,
    weights,
    grads,
    hid,
    dgate,
    dup,
    resid,
    sums_in,
    backs,
    outs,
    load_sems,
    cot_sems,
    ring_send,
    ring_recv,
    sum_send,
    sum_recv,
    out_sems,
    swap_sems,
    far_sems,
    swap_ready,
):
    tokens, width = normed_ref.shape
    units = gate_ref.shape[0]
    half = tokens // 2
    me = lax.axis_index("fsdp")
    seq = lax.axis_index("seq")
    place = ring_place(me, size)
    right = ring_member((place + 1) % size, size)
    left = ring_member((place + size - 1) % size, size)
    core, far, diagonal = seq_partners(seq)
    sides = ((right, pl.ds(0, half)), (left, pl.ds(half, half)))

    def owner_of(step, side):
        return ring_member((place + size - step if side == 0 else place + step) % size, size)

    own_load = pltpu.make_async_copy(normed_ref, rows_all.at[0], load_sems.at[3])
    resid_load = pltpu.make_async_copy(resid_ref, resid, load_sems.at[4])
    weight_loads = [
        pltpu.make_async_copy(ref, weights.at[at], load_sems.at[at])
        for at, ref in enumerate((gate_ref, up_ref, down_ref))
    ]
    own_load.start()
    greet(({"fsdp": right}, {"fsdp": left}, {"seq": core}, {"seq": far}))

    def cot_copies(step):
        return [
            pltpu.make_async_copy(
                cots_ref.at[
                    pl.ds(
                        pl.multiple_of(owner_of(step, side) * tokens + side * half, half), half
                    )
                ],
                cots.at[step % 2, sides[side][1]],
                cot_sems.at[step % 2, side],
            )
            for side in range(2)
        ]


    def row_copy(step, side):
        target, span = sides[side]
        return pltpu.make_async_remote_copy(
            src_ref=rows_all.at[step, span],
            dst_ref=rows_all.at[step + 1, span],
            send_sem=ring_send.at[side, step],
            recv_sem=ring_recv.at[side, step + 1],
            device_id={"fsdp": target},
            device_id_type=MESH,
        )

    def sum_span(side, sub):
        return pl.ds(side * half + sub * (half // 2), half // 2)

    def sum_copy(step, side, sub):
        target, span = sides[side][0], sum_span(side, sub)
        return pltpu.make_async_remote_copy(
            src_ref=backs.at[step, span],
            dst_ref=sums_in.at[step, span],
            send_sem=sum_send.at[side, sub, step],
            recv_sem=sum_recv.at[side, sub, step],
            device_id={"fsdp": target},
            device_id_type=MESH,
        )

    def sum_step(step):
        for sub in range(2):
            for side in range(2):
                span = sum_span(side, sub)
                if step >= 2:
                    sum_copy(step - 1, side, sub).wait_recv()
                    backs[step, span] = (
                        backs[step, span].astype(jnp.float32)
                        + sums_in[step - 1, span].astype(jnp.float32)
                    ).astype(jnp.bfloat16)
                sum_copy(step, side, sub).start()

    def out_copy(step, side):
        at = pl.multiple_of(owner_of(step, side) * tokens + side * half, half)
        return pltpu.make_async_copy(
            outs.at[step % 2, sides[side][1]], outs_ref.at[pl.ds(at, half)], out_sems.at[side, step]
        )

    def elementwise(step, span):
        rows = rows_all[step]
        gate = matmul(rows, weights[0, span, :], NT)
        up = matmul(rows, weights[1, span, :], NT)
        grad_hidden = matmul(cots[step % 2], weights[2, span, :], NT)
        sigmoid = jax.nn.sigmoid(gate)
        activated = gate * sigmoid
        hid[:, span] = (activated * up).astype(jnp.bfloat16)
        dgate[:, span] = (
            grad_hidden * up * sigmoid * (1.0 + gate * (1.0 - sigmoid))
        ).astype(jnp.bfloat16)
        dup[:, span] = (grad_hidden * activated).astype(jnp.bfloat16)

    own_load.wait()
    for side in range(2):
        row_copy(0, side).start()
    for load in weight_loads + cot_copies(0) + [resid_load]:
        load.start()

    @pl.loop(0, units // 16)
    def _(at):
        zeros = jnp.zeros((3, 16, width), jnp.float32)
        grads[:, pl.ds(pl.multiple_of(at * 16, 16), 16), :] = zeros

    for load in weight_loads:
        load.wait()

    @pl.loop(0, size)
    def _(step):
        slot = step % 2

        @pl.when(step >= 1)
        def _():
            for side in range(2):
                row_copy(step - 1, side).wait_recv()

        @pl.when((step >= 1) & (step < size - 1))
        def _():
            for side in range(2):
                row_copy(step, side).start()

        for load in cot_copies(step):
            load.wait()

        @pl.when(step < size - 1)
        def _():
            for load in cot_copies(step + 1):
                load.start()

        for_blocks(units, 256, functools.partial(elementwise, step))

        def back_part(span):
            backs[step, :, span] = (
                matmul(dgate[...], weights[0, :, span], NN)
                + matmul(dup[...], weights[1, :, span], NN)
            ).astype(jnp.bfloat16)

        for_blocks(width, 256, back_part)

        for when, at in IN_LOOP:

            @pl.when(step == when)
            def _():
                sum_step(at)

        @pl.when(step >= 2)
        def _():
            for side in range(2):
                out_copy(step - 2, side).wait()

        def out_part(span):
            outs[slot, :, span] = matmul(hid[...], weights[2, :, span], NN).astype(jnp.bfloat16)

        for_blocks(width, 256, out_part)
        for side in range(2):
            out_copy(step, side).start()

        def weight_part(span):
            rows, cot = rows_all[step, :, span], cots[slot, :, span]
            grads[0, :, span] += matmul(dgate[...], rows, TN)
            grads[1, :, span] += matmul(dup[...], rows, TN)
            grads[2, :, span] += matmul(hid[...], cot, TN)

        for_blocks(width, 256, weight_part)

    share = units // 2
    kept = pl.multiple_of((seq % 2) * share, 16)
    given = pl.multiple_of((1 - seq % 2) * share, 16)
    chunk = share // CHUNKS
    pl.semaphore_signal(swap_ready, inc=1, device_id={"seq": core}, device_id_type=MESH)

    def to_seq(source, target, sems, at, device):
        return pltpu.make_async_remote_copy(
            src_ref=source,
            dst_ref=target,
            send_sem=sems.at[0, at],
            recv_sem=sems.at[1, at],
            device_id={"seq": device},
            device_id_type=MESH,
        )

    swaps = [
        to_seq(
            weights.at[at, pl.ds(given, share)],
            weights.at[at, pl.ds(given, share)],
            swap_sems,
            at,
            core,
        )
        for at in range(3)
    ]
    waiting = [at for at in range(1, size) if at not in [pair[1] for pair in IN_LOOP]]
    sum_step(waiting[0])
    for at in range(3):

        @pl.loop(0, share // 16)
        def _(block):
            span = pl.ds(pl.multiple_of(given + block * 16, 16), 16)
            weights[at, span, :] = grads[at, span, :].astype(jnp.bfloat16)

        if at == 0:
            pl.semaphore_wait(swap_ready, 1)
        swaps[at].start()

    stores = []

    def kept_rows(at):
        return pl.ds(pl.multiple_of(kept + at * chunk, 16), chunk)

    far_copies = [
        to_seq(weights.at[0, kept_rows(at)], far_ref.at[kept_rows(at)], far_sems, at, far)
        for at in range(CHUNKS)
    ]
    def swap_finish(at):
        swaps[at].wait_recv()

        @pl.loop(0, share // 16)
        def _(block):
            span = pl.ds(pl.multiple_of(kept + block * 16, 16), 16)
            weights[at, span, :] = (
                grads[at, span, :] + weights[at, span, :].astype(jnp.float32)
            ).astype(jnp.bfloat16)

        done = weights.at[at, pl.ds(kept, share)]
        stores.append(
            pltpu.make_async_copy(done, sums_ref.at[at, pl.ds(kept, share)], load_sems.at[at])
        )
        if at == 0:
            for copy in far_copies:
                copy.start()
        stores[-1].start()

    cot_own = pltpu.make_async_copy(
        cots_ref.at[pl.ds(pl.multiple_of(me * tokens, tokens), tokens)],
        cots.at[0],
        load_sems.at[7],
    )
    cot_own.start()
    for turn, at in enumerate(waiting[1:]):
        sum_step(at)
        if turn < 3:
            swap_finish(turn)
    for turn in range(len(waiting) - 1, 3):
        swap_finish(turn)

    for side in range(2):
        for sub in range(2):
            sum_copy(size - 1, side, sub).wait_recv()
    grad_normed = backs[0].astype(jnp.float32) + sums_in[size - 1].astype(jnp.float32)
    resid_load.wait()
    inverse = inverse_of(resid[...])
    unit_rows = resid[...] * inverse
    gain_grad_ref[...] = jnp.sum(grad_normed * unit_rows, axis=0, keepdims=True)
    grad_unit = grad_normed * gain_ref[1:2, :]
    cot_own.wait()
    back_ref[...] = cots[0].astype(jnp.float32) + inverse * (
        grad_unit - unit_rows * jnp.mean(grad_unit * unit_rows, axis=-1, keepdims=True)
    )
    for side in range(2):
        out_copy(size - 2, side).wait()
        out_copy(size - 1, side).wait()

        @pl.loop(0, size - 1)
        def _(step):
            row_copy(step, side).wait_send()
            for sub in range(2):
                sum_copy(step + 1, side, sub).wait_send()

    for copy in swaps + far_copies:
        copy.wait_send()
    for copy in far_copies:
        copy.wait_recv()
    for store in stores:
        store.wait()


def mlp_ring(normed, resid, gain, cots, gate_weight, up_weight, down_weight):
    size = lax.axis_size("fsdp")
    tokens, width = normed.shape
    units = gate_weight.shape[0]
    anywhere = pl.BlockSpec(memory_space=pl.ANY)
    inside = pl.BlockSpec(memory_space=pltpu.VMEM)
    bf16, f32 = jnp.bfloat16, jnp.float32
    dma = pltpu.SemaphoreType.DMA
    return pl.pallas_call(
        functools.partial(mlp_kernel, size),
        out_shape=(
            jax.ShapeDtypeStruct((size * tokens, width), bf16),
            jax.ShapeDtypeStruct((tokens, width), f32),
            jax.ShapeDtypeStruct((1, width), f32),
            jax.ShapeDtypeStruct((3, units, width), bf16),
            jax.ShapeDtypeStruct((units, width), bf16),
        ),
        in_specs=[anywhere, anywhere, inside, anywhere, anywhere, anywhere, anywhere],
        out_specs=(anywhere, inside, inside, anywhere, anywhere),
        scratch_shapes=[
            pltpu.VMEM((size, tokens, width), bf16),
            pltpu.VMEM((2, tokens, width), bf16),
            pltpu.VMEM((3, units, width), bf16),
            pltpu.VMEM((3, units, width), f32),
            pltpu.VMEM((tokens, units), bf16),
            pltpu.VMEM((tokens, units), bf16),
            pltpu.VMEM((tokens, units), bf16),
            pltpu.VMEM((tokens, width), f32),
            pltpu.VMEM((size, tokens, width), bf16),
            pltpu.VMEM((size, tokens, width), bf16),
            pltpu.VMEM((2, tokens, width), bf16),
            dma((9,)),
            dma((2, 2)),
            dma((2, size)),
            dma((2, size)),
            dma((2, 2, size)),
            dma((2, 2, size)),
            dma((2, size)),
            dma((2, 3)),
            dma((2, CHUNKS)),
            pltpu.SemaphoreType.REGULAR,
        ],
        compiler_params=pltpu.CompilerParams(
            collective_id=0, has_side_effects=True, vmem_limit_bytes=VMEM_BYTES
        ),
        name="mlp_ring",
    )(normed, resid, gain, cots, gate_weight, up_weight, down_weight)


def attend_backward_kernel(
    size,
    heads_ref,
    attended_ref,
    log_ref,
    proj_ref,
    weight_ref,
    normed_ref,
    trig_ref,
    hidden_ref,
    resid_grad_ref,
    gain_ref,
    gain_grad_ref,
    resid_ref,
    outs_ref,
    units_in_ref,
    far_gate_in_ref,
    grad_in_ref,
    hidden_out_ref,
    small_ref,
    shards_ref,
    halves_ref,
    far_units_ref,
    units_ref,
    far_gate_ref,
    grads_all,
    grad_heads,
    grad_mixed,
    grad_keys,
    grad_values,
    grad_normed,
    term_qkv,
    term_out,
    out_columns,
    qkv_in,
    out_in,
    qkv_sum,
    out_sum,
    shard,
    shard_all,
    half_shard,
    half_all,
    out_own,
    out_recv,
    out_send,
    resid,
    seq_in,
    far_sum,
    small_in,
    load_sems,
    own_sems,
    out_sems,
    term_sems,
    column_sems,
    seq_sems,
    shard_sems,
    small_sems,
    unit_sems,
    pass_sems,
    share_sems,
    gate_sems,
    grad_sems,
):
    length = heads_ref.shape[0]
    tokens, width = hidden_ref.shape
    used = heads_ref.shape[1]
    own = attended_ref.shape[1]
    count = own // HEAD_DIM
    scale = HEAD_DIM**-0.5
    half = tokens // 2
    block = tokens
    depth = width // size
    chip_pieces = size // 2
    half_width = width // 2
    term_half = depth // 2
    units = units_ref.shape[1]
    f32, bf16 = jnp.float32, jnp.bfloat16
    me = lax.axis_index("fsdp")
    seq = lax.axis_index("seq")
    place = ring_place(me, size)
    right = ring_member((place + 1) % size, size)
    left = ring_member((place + size - 1) % size, size)
    core, far, diagonal = seq_partners(seq)
    rounds = size.bit_length() - 1
    mirrors = [me + (1 - 2 * ((me // 2**at) % 2)) * 2**at for at in range(rounds)]
    ring = ({"fsdp": right}, {"fsdp": left})

    def owner_of(step, side):
        return ring_member((place + size - step if side == 0 else place + step) % size, size)

    def remote(source, target, sems, at, device):
        return pltpu.make_async_remote_copy(
            src_ref=source,
            dst_ref=target,
            send_sem=sems.at[(0,) + at],
            recv_sem=sems.at[(1,) + at],
            device_id=device,
            device_id_type=MESH,
        )

    greet(
        ring
        + ({"seq": core}, {"seq": far})
        + tuple({"fsdp": mirror} for mirror in mirrors)
    )

    def own_load(step, side):
        at = pl.multiple_of(owner_of(step, side) * tokens + side * half, half)
        return pltpu.make_async_copy(
            outs_ref.at[pl.ds(at, half)],
            out_own.at[step % 2, pl.ds(side * half, half)],
            own_sems.at[step % 2, side],
        )

    def out_copy(step, side):
        span = pl.ds(side * half, half)
        return remote(
            out_send.at[step % 2, span], out_recv.at[step, span], out_sems, (side, step), ring[side]
        )

    def out_step(step):
        for side in range(2):
            own_load(step, side).wait()
            if step < size - 1:
                own_load(step + 1, side).start()
            if step >= 3:
                out_copy(step - 2, side).wait_send()
            if step >= 2:
                out_copy(step - 1, side).wait_recv()
        total = out_own[step % 2].astype(f32)
        if step >= 2:
            total += out_recv[step - 1].astype(f32)
        out_send[step % 2] = total.astype(bf16)
        for side in range(2):
            out_copy(step, side).start()

    resid_load = pltpu.make_async_copy(resid_ref, resid, load_sems.at[0])

    def out_finish():
        step = size
        for side in range(2):
            out_copy(step - 2, side).wait_send()
            out_copy(step - 1, side).wait_send()
            out_copy(step - 1, side).wait_recv()
        mine = pltpu.make_async_copy(
            outs_ref.at[pl.ds(pl.multiple_of(me * tokens, tokens), tokens)],
            out_own.at[0],
            load_sems.at[1],
        )
        mine.start()
        mine.wait()
        resid_load.wait()
        hidden_out_ref[...] = (
            resid[...] + out_own[0].astype(f32) + out_recv[size - 1].astype(f32)
        ).astype(bf16)

    share = units // 2
    piece = share // CHUNKS
    kept = (seq % 2) * share

    def unit_slice(ref, at):
        start = pl.multiple_of(kept + (at % CHUNKS) * piece, 16)
        return ref.at[at // CHUNKS, pl.ds(start, piece)]

    def unit_copy(at):
        return remote(
            unit_slice(units_ref, at + CHUNKS), unit_slice(far_units_ref, at), unit_sems, (at,), {"seq": far}
        )

    def unit_pass(at):
        part = unit_slice(far_units_ref, at)
        return remote(part, part, pass_sems, (at,), {"seq": core})

    def unit_share(at):
        part = unit_slice(units_ref, at)
        return remote(part, part, share_sems, (at,), {"seq": core})

    def gate_pass(at):
        part = far_gate_ref.at[pl.ds(pl.multiple_of(kept + at * piece, 16), piece)]
        return remote(part, part, gate_sems, (at,), {"seq": core})

    chunks = 2 * CHUNKS
    starts, passes = iter(range(chunks)), iter(range(chunks))

    def send_units(number):
        for _ in range(number):
            unit_copy(next(starts)).start()

    def pass_units(number):
        for _ in range(number):
            at = next(passes)
            unit_copy(at).wait_recv()
            unit_pass(at).start()

    def grad_copy(source, target, at):
        span = grads_all.at[source]
        return remote(span, span, grad_sems, (at,), {"seq": target})

    to_far_grads = grad_copy(seq, far, 0)
    to_core_grads = grad_copy(seq, core, 1)
    passed_grads = grad_copy(far, core, 2)
    grads_all[seq] = resid_grad_ref[...].astype(bf16)
    to_far_grads.start()
    to_core_grads.start()
    resid_load.start()
    for side in range(2):
        own_load(1, side).start()
    out_step(1)

    grad_keys[...] = jnp.zeros_like(grad_keys)
    grad_values[...] = jnp.zeros_like(grad_values)
    lane = lax.broadcasted_iota(jnp.int32, (block, HEAD_DIM), 1)
    keys = slice(own, own + HEAD_DIM)
    values = slice(own + HEAD_DIM, used)

    def attend_block(at_block):
        start = at_block * block
        span = slice(start, start + block)
        seen = slice(0, start + block)
        cosine, sine = turn_tables(trig_ref[span, :])
        grad_heads[span, :] = matmul(grads_all[at_block], proj_ref[...], NT).astype(bf16)

        @pl.loop(0, count)
        def _(at):
            head = pl.ds(pl.multiple_of(at * HEAD_DIM, HEAD_DIM), HEAD_DIM)
            query = heads_ref[span, head]
            grad = grad_heads[span, head]
            logs = jnp.sum(jnp.where(lane == at, log_ref[span, :], 0.0), axis=-1, keepdims=True)
            scores = causal(matmul(query, heads_ref[seen, keys], NT) * scale, start)
            probability = jnp.exp(scores - logs)
            grad_probs = matmul(grad, heads_ref[seen, values], NT)
            delta = jnp.sum(probability * grad_probs, axis=-1, keepdims=True)
            grad_scores = (probability * (grad_probs - delta)).astype(bf16)
            grad_query = matmul(grad_scores, heads_ref[seen, keys], NN) * scale
            grad_query = grad_query.astype(bf16).astype(f32)
            grad_mixed[span, head] = (
                grad_query * cosine + pltpu.roll(grad_query * sine, HEAD_DIM // 2, 1)
            ).astype(bf16)
            grad_keys[seen, :] += matmul(grad_scores, query, TN) * scale
            grad_values[seen, :] += matmul(probability.astype(bf16), grad, TN)

    @pl.loop(0, 4)
    def _(turn):
        @pl.when(turn == 1)
        def _():
            to_core_grads.wait_recv()

        @pl.when(turn == 2)
        def _():
            to_far_grads.wait_recv()
            passed_grads.start()
            unit_copy(0).start()

        @pl.when(turn == 3)
        def _():
            passed_grads.wait_recv()
            unit_copy(1).start()

        @pl.when(turn == 2)
        def _():
            out_step(2)

        for shared in range(3):
            unit_share(turn * 3 + shared).start()
        gate_pass(turn).start()
        at_block = ((seq // 2 + turn // 2) % 2) * 2 + (seq % 2 + turn % 2) % 2
        for at in range(4):

            @pl.when(at_block == at)
            def _():
                attend_block(at)

    next(starts)
    next(starts)
    send_units(1)
    for shared in range(12, 3 * CHUNKS):
        unit_share(shared).start()
    gate_pass(4).start()
    out_step(3)

    for start in range(0, length, block):
        span = slice(start, start + block)
        cosine, sine = turn_tables(trig_ref[span, :])
        part = grad_keys[span, :].astype(bf16).astype(f32)
        grad_mixed[span, keys] = (
            part * cosine + pltpu.roll(part * sine, HEAD_DIM // 2, 1)
        ).astype(bf16)
        grad_mixed[span, values] = grad_values[span, :].astype(bf16)

    def normed_part(span):
        grad_normed[:, span] = matmul(grad_mixed[...], weight_ref[span, :used], NT).astype(bf16)

    loop_blocks(width, 256, normed_part)

    def block_rows(at):
        return grad_normed.at[pl.ds(pl.multiple_of(at * tokens, tokens), tokens)]

    to_core = [
        remote(block_rows(diagonal), seq_in.at[0], seq_sems, (0,), {"seq": core}),
        remote(block_rows(core), seq_in.at[1], seq_sems, (1,), {"seq": core}),
    ]
    to_far = remote(far_sum, seq_in.at[2], seq_sems, (2,), {"seq": far})
    for copy in to_core:
        copy.start()

    def out_term(span):
        term_out[:, span] = matmul(
            attended_ref[...], grads_all[:, :, span].reshape(length, span.size), TN
        ).astype(bf16)

    loop_blocks(width, 256, out_term)
    my_row = pl.multiple_of((seq % 2) * own, 16)
    my_lane = pl.multiple_of((seq % 2) * half_width, 128)
    core_lane = pl.multiple_of((1 - seq % 2) * half_width, 128)
    columns = remote(
        term_out.at[:, pl.ds(core_lane, half_width)],
        out_columns.at[pl.ds(my_row, own)],
        column_sems,
        (0,),
        {"seq": core},
    )
    columns.start()
    out_columns[pl.ds(my_row, own), :] = term_out[:, pl.ds(my_lane, half_width)]

    def qkv_term(span):
        term_qkv[span, :] = matmul(normed_ref[:, span], grad_mixed[...], TN).astype(bf16)

    loop_blocks(width, 256, qkv_term)
    to_core[0].wait_recv()
    far_sum[...] = (block_rows(far)[...].astype(f32) + seq_in[0].astype(f32)).astype(bf16)
    to_far.start()
    out_step(4)
    small_in[0] = jnp.zeros((8, width), f32)
    small_in[0, 1:2, :] = gain_grad_ref[...]
    bias = jnp.sum(grad_mixed[...].astype(f32), axis=0, keepdims=True)
    small_in[0, 2:3, pl.ds(pl.multiple_of(seq * own, 128), own)] = bias[:, :own]
    kv_lane = pl.multiple_of((seq // 2) * HEAD_DIM, HEAD_DIM)
    small_in[0, 3:4, pl.ds(kv_lane, HEAD_DIM)] = bias[:, keys]
    small_in[0, 3:4, pl.ds(kv_lane + KV_HEADS * HEAD_DIM, HEAD_DIM)] = bias[:, values]

    def term_copy(step, side):
        span = pl.ds(side * term_half, term_half)
        return remote(
            qkv_sum.at[step, span], qkv_in.at[step, span], term_sems, (0, side, step), ring[side]
        )

    def half_copy(step, side):
        span = pl.ds(side * term_half, term_half)
        return remote(
            out_sum.at[step, span], out_in.at[step, span], term_sems, (1, side, step), ring[side]
        )

    def here(owner):
        return owner // chip_pieces == seq // 2

    def half_rows(owner, side):
        start = (owner % chip_pieces) * depth + side * term_half
        return pl.ds(pl.multiple_of(start, 16), term_half)

    def term_step(step):
        for side in range(2):
            span = pl.ds(side * term_half, term_half)
            start = owner_of(step, side) * depth + side * term_half
            total = term_qkv[pl.ds(pl.multiple_of(start, 16), term_half), :].astype(f32)
            if step >= 2:
                term_copy(step - 1, side).wait_recv()
                total += qkv_in[step - 1, span, :].astype(f32)
            qkv_sum[step, span, :] = total.astype(bf16)
            term_copy(step, side).start()

    def half_step(step):
        for side in range(2):
            owner = owner_of(step, side)

            @pl.when(here(owner))
            def _():
                span = pl.ds(side * term_half, term_half)
                total = out_columns[half_rows(owner, side), :].astype(f32)
                if step >= 2:
                    half_copy(step - 1, side).wait_recv()
                    total += out_in[step - 1, span, :].astype(f32)
                out_sum[step, span, :] = total.astype(bf16)
                half_copy(step, side).start()

    def small_copy(at):
        device = ({"seq": core}, {"seq": far})[at] if at < 2 else {"fsdp": mirrors[at - 2]}
        return remote(small_in.at[2 * at], small_in.at[2 * at + 1], small_sems, (at,), device)

    def small_step(at):
        small_copy(at).wait_recv()
        small_in[2 * at + 2] = small_in[2 * at] + small_in[2 * at + 1]

    term_step(1)
    columns.wait_recv()
    half_step(1)
    term_step(2)
    half_step(2)
    out_step(5)
    to_core[1].wait_recv()
    send_units(1)
    to_far.wait_recv()
    rows = hidden_ref[...].astype(f32)
    inverse = lax.rsqrt(jnp.mean(rows * rows, axis=-1, keepdims=True) + norm_eps)
    unit_rows = rows * inverse
    grad_rows = (
        block_rows(seq)[...].astype(f32) + seq_in[1].astype(f32) + seq_in[2].astype(f32)
    )
    small_in[0, 0:1, :] = jnp.sum(grad_rows * unit_rows, axis=0, keepdims=True)
    small_copy(0).start()
    grad_unit = grad_rows * gain_ref[0:1, :]
    grad_in_ref[...] = resid_grad_ref[...] + inverse * (
        grad_unit - unit_rows * jnp.mean(grad_unit * unit_rows, axis=-1, keepdims=True)
    )
    total_rounds = rounds + 2
    small_step(0)
    small_copy(1).start()
    done = 1
    send_units(2)
    for step in range(3, size):
        term_step(step)
        half_step(step)
        if done < total_rounds:
            small_step(done)
            done += 1
            if done < total_rounds:
                small_copy(done).start()
        if step == 3:
            send_units(2)
        if step % 2 == 0:
            pass_units(2)
    while done < total_rounds:
        small_step(done)
        done += 1
        if done < total_rounds:
            small_copy(done).start()
    small_ref[...] = small_in[2 * total_rounds]
    source_chip = here(me)
    for side in range(2):
        span = pl.ds(side * term_half, term_half)
        start = me * depth + side * term_half
        term_copy(size - 1, side).wait_recv()
        shard[span, :] = (
            term_qkv[pl.ds(pl.multiple_of(start, 16), term_half), :].astype(f32)
            + qkv_in[size - 1, span, :].astype(f32)
        ).astype(bf16)

        @pl.when(source_chip)
        def _():
            half_copy(size - 1, side).wait_recv()
            half_shard[span, :] = (
                out_columns[half_rows(me, side), :].astype(f32)
                + out_in[size - 1, span, :].astype(f32)
            ).astype(bf16)

    def shard_copy(source, at, block_at, target):
        return remote(source, shard_all.at[block_at], shard_sems, (at,), {"seq": target})

    def half_move(source, at, target):
        return remote(source, half_all.at[seq % 2], shard_sems, (at,), {"seq": target})

    shard_far = shard_copy(shard, 0, seq, far)
    shard_core = shard_copy(shard, 1, seq, core)
    shard_pass = shard_copy(shard_all.at[far], 2, far, core)
    half_far = half_move(half_shard, 3, far)
    half_core = half_move(half_shard, 4, core)
    half_pass = half_move(half_all.at[seq % 2], 5, core)
    shard_far.start()
    shard_core.start()

    @pl.when(source_chip)
    def _():
        half_far.start()
        half_core.start()
        half_all[seq % 2] = half_shard[...]

    send_units(2)
    shard_all[seq] = shard[...]
    out_step(6)
    shard_far.wait_recv()
    shard_pass.start()

    @pl.when(jnp.logical_not(source_chip))
    def _():
        half_far.wait_recv()
        half_pass.start()

    pass_units(3)
    out_step(7)
    pass_units(3)
    out_finish()
    shard_core.wait_recv()
    shard_pass.wait_recv()
    shard_store = pltpu.make_async_copy(shard_all, shards_ref, load_sems.at[1])
    shard_store.start()

    @pl.when(source_chip)
    def _():
        half_core.wait_recv()
        half_core.wait_send()
        half_far.wait_send()

    @pl.when(jnp.logical_not(source_chip))
    def _():
        half_pass.wait_recv()
        half_pass.wait_send()

    half_store = pltpu.make_async_copy(half_all, halves_ref, load_sems.at[2])
    half_store.start()
    for step in range(1, size):
        for side in range(2):
            term_copy(step, side).wait_send()

            @pl.when(here(owner_of(step, side)))
            def _():
                half_copy(step, side).wait_send()

    for copy in [unit_share(at) for at in range(3 * CHUNKS)] + [
        gate_pass(at) for at in range(CHUNKS)
    ]:
        copy.wait_send()
        copy.wait_recv()
    for at in range(chunks):
        unit_pass(at).wait_recv()
        unit_copy(at).wait_send()
        unit_pass(at).wait_send()
    for at in range(total_rounds):
        small_copy(at).wait_send()
    for copy in to_core + [to_far, columns, shard_far, shard_core, shard_pass]:
        copy.wait_send()
    for copy in (to_far_grads, to_core_grads, passed_grads):
        copy.wait_send()
    shard_store.wait()
    half_store.wait()


def attend_group_backward(
    heads,
    attended,
    logs,
    proj,
    weight,
    normed,
    trig,
    hidden,
    resid_grad,
    gain,
    gain_grad,
    resid,
    outs,
    units,
    far_gate,
):
    size = lax.axis_size("fsdp")
    groups = lax.axis_size("seq")
    length = heads.shape[0]
    tokens, width = hidden.shape
    used = heads.shape[1]
    own = attended.shape[1]
    depth = width // size
    rounds = size.bit_length() + 1
    bf16, f32 = jnp.bfloat16, jnp.float32
    anywhere = pl.BlockSpec(memory_space=pl.ANY)
    inside = pl.BlockSpec(memory_space=pltpu.VMEM)
    dma = pltpu.SemaphoreType.DMA
    vmem = pltpu.VMEM
    return pl.pallas_call(
        functools.partial(attend_backward_kernel, size),
        out_shape=(
            jax.ShapeDtypeStruct((tokens, width), f32),
            jax.ShapeDtypeStruct((tokens, width), bf16),
            jax.ShapeDtypeStruct((8, width), f32),
            jax.ShapeDtypeStruct((groups, depth, used), bf16),
            jax.ShapeDtypeStruct((2, depth, width // 2), bf16),
            jax.ShapeDtypeStruct((2,) + units.shape[1:], bf16),
            jax.ShapeDtypeStruct(units.shape, bf16),
            jax.ShapeDtypeStruct(far_gate.shape, bf16),
        ),
        in_specs=[inside] * 11 + [anywhere] * 4,
        out_specs=(inside, inside, inside) + (anywhere,) * 5,
        input_output_aliases={13: 6, 14: 7},
        scratch_shapes=[
            vmem((groups, tokens, width), bf16),
            vmem((length, own), bf16),
            vmem((length, used), bf16),
            vmem((length, HEAD_DIM), f32),
            vmem((length, HEAD_DIM), f32),
            vmem((length, width), bf16),
            vmem((width, used), bf16),
            vmem((own, width), bf16),
            vmem((2 * own, width // 2), bf16),
            vmem((size, depth, used), bf16),
            vmem((size, depth, width // 2), bf16),
            vmem((size, depth, used), bf16),
            vmem((size, depth, width // 2), bf16),
            vmem((depth, used), bf16),
            vmem((groups, depth, used), bf16),
            vmem((depth, width // 2), bf16),
            vmem((2, depth, width // 2), bf16),
            vmem((2, tokens, width), bf16),
            vmem((size, tokens, width), bf16),
            vmem((2, tokens, width), bf16),
            vmem((tokens, width), f32),
            vmem((3, tokens, width), bf16),
            vmem((tokens, width), bf16),
            vmem((2 * rounds + 1, 8, width), f32),
            dma((3,)),
            dma((2, 2)),
            dma((2, 2, size)),
            dma((2, 2, 2, size)),
            dma((2, 1)),
            dma((2, 3)),
            dma((2, 6)),
            dma((2, rounds)),
            dma((2, 2 * CHUNKS)),
            dma((2, 2 * CHUNKS)),
            dma((2, 3 * CHUNKS)),
            dma((2, CHUNKS)),
            dma((2, 3)),
        ],
        compiler_params=pltpu.CompilerParams(
            collective_id=2, has_side_effects=True, vmem_limit_bytes=VMEM_BYTES
        ),
        name="attend_backward",
    )(
        heads,
        attended,
        logs,
        proj,
        weight,
        normed,
        trig,
        hidden,
        resid_grad,
        gain,
        gain_grad,
        resid,
        outs,
        units,
        far_gate,
    )


def finish_kernel(
    sums_ref,
    far_gate_ref,
    far_ref,
    grad_in_ref,
    hidden_ref,
    shards_ref,
    halves_ref,
    gate_out,
    up_out,
    down_out,
    grad_in_out,
    hidden_out,
    qkv_out,
    proj_out,
):
    f32 = jnp.float32
    gate_out[...] = sums_ref[0].astype(f32) + far_gate_ref[...].astype(f32)
    up_out[...] = sums_ref[1].astype(f32) + far_ref[0].astype(f32)
    down_out[...] = sums_ref[2].astype(f32) + far_ref[1].astype(f32)
    grad_in_out[...] = grad_in_ref[...]
    hidden_out[...] = hidden_ref[...]
    groups, _, used = shards_ref.shape
    own = used - 2 * HEAD_DIM
    for at in range(groups):
        qkv_out[:, at * own : (at + 1) * own] = shards_ref[at, :, :own].astype(f32)
    for which in range(2):
        lanes = slice(own + which * HEAD_DIM, own + (which + 1) * HEAD_DIM)
        for head in range(KV_HEADS):
            at = groups * own + (which * KV_HEADS + head) * HEAD_DIM
            qkv_out[:, at : at + HEAD_DIM] = shards_ref[2 * head, :, lanes].astype(
                f32
            ) + shards_ref[2 * head + 1, :, lanes].astype(f32)
    half = halves_ref.shape[2]
    for which in range(2):
        proj_out[:, which * half : (which + 1) * half] = halves_ref[which].astype(f32)


def finish_totals(unit_sums, far_gate, far_sums, grad_in, hidden, shards, halves):
    f32, bf16 = jnp.float32, jnp.bfloat16
    _, units, width = unit_sums.shape
    groups, depth, used = shards.shape
    joint = groups * (used - 2 * HEAD_DIM) + 2 * KV_HEADS * HEAD_DIM
    tokens = grad_in.shape[0]
    steps, few = 4, 4

    def spec(*dims, many=False):
        lead = len(dims) - 2
        return pl.BlockSpec(
            dims,
            lambda at: (0,) * lead + (at if many else jnp.minimum(at, few - 1), 0),
        )

    rows = units // steps
    return pl.pallas_call(
        finish_kernel,
        grid=(steps,),
        out_shape=(
            jax.ShapeDtypeStruct((units, width), f32),
            jax.ShapeDtypeStruct((units, width), f32),
            jax.ShapeDtypeStruct((units, width), f32),
            jax.ShapeDtypeStruct((tokens, width), f32),
            jax.ShapeDtypeStruct((tokens, width), bf16),
            jax.ShapeDtypeStruct((depth, joint), f32),
            jax.ShapeDtypeStruct((depth, width), f32),
        ),
        in_specs=[
            spec(3, rows, width, many=True),
            spec(rows, width, many=True),
            spec(2, rows, width, many=True),
            spec(tokens // few, width),
            spec(tokens // few, width),
            spec(groups, depth // few, used),
            spec(2, depth // few, width // 2),
        ],
        out_specs=(
            spec(rows, width, many=True),
            spec(rows, width, many=True),
            spec(rows, width, many=True),
            spec(tokens // few, width),
            spec(tokens // few, width),
            spec(depth // few, joint),
            spec(depth // few, width),
        ),
        compiler_params=pltpu.CompilerParams(vmem_limit_bytes=VMEM_BYTES),
        name="finish_totals",
    )(unit_sums, far_gate, far_sums, grad_in, hidden, shards, halves)


def kernels_fit(hidden_in, positions, attn_gain, qkv_weight, qkv_bias, out_weight, *rest):
    size, groups = lax.axis_size("fsdp"), lax.axis_size("seq")
    _, tokens, width = hidden_in.shape
    units = rest[1].shape[0]
    if groups != 4 or size != 8 or tokens % 256 or units % 160 or width % 512:
        return False
    if (width // size) % 32 or qkv_bias.shape[0] > 256 or KV_HEADS != 2:
        return False
    rows = tokens * width * (4 * size + 34)
    return rows + units * (18 * width + 6 * tokens) < 64_000_000


def per_device_kernels(
    hidden_in,
    positions,
    attn_gain,
    qkv_weight,
    qkv_bias,
    out_weight,
    mlp_gain,
    gate_weight,
    up_weight,
    down_weight,
    cotangent,
):
    f32, bf16 = jnp.float32, jnp.bfloat16
    groups = lax.axis_size("seq")
    size = lax.axis_size("fsdp")
    _, tokens, width = hidden_in.shape
    length = tokens * groups
    lane = jnp.arange(HEAD_DIM)
    frequency = jnp.exp(
        -((lane % (HEAD_DIM // 2)).astype(f32) * 2.0 / HEAD_DIM) * math.log(rope_base)
    )
    angles = positions[0].astype(f32)[:, None] * frequency[None, :]
    trig = jnp.where(lane[None, :] < HEAD_DIM // 2, jnp.cos(angles), jnp.sin(angles))
    small = jnp.concatenate(
        [
            jnp.pad(row.astype(f32), (0, 256 - row.shape[0]))
            for row in (attn_gain, mlp_gain, qkv_bias)
        ]
    )[None]
    (
        normed_one,
        heads,
        attended,
        logs,
        weight,
        proj,
        trig_all,
        gains,
        normed_two,
        residual,
        all_cots,
    ) = attend_group(
        hidden_in[0], trig, qkv_weight, out_weight, small, qkv_bias.shape[0], cotangent[0]
    )
    shard = width // size
    outs, grad_residual, term_gain_two, unit_sums, far_gate = mlp_ring(
        normed_two,
        residual,
        gains,
        all_cots.reshape(size * tokens, width),
        gate_weight,
        up_weight,
        down_weight,
    )
    (
        grad_rows,
        hidden_out,
        smalls,
        shards,
        halves,
        far_sums,
        unit_sums,
        far_gate,
    ) = attend_group_backward(
        heads,
        attended,
        logs,
        proj,
        weight,
        normed_one,
        trig_all.reshape(length, HEAD_DIM),
        hidden_in[0],
        grad_residual,
        gains,
        term_gain_two,
        residual,
        outs,
        unit_sums,
        far_gate,
    )
    grad_gate, grad_up, grad_down, grad_rows, hidden_out, grad_qkv, grad_out = finish_totals(
        unit_sums, far_gate, far_sums, grad_rows, hidden_out, shards, halves
    )
    me = lax.axis_index("fsdp")
    bias_sums = jnp.concatenate([smalls[2], smalls[3, : 2 * KV_HEADS * HEAD_DIM]])
    bias_shard = qkv_bias.shape[0]
    return (
        hidden_out[None],
        grad_rows[None],
        lax.dynamic_slice_in_dim(smalls[0], me * shard, shard),
        grad_qkv,
        lax.dynamic_slice_in_dim(bias_sums, me * bias_shard, bias_shard),
        grad_out,
        lax.dynamic_slice_in_dim(smalls[1], me * shard, shard),
        grad_gate,
        grad_up,
        grad_down,
    )


def per_device_gathered(
    hidden_in,
    positions,
    attn_gain,
    qkv_weight,
    qkv_bias,
    out_weight,
    mlp_gain,
    gate_weight,
    up_weight,
    down_weight,
    cotangent,
):
    groups = lax.axis_size("seq")
    group_heads = HEADS // groups
    repeat = groups // KV_HEADS
    tokens = hidden_in.shape[1]
    width_query = HEADS * HEAD_DIM
    width_key = KV_HEADS * HEAD_DIM
    residual = hidden_in[0].astype(jnp.float32)
    cosine, sine = rope_tables(positions[0])
    gains_one, gains_two, qkv_full, bias_full, out_full = (
        lax.all_gather(attn_gain, "fsdp", axis=0, tiled=True),
        lax.all_gather(mlp_gain, "fsdp", axis=0, tiled=True),
        lax.all_gather(qkv_weight, "fsdp", axis=0, tiled=True),
        lax.all_gather(qkv_bias, "fsdp", axis=0, tiled=True),
        lax.all_gather(out_weight, "fsdp", axis=0, tiled=True),
    )
    gain_one = gains_one.astype(jnp.float32)
    gain_two = gains_two.astype(jnp.float32)
    unit_one, inverse_one, normed_one = norm_forward(residual, gain_one)
    qkv_mixed = jnp.dot(
        normed_one, qkv_full, preferred_element_type=jnp.float32
    ) + bias_full.astype(jnp.float32)
    query_part = qkv_mixed[:, :width_query].reshape(tokens, HEADS, HEAD_DIM)
    key_part = qkv_mixed[:, width_query : width_query + width_key].reshape(
        tokens, KV_HEADS, HEAD_DIM
    )
    value_part = qkv_mixed[:, width_query + width_key :].reshape(tokens, KV_HEADS, HEAD_DIM)
    queries = (
        rotate(query_part, cosine, sine)
        .astype(jnp.bfloat16)
        .reshape(tokens, groups, group_heads * HEAD_DIM)
    )
    keys_rep = jnp.repeat(rotate(key_part, cosine, sine).astype(jnp.bfloat16), repeat, axis=1)
    values_rep = jnp.repeat(value_part.astype(jnp.bfloat16), repeat, axis=1)
    head_queries, head_keys, head_values = (
        lax.all_to_all(queries, "seq", split_axis=1, concat_axis=0, tiled=True),
        lax.all_to_all(keys_rep, "seq", split_axis=1, concat_axis=0, tiled=True),
        lax.all_to_all(values_rep, "seq", split_axis=1, concat_axis=0, tiled=True),
    )
    head_queries = head_queries.reshape(-1, group_heads, HEAD_DIM)
    head_keys = head_keys.reshape(-1, HEAD_DIM)
    head_values = head_values.reshape(-1, HEAD_DIM)
    attended, log_totals = attend_forward(head_queries, head_keys, head_values)
    returned = lax.all_to_all(
        attended.reshape(-1, 1, group_heads * HEAD_DIM),
        "seq",
        split_axis=0,
        concat_axis=1,
        tiled=True,
    )
    attn_rows = returned.reshape(tokens, width_query)
    residual_two = residual + jnp.dot(attn_rows, out_full, preferred_element_type=jnp.float32)
    unit_two, inverse_two, normed_two = norm_forward(residual_two, gain_two)
    grad_output = cotangent[0].astype(jnp.float32)
    grad_mlp = grad_output.astype(jnp.bfloat16)
    all_rows = lax.all_gather(normed_two, "fsdp", axis=0, tiled=True)
    gate_pre = jnp.einsum("td,fd->tf", all_rows, gate_weight, preferred_element_type=jnp.float32)
    up_pre = jnp.einsum("td,fd->tf", all_rows, up_weight, preferred_element_type=jnp.float32)
    sigmoid_gate = jax.nn.sigmoid(gate_pre)
    activated = gate_pre * sigmoid_gate
    hidden = (activated * up_pre).astype(jnp.bfloat16)
    partial_out = jnp.dot(hidden, down_weight, preferred_element_type=jnp.float32)
    mlp_out = lax.psum_scatter(
        partial_out.astype(jnp.bfloat16), "fsdp", scatter_dimension=0, tiled=True
    ).astype(jnp.float32)
    all_grads = lax.all_gather(grad_mlp, "fsdp", axis=0, tiled=True)
    grad_hidden = jnp.einsum(
        "tm,fm->tf", all_grads, down_weight, preferred_element_type=jnp.float32
    )
    grad_gate = (
        grad_hidden * up_pre * sigmoid_gate * (1.0 + gate_pre * (1.0 - sigmoid_gate))
    ).astype(jnp.bfloat16)
    grad_up = (grad_hidden * activated).astype(jnp.bfloat16)
    partial_back = jnp.dot(grad_gate, gate_weight, preferred_element_type=jnp.float32) + jnp.dot(
        grad_up, up_weight, preferred_element_type=jnp.float32
    )
    grad_normed_two = lax.psum_scatter(partial_back, "fsdp", scatter_dimension=0, tiled=True)
    shard_gate = jnp.einsum("tf,td->fd", grad_gate, all_rows, preferred_element_type=jnp.float32)
    shard_up = jnp.einsum("tf,td->fd", grad_up, all_rows, preferred_element_type=jnp.float32)
    shard_down = jnp.einsum("tf,td->fd", hidden, all_grads, preferred_element_type=jnp.float32)
    hidden_out = (residual_two + mlp_out).astype(jnp.bfloat16)
    grad_norm_two, term_gain_two = norm_backward(grad_normed_two, unit_two, inverse_two, gain_two)
    grad_residual_two = grad_output + grad_norm_two
    grad_proj = grad_residual_two.astype(jnp.bfloat16)
    grad_attn_rows = jnp.einsum(
        "td,ed->te", grad_proj, out_full, preferred_element_type=jnp.float32
    ).astype(jnp.bfloat16)
    term_out = jnp.einsum("te,td->ed", attn_rows, grad_proj, preferred_element_type=jnp.float32)
    grad_heads = lax.all_to_all(
        grad_attn_rows.reshape(tokens, groups, group_heads * HEAD_DIM),
        "seq",
        split_axis=1,
        concat_axis=0,
        tiled=True,
    )
    grad_query, grad_keys, grad_values = attend_backward(
        head_queries,
        head_keys,
        head_values,
        log_totals,
        grad_heads.reshape(-1, group_heads, HEAD_DIM),
    )
    back_query, back_keys, back_values = (
        lax.all_to_all(
            grad_query.astype(jnp.bfloat16).reshape(-1, 1, group_heads * HEAD_DIM),
            "seq",
            split_axis=0,
            concat_axis=1,
            tiled=True,
        ),
        lax.all_to_all(
            grad_keys.astype(jnp.bfloat16)[:, None, :],
            "seq",
            split_axis=0,
            concat_axis=1,
            tiled=True,
        ),
        lax.all_to_all(
            grad_values.astype(jnp.bfloat16)[:, None, :],
            "seq",
            split_axis=0,
            concat_axis=1,
            tiled=True,
        ),
    )
    grad_query_rows = unrotate(
        back_query.reshape(tokens, HEADS, HEAD_DIM).astype(jnp.float32), cosine, sine
    )
    grad_key_rows = unrotate(
        jnp.sum(back_keys.astype(jnp.float32).reshape(tokens, KV_HEADS, repeat, HEAD_DIM), axis=2),
        cosine,
        sine,
    )
    grad_value_rows = jnp.sum(
        back_values.astype(jnp.float32).reshape(tokens, KV_HEADS, repeat, HEAD_DIM), axis=2
    )
    grad_mixed = jnp.concatenate(
        [
            grad_query_rows.reshape(tokens, width_query),
            grad_key_rows.reshape(tokens, width_key),
            grad_value_rows.reshape(tokens, width_key),
        ],
        axis=1,
    ).astype(jnp.bfloat16)
    term_qkv = jnp.einsum("td,tc->dc", normed_one, grad_mixed, preferred_element_type=jnp.float32)
    term_bias = jnp.sum(grad_mixed.astype(jnp.float32), axis=0)
    grad_normed_one = jnp.einsum(
        "tc,dc->td", grad_mixed, qkv_full, preferred_element_type=jnp.float32
    )
    grad_norm_one, term_gain_one = norm_backward(grad_normed_one, unit_one, inverse_one, gain_one)
    grad_rows = grad_residual_two + grad_norm_one
    shard_gain_one, shard_qkv, shard_bias, shard_out, shard_gain_two = (
        lax.psum_scatter(
            term_gain_one.astype(jnp.bfloat16), "fsdp", scatter_dimension=0, tiled=True
        ).astype(jnp.float32),
        lax.psum_scatter(
            term_qkv.astype(jnp.bfloat16), "fsdp", scatter_dimension=0, tiled=True
        ).astype(jnp.float32),
        lax.psum_scatter(
            term_bias.astype(jnp.bfloat16), "fsdp", scatter_dimension=0, tiled=True
        ).astype(jnp.float32),
        lax.psum_scatter(
            term_out.astype(jnp.bfloat16), "fsdp", scatter_dimension=0, tiled=True
        ).astype(jnp.float32),
        lax.psum_scatter(
            term_gain_two.astype(jnp.bfloat16), "fsdp", scatter_dimension=0, tiled=True
        ).astype(jnp.float32),
    )
    totals = (
        lax.psum(shard_gain_one.astype(jnp.bfloat16), "seq").astype(jnp.float32),
        lax.psum(shard_qkv.astype(jnp.bfloat16), "seq").astype(jnp.float32),
        lax.psum(shard_bias.astype(jnp.bfloat16), "seq").astype(jnp.float32),
        lax.psum(shard_out.astype(jnp.bfloat16), "seq").astype(jnp.float32),
        lax.psum(shard_gain_two.astype(jnp.bfloat16), "seq").astype(jnp.float32),
        lax.psum(shard_gate.astype(jnp.bfloat16), "seq").astype(jnp.float32),
        lax.psum(shard_up.astype(jnp.bfloat16), "seq").astype(jnp.float32),
        lax.psum(shard_down.astype(jnp.bfloat16), "seq").astype(jnp.float32),
    )
    return (
        hidden_out[None],
        grad_rows[None],
        totals[0],
        totals[1],
        totals[2],
        totals[3],
        totals[4],
        totals[5],
        totals[6],
        totals[7],
    )


def per_device(*arguments):
    return (per_device_kernels if kernels_fit(*arguments) else per_device_gathered)(*arguments)


def solution(mesh):
    placed = (
        P("fsdp", "seq", None),
        P("fsdp", "seq"),
        P("fsdp"),
        P("fsdp", None),
        P("fsdp"),
        P("fsdp", None),
        P("fsdp"),
        P("fsdp", None),
        P("fsdp", None),
        P("fsdp", None),
        P("fsdp", "seq", None),
    )
    return jax.shard_map(
        per_device,
        mesh=mesh,
        in_specs=placed,
        out_specs=(
            P("fsdp", "seq", None),
            P("fsdp", "seq", None),
            P("fsdp"),
            P("fsdp", None),
            P("fsdp"),
            P("fsdp", None),
            P("fsdp"),
            P("fsdp", None),
            P("fsdp", None),
            P("fsdp", None),
        ),
        check_vma=False,
    )
```
